32 devices in a mesh: section: 4 (over y, x), dp: 8 (over z, core).
Axes of the slice: x: 2, y: 2, z: 4, core: 2. Of those that a mesh axis runs over, the one named last changes fastest.
Arguments:
- latents: bfloat16 [2048, 1536], P('dp'), may hold values from -6 to 6
- media: bfloat16 [8192, 1536], P('dp'), may hold values from -6 to 6
- segment_ids: int32 [8, 1024], P('dp'), may hold values from -1 to 3, as said below
- slot_map: int32 [8, 4], P('dp'), may hold values from 0 to 3, each once within a row
- gains: float32 [2, 3, 1536], P(None, None, ('section', 'dp')), may hold values from 0.5 to 1.5
- w_query: bfloat16 [4, 1536, 768], P('section', 'dp'), may hold values from -0.15625 to 0.15625
- w_key: bfloat16 [4, 1536, 768], P('section', 'dp'), may hold values from -0.15625 to 0.15625
- w_value: bfloat16 [4, 1536, 768], P('section', 'dp'), may hold values from -0.15625 to 0.15625
- w_out: bfloat16 [4, 768, 1536], P('section', 'dp'), may hold values from -1.25 to 1.25
- w_up: bfloat16 [4, 1536, 3072], P('section', 'dp'), may hold values from -0.15625 to 0.15625
- w_down: bfloat16 [4, 3072, 1536], P('section', 'dp'), may hold values from -0.078125 to 0.078125
- cotangent: bfloat16 [2048, 1536], P('dp'), may hold values from -6 to 6
Outputs:
- latents_out: float32 [2048, 1536], P('dp', 'section')
- latent_grad: float32 [2048, 1536], P('dp', 'section')
- media_grad: float32 [8192, 1536], P('dp')
- gain_grad: float32 [2, 3, 1536], P(None, None, ('section', 'dp'))
- query_grad: float32 [4, 1536, 768], P('section', 'dp')
- key_grad: float32 [4, 1536, 768], P('section', 'dp')
- value_grad: float32 [4, 1536, 768], P('section', 'dp')
- out_grad: float32 [4, 768, 1536], P('section', 'dp')
- up_grad: float32 [4, 1536, 3072], P('section', 'dp')
- down_grad: float32 [4, 3072, 1536], P('section', 'dp')
The draws below stay inside these ranges and needn't reach their ends.
Inputs may be any that keep to these rules, and one draw needn't show every extreme that they name: `segment_ids`: in each sequence, images 0 to 3 each hold one run of one or more consecutive rows, in that order, and one or more pad rows (-1) follow them. `slot_map`: each row is a permutation of 0 to 3.
All inputs are finite; a program needn't handle non-finite values.
Results may differ from the reference program's by a relative error of at most 0.024.
Values may be sent and summed in bfloat16 or wider, within the bound.
No kernel may reach another device: no remote copies, remote signals or barrier semaphores. Data moves between devices by JAX's collectives and lax.ppermute only.
A program may use at most 256 MiB of HBM per device.

```python
import math
import jax
import jax.numpy as jnp
from jax import lax

D = 1536
HEADS = 16
HEAD_DIM = 96
FF = 6144
LATENTS = 64
LAYERS = 2
SEQ = 1024
SLOTS = 4
INNER = 1536
SEQS = 8
LAT_ROWS = 2048
MEDIA_ROWS = 8192


def draw_segment_ids(key, part):
    low_count = SEQ // (2 * SLOTS)
    high_count = SEQ * 15 // (16 * SLOTS)
    counts = jax.random.randint(key, (SEQS, SLOTS), low_count, high_count + 1, dtype=jnp.int32)
    boundary = jnp.cumsum(counts, axis=1)
    position = jnp.arange(SEQ, dtype=jnp.int32)[None, :, None]
    image_index = jnp.sum((position >= boundary[:, None, :]).astype(jnp.int32), axis=2)
    return jnp.where(image_index < SLOTS, image_index, -1).astype(jnp.int32)


def block_scale(key, extent, cuts, least, top_value):
    def one(axis_at, blocks):
        steps = jax.random.uniform(jax.random.fold_in(jax.random.fold_in(key, 6), axis_at), (blocks,), jnp.float32, least / len(cuts), top_value / len(cuts))
        return jnp.repeat(jnp.exp(steps), extent[axis_at] // blocks).reshape((-1,) + (1,) * (len(extent) - axis_at - 1))

    level = one(*cuts[0])
    for cut in cuts[1:]:
        level = level * one(*cut)
    return level


def centred(key, extent, spread, reach, split=(), held_as=jnp.bfloat16):
    drawn = spread * jax.random.normal(key, extent, jnp.float32)
    if split:
        drawn = drawn * block_scale(key, extent, split, -0.22, 0.18)
    return jnp.clip(drawn, -reach, reach).astype(held_as)


def setup_inputs(seed: int = 0) -> dict:
    key_list = jax.random.split(jax.random.key(seed), 13)
    return {
        "latents": centred(key_list[0], (LAT_ROWS, D), 1.0, 6.0, ((0, 8),)),
        "media": centred(key_list[1], (MEDIA_ROWS, D), 1.0, 6.0, ((0, 8),)),
        "segment_ids": draw_segment_ids(jax.random.fold_in(key_list[12], 71), 0),
        "slot_map": jax.vmap(lambda own: jax.random.permutation(own, SLOTS))(jax.random.split(key_list[3], SEQS)).reshape((SEQS, SLOTS)).astype(jnp.int32),
        "gains": jnp.clip(1.0 + 0.1 * jax.random.normal(key_list[4], (LAYERS, 3, D), jnp.float32), 0.5, 1.5),
        "w_query": centred(key_list[5], (2 * LAYERS, D, INNER // 2), D ** -0.5, 0.15625, ((0, 4), (1, 8))),
        "w_key": centred(key_list[6], (2 * LAYERS, D, INNER // 2), D ** -0.5, 0.15625, ((0, 4), (1, 8))),
        "w_value": centred(key_list[7], (2 * LAYERS, D, INNER // 2), D ** -0.5, 0.15625, ((0, 4), (1, 8))),
        "w_out": centred(key_list[8], (2 * LAYERS, INNER // 2, D), (INNER // 64) ** -0.5, 1.25, ((0, 4), (1, 8))),
        "w_up": centred(key_list[9], (2 * LAYERS, D, FF // 2), D ** -0.5, 0.15625, ((0, 4), (1, 8))),
        "w_down": centred(key_list[10], (2 * LAYERS, FF // 2, D), FF ** -0.5, 0.078125, ((0, 4), (1, 8))),
        "cotangent": centred(key_list[11], (LAT_ROWS, D), 1.0, 6.0, ((0, 8),)),
    }


@jax.custom_vjp
def low(v):
    return lax.optimization_barrier(v.astype(jnp.bfloat16)).astype(jnp.float32)

@jax.custom_vjp
def low_back(v):
    return v

def low_keep(v):
    return (low(v), None)

def low_pass(kept, grad):
    return (grad,)

def back_keep(v):
    return (v, None)

def back_low(kept, grad):
    return (low(grad),)
low.defvjp(low_keep, low_pass)
low_back.defvjp(back_keep, back_low)
epsilon = 1e-05

def round_both(values):
    return low(low_back(values))

def product(left, right):
    return jnp.dot(left, right, precision=lax.Precision.HIGHEST, preferred_element_type=jnp.float32)

def normalize(values, gain_row):
    centered = values - lax.optimization_barrier(jnp.mean(values, axis=-1, keepdims=True))
    variance = lax.optimization_barrier(jnp.mean(centered * centered, axis=-1, keepdims=True))
    return centered * lax.rsqrt(variance + epsilon) * gain_row

def attend_sequence(pieces):
    query_heads, key_heads, value_heads, key_slot = pieces
    query_slot = jnp.arange(query_heads.shape[0], dtype=jnp.int32) // LATENTS
    score_scale = 1.0 / math.sqrt(HEAD_DIM)
    scores = jnp.einsum('qhd,khd->hqk', query_heads, key_heads, precision=lax.Precision.HIGHEST)
    scores = low_back(scores * score_scale)
    allowed = query_slot[:, None] == key_slot[None, :]
    scores = jnp.where(allowed[None], scores, -1e+30)
    row_max = lax.optimization_barrier(jnp.max(scores, axis=-1, keepdims=True))
    exponent = jnp.exp(scores - row_max)
    weights_low = low(exponent / lax.optimization_barrier(jnp.sum(exponent, axis=-1, keepdims=True)))
    attended = jnp.einsum('hqk,khd->qhd', weights_low, value_heads, precision=lax.Precision.HIGHEST)
    return attended.reshape(attended.shape[0], -1)

def cross_attention(latent_rows, media_rows, gain_media, gain_latent, query_w, key_w, value_w, out_w, key_slot):
    seq_total = key_slot.shape[0]
    head_shape = (seq_total, -1, HEADS, HEAD_DIM)
    media_low = low(normalize(media_rows, gain_media))
    latent_low = low(normalize(latent_rows, gain_latent))
    query_heads = round_both(product(latent_low, query_w)).reshape(head_shape)
    media_key = round_both(product(media_low, key_w)).reshape(head_shape)
    media_value = round_both(product(media_low, value_w)).reshape(head_shape)
    latent_key = round_both(product(latent_low, key_w)).reshape(head_shape)
    latent_value = round_both(product(latent_low, value_w)).reshape(head_shape)
    key_heads = jnp.concatenate([media_key, latent_key], axis=1)
    value_heads = jnp.concatenate([media_value, latent_value], axis=1)
    attended = lax.map(jax.checkpoint(attend_sequence), (query_heads, key_heads, value_heads, key_slot))
    attended = round_both(attended.reshape(latent_rows.shape[0], -1))
    return latent_rows + low_back(product(attended, out_w))

def feed_forward(latent_rows, gain_ffn, up_w, down_w):
    ffn_low = low(normalize(latent_rows, gain_ffn))
    hidden_pre = low_back(product(ffn_low, up_w))
    active_low = low(jax.nn.gelu(hidden_pre, approximate=False))
    return latent_rows + low_back(product(active_low, down_w))

def reference(latents, media, segment_ids, slot_map, gains, w_query, w_key, w_value, w_out, w_up, w_down, cotangent):
    seq_total = segment_ids.shape[0]
    image_hot = segment_ids[:, :, None] == jnp.arange(SLOTS, dtype=jnp.int32)[None, None, :]
    media_slot = lax.optimization_barrier(jnp.sum(jnp.where(image_hot, slot_map[:, None, :], 0), axis=2)) - (segment_ids < 0).astype(jnp.int32)
    latent_slot = jnp.arange(SLOTS * LATENTS, dtype=jnp.int32) // LATENTS
    latent_slot = jnp.broadcast_to(latent_slot[None, :], (seq_total, SLOTS * LATENTS))
    key_slot = jnp.concatenate([media_slot, latent_slot], axis=1).astype(jnp.int32)

    def forward(latent_rows, media_rows, gain_all, query_all, key_all, value_all, out_all, up_all, down_all):
        current = latent_rows
        for layer_index in range(LAYERS):
            first = 2 * layer_index
            second = 2 * layer_index + 1
            query_w = jnp.concatenate([query_all[first], query_all[second]], axis=1)
            key_w = jnp.concatenate([key_all[first], key_all[second]], axis=1)
            value_w = jnp.concatenate([value_all[first], value_all[second]], axis=1)
            out_w = jnp.concatenate([out_all[first], out_all[second]], axis=0)
            up_w = jnp.concatenate([up_all[first], up_all[second]], axis=1)
            down_w = jnp.concatenate([down_all[first], down_all[second]], axis=0)
            current = cross_attention(current, media_rows, gain_all[layer_index, 0], gain_all[layer_index, 1], query_w, key_w, value_w, out_w, key_slot)
            current = feed_forward(current, gain_all[layer_index, 2], up_w, down_w)
        return current
    latents_out, pullback = jax.vjp(forward, latents.astype(jnp.float32), media.astype(jnp.float32), gains.astype(jnp.float32), w_query.astype(jnp.float32), w_key.astype(jnp.float32), w_value.astype(jnp.float32), w_out.astype(jnp.float32), w_up.astype(jnp.float32), w_down.astype(jnp.float32))
    grads = pullback(cotangent.astype(jnp.float32))
    return (latents_out, grads[0], grads[1], grads[2], grads[3], grads[4], grads[5], grads[6], grads[7], grads[8])
```

```python
import math

import jax
import jax.numpy as jnp
from jax import lax
from jax.sharding import PartitionSpec as P

HEAD_DIM = 96
LATENTS = 64
LAYERS = 2
HALF_HEADS = 8

epsilon = 1e-05
low = jnp.bfloat16
full = jnp.float32


def unit_rows(values):
    centered = values - jnp.mean(values, axis=-1, keepdims=True)
    variance = jnp.mean(centered * centered, axis=-1, keepdims=True)
    inverse = lax.rsqrt(variance + epsilon)
    return centered * inverse, inverse


def norm_back(unit, inverse, scaled):
    first = jnp.mean(scaled, axis=-1, keepdims=True)
    second = jnp.mean(scaled * unit, axis=-1, keepdims=True)
    return (scaled - first - unit * second) * inverse


def gelu_exact(values):
    return jax.nn.gelu(values, approximate=False)


def matmul(left, right):
    return jnp.dot(left, right, preferred_element_type=full)


def matmul_nt(left, right):
    return lax.dot_general(left, right, (((1,), (1,)), ((), ())), preferred_element_type=full)


def matmul_tn(left, right):
    return lax.dot_general(left, right, (((0,), (0,)), ((), ())), preferred_element_type=full)


def attend_forward(query_heads, key_heads, value_heads, allowed, score_scale):
    scores = jnp.einsum("qhd,khd->hqk", query_heads, key_heads, preferred_element_type=full)
    scores = jnp.where(allowed, scores * score_scale, -1e30)
    row_max = jnp.max(scores, axis=-1, keepdims=True)
    exponent = jnp.exp(scores - row_max)
    row_total = jnp.sum(exponent, axis=-1, keepdims=True)
    weights_low = (exponent / row_total).astype(low)
    attended = jnp.einsum("hqk,khd->qhd", weights_low, value_heads, preferred_element_type=full)
    return attended, row_max + jnp.log(row_total)


def attend_backward(
    query_heads, key_heads, value_heads, allowed, score_scale, log_total, grad_heads
):
    scores = jnp.einsum("qhd,khd->hqk", query_heads, key_heads, preferred_element_type=full)
    scores = jnp.where(allowed, scores * score_scale, -1e30)
    weights_full = jnp.exp(scores - log_total)
    weights_low = weights_full.astype(low)
    grad_value = jnp.einsum("hqk,qhd->khd", weights_low, grad_heads, preferred_element_type=full)
    grad_weights = jnp.einsum(
        "qhd,khd->hqk", grad_heads, value_heads, preferred_element_type=full
    )
    row_inner = jnp.sum(weights_full * grad_weights, axis=-1, keepdims=True)
    grad_scores = (weights_full * (grad_weights - row_inner)).astype(low)
    grad_query = (
        jnp.einsum("hqk,khd->qhd", grad_scores, key_heads, preferred_element_type=full)
        * score_scale
    )
    grad_key = (
        jnp.einsum("hqk,qhd->khd", grad_scores, query_heads, preferred_element_type=full)
        * score_scale
    )
    return grad_query, grad_key, grad_value


def per_device(
    latents,
    media,
    segment_ids,
    slot_map,
    gains,
    w_query,
    w_key,
    w_value,
    w_out,
    w_up,
    w_down,
    cotangent,
):
    section = lax.axis_index("section")
    section_count = lax.axis_size("section")
    dp_index = lax.axis_index("dp")
    dp_count = lax.axis_size("dp")
    layer_bit = section // 2
    on_first = layer_bit == 0
    stride = dp_count // HALF_HEADS
    row_bit = (dp_index // stride) % 2
    row_first = row_bit == 0
    seq_rows = segment_ids.shape[1]
    slot_count = slot_map.shape[1]
    feature_width = latents.shape[1]
    latent_rows = latents.shape[0]
    heads = HALF_HEADS // 2
    inner = heads * HEAD_DIM
    score_scale = 1.0 / math.sqrt(HEAD_DIM)

    def pick(first, second):
        return jnp.where(on_first, first, second), jnp.where(on_first, second, first)

    def swap_layer(value):
        pairs = [(source, source ^ 2) for source in range(section_count)]
        return lax.ppermute(value, "section", pairs)

    def with_bit(index, bit):
        high, lowest = index // (2 * stride), index % stride
        return (2 * high + bit) * stride + lowest

    def bit_of(index):
        return (index // stride) % 2

    def turn_pairs(flip, back):
        pairs = []
        for source in range(section_count):
            for index in range(dp_count):
                layer, half = divmod(source, 2)
                target = (bit_of(index) * 2 + half) * dp_count + with_bit(index, layer ^ flip)
                pair = (source * dp_count + index, target)
                pairs.append(pair[::-1] if back else pair)
        return pairs

    def column_parts(weight, block):
        rows, width = weight.shape
        split = weight.reshape(rows, width // (2 * block), 2, block)
        return split[:, :, 0].reshape(rows, -1), split[:, :, 1].reshape(rows, -1)

    def exchange_columns(even, odd):
        own, other = pick(even, odd)
        return pick(own, swap_layer(other))

    def join_columns(first, second, block):
        own, other = pick(first, second)
        even, odd = pick(own, swap_layer(other))
        rows, width = even.shape
        pieces = [part.reshape(rows, width // block, 1, block) for part in (even, odd)]
        return jnp.concatenate(pieces, axis=2).reshape(rows, 2 * width).astype(full)

    def exchange_rows(weight):
        half = weight.shape[0] // 2
        near, far = pick(weight[:half], weight[half:])
        first = lax.ppermute(near, ("section", "dp"), turn_pairs(0, False))
        second = lax.ppermute(far, ("section", "dp"), turn_pairs(1, False))
        return (
            jnp.where(row_first, first, second),
            jnp.where(row_first, second, first),
        )

    def join_rows(first, second):
        near = jnp.where(row_first, first, second)
        far = jnp.where(row_first, second, first)
        near = lax.ppermute(near, ("section", "dp"), turn_pairs(0, True))
        far = lax.ppermute(far, ("section", "dp"), turn_pairs(1, True))
        return jnp.concatenate(pick(near, far), axis=0).astype(full)

    def gather_rows(piece):
        gathered = lax.all_gather(piece, "dp", axis=0, tiled=True)
        if stride > 1:
            width = gathered.shape[1]
            gathered = gathered.reshape(-1, 2, stride, piece.shape[0], width)
            gathered = gathered.transpose(0, 2, 1, 3, 4).reshape(-1, width)
        return gathered

    def scatter_rows(grad):
        if stride > 1:
            width = grad.shape[1]
            piece = grad.shape[0] // dp_count
            grad = grad.reshape(-1, stride, 2, piece, width)
            grad = grad.transpose(0, 2, 1, 3, 4).reshape(-1, width)
        return lax.psum_scatter(grad.astype(low), "dp", scatter_dimension=0, tiled=True)

    def scatter_columns(grad):
        return lax.psum_scatter(grad.astype(low), "dp", scatter_dimension=0, tiled=True)

    def sum_to_slots(partial):
        blocks = partial.astype(low).reshape(section_count, -1, feature_width)
        arrived = lax.all_to_all(blocks, "section", split_axis=0, concat_axis=0)
        return jnp.sum(arrived.astype(full), axis=0)

    def from_slots(rows):
        return lax.all_gather(rows, "section", axis=0, tiled=True)

    def to_columns(rows):
        moved = lax.all_to_all(
            rows.astype(low), "section", split_axis=1, concat_axis=0, tiled=True
        )
        return moved.astype(full)

    query_parts = column_parts(w_query[0], HEAD_DIM)
    key_parts = column_parts(w_key[0], HEAD_DIM)
    value_parts = column_parts(w_value[0], HEAD_DIM)
    joined = [
        jnp.concatenate([query_parts[i], key_parts[i], value_parts[i]], axis=1) for i in range(2)
    ]
    qkv_pieces = exchange_columns(joined[0], joined[1])
    out_pieces = exchange_rows(w_out[0])
    hidden_block = w_up.shape[2] // HALF_HEADS
    up_pieces = exchange_columns(*column_parts(w_up[0], hidden_block))
    down_pieces = exchange_rows(w_down[0])
    qkv_w, out_w, up_w, down_w = [], [], [], []
    for layer in range(LAYERS):
        qkv_w.append(lax.all_gather(qkv_pieces[layer], "dp", axis=0, tiled=True))
        out_w.append(gather_rows(out_pieces[layer]))
        up_w.append(lax.all_gather(up_pieces[layer], "dp", axis=0, tiled=True))
        down_w.append(gather_rows(down_pieces[layer]))
    query_w = [weight[:, :inner] for weight in qkv_w]
    key_w = [weight[:, inner : 2 * inner] for weight in qkv_w]
    value_w = [weight[:, 2 * inner :] for weight in qkv_w]

    all_gains = lax.all_gather(gains, ("section", "dp"), axis=2, tiled=True)
    image_hot = segment_ids[:, :, None] == jnp.arange(slot_count, dtype=jnp.int32)[None, None, :]
    media_slot = jnp.sum(jnp.where(image_hot, slot_map[:, None, :], 0), axis=2) - (
        segment_ids < 0
    ).astype(jnp.int32)
    media_unit, media_inverse = unit_rows(media.astype(full))
    latent_slot = jnp.arange(latent_rows, dtype=jnp.int32) // LATENTS
    key_slot = jnp.concatenate([media_slot[0], latent_slot])
    allowed = latent_slot[None, :, None] == key_slot[None, None, :]

    def split_heads(rows):
        return rows.reshape(rows.shape[0], heads, HEAD_DIM)

    media_low = []
    media_key = []
    media_value = []
    for layer in range(LAYERS):
        media_low.append((media_unit * all_gains[layer, 0]).astype(low))
        media_key.append(matmul(media_low[layer], key_w[layer]).astype(low))
        media_value.append(matmul(media_low[layer], value_w[layer]).astype(low))

    saved = []
    slot_rows = latent_rows // section_count
    current = lax.dynamic_slice_in_dim(latents, section * slot_rows, slot_rows, 0).astype(full)
    for layer in range(LAYERS):
        unit_in, inverse_in = unit_rows(current)
        if layer == 0:
            whole_unit = unit_rows(latents.astype(full))[0]
            latent_low = (whole_unit * all_gains[layer, 1]).astype(low)
        else:
            latent_low = from_slots((unit_in * all_gains[layer, 1]).astype(low))
        projected = matmul(latent_low, qkv_w[layer]).astype(low)
        query_low = projected[:, :inner]
        key_heads = split_heads(
            jnp.concatenate([media_key[layer], projected[:, inner : 2 * inner]], axis=0)
        )
        value_heads = split_heads(
            jnp.concatenate([media_value[layer], projected[:, 2 * inner :]], axis=0)
        )
        query_heads = split_heads(query_low)
        attended, log_total = attend_forward(
            query_heads, key_heads, value_heads, allowed, score_scale
        )
        attended_low = attended.reshape(-1, inner).astype(low)
        middle = current + sum_to_slots(matmul(attended_low, out_w[layer]))
        unit_mid, inverse_mid = unit_rows(middle)
        ffn_low = from_slots((unit_mid * all_gains[layer, 2]).astype(low))
        hidden_pre = matmul(ffn_low, up_w[layer])
        active_low = gelu_exact(hidden_pre).astype(low)
        current = middle + sum_to_slots(matmul(active_low, down_w[layer]))
        saved.append(
            (
                unit_in,
                inverse_in,
                latent_low,
                query_heads,
                key_heads,
                value_heads,
                log_total,
                attended_low,
                unit_mid,
                inverse_mid,
                ffn_low,
                hidden_pre,
                active_low,
            )
        )
    latents_out = to_columns(current)

    gain_rows = [None] * LAYERS
    media_scaled = None
    pieces = [None] * LAYERS
    grad_low = cotangent
    grad_rows = lax.dynamic_slice_in_dim(cotangent, section * slot_rows, slot_rows, 0).astype(full)
    for layer in (1, 0):
        (
            unit_in,
            inverse_in,
            latent_low,
            query_heads,
            key_heads,
            value_heads,
            log_total,
            attended_low,
            unit_mid,
            inverse_mid,
            ffn_low,
            hidden_pre,
            active_low,
        ) = saved[layer]
        grad_active = matmul_nt(grad_low, down_w[layer])
        grad_hidden = jax.vjp(gelu_exact, hidden_pre)[1](grad_active)[0].astype(low)
        down_piece = scatter_rows(matmul_tn(active_low, grad_low))
        up_piece = scatter_columns(matmul_tn(ffn_low, grad_hidden))
        ffn_grad = sum_to_slots(matmul_nt(grad_hidden, up_w[layer]))
        gain_ffn_grad = jnp.sum(ffn_grad * unit_mid, axis=0)
        grad_middle = grad_rows + norm_back(
            unit_mid, inverse_mid, ffn_grad * all_gains[layer, 2]
        )
        middle_low = from_slots(grad_middle.astype(low))
        grad_heads = split_heads(matmul_nt(middle_low, out_w[layer]).astype(low))
        out_piece = scatter_rows(matmul_tn(attended_low, middle_low))
        grad_query, grad_key, grad_value = attend_backward(
            query_heads, key_heads, value_heads, allowed, score_scale, log_total, grad_heads
        )
        grad_query = grad_query.reshape(-1, inner).astype(low)
        grad_key = grad_key.reshape(-1, inner).astype(low)
        grad_value = grad_value.reshape(-1, inner).astype(low)
        latent_part = (
            matmul_nt(grad_query, query_w[layer])
            + matmul_nt(grad_key[seq_rows:], key_w[layer])
            + matmul_nt(grad_value[seq_rows:], value_w[layer])
        )
        latent_grad_rows = sum_to_slots(latent_part)
        gain_latent_grad = jnp.sum(latent_grad_rows * unit_in, axis=0)
        grad_rows = grad_middle + norm_back(
            unit_in, inverse_in, latent_grad_rows * all_gains[layer, 1]
        )
        if layer > 0:
            grad_low = from_slots(grad_rows.astype(low))
        both_low = jnp.concatenate([media_low[layer], latent_low], axis=0)
        query_grad = matmul_tn(latent_low, grad_query)
        key_grad = matmul_tn(both_low, grad_key)
        value_grad = matmul_tn(both_low, grad_value)
        qkv_piece = scatter_columns(
            jnp.concatenate(
                [query_grad.astype(low), key_grad.astype(low), value_grad.astype(low)], axis=1
            )
        )
        media_part = matmul_nt(grad_key[:seq_rows], key_w[layer]) + matmul_nt(
            grad_value[:seq_rows], value_w[layer]
        )
        gain_media_grad = jnp.sum(media_part * media_unit, axis=0)
        scaled = media_part * all_gains[layer, 0]
        media_scaled = scaled if media_scaled is None else media_scaled + scaled
        gain_rows[layer] = jnp.stack([gain_media_grad, gain_latent_grad, gain_ffn_grad])
        pieces[layer] = (qkv_piece, out_piece, up_piece, down_piece)
    latent_grad = to_columns(grad_rows)
    media_grad = lax.psum(
        norm_back(media_unit, media_inverse, media_scaled).astype(low), "section"
    ).astype(full)
    gain_grad = lax.psum_scatter(
        jnp.stack(gain_rows), ("section", "dp"), scatter_dimension=2, tiled=True
    )
    qkv_grads = [
        join_columns(
            pieces[0][0][:, i * inner : (i + 1) * inner],
            pieces[1][0][:, i * inner : (i + 1) * inner],
            HEAD_DIM,
        )
        for i in range(3)
    ]
    out_grad = join_rows(pieces[0][1], pieces[1][1])
    up_grad = join_columns(pieces[0][2], pieces[1][2], hidden_block)
    down_grad = join_rows(pieces[0][3], pieces[1][3])
    return (
        latents_out,
        latent_grad,
        media_grad,
        gain_grad,
        qkv_grads[0][None],
        qkv_grads[1][None],
        qkv_grads[2][None],
        out_grad[None],
        up_grad[None],
        down_grad[None],
    )


def solution(mesh):
    placed = (
        P("dp", None),
        P("dp", None),
        P("dp", None),
        P("dp", None),
        P(None, None, ("section", "dp")),
        P("section", "dp", None),
        P("section", "dp", None),
        P("section", "dp", None),
        P("section", "dp", None),
        P("section", "dp", None),
        P("section", "dp", None),
        P("dp", None),
    )
    return jax.shard_map(
        per_device,
        mesh=mesh,
        in_specs=placed,
        out_specs=(
            P("dp", "section"),
            P("dp", "section"),
            P("dp", None),
            P(None, None, ("section", "dp")),
            P("section", "dp", None),
            P("section", "dp", None),
            P("section", "dp", None),
            P("section", "dp", None),
            P("section", "dp", None),
            P("section", "dp", None),
        ),
        check_vma=False,
    )
```

```python
import math

import jax
import jax.numpy as jnp
from jax import lax
from jax.sharding import Mesh, PartitionSpec as P

HEAD_DIM = 96
LATENTS = 64
LAYERS = 2
HALF_HEADS = 8

epsilon = 1e-05
low = jnp.bfloat16
full = jnp.float32


def unit_rows(values):
    centered = values - jnp.mean(values, axis=-1, keepdims=True)
    variance = jnp.mean(centered * centered, axis=-1, keepdims=True)
    inverse = lax.rsqrt(variance + epsilon)
    return centered * inverse, inverse


def norm_back(unit, inverse, scaled):
    first = jnp.mean(scaled, axis=-1, keepdims=True)
    second = jnp.mean(scaled * unit, axis=-1, keepdims=True)
    return (scaled - first - unit * second) * inverse


def gelu_exact(values):
    return jax.nn.gelu(values, approximate=False)


def matmul(left, right):
    return jnp.dot(left, right, preferred_element_type=full)


def matmul_nt(left, right):
    return lax.dot_general(left, right, (((1,), (1,)), ((), ())), preferred_element_type=full)


def matmul_tn(left, right):
    return lax.dot_general(left, right, (((0,), (0,)), ((), ())), preferred_element_type=full)


def attend_forward(query_heads, key_heads, value_heads, allowed, score_scale):
    scores = jnp.einsum("qhd,khd->hqk", query_heads, key_heads, preferred_element_type=full)
    scores = jnp.where(allowed, scores * score_scale, -1e30)
    row_max = jnp.max(scores, axis=-1, keepdims=True)
    exponent = jnp.exp(scores - row_max)
    row_total = jnp.sum(exponent, axis=-1, keepdims=True)
    weights_low = (exponent / row_total).astype(low)
    attended = jnp.einsum("hqk,khd->qhd", weights_low, value_heads, preferred_element_type=full)
    return attended, row_max + jnp.log(row_total)


def attend_backward(
    query_heads, key_heads, value_heads, allowed, score_scale, log_total, grad_heads
):
    scores = jnp.einsum("qhd,khd->hqk", query_heads, key_heads, preferred_element_type=full)
    scores = jnp.where(allowed, scores * score_scale, -1e30)
    weights_full = jnp.exp(scores - log_total)
    weights_low = weights_full.astype(low)
    grad_value = jnp.einsum("hqk,qhd->khd", weights_low, grad_heads, preferred_element_type=full)
    grad_weights = jnp.einsum(
        "qhd,khd->hqk", grad_heads, value_heads, preferred_element_type=full
    )
    row_inner = jnp.sum(weights_full * grad_weights, axis=-1, keepdims=True)
    grad_scores = (weights_full * (grad_weights - row_inner)).astype(low)
    grad_query = (
        jnp.einsum("hqk,khd->qhd", grad_scores, key_heads, preferred_element_type=full)
        * score_scale
    )
    grad_key = (
        jnp.einsum("hqk,qhd->khd", grad_scores, query_heads, preferred_element_type=full)
        * score_scale
    )
    return grad_query, grad_key, grad_value


def per_device(
    latents,
    media,
    segment_ids,
    slot_map,
    gains,
    w_query,
    w_key,
    w_value,
    w_out,
    w_up,
    w_down,
    cotangent,
):
    dp = ("pair", "core")
    section = lax.axis_index("section")
    section_count = lax.axis_size("section")
    dp_index = lax.axis_index(dp)
    dp_count = lax.axis_size("pair") * lax.axis_size("core")
    on_first = section // 2 == 0
    stride = dp_count // HALF_HEADS
    row_first = (dp_index // stride) % 2 == 0
    seq_rows = segment_ids.shape[1]
    slot_count = slot_map.shape[1]
    feature_width = latents.shape[1]
    latent_rows = latents.shape[0]
    slot_rows = latent_rows // section_count
    heads = HALF_HEADS // 2
    inner = heads * HEAD_DIM
    score_scale = 1.0 / math.sqrt(HEAD_DIM)

    def pick(first, second):
        return jnp.where(on_first, first, second), jnp.where(on_first, second, first)

    def swapped(value, mask):
        pairs = [(source, source ^ mask) for source in range(section_count)]
        return lax.ppermute(value, "section", pairs)

    def to_second(value):
        return lax.ppermute(value, "section", [(0, 2), (1, 3)])

    def to_first(value):
        return lax.ppermute(value, "section", [(2, 0), (3, 1)])

    def turn_pairs(flip, back):
        pairs = []
        for source in range(section_count):
            for index in range(dp_count):
                layer, half = divmod(source, 2)
                high, bit, lowest = (
                    index // (2 * stride),
                    (index // stride) % 2,
                    index % stride,
                )
                moved = (2 * high + (layer ^ flip)) * stride + lowest
                target = (bit * 2 + half) * dp_count + moved
                pair = (source * dp_count + index, target)
                pairs.append(pair[::-1] if back else pair)
        return pairs

    everywhere = ("section",) + dp

    def column_parts(weight, block):
        rows, width = weight.shape
        split = weight.reshape(rows, width // (2 * block), 2, block)
        return split[:, :, 0].reshape(rows, -1), split[:, :, 1].reshape(rows, -1)

    def interleave(even, odd, block):
        rows, width = even.shape
        pieces = [part.reshape(rows, width // block, 1, block) for part in (even, odd)]
        return jnp.concatenate(pieces, axis=2).reshape(rows, 2 * width)

    def exchange_columns(even, odd):
        own, other = pick(even, odd)
        return pick(own, swapped(other, 2))

    def join_columns(first, second):
        own, other = pick(first, second)
        return pick(own, swapped(other, 2))

    def exchange_rows(weight):
        half = weight.shape[0] // 2
        near, far = pick(weight[:half], weight[half:])
        first = lax.ppermute(near, everywhere, turn_pairs(0, False))
        second = lax.ppermute(far, everywhere, turn_pairs(1, False))
        return (
            jnp.where(row_first, first, second),
            jnp.where(row_first, second, first),
        )

    def join_rows(first, second):
        near = jnp.where(row_first, first, second)
        far = jnp.where(row_first, second, first)
        near = lax.ppermute(near, everywhere, turn_pairs(0, True))
        far = lax.ppermute(far, everywhere, turn_pairs(1, True))
        return jnp.concatenate(pick(near, far), axis=0).astype(full)

    def rows_in_order(stacked):
        width = stacked.shape[-1]
        if stride > 1:
            piece = stacked.shape[1]
            stacked = stacked.reshape(-1, 2, stride, piece, width).transpose(0, 2, 1, 3, 4)
        return stacked.reshape(-1, width)

    def rows_by_device(grad):
        width = grad.shape[-1]
        piece = grad.shape[0] // dp_count
        if stride > 1:
            grad = grad.reshape(-1, stride, 2, piece, width).transpose(0, 2, 1, 3, 4)
        return grad.reshape(dp_count, piece, width)

    def sum_to_slots(partial):
        blocks = partial.astype(low).reshape(section_count, -1, feature_width)
        arrived = lax.all_to_all(blocks, "section", split_axis=0, concat_axis=0)
        return jnp.sum(arrived.astype(full), axis=0)

    def from_slots(rows):
        return lax.all_gather(rows, "section", axis=0, tiled=True)

    def to_columns(rows):
        moved = lax.all_to_all(
            rows.astype(low), "section", split_axis=1, concat_axis=0, tiled=True
        )
        return moved.astype(full)

    def from_sequences(rows):
        pairs = lax.all_gather(rows, "pair", axis=0)
        both = lax.all_gather(pairs, "core", axis=1)
        return both.reshape(-1, feature_width)

    def sum_to_sequence(partial):
        blocks = partial.astype(low).reshape(-1, 2, slot_rows, feature_width)
        halves = lax.all_to_all(blocks, "core", split_axis=1, concat_axis=1)
        halves = jnp.sum(halves.astype(full), axis=1).astype(low)
        arrived = lax.all_to_all(halves, "pair", split_axis=0, concat_axis=0)
        return jnp.sum(arrived.astype(full), axis=0)

    def spread(shard):
        own = jnp.where(on_first, to_first(shard), shard)
        return own, swapped(own, 1)

    def collect(own, other):
        total = own + swapped(other.astype(low), 1).astype(full)
        return total + to_second(total.astype(low)).astype(full)

    def block_of(blocks, mask):
        return lax.dynamic_index_in_dim(blocks, section ^ mask, 0, keepdims=False)

    def sum_over_sections(partial):
        blocks = partial.reshape(section_count, -1, feature_width)
        half = blocks.shape[1] // 2
        own, side, ahead, across = [block_of(blocks, mask) for mask in range(4)]
        across = across.astype(low)
        upper = swapped(across[:half], 2).astype(full)
        lower = swapped(across[half:], 1).astype(full)
        side = jnp.concatenate([side[:half] + upper, side[half:]], axis=0).astype(low)
        ahead = jnp.concatenate([ahead[:half], ahead[half:] + lower], axis=0).astype(low)
        return own + swapped(side, 1).astype(full) + swapped(ahead, 2).astype(full)

    def gather_sections(rows):
        half = rows.shape[0] // 2
        side = swapped(rows, 1)
        ahead = swapped(rows, 2)
        upper = swapped(side[:half], 2)
        lower = swapped(ahead[half:], 1)
        across = jnp.concatenate([upper, lower], axis=0)
        by_mask = [rows, side, ahead, across]
        ordered = []
        for target in range(section_count):
            chosen = by_mask[0]
            for mask in range(1, section_count):
                chosen = jnp.where(section ^ mask == target, by_mask[mask], chosen)
            ordered.append(chosen)
        return jnp.concatenate(ordered, axis=0)

    query_parts = column_parts(w_query[0], HEAD_DIM)
    key_parts = column_parts(w_key[0], HEAD_DIM)
    value_parts = column_parts(w_value[0], HEAD_DIM)
    joined = [
        jnp.concatenate([query_parts[i], key_parts[i], value_parts[i]], axis=1) for i in range(2)
    ]
    qkv_pieces = exchange_columns(joined[0], joined[1])
    out_pieces = exchange_rows(w_out[0])
    hidden_block = w_down.shape[1] // 2
    up_even, up_odd = column_parts(w_up[0], hidden_block)
    up_piece = jnp.where(on_first, up_even, to_second(up_odd))
    down_piece = jnp.where(
        on_first, w_down[0, :hidden_block], to_second(w_down[0, hidden_block:])
    )
    out_piece_rows = out_pieces[0].shape[0]

    def gather(piece):
        return lax.all_gather(piece, dp, axis=0)

    qkv_first = gather(qkv_pieces[0]).reshape(-1, 3 * inner)
    stacked = gather(jnp.concatenate([out_pieces[0], down_piece], axis=0))
    out_first = rows_in_order(stacked[:, :out_piece_rows])
    down_first = stacked[:, out_piece_rows:].reshape(-1, feature_width)
    up_first = gather(up_piece).reshape(feature_width, -1)
    qkv_piece_rows = qkv_pieces[1].size // feature_width
    stacked = gather(
        jnp.concatenate([qkv_pieces[1].reshape(-1, feature_width), out_pieces[1]], axis=0)
    )
    qkv_second = stacked[:, :qkv_piece_rows].reshape(-1, 3 * inner)
    out_second = rows_in_order(stacked[:, qkv_piece_rows:])
    qkv_w = (qkv_first, qkv_second)
    out_w = (out_first, out_second)
    query_w = [weight[:, :inner] for weight in qkv_w]
    key_w = [weight[:, inner : 2 * inner] for weight in qkv_w]
    value_w = [weight[:, 2 * inner :] for weight in qkv_w]
    down_second = jnp.concatenate(spread(w_down[0]), axis=0)
    up_turned = lax.all_to_all(w_up[0], dp, split_axis=1, concat_axis=0, tiled=True)
    up_second = jnp.concatenate(spread(up_turned), axis=1)

    near_gains = lax.all_gather(gains, dp, axis=2, tiled=True)
    all_gains = lax.all_gather(near_gains, "section", axis=2, tiled=True)
    image_hot = segment_ids[:, :, None] == jnp.arange(slot_count, dtype=jnp.int32)[None, None, :]
    media_slot = jnp.sum(jnp.where(image_hot, slot_map[:, None, :], 0), axis=2) - (
        segment_ids < 0
    ).astype(jnp.int32)
    media_unit, media_inverse = unit_rows(media.astype(full))
    latent_slot = jnp.arange(latent_rows, dtype=jnp.int32) // LATENTS
    key_slot = jnp.concatenate([media_slot[0], latent_slot])
    allowed = latent_slot[None, :, None] == key_slot[None, None, :]

    def split_heads(rows):
        return rows.reshape(rows.shape[0], heads, HEAD_DIM)

    media_low = []
    media_key = []
    media_value = []
    for layer in range(LAYERS):
        media_low.append((media_unit * all_gains[layer, 0]).astype(low))
        media_key.append(matmul(media_low[layer], key_w[layer]).astype(low))
        media_value.append(matmul(media_low[layer], value_w[layer]).astype(low))

    saved = []
    current = lax.dynamic_slice_in_dim(latents, section * slot_rows, slot_rows, 0).astype(full)
    grad_low = lax.dynamic_slice_in_dim(cotangent, section * slot_rows, slot_rows, 0)
    grad_rows = grad_low.astype(full)
    grad_low = from_sequences(grad_low)
    for layer in range(LAYERS):
        unit_in, inverse_in = unit_rows(current)
        if layer == 0:
            whole_unit = unit_rows(latents.astype(full))[0]
            latent_low = (whole_unit * all_gains[layer, 1]).astype(low)
        else:
            latent_low = from_slots((unit_in * all_gains[layer, 1]).astype(low))
        projected = matmul(latent_low, qkv_w[layer]).astype(low)
        query_low = projected[:, :inner]
        key_heads = split_heads(
            jnp.concatenate([media_key[layer], projected[:, inner : 2 * inner]], axis=0)
        )
        value_heads = split_heads(
            jnp.concatenate([media_value[layer], projected[:, 2 * inner :]], axis=0)
        )
        query_heads = split_heads(query_low)
        attended, log_total = attend_forward(
            query_heads, key_heads, value_heads, allowed, score_scale
        )
        attended_low = attended.reshape(-1, inner).astype(low)
        middle = current + sum_to_slots(matmul(attended_low, out_w[layer]))
        unit_mid, inverse_mid = unit_rows(middle)
        ffn_low = (unit_mid * all_gains[layer, 2]).astype(low)
        ffn_low = from_slots(ffn_low) if layer == 0 else from_sequences(ffn_low)
        hidden_pre = matmul(ffn_low, up_first if layer == 0 else up_second)
        active_low = gelu_exact(hidden_pre).astype(low)
        if layer == 0:
            current = middle + sum_to_slots(matmul(active_low, down_first))
        else:
            current = middle + sum_to_sequence(matmul(active_low, down_second))
        saved.append(
            (
                unit_in,
                inverse_in,
                latent_low,
                query_heads,
                key_heads,
                value_heads,
                log_total,
                attended_low,
                unit_mid,
                inverse_mid,
                ffn_low,
                hidden_pre,
                active_low,
            )
        )
    latents_out = to_columns(current)

    def scatter(blocks):
        return lax.psum_scatter(blocks, dp, scatter_dimension=0, tiled=False)

    def after(value, earlier):
        return lax.optimization_barrier((value, earlier))

    gain_rows = [None] * LAYERS
    media_scaled = None
    qkv_pieces = [None] * LAYERS
    out_pieces = [None] * LAYERS
    last_piece = None
    for layer in (1, 0):
        (
            unit_in,
            inverse_in,
            latent_low,
            query_heads,
            key_heads,
            value_heads,
            log_total,
            attended_low,
            unit_mid,
            inverse_mid,
            ffn_low,
            hidden_pre,
            active_low,
        ) = saved[layer]
        grad_active = matmul_nt(grad_low, down_first if layer == 0 else down_second)
        grad_hidden = jax.vjp(gelu_exact, hidden_pre)[1](grad_active)[0].astype(low)
        down_grad = matmul_tn(active_low, grad_low)
        up_grad = matmul_tn(ffn_low, grad_hidden)
        if layer == 0:
            blocks = jnp.concatenate(
                [
                    up_grad.astype(low).reshape(dp_count, -1, feature_width),
                    down_grad.astype(low).reshape(dp_count, -1, feature_width),
                ],
                axis=1,
            )
            blocks, qkv_pieces[1] = after(blocks, qkv_pieces[1])
            ffn_piece = scatter(blocks)
            last_piece = ffn_piece
            ffn_grad = sum_to_slots(matmul_nt(grad_hidden, up_first))
        else:
            middle_of = down_grad.shape[0] // 2
            down_second_grad = collect(down_grad[:middle_of], down_grad[middle_of:])
            middle_of = up_grad.shape[1] // 2
            up_second_grad = collect(up_grad[:, :middle_of], up_grad[:, middle_of:])
            ffn_grad = sum_to_sequence(matmul_nt(grad_hidden, up_second))
        gain_ffn_grad = jnp.sum(ffn_grad * unit_mid, axis=0)
        grad_middle = grad_rows + norm_back(
            unit_mid, inverse_mid, ffn_grad * all_gains[layer, 2]
        )
        middle_low = from_slots(grad_middle.astype(low))
        grad_heads = split_heads(matmul_nt(middle_low, out_w[layer]).astype(low))
        out_grad = matmul_tn(attended_low, middle_low)
        grad_query, grad_key, grad_value = attend_backward(
            query_heads, key_heads, value_heads, allowed, score_scale, log_total, grad_heads
        )
        grad_query = grad_query.reshape(-1, inner).astype(low)
        grad_key = grad_key.reshape(-1, inner).astype(low)
        grad_value = grad_value.reshape(-1, inner).astype(low)
        latent_part = (
            matmul_nt(grad_query, query_w[layer])
            + matmul_nt(grad_key[seq_rows:], key_w[layer])
            + matmul_nt(grad_value[seq_rows:], value_w[layer])
        )
        latent_grad_rows = sum_to_slots(latent_part)
        gain_latent_grad = jnp.sum(latent_grad_rows * unit_in, axis=0)
        grad_rows = grad_middle + norm_back(
            unit_in, inverse_in, latent_grad_rows * all_gains[layer, 1]
        )
        if layer > 0:
            grad_low = from_slots(grad_rows.astype(low))
        both_low = jnp.concatenate([media_low[layer], latent_low], axis=0)
        query_grad = matmul_tn(latent_low, grad_query)
        key_grad = matmul_tn(both_low, grad_key)
        value_grad = matmul_tn(both_low, grad_value)
        qkv_grad = jnp.concatenate(
            [query_grad.astype(low), key_grad.astype(low), value_grad.astype(low)], axis=1
        )
        blocks = jnp.concatenate(
            [
                qkv_grad.reshape(dp_count, -1, feature_width),
                rows_by_device(out_grad.astype(low)),
            ],
            axis=1,
        )
        if layer == 0:
            blocks, ffn_piece = after(blocks, ffn_piece)
        piece = scatter(blocks)
        qkv_pieces[layer] = piece
        media_part = matmul_nt(grad_key[:seq_rows], key_w[layer]) + matmul_nt(
            grad_value[:seq_rows], value_w[layer]
        )
        gain_media_grad = jnp.sum(media_part * media_unit, axis=0)
        scaled = media_part * all_gains[layer, 0]
        media_scaled = scaled if media_scaled is None else media_scaled + scaled
        gain_rows[layer] = jnp.stack([gain_media_grad, gain_latent_grad, gain_ffn_grad])
    latent_grad = to_columns(grad_rows)
    media_rows = seq_rows // section_count
    media_sum = sum_over_sections(media_scaled)
    own_unit = lax.dynamic_slice_in_dim(media_unit, section * media_rows, media_rows, 0)
    own_inverse = lax.dynamic_slice_in_dim(media_inverse, section * media_rows, media_rows, 0)
    media_grad = gather_sections(norm_back(own_unit, own_inverse, media_sum).astype(low)).astype(
        full
    )
    gain_parts = jnp.stack(gain_rows).reshape(LAYERS, 3, section_count, -1)
    gain_parts = jnp.sum(
        lax.all_to_all(gain_parts, "section", split_axis=2, concat_axis=2), axis=2
    )
    gain_parts = gain_parts.reshape(LAYERS, 3, dp_count, -1)
    gain_grad = jnp.sum(lax.all_to_all(gain_parts, dp, split_axis=2, concat_axis=2), axis=2)

    qkv_parts = []
    for layer in range(LAYERS):
        out_pieces[layer] = qkv_pieces[layer][qkv_piece_rows:]
        qkv_parts.append(qkv_pieces[layer][:qkv_piece_rows].reshape(-1, 3 * inner))
    even, odd = join_columns(qkv_parts[0], qkv_parts[1])
    qkv_grads = [
        interleave(
            even[:, i * inner : (i + 1) * inner], odd[:, i * inner : (i + 1) * inner], HEAD_DIM
        ).astype(full)
        for i in range(3)
    ]
    out_grad = join_rows(out_pieces[0], out_pieces[1])
    back = to_first(ffn_piece)
    up_rows = feature_width * feature_width // dp_count // feature_width
    up_first_grad = interleave(ffn_piece[:up_rows], back[:up_rows], hidden_block)
    down_first_grad = jnp.concatenate([ffn_piece[up_rows:], back[up_rows:]], axis=0)
    up_second_grad = lax.all_to_all(
        up_second_grad.astype(low), dp, split_axis=0, concat_axis=1, tiled=True
    )
    up_grad = jnp.where(on_first, up_first_grad.astype(full), up_second_grad.astype(full))
    down_grad = jnp.where(on_first, down_first_grad.astype(full), down_second_grad)
    return (
        latents_out,
        latent_grad,
        media_grad,
        gain_grad,
        qkv_grads[0][None],
        qkv_grads[1][None],
        qkv_grads[2][None],
        out_grad[None],
        up_grad[None],
        down_grad[None],
    )


def solution(mesh):
    section_count, dp_count = mesh.devices.shape
    fine = Mesh(
        mesh.devices.reshape(section_count, dp_count // 2, 2), ("section", "pair", "core")
    )
    dp = ("pair", "core")
    placed = (
        P(dp, None),
        P(dp, None),
        P(dp, None),
        P(dp, None),
        P(None, None, ("section",) + dp),
        P("section", dp, None),
        P("section", dp, None),
        P("section", dp, None),
        P("section", dp, None),
        P("section", dp, None),
        P("section", dp, None),
        P(dp, None),
    )
    return jax.shard_map(
        per_device,
        mesh=fine,
        in_specs=placed,
        out_specs=(
            P(dp, "section"),
            P(dp, "section"),
            P(dp, None),
            P(None, None, ("section",) + dp),
            P("section", dp, None),
            P("section", dp, None),
            P("section", dp, None),
            P("section", dp, None),
            P("section", dp, None),
            P("section", dp, None),
        ),
        check_vma=False,
    )
```

```python
import math

import jax
import jax.numpy as jnp
from jax import lax
from jax.sharding import Mesh, PartitionSpec as P

HEAD_DIM = 96
LATENTS = 64
LAYERS = 2

epsilon = 1e-05
low = jnp.bfloat16
full = jnp.float32


def unit_rows(values):
    centered = values - jnp.mean(values, axis=-1, keepdims=True)
    variance = jnp.mean(centered * centered, axis=-1, keepdims=True)
    inverse = lax.rsqrt(variance + epsilon)
    return centered * inverse, inverse


def norm_back(unit, inverse, scaled):
    first = jnp.mean(scaled, axis=-1, keepdims=True)
    second = jnp.mean(scaled * unit, axis=-1, keepdims=True)
    return (scaled - first - unit * second) * inverse


def gelu_exact(values):
    return jax.nn.gelu(values, approximate=False)


def matmul(left, right):
    return jnp.dot(left, right, preferred_element_type=full)


def matmul_nt(left, right):
    return lax.dot_general(left, right, (((1,), (1,)), ((), ())), preferred_element_type=full)


def matmul_tn(left, right):
    return lax.dot_general(left, right, (((0,), (0,)), ((), ())), preferred_element_type=full)


def attend_forward(query_heads, key_heads, value_heads, allowed, score_scale):
    scores = jnp.einsum("qhd,khd->hqk", query_heads, key_heads, preferred_element_type=full)
    scores = jnp.where(allowed, scores * score_scale, -1e30)
    row_max = jnp.max(scores, axis=-1, keepdims=True)
    exponent = jnp.exp(scores - row_max)
    row_total = jnp.sum(exponent, axis=-1, keepdims=True)
    weights_low = (exponent / row_total).astype(low)
    attended = jnp.einsum("hqk,khd->qhd", weights_low, value_heads, preferred_element_type=full)
    return attended, row_max + jnp.log(row_total)


def attend_backward(
    query_heads, key_heads, value_heads, allowed, score_scale, log_total, grad_heads
):
    scores = jnp.einsum("qhd,khd->hqk", query_heads, key_heads, preferred_element_type=full)
    scores = jnp.where(allowed, scores * score_scale, -1e30)
    weights_full = jnp.exp(scores - log_total)
    weights_low = weights_full.astype(low)
    grad_value = jnp.einsum("hqk,qhd->khd", weights_low, grad_heads, preferred_element_type=full)
    grad_weights = jnp.einsum(
        "qhd,khd->hqk", grad_heads, value_heads, preferred_element_type=full
    )
    row_inner = jnp.sum(weights_full * grad_weights, axis=-1, keepdims=True)
    grad_scores = (weights_full * (grad_weights - row_inner)).astype(low)
    grad_query = (
        jnp.einsum("hqk,khd->qhd", grad_scores, key_heads, preferred_element_type=full)
        * score_scale
    )
    grad_key = (
        jnp.einsum("hqk,qhd->khd", grad_scores, query_heads, preferred_element_type=full)
        * score_scale
    )
    return grad_query, grad_key, grad_value


def per_device(
    latents,
    media,
    segment_ids,
    slot_map,
    gains,
    w_query,
    w_key,
    w_value,
    w_out,
    w_up,
    w_down,
    cotangent,
):
    dp = ("pair", "core")
    everywhere = ("section",) + dp
    section = lax.axis_index("section")
    section_count = lax.axis_size("section")
    dp_index = lax.axis_index(dp)
    dp_count = lax.axis_size("pair") * lax.axis_size("core")
    on_first = section // 2 == 0
    stride = dp_count // 2
    row_first = dp_index // stride == 0
    seq_rows = segment_ids.shape[1]
    slot_count = slot_map.shape[1]
    feature_width = latents.shape[1]
    latent_rows = latents.shape[0]
    slot_rows = latent_rows // section_count
    inner = w_query.shape[2] // 2
    heads = inner // HEAD_DIM
    score_scale = 1.0 / math.sqrt(HEAD_DIM)

    def pick(first, second):
        return jnp.where(on_first, first, second), jnp.where(on_first, second, first)

    def swapped(value, mask):
        pairs = [(source, source ^ mask) for source in range(section_count)]
        return lax.ppermute(value, "section", pairs)

    def other_core(value):
        return lax.ppermute(value, "core", [(0, 1), (1, 0)])

    def to_second(value):
        return lax.ppermute(value, "section", [(0, 2), (1, 3)])

    def to_first(value):
        return lax.ppermute(value, "section", [(2, 0), (3, 1)])

    def after(value, earlier):
        return lax.optimization_barrier((value, earlier))[0]

    def turn_pairs(flip, back):
        pairs = []
        for source in range(section_count):
            for index in range(dp_count):
                layer, half = divmod(source, 2)
                bit, lowest = divmod(index, stride)
                moved = (layer ^ flip) * stride + lowest
                target = (bit * 2 + half) * dp_count + moved
                pair = (source * dp_count + index, target)
                pairs.append(pair[::-1] if back else pair)
        return pairs

    def exchange_rows(weight):
        half = weight.shape[0] // 2
        near, far = pick(weight[:half], weight[half:])
        first = lax.ppermute(near, everywhere, turn_pairs(0, False))
        second = lax.ppermute(far, everywhere, turn_pairs(1, False))
        return (
            jnp.where(row_first, first, second),
            jnp.where(row_first, second, first),
        )

    def join_rows(first, second):
        near = jnp.where(row_first, first, second)
        far = jnp.where(row_first, second, first)
        near = lax.ppermute(near, everywhere, turn_pairs(0, True))
        far = lax.ppermute(far, everywhere, turn_pairs(1, True))
        return jnp.concatenate(pick(near, far), axis=0).astype(full)

    def rows_in_order(stacked):
        width = stacked.shape[-1]
        stacked = stacked.reshape(2, stride, -1, width).transpose(1, 0, 2, 3)
        return stacked.reshape(-1, width)

    def rows_by_device(grad):
        width = grad.shape[-1]
        grad = grad.reshape(stride, 2, -1, width).transpose(1, 0, 2, 3)
        return grad.reshape(dp_count, -1, width)

    def sum_to_slots(partial):
        blocks = partial.astype(low).reshape(section_count, -1, feature_width)
        arrived = lax.all_to_all(blocks, "section", split_axis=0, concat_axis=0)
        return jnp.sum(arrived.astype(full), axis=0)

    def from_slots(rows):
        return lax.all_gather(rows, "section", axis=0, tiled=True)

    def to_columns(rows):
        moved = lax.all_to_all(
            rows.astype(low), "section", split_axis=1, concat_axis=0, tiled=True
        )
        return moved.astype(full)

    def from_sequences(rows):
        near = lax.all_gather(rows, "pair", axis=0, tiled=True)
        return jnp.concatenate([near, other_core(near)], axis=0)

    def sum_to_sequence(left, right, product):
        half = left.shape[0] // 2
        far = product(left[half:], right).astype(low)
        near = product(left[:half], right) + other_core(far).astype(full)
        blocks = near.astype(low).reshape(-1, slot_rows, feature_width)
        arrived = lax.all_to_all(blocks, "pair", split_axis=0, concat_axis=0)
        return jnp.sum(arrived.astype(full), axis=0)

    def by_distance(rows):
        half = rows.shape[0] // 2
        side = swapped(rows, 1)
        ahead = swapped(rows, 2)
        upper = swapped(side[:half], 2)
        lower = swapped(ahead[half:], 1)
        return rows, side, ahead, jnp.concatenate([upper, lower], axis=0)

    def for_layers(rows, axis):
        own, side, ahead, across = by_distance(rows)
        near = pick(own, ahead)
        far = pick(side, across)
        return [jnp.concatenate([near[i], far[i]], axis=axis) for i in range(LAYERS)]

    def collect(own, other, layer):
        total = own + swapped(other.astype(low), 1).astype(full)
        move = to_second if layer else to_first
        return total + move(total.astype(low)).astype(full)

    def block_of(blocks, mask):
        return lax.dynamic_index_in_dim(blocks, section ^ mask, 0, keepdims=False)

    def sum_over_sections(partial):
        blocks = partial.reshape(section_count, -1, feature_width)
        half = blocks.shape[1] // 2
        own, side, ahead, across = [block_of(blocks, mask) for mask in range(4)]
        across = across.astype(low)
        upper = swapped(across[:half], 2).astype(full)
        lower = swapped(across[half:], 1).astype(full)
        side = jnp.concatenate([side[:half] + upper, side[half:]], axis=0).astype(low)
        ahead = jnp.concatenate([ahead[:half], ahead[half:] + lower], axis=0).astype(low)
        return own + swapped(side, 1).astype(full) + swapped(ahead, 2).astype(full)

    def gather_sections(rows):
        by_mask = by_distance(rows)
        ordered = []
        for target in range(section_count):
            chosen = by_mask[0]
            for mask in range(1, section_count):
                chosen = jnp.where(section ^ mask == target, by_mask[mask], chosen)
            ordered.append(chosen)
        return jnp.concatenate(ordered, axis=0)

    halves = [pick(weight[0, :, :inner], weight[0, :, inner:]) for weight in (w_query, w_key, w_value)]
    own_heads = jnp.concatenate([half[0] for half in halves], axis=1)
    other_heads = swapped(jnp.concatenate([half[1] for half in halves], axis=1), 2)
    qkv_pieces = pick(own_heads, other_heads)
    out_pieces = exchange_rows(w_out[0])
    out_rows = out_pieces[0].shape[0]
    qkv_rows = qkv_pieces[1].size // feature_width

    def gather(piece):
        return lax.all_gather(piece, dp, axis=0)

    qkv_first = gather(qkv_pieces[0]).reshape(-1, 3 * inner)
    out_first = rows_in_order(gather(out_pieces[0]))
    stacked = gather(
        jnp.concatenate([qkv_pieces[1].reshape(-1, feature_width), out_pieces[1]], axis=0)
    )
    qkv_second = stacked[:, :qkv_rows].reshape(-1, 3 * inner)
    out_second = rows_in_order(stacked[:, qkv_rows:])
    qkv_w = (qkv_first, qkv_second)
    out_w = (out_first, out_second)
    query_w = [weight[:, :inner] for weight in qkv_w]
    key_w = [weight[:, inner : 2 * inner] for weight in qkv_w]
    value_w = [weight[:, 2 * inner :] for weight in qkv_w]
    down_w = for_layers(w_down[0], 0)
    up_turned = lax.all_to_all(w_up[0], dp, split_axis=1, concat_axis=0, tiled=True)
    up_w = for_layers(up_turned, 1)

    near_gains = lax.all_gather(gains, dp, axis=2, tiled=True)
    all_gains = lax.all_gather(near_gains, "section", axis=2, tiled=True)
    image_hot = segment_ids[:, :, None] == jnp.arange(slot_count, dtype=jnp.int32)[None, None, :]
    media_slot = jnp.sum(jnp.where(image_hot, slot_map[:, None, :], 0), axis=2) - (
        segment_ids < 0
    ).astype(jnp.int32)
    media_unit, media_inverse = unit_rows(media.astype(full))
    latent_slot = jnp.arange(latent_rows, dtype=jnp.int32) // LATENTS
    key_slot = jnp.concatenate([media_slot[0], latent_slot])
    allowed = latent_slot[None, :, None] == key_slot[None, None, :]

    def split_heads(rows):
        return rows.reshape(rows.shape[0], heads, HEAD_DIM)

    media_low = []
    media_key = []
    media_value = []
    for layer in range(LAYERS):
        media_low.append((media_unit * all_gains[layer, 0]).astype(low))
        media_key.append(matmul(media_low[layer], key_w[layer]).astype(low))
        media_value.append(matmul(media_low[layer], value_w[layer]).astype(low))

    saved = []
    current = lax.dynamic_slice_in_dim(latents, section * slot_rows, slot_rows, 0).astype(full)
    grad_low = lax.dynamic_slice_in_dim(cotangent, section * slot_rows, slot_rows, 0)
    grad_rows = grad_low.astype(full)
    grad_low = from_sequences(grad_low)
    for layer in range(LAYERS):
        unit_in, inverse_in = unit_rows(current)
        if layer == 0:
            whole_unit = unit_rows(latents.astype(full))[0]
            latent_low = (whole_unit * all_gains[layer, 1]).astype(low)
        else:
            latent_low = from_slots((unit_in * all_gains[layer, 1]).astype(low))
        projected = matmul(latent_low, qkv_w[layer]).astype(low)
        query_low = projected[:, :inner]
        key_heads = split_heads(
            jnp.concatenate([media_key[layer], projected[:, inner : 2 * inner]], axis=0)
        )
        value_heads = split_heads(
            jnp.concatenate([media_value[layer], projected[:, 2 * inner :]], axis=0)
        )
        query_heads = split_heads(query_low)
        attended, log_total = attend_forward(
            query_heads, key_heads, value_heads, allowed, score_scale
        )
        attended_low = attended.reshape(-1, inner).astype(low)
        if layer == 0:
            attended_low = after(attended_low, (up_w, down_w, grad_low))
        middle = current + sum_to_slots(matmul(attended_low, out_w[layer]))
        unit_mid, inverse_mid = unit_rows(middle)
        ffn_low = from_sequences((unit_mid * all_gains[layer, 2]).astype(low))
        hidden_pre = matmul(ffn_low, up_w[layer])
        active_low = gelu_exact(hidden_pre).astype(low)
        current = middle + sum_to_sequence(active_low, down_w[layer], matmul)
        saved.append(
            (
                unit_in,
                inverse_in,
                latent_low,
                query_heads,
                key_heads,
                value_heads,
                log_total,
                attended_low,
                unit_mid,
                inverse_mid,
                ffn_low,
                hidden_pre,
                active_low,
            )
        )

    def scatter(blocks):
        return lax.psum_scatter(blocks, dp, scatter_dimension=0, tiled=False)

    gain_rows = [None] * LAYERS
    media_scaled = None
    pieces = [None] * LAYERS
    up_grads = [None] * LAYERS
    down_grads = [None] * LAYERS
    for layer in (1, 0):
        (
            unit_in,
            inverse_in,
            latent_low,
            query_heads,
            key_heads,
            value_heads,
            log_total,
            attended_low,
            unit_mid,
            inverse_mid,
            ffn_low,
            hidden_pre,
            active_low,
        ) = saved[layer]
        grad_active = matmul_nt(grad_low, down_w[layer])
        grad_hidden = jax.vjp(gelu_exact, hidden_pre)[1](grad_active)[0].astype(low)
        ffn_grad = sum_to_sequence(grad_hidden, up_w[layer], matmul_nt)
        down_grad = matmul_tn(active_low, grad_low)
        up_grad = matmul_tn(ffn_low, grad_hidden)
        middle_of = down_grad.shape[0] // 2
        down_grads[layer] = collect(down_grad[:middle_of], down_grad[middle_of:], layer)
        up_grads[layer] = collect(up_grad[:, :middle_of], up_grad[:, middle_of:], layer)
        gain_ffn_grad = jnp.sum(ffn_grad * unit_mid, axis=0)
        grad_middle = grad_rows + norm_back(
            unit_mid, inverse_mid, ffn_grad * all_gains[layer, 2]
        )
        middle_low = from_slots(grad_middle.astype(low))
        grad_heads = split_heads(matmul_nt(middle_low, out_w[layer]).astype(low))
        out_grad = matmul_tn(attended_low, middle_low)
        grad_query, grad_key, grad_value = attend_backward(
            query_heads, key_heads, value_heads, allowed, score_scale, log_total, grad_heads
        )
        grad_query = grad_query.reshape(-1, inner).astype(low)
        grad_key = grad_key.reshape(-1, inner).astype(low)
        grad_value = grad_value.reshape(-1, inner).astype(low)
        latent_part = (
            matmul_nt(grad_query, query_w[layer])
            + matmul_nt(grad_key[seq_rows:], key_w[layer])
            + matmul_nt(grad_value[seq_rows:], value_w[layer])
        )
        latent_grad_rows = sum_to_slots(latent_part)
        gain_latent_grad = jnp.sum(latent_grad_rows * unit_in, axis=0)
        grad_rows = grad_middle + norm_back(
            unit_in, inverse_in, latent_grad_rows * all_gains[layer, 1]
        )
        both_low = jnp.concatenate([media_low[layer], latent_low], axis=0)
        query_grad = matmul_tn(latent_low, grad_query)
        key_grad = matmul_tn(both_low, grad_key)
        value_grad = matmul_tn(both_low, grad_value)
        qkv_grad = jnp.concatenate(
            [query_grad.astype(low), key_grad.astype(low), value_grad.astype(low)], axis=1
        )
        pieces[layer] = scatter(
            jnp.concatenate(
                [
                    qkv_grad.reshape(dp_count, -1, feature_width),
                    rows_by_device(out_grad.astype(low)),
                ],
                axis=1,
            )
        )
        if layer > 0:
            grad_low = from_sequences(grad_rows.astype(low))
            grad_low = after(grad_low, (up_grads[layer], down_grads[layer]))
        media_part = matmul_nt(grad_key[:seq_rows], key_w[layer]) + matmul_nt(
            grad_value[:seq_rows], value_w[layer]
        )
        gain_media_grad = jnp.sum(media_part * media_unit, axis=0)
        scaled = media_part * all_gains[layer, 0]
        media_scaled = scaled if media_scaled is None else media_scaled + scaled
        gain_rows[layer] = jnp.stack([gain_media_grad, gain_latent_grad, gain_ffn_grad])
    latents_out = to_columns(current)
    latent_grad = to_columns(grad_rows)
    media_rows = seq_rows // section_count
    media_sum = sum_over_sections(media_scaled)
    own_unit = lax.dynamic_slice_in_dim(media_unit, section * media_rows, media_rows, 0)
    own_inverse = lax.dynamic_slice_in_dim(media_inverse, section * media_rows, media_rows, 0)
    media_grad = gather_sections(norm_back(own_unit, own_inverse, media_sum).astype(low)).astype(
        full
    )
    gain_parts = jnp.stack(gain_rows).reshape(LAYERS, 3, section_count, -1)
    gain_parts = jnp.sum(
        lax.all_to_all(gain_parts, "section", split_axis=2, concat_axis=2), axis=2
    )
    gain_parts = gain_parts.reshape(LAYERS, 3, dp_count, -1)
    gain_grad = jnp.sum(lax.all_to_all(gain_parts, dp, split_axis=2, concat_axis=2), axis=2)

    qkv_parts = [piece[:qkv_rows].reshape(-1, 3 * inner) for piece in pieces]
    own, other = pick(qkv_parts[0], qkv_parts[1])
    lower, upper = pick(own, swapped(other, 2))
    qkv_grads = [
        jnp.concatenate(
            [lower[:, i * inner : (i + 1) * inner], upper[:, i * inner : (i + 1) * inner]], axis=1
        ).astype(full)
        for i in range(3)
    ]
    out_grad = join_rows(pieces[0][qkv_rows:], pieces[1][qkv_rows:])
    up_grad = jnp.where(on_first, up_grads[0], up_grads[1]).astype(low)
    up_grad = lax.all_to_all(up_grad, dp, split_axis=0, concat_axis=1, tiled=True).astype(full)
    down_grad = jnp.where(on_first, down_grads[0], down_grads[1])
    return (
        latents_out,
        latent_grad,
        media_grad,
        gain_grad,
        qkv_grads[0][None],
        qkv_grads[1][None],
        qkv_grads[2][None],
        out_grad[None],
        up_grad[None],
        down_grad[None],
    )


def solution(mesh):
    section_count, dp_count = mesh.devices.shape
    fine = Mesh(
        mesh.devices.reshape(section_count, dp_count // 2, 2), ("section", "pair", "core")
    )
    dp = ("pair", "core")
    placed = (
        P(dp, None),
        P(dp, None),
        P(dp, None),
        P(dp, None),
        P(None, None, ("section",) + dp),
        P("section", dp, None),
        P("section", dp, None),
        P("section", dp, None),
        P("section", dp, None),
        P("section", dp, None),
        P("section", dp, None),
        P(dp, None),
    )
    return jax.shard_map(
        per_device,
        mesh=fine,
        in_specs=placed,
        out_specs=(
            P(dp, "section"),
            P(dp, "section"),
            P(dp, None),
            P(None, None, ("section",) + dp),
            P("section", dp, None),
            P("section", dp, None),
            P("section", dp, None),
            P("section", dp, None),
            P("section", dp, None),
            P("section", dp, None),
        ),
        check_vma=False,
    )
```

```python
import math

import jax
import jax.numpy as jnp
from jax import lax
from jax.sharding import Mesh, PartitionSpec as P

HEAD_DIM = 96
LATENTS = 64
LAYERS = 2

epsilon = 1e-05
low = jnp.bfloat16
full = jnp.float32


def unit_rows(values):
    centered = values - jnp.mean(values, axis=-1, keepdims=True)
    variance = jnp.mean(centered * centered, axis=-1, keepdims=True)
    inverse = lax.rsqrt(variance + epsilon)
    return centered * inverse, inverse


def norm_back(unit, inverse, scaled):
    first = jnp.mean(scaled, axis=-1, keepdims=True)
    second = jnp.mean(scaled * unit, axis=-1, keepdims=True)
    return (scaled - first - unit * second) * inverse


def gelu_exact(values):
    return jax.nn.gelu(values, approximate=False)


def matmul(left, right):
    return jnp.dot(left, right, preferred_element_type=full)


def matmul_nt(left, right):
    return lax.dot_general(left, right, (((1,), (1,)), ((), ())), preferred_element_type=full)


def matmul_tn(left, right):
    return lax.dot_general(left, right, (((0,), (0,)), ((), ())), preferred_element_type=full)


def attend_forward(query_heads, key_heads, value_heads, allowed, score_scale):
    scores = jnp.einsum("qhd,khd->hqk", query_heads, key_heads, preferred_element_type=full)
    scores = jnp.where(allowed, scores * score_scale, -1e30)
    row_max = jnp.max(scores, axis=-1, keepdims=True)
    exponent = jnp.exp(scores - row_max)
    row_total = jnp.sum(exponent, axis=-1, keepdims=True)
    weights_low = (exponent / row_total).astype(low)
    attended = jnp.einsum("hqk,khd->qhd", weights_low, value_heads, preferred_element_type=full)
    return attended, row_max + jnp.log(row_total)


def attend_backward(
    query_heads, key_heads, value_heads, allowed, score_scale, log_total, grad_heads
):
    scores = jnp.einsum("qhd,khd->hqk", query_heads, key_heads, preferred_element_type=full)
    scores = jnp.where(allowed, scores * score_scale, -1e30)
    weights_full = jnp.exp(scores - log_total)
    weights_low = weights_full.astype(low)
    grad_value = jnp.einsum("hqk,qhd->khd", weights_low, grad_heads, preferred_element_type=full)
    grad_weights = jnp.einsum(
        "qhd,khd->hqk", grad_heads, value_heads, preferred_element_type=full
    )
    row_inner = jnp.sum(weights_full * grad_weights, axis=-1, keepdims=True)
    grad_scores = (weights_full * (grad_weights - row_inner)).astype(low)
    grad_query = (
        jnp.einsum("hqk,khd->qhd", grad_scores, key_heads, preferred_element_type=full)
        * score_scale
    )
    grad_key = (
        jnp.einsum("hqk,qhd->khd", grad_scores, query_heads, preferred_element_type=full)
        * score_scale
    )
    return grad_query, grad_key, grad_value


def per_device(
    latents,
    media,
    segment_ids,
    slot_map,
    gains,
    w_query,
    w_key,
    w_value,
    w_out,
    w_up,
    w_down,
    cotangent,
):
    dp = ("pair", "core")
    everywhere = ("section",) + dp
    section = lax.axis_index("section")
    section_count = lax.axis_size("section")
    dp_index = lax.axis_index(dp)
    dp_count = lax.axis_size("pair") * lax.axis_size("core")
    on_first = section // 2 == 0
    stride = dp_count // 2
    row_first = dp_index // stride == 0
    seq_rows = segment_ids.shape[1]
    slot_count = slot_map.shape[1]
    feature_width = latents.shape[1]
    latent_rows = latents.shape[0]
    slot_rows = latent_rows // section_count
    inner = w_query.shape[2] // 2
    heads = inner // HEAD_DIM
    score_scale = 1.0 / math.sqrt(HEAD_DIM)

    def pick(first, second):
        return jnp.where(on_first, first, second), jnp.where(on_first, second, first)

    def swapped(value, mask):
        pairs = [(source, source ^ mask) for source in range(section_count)]
        return lax.ppermute(value, "section", pairs)

    def other_core(value):
        return lax.ppermute(value, "core", [(0, 1), (1, 0)])

    def to_second(value):
        return lax.ppermute(value, "section", [(0, 2), (1, 3)])

    def to_first(value):
        return lax.ppermute(value, "section", [(2, 0), (3, 1)])

    def after(value, earlier):
        return lax.optimization_barrier((value, earlier))[0]

    def turn_pairs(flip, back):
        pairs = []
        for source in range(section_count):
            for index in range(dp_count):
                layer, half = divmod(source, 2)
                bit, lowest = divmod(index, stride)
                moved = (layer ^ flip) * stride + lowest
                target = (bit * 2 + half) * dp_count + moved
                pair = (source * dp_count + index, target)
                pairs.append(pair[::-1] if back else pair)
        return pairs

    def exchange_rows(weight):
        half = weight.shape[0] // 2
        near, far = pick(weight[:half], weight[half:])
        first = lax.ppermute(near, everywhere, turn_pairs(0, False))
        second = lax.ppermute(far, everywhere, turn_pairs(1, False))
        return (
            jnp.where(row_first, first, second),
            jnp.where(row_first, second, first),
        )

    def join_rows(first, second):
        near = jnp.where(row_first, first, second)
        far = jnp.where(row_first, second, first)
        near = lax.ppermute(near, everywhere, turn_pairs(0, True))
        far = lax.ppermute(far, everywhere, turn_pairs(1, True))
        return jnp.concatenate(pick(near, far), axis=0).astype(full)

    def fold(piece):
        blocks = [piece[:, i * inner : (i + 1) * inner] for i in range(feature_width // inner)]
        return jnp.concatenate(blocks, axis=0)

    def unfold(stacked):
        count = feature_width // inner
        blocks = stacked.reshape(2, stride, count, -1, inner).transpose(1, 0, 3, 2, 4)
        return blocks.reshape(-1, feature_width)

    def fold_grad(grad):
        count = feature_width // inner
        blocks = grad.reshape(stride, 2, -1, count, inner).transpose(1, 0, 3, 2, 4)
        return blocks.reshape(-1, inner)

    def unfold_piece(piece):
        count = feature_width // inner
        rows = piece.shape[0] // count
        blocks = [piece[i * rows : (i + 1) * rows] for i in range(count)]
        return jnp.concatenate(blocks, axis=1)

    def sum_to_slots(partial):
        blocks = partial.astype(low).reshape(section_count, -1, feature_width)
        arrived = lax.all_to_all(blocks, "section", split_axis=0, concat_axis=0)
        return jnp.sum(arrived.astype(full), axis=0)

    def from_slots(rows):
        return lax.all_gather(rows, "section", axis=0, tiled=True)

    def to_columns(rows):
        moved = lax.all_to_all(
            rows.astype(low), "section", split_axis=1, concat_axis=0, tiled=True
        )
        return moved.astype(full)

    def from_sequences(rows):
        near = lax.all_gather(rows, "pair", axis=0, tiled=True)
        return jnp.concatenate([near, other_core(near)], axis=0)

    def sum_to_sequence(left, right, product):
        half = left.shape[0] // 2
        far = product(left[half:], right).astype(low)
        near = product(left[:half], right) + other_core(far).astype(full)
        blocks = near.astype(low).reshape(-1, slot_rows, feature_width)
        arrived = lax.all_to_all(blocks, "pair", split_axis=0, concat_axis=0)
        return jnp.sum(arrived.astype(full), axis=0)

    def by_distance(rows):
        half = rows.shape[0] // 2
        side = swapped(rows, 1)
        ahead = swapped(rows, 2)
        upper = swapped(side[:half], 2)
        lower = swapped(ahead[half:], 1)
        return rows, side, ahead, jnp.concatenate([upper, lower], axis=0)

    def for_layers(rows, axis):
        own, side, ahead, across = by_distance(rows)
        near = pick(own, ahead)
        far = pick(side, across)
        return [jnp.concatenate([near[i], far[i]], axis=axis) for i in range(LAYERS)]

    def collect_side(own, other):
        return own + swapped(other.astype(low), 1).astype(full)

    def collect_ahead(total, layer):
        move = to_second if layer else to_first
        return total + move(total.astype(low)).astype(full)

    def block_of(blocks, mask):
        return lax.dynamic_index_in_dim(blocks, section ^ mask, 0, keepdims=False)

    def sum_over_sections(partial):
        blocks = partial.reshape(section_count, -1, feature_width)
        half = blocks.shape[1] // 2
        own, side, ahead, across = [block_of(blocks, mask) for mask in range(4)]
        across = across.astype(low)
        upper = swapped(across[:half], 2).astype(full)
        lower = swapped(across[half:], 1).astype(full)
        side = jnp.concatenate([side[:half] + upper, side[half:]], axis=0).astype(low)
        ahead = jnp.concatenate([ahead[:half], ahead[half:] + lower], axis=0).astype(low)
        return own + swapped(side, 1).astype(full) + swapped(ahead, 2).astype(full)

    def gather_sections(rows):
        by_mask = by_distance(rows)
        ordered = []
        for target in range(section_count):
            chosen = by_mask[0]
            for mask in range(1, section_count):
                chosen = jnp.where(section ^ mask == target, by_mask[mask], chosen)
            ordered.append(chosen)
        return jnp.concatenate(ordered, axis=0)

    near_gains = lax.all_gather(gains, dp, axis=2, tiled=True)
    all_gains = lax.all_gather(near_gains, "section", axis=2, tiled=True)
    halves = [pick(weight[0, :, :inner], weight[0, :, inner:]) for weight in (w_query, w_key, w_value)]
    own_heads = jnp.concatenate([half[0] for half in halves], axis=1)
    other_heads = swapped(jnp.concatenate([half[1] for half in halves], axis=1), 2)
    qkv_pieces = pick(own_heads, other_heads)
    down_in, up_in = after((w_down[0], w_up[0]), all_gains)
    out_pieces = exchange_rows(after(w_out[0], all_gains))

    def gather(piece):
        return lax.all_gather(piece, dp, axis=0, tiled=True)

    qkv_first = gather(after(qkv_pieces[0], all_gains))
    out_first = gather(after(fold(out_pieces[0]), qkv_first))
    stacked = gather(
        after(jnp.concatenate([qkv_pieces[1], fold(out_pieces[1])], axis=1), out_first)
    )
    out_first = unfold(out_first)
    qkv_second = stacked[:, : 3 * inner]
    out_second = unfold(stacked[:, 3 * inner :])
    qkv_w = (qkv_first, qkv_second)
    out_w = (out_first, out_second)
    query_w = [weight[:, :inner] for weight in qkv_w]
    key_w = [weight[:, inner : 2 * inner] for weight in qkv_w]
    value_w = [weight[:, 2 * inner :] for weight in qkv_w]
    down_w = for_layers(down_in, 0)
    up_turned = lax.all_to_all(up_in, dp, split_axis=1, concat_axis=0, tiled=True)
    up_w = for_layers(up_turned, 1)

    image_hot = segment_ids[:, :, None] == jnp.arange(slot_count, dtype=jnp.int32)[None, None, :]
    media_slot = jnp.sum(jnp.where(image_hot, slot_map[:, None, :], 0), axis=2) - (
        segment_ids < 0
    ).astype(jnp.int32)
    media_unit, media_inverse = unit_rows(media.astype(full))
    latent_slot = jnp.arange(latent_rows, dtype=jnp.int32) // LATENTS
    key_slot = jnp.concatenate([media_slot[0], latent_slot])
    allowed = latent_slot[None, :, None] == key_slot[None, None, :]

    def split_heads(rows):
        return rows.reshape(rows.shape[0], heads, HEAD_DIM)

    media_low = []
    media_key = []
    media_value = []
    for layer in range(LAYERS):
        media_low.append((media_unit * all_gains[layer, 0]).astype(low))
        media_key.append(matmul(media_low[layer], key_w[layer]).astype(low))
        media_value.append(matmul(media_low[layer], value_w[layer]).astype(low))

    saved = []
    current = lax.dynamic_slice_in_dim(latents, section * slot_rows, slot_rows, 0).astype(full)
    grad_low = lax.dynamic_slice_in_dim(cotangent, section * slot_rows, slot_rows, 0)
    grad_rows = grad_low.astype(full)
    grad_low = from_sequences(grad_low)
    for layer in range(LAYERS):
        unit_in, inverse_in = unit_rows(current)
        if layer == 0:
            whole_unit = unit_rows(latents.astype(full))[0]
            latent_low = (whole_unit * all_gains[layer, 1]).astype(low)
        else:
            latent_low = from_slots((unit_in * all_gains[layer, 1]).astype(low))
        projected = matmul(latent_low, qkv_w[layer]).astype(low)
        query_low = projected[:, :inner]
        key_heads = split_heads(
            jnp.concatenate([media_key[layer], projected[:, inner : 2 * inner]], axis=0)
        )
        value_heads = split_heads(
            jnp.concatenate([media_value[layer], projected[:, 2 * inner :]], axis=0)
        )
        query_heads = split_heads(query_low)
        attended, log_total = attend_forward(
            query_heads, key_heads, value_heads, allowed, score_scale
        )
        attended_low = attended.reshape(-1, inner).astype(low)
        if layer == 0:
            attended_low = after(attended_low, (up_w, down_w, grad_low))
        middle = current + sum_to_slots(matmul(attended_low, out_w[layer]))
        unit_mid, inverse_mid = unit_rows(middle)
        ffn_low = from_sequences((unit_mid * all_gains[layer, 2]).astype(low))
        hidden_pre = matmul(ffn_low, up_w[layer])
        active_low = gelu_exact(hidden_pre).astype(low)
        current = middle + sum_to_sequence(active_low, down_w[layer], matmul)
        saved.append(
            (
                unit_in,
                inverse_in,
                latent_low,
                query_heads,
                key_heads,
                value_heads,
                log_total,
                attended_low,
                unit_mid,
                inverse_mid,
                ffn_low,
                hidden_pre,
                active_low,
            )
        )

    def scatter(blocks):
        return lax.psum_scatter(blocks, dp, scatter_dimension=0, tiled=True)

    gain_rows = [None] * LAYERS
    media_scaled = None
    pieces = [None] * LAYERS
    up_grads = [None] * LAYERS
    down_grads = [None] * LAYERS
    for layer in (1, 0):
        (
            unit_in,
            inverse_in,
            latent_low,
            query_heads,
            key_heads,
            value_heads,
            log_total,
            attended_low,
            unit_mid,
            inverse_mid,
            ffn_low,
            hidden_pre,
            active_low,
        ) = saved[layer]
        grad_active = matmul_nt(grad_low, down_w[layer])
        grad_hidden = jax.vjp(gelu_exact, hidden_pre)[1](grad_active)[0].astype(low)
        ffn_grad = sum_to_sequence(grad_hidden, up_w[layer], matmul_nt)
        down_grad = matmul_tn(active_low, grad_low)
        up_grad = matmul_tn(ffn_low, grad_hidden)
        middle_of = down_grad.shape[0] // 2
        down_side = collect_side(down_grad[:middle_of], down_grad[middle_of:])
        up_side = collect_side(up_grad[:, :middle_of], up_grad[:, middle_of:])
        gain_ffn_grad = jnp.sum(ffn_grad * unit_mid, axis=0)
        grad_middle = grad_rows + norm_back(
            unit_mid, inverse_mid, ffn_grad * all_gains[layer, 2]
        )
        middle_low = from_slots(after(grad_middle.astype(low), down_side))
        grad_heads = split_heads(matmul_nt(middle_low, out_w[layer]).astype(low))
        out_grad = matmul_tn(attended_low, middle_low)
        grad_query, grad_key, grad_value = attend_backward(
            query_heads, key_heads, value_heads, allowed, score_scale, log_total, grad_heads
        )
        grad_query = grad_query.reshape(-1, inner).astype(low)
        grad_key = grad_key.reshape(-1, inner).astype(low)
        grad_value = grad_value.reshape(-1, inner).astype(low)
        latent_part = (
            matmul_nt(grad_query, query_w[layer])
            + matmul_nt(grad_key[seq_rows:], key_w[layer])
            + matmul_nt(grad_value[seq_rows:], value_w[layer])
        )
        down_grads[layer] = collect_ahead(down_side, layer)
        up_grads[layer] = collect_ahead(up_side, layer)
        if layer > 0:
            latent_part = after(latent_part, (up_side, down_grads[layer]))
        latent_grad_rows = sum_to_slots(latent_part)
        gain_latent_grad = jnp.sum(latent_grad_rows * unit_in, axis=0)
        grad_rows = grad_middle + norm_back(
            unit_in, inverse_in, latent_grad_rows * all_gains[layer, 1]
        )
        both_low = jnp.concatenate([media_low[layer], latent_low], axis=0)
        query_grad = matmul_tn(latent_low, grad_query)
        key_grad = matmul_tn(both_low, grad_key)
        value_grad = matmul_tn(both_low, grad_value)
        qkv_grad = jnp.concatenate(
            [query_grad.astype(low), key_grad.astype(low), value_grad.astype(low)], axis=1
        )
        pieces[layer] = scatter(
            jnp.concatenate([qkv_grad, fold_grad(out_grad.astype(low))], axis=1)
        )
        if layer > 0:
            grad_low = from_sequences(grad_rows.astype(low))
            grad_low = after(grad_low, up_grads[layer])
        media_part = matmul_nt(grad_key[:seq_rows], key_w[layer]) + matmul_nt(
            grad_value[:seq_rows], value_w[layer]
        )
        gain_media_grad = jnp.sum(media_part * media_unit, axis=0)
        scaled = media_part * all_gains[layer, 0]
        media_scaled = scaled if media_scaled is None else media_scaled + scaled
        gain_rows[layer] = jnp.stack([gain_media_grad, gain_latent_grad, gain_ffn_grad])
    latents_out = to_columns(current)
    latent_grad = to_columns(grad_rows)
    media_rows = seq_rows // section_count
    media_sum = sum_over_sections(media_scaled)
    own_unit = lax.dynamic_slice_in_dim(media_unit, section * media_rows, media_rows, 0)
    own_inverse = lax.dynamic_slice_in_dim(media_inverse, section * media_rows, media_rows, 0)
    media_grad = gather_sections(norm_back(own_unit, own_inverse, media_sum).astype(low)).astype(
        full
    )
    gain_parts = jnp.stack(gain_rows).reshape(LAYERS, 3, section_count, -1)
    gain_parts = jnp.sum(
        lax.all_to_all(gain_parts, "section", split_axis=2, concat_axis=2), axis=2
    )
    gain_parts = gain_parts.reshape(LAYERS, 3, dp_count, -1)
    gain_grad = jnp.sum(lax.all_to_all(gain_parts, dp, split_axis=2, concat_axis=2), axis=2)

    qkv_parts = [piece[:, : 3 * inner] for piece in pieces]
    own, other = pick(qkv_parts[0], qkv_parts[1])
    lower, upper = pick(own, swapped(other, 2))
    qkv_grads = [
        jnp.concatenate(
            [lower[:, i * inner : (i + 1) * inner], upper[:, i * inner : (i + 1) * inner]], axis=1
        ).astype(full)
        for i in range(3)
    ]
    out_grad = join_rows(*[unfold_piece(piece[:, 3 * inner :]) for piece in pieces])
    up_grad = jnp.where(on_first, up_grads[0], up_grads[1]).astype(low)
    up_grad = lax.all_to_all(up_grad, dp, split_axis=0, concat_axis=1, tiled=True).astype(full)
    down_grad = jnp.where(on_first, down_grads[0], down_grads[1])
    return (
        latents_out,
        latent_grad,
        media_grad,
        gain_grad,
        qkv_grads[0][None],
        qkv_grads[1][None],
        qkv_grads[2][None],
        out_grad[None],
        up_grad[None],
        down_grad[None],
    )


def solution(mesh):
    section_count, dp_count = mesh.devices.shape
    fine = Mesh(
        mesh.devices.reshape(section_count, dp_count // 2, 2), ("section", "pair", "core")
    )
    dp = ("pair", "core")
    placed = (
        P(dp, None),
        P(dp, None),
        P(dp, None),
        P(dp, None),
        P(None, None, ("section",) + dp),
        P("section", dp, None),
        P("section", dp, None),
        P("section", dp, None),
        P("section", dp, None),
        P("section", dp, None),
        P("section", dp, None),
        P(dp, None),
    )
    return jax.shard_map(
        per_device,
        mesh=fine,
        in_specs=placed,
        out_specs=(
            P(dp, "section"),
            P(dp, "section"),
            P(dp, None),
            P(None, None, ("section",) + dp),
            P("section", dp, None),
            P("section", dp, None),
            P("section", dp, None),
            P("section", dp, None),
            P("section", dp, None),
            P("section", dp, None),
        ),
        check_vma=False,
    )
```

```python
import math

import jax
import jax.numpy as jnp
from jax import lax
from jax.sharding import Mesh, PartitionSpec as P

HEAD_DIM = 96
LATENTS = 64
LAYERS = 2

epsilon = 1e-05
low = jnp.bfloat16
full = jnp.float32


def unit_rows(values):
    centered = values - jnp.mean(values, axis=-1, keepdims=True)
    variance = jnp.mean(centered * centered, axis=-1, keepdims=True)
    inverse = lax.rsqrt(variance + epsilon)
    return centered * inverse, inverse


def norm_back(unit, inverse, scaled):
    first = jnp.mean(scaled, axis=-1, keepdims=True)
    second = jnp.mean(scaled * unit, axis=-1, keepdims=True)
    return (scaled - first - unit * second) * inverse


def gelu_exact(values):
    return jax.nn.gelu(values, approximate=False)


def matmul(left, right):
    return jnp.dot(left, right, preferred_element_type=full)


def matmul_nt(left, right):
    return lax.dot_general(left, right, (((1,), (1,)), ((), ())), preferred_element_type=full)


def matmul_tn(left, right):
    return lax.dot_general(left, right, (((0,), (0,)), ((), ())), preferred_element_type=full)


def attend_forward(query_heads, key_heads, value_heads, allowed, score_scale):
    scores = jnp.einsum("qhd,khd->hqk", query_heads, key_heads, preferred_element_type=full)
    scores = jnp.where(allowed, scores * score_scale, -1e30)
    row_max = jnp.max(scores, axis=-1, keepdims=True)
    exponent = jnp.exp(scores - row_max)
    row_total = jnp.sum(exponent, axis=-1, keepdims=True)
    weights_low = (exponent / row_total).astype(low)
    attended = jnp.einsum("hqk,khd->qhd", weights_low, value_heads, preferred_element_type=full)
    return attended, row_max + jnp.log(row_total)


def attend_backward(
    query_heads, key_heads, value_heads, allowed, score_scale, log_total, grad_heads
):
    scores = jnp.einsum("qhd,khd->hqk", query_heads, key_heads, preferred_element_type=full)
    scores = jnp.where(allowed, scores * score_scale, -1e30)
    weights_full = jnp.exp(scores - log_total)
    weights_low = weights_full.astype(low)
    grad_value = jnp.einsum("hqk,qhd->khd", weights_low, grad_heads, preferred_element_type=full)
    grad_weights = jnp.einsum(
        "qhd,khd->hqk", grad_heads, value_heads, preferred_element_type=full
    )
    row_inner = jnp.sum(weights_full * grad_weights, axis=-1, keepdims=True)
    grad_scores = (weights_full * (grad_weights - row_inner)).astype(low)
    grad_query = (
        jnp.einsum("hqk,khd->qhd", grad_scores, key_heads, preferred_element_type=full)
        * score_scale
    )
    grad_key = (
        jnp.einsum("hqk,qhd->khd", grad_scores, query_heads, preferred_element_type=full)
        * score_scale
    )
    return grad_query, grad_key, grad_value


def per_device(
    latents,
    media,
    segment_ids,
    slot_map,
    gains,
    w_query,
    w_key,
    w_value,
    w_out,
    w_up,
    w_down,
    cotangent,
):
    dp = ("pair", "core")
    everywhere = ("section",) + dp
    section = lax.axis_index("section")
    section_count = lax.axis_size("section")
    dp_index = lax.axis_index(dp)
    dp_count = lax.axis_size("pair") * lax.axis_size("core")
    on_first = section // 2 == 0
    stride = dp_count // 2
    row_first = dp_index // stride == 0
    seq_rows = segment_ids.shape[1]
    slot_count = slot_map.shape[1]
    feature_width = latents.shape[1]
    latent_rows = latents.shape[0]
    slot_rows = latent_rows // section_count
    inner = w_query.shape[2] // 2
    heads = inner // HEAD_DIM
    score_scale = 1.0 / math.sqrt(HEAD_DIM)

    def pick(first, second):
        return jnp.where(on_first, first, second), jnp.where(on_first, second, first)

    def swapped(value, mask):
        pairs = [(source, source ^ mask) for source in range(section_count)]
        return lax.ppermute(value, "section", pairs)

    def other_core(value):
        return lax.ppermute(value, "core", [(0, 1), (1, 0)])

    def to_second(value):
        return lax.ppermute(value, "section", [(0, 2), (1, 3)])

    def to_first(value):
        return lax.ppermute(value, "section", [(2, 0), (3, 1)])

    def after(value, earlier):
        return lax.optimization_barrier((value, earlier))[0]

    def turn_pairs(flip, back):
        pairs = []
        for source in range(section_count):
            for index in range(dp_count):
                layer, half = divmod(source, 2)
                bit, lowest = divmod(index, stride)
                moved = (layer ^ flip) * stride + lowest
                target = (bit * 2 + half) * dp_count + moved
                pair = (source * dp_count + index, target)
                pairs.append(pair[::-1] if back else pair)
        return pairs

    def exchange_rows(weight):
        half = weight.shape[0] // 2
        near, far = pick(weight[:half], weight[half:])
        first = lax.ppermute(near, everywhere, turn_pairs(0, False))
        second = lax.ppermute(far, everywhere, turn_pairs(1, False))
        return (
            jnp.where(row_first, first, second),
            jnp.where(row_first, second, first),
        )

    def join_rows(first, second):
        near = jnp.where(row_first, first, second)
        far = jnp.where(row_first, second, first)
        near = lax.ppermute(near, everywhere, turn_pairs(0, True))
        far = lax.ppermute(far, everywhere, turn_pairs(1, True))
        return jnp.concatenate(pick(near, far), axis=0).astype(full)

    def fold(piece):
        blocks = [piece[:, i * inner : (i + 1) * inner] for i in range(feature_width // inner)]
        return jnp.concatenate(blocks, axis=0)

    def unfold(stacked):
        count = feature_width // inner
        blocks = stacked.reshape(2, stride, count, -1, inner).transpose(1, 0, 3, 2, 4)
        return blocks.reshape(-1, feature_width)

    def fold_grad(grad):
        count = feature_width // inner
        blocks = grad.reshape(stride, 2, -1, count, inner).transpose(1, 0, 3, 2, 4)
        return blocks.reshape(-1, inner)

    def unfold_piece(piece):
        count = feature_width // inner
        rows = piece.shape[0] // count
        blocks = [piece[i * rows : (i + 1) * rows] for i in range(count)]
        return jnp.concatenate(blocks, axis=1)

    def sum_to_slots(partial):
        blocks = partial.astype(low).reshape(section_count, -1, feature_width)
        arrived = lax.all_to_all(blocks, "section", split_axis=0, concat_axis=0)
        return jnp.sum(arrived.astype(full), axis=0)

    def from_slots(rows):
        return lax.all_gather(rows, "section", axis=0, tiled=True)

    def to_columns(rows):
        moved = lax.all_to_all(
            rows.astype(low), "section", split_axis=1, concat_axis=0, tiled=True
        )
        return moved.astype(full)

    def from_sequences(rows):
        near = lax.all_gather(rows, "pair", axis=0, tiled=True)
        return jnp.concatenate([near, other_core(near)], axis=0)

    def sum_to_sequence(left, right, product):
        half = left.shape[0] // 2
        far = product(left[half:], right).astype(low)
        near = product(left[:half], right) + other_core(far).astype(full)
        blocks = near.astype(low).reshape(-1, slot_rows, feature_width)
        arrived = lax.all_to_all(blocks, "pair", split_axis=0, concat_axis=0)
        return jnp.sum(arrived.astype(full), axis=0)

    def by_distance(rows):
        half = rows.shape[0] // 2
        side = swapped(rows, 1)
        ahead = swapped(rows, 2)
        upper = swapped(side[:half], 2)
        lower = swapped(ahead[half:], 1)
        return rows, side, ahead, jnp.concatenate([upper, lower], axis=0)

    def sum_by_distance(own, side, ahead, across):
        half = own.shape[0] // 2
        across = across.astype(low)
        upper = swapped(across[:half], 2).astype(full)
        lower = swapped(across[half:], 1).astype(full)
        side = jnp.concatenate([side[:half] + upper, side[half:]], axis=0).astype(low)
        ahead = jnp.concatenate([ahead[:half], ahead[half:] + lower], axis=0).astype(low)
        return own + swapped(side, 1).astype(full) + swapped(ahead, 2).astype(full)

    def share_first(lower, upper):
        return jnp.where(on_first, lower, to_second(upper))

    def sum_over_sections(partial):
        blocks = partial.reshape(section_count, -1, feature_width)
        return sum_by_distance(
            *[
                lax.dynamic_index_in_dim(blocks, section ^ mask, 0, keepdims=False)
                for mask in range(4)
            ]
        )

    def gather_sections(rows):
        by_mask = by_distance(rows)
        ordered = []
        for target in range(section_count):
            chosen = by_mask[0]
            for mask in range(1, section_count):
                chosen = jnp.where(section ^ mask == target, by_mask[mask], chosen)
            ordered.append(chosen)
        return jnp.concatenate(ordered, axis=0)

    def column_parts(weight, block):
        rows, width = weight.shape
        split = weight.reshape(rows, width // (2 * block), 2, block)
        return split[:, :, 0].reshape(rows, -1), split[:, :, 1].reshape(rows, -1)

    def interleave(even, odd, block):
        rows, width = even.shape
        parts = [part.reshape(rows, width // block, 1, block) for part in (even, odd)]
        return jnp.concatenate(parts, axis=2).reshape(rows, 2 * width)

    halves = [pick(weight[0, :, :inner], weight[0, :, inner:]) for weight in (w_query, w_key, w_value)]
    own_heads = jnp.concatenate([half[0] for half in halves], axis=1)
    other_heads = swapped(jnp.concatenate([half[1] for half in halves], axis=1), 2)
    qkv_pieces = pick(own_heads, other_heads)
    near_gains = lax.all_gather(after(gains, other_heads), dp, axis=2, tiled=True)
    all_gains = lax.all_gather(near_gains, "section", axis=2, tiled=True)
    out_pieces = exchange_rows(after(w_out[0], other_heads))

    def gather(piece):
        return lax.all_gather(piece, dp, axis=0, tiled=True)

    half_hidden = w_down.shape[1] // 2
    half_depth = w_up.shape[1] // 2
    down_shared = by_distance(
        share_first(*[after(half, other_heads) for half in (w_down[0, :half_hidden], w_down[0, half_hidden:])])
    )
    up_turned = lax.all_to_all(
        after(share_first(w_up[0, :half_depth], w_up[0, half_depth:]), (all_gains, down_shared[3])),
        dp,
        split_axis=1,
        concat_axis=0,
        tiled=True,
    )
    up_shared = by_distance(up_turned)

    def in_depth(near, far):
        parts = [part.reshape(dp_count, 1, half_depth, -1) for part in pick(near, far)]
        return jnp.concatenate(parts, axis=1).reshape(feature_width, -1)

    down_first = jnp.concatenate(
        pick(down_shared[0], down_shared[2]) + pick(down_shared[1], down_shared[3]), axis=0
    )
    up_first = jnp.concatenate(
        [in_depth(up_shared[0], up_shared[2]), in_depth(up_shared[1], up_shared[3])], axis=1
    )

    qkv_first = gather(qkv_pieces[0])
    out_first = unfold(gather(after(fold(out_pieces[0]), qkv_pieces[0])))
    stacked = gather(
        jnp.concatenate([qkv_pieces[1], fold(out_pieces[1])], axis=1)
    )
    up_even, up_odd = column_parts(w_up[0], half_hidden)
    up_piece, down_piece = after(
        (up_even, w_down[0, :half_hidden]), (up_turned, down_shared[3])
    )
    ffn_piece = jnp.concatenate(
        [
            jnp.where(on_first, to_first(up_piece), up_odd),
            jnp.where(on_first, to_first(down_piece), w_down[0, half_hidden:]),
        ],
        axis=1,
    )
    ffn_second = gather(ffn_piece)
    hidden_width = up_even.shape[1]
    qkv_second = stacked[:, : 3 * inner]
    out_second = unfold(stacked[:, 3 * inner :])
    up_w = (up_first, ffn_second[:, :hidden_width])
    down_w = (down_first, ffn_second[:, hidden_width:])
    qkv_w = (qkv_first, qkv_second)
    out_w = (out_first, out_second)
    query_w = [weight[:, :inner] for weight in qkv_w]
    key_w = [weight[:, inner : 2 * inner] for weight in qkv_w]
    value_w = [weight[:, 2 * inner :] for weight in qkv_w]

    image_hot = segment_ids[:, :, None] == jnp.arange(slot_count, dtype=jnp.int32)[None, None, :]
    media_slot = jnp.sum(jnp.where(image_hot, slot_map[:, None, :], 0), axis=2) - (
        segment_ids < 0
    ).astype(jnp.int32)
    media_unit, media_inverse = unit_rows(media.astype(full))
    latent_slot = jnp.arange(latent_rows, dtype=jnp.int32) // LATENTS
    key_slot = jnp.concatenate([media_slot[0], latent_slot])
    allowed = latent_slot[None, :, None] == key_slot[None, None, :]

    def split_heads(rows):
        return rows.reshape(rows.shape[0], heads, HEAD_DIM)

    media_low = []
    media_key = []
    media_value = []
    for layer in range(LAYERS):
        media_low.append((media_unit * all_gains[layer, 0]).astype(low))
        media_key.append(matmul(media_low[layer], key_w[layer]).astype(low))
        media_value.append(matmul(media_low[layer], value_w[layer]).astype(low))

    saved = []
    current = lax.dynamic_slice_in_dim(latents, section * slot_rows, slot_rows, 0).astype(full)
    grad_rows = lax.dynamic_slice_in_dim(cotangent, section * slot_rows, slot_rows, 0).astype(full)
    grad_low = cotangent
    for layer in range(LAYERS):
        unit_in, inverse_in = unit_rows(current)
        if layer == 0:
            whole_unit = unit_rows(latents.astype(full))[0]
            latent_low = (whole_unit * all_gains[layer, 1]).astype(low)
        else:
            latent_low = from_slots((unit_in * all_gains[layer, 1]).astype(low))
        projected = matmul(latent_low, qkv_w[layer]).astype(low)
        query_low = projected[:, :inner]
        key_heads = split_heads(
            jnp.concatenate([media_key[layer], projected[:, inner : 2 * inner]], axis=0)
        )
        value_heads = split_heads(
            jnp.concatenate([media_value[layer], projected[:, 2 * inner :]], axis=0)
        )
        query_heads = split_heads(query_low)
        attended, log_total = attend_forward(
            query_heads, key_heads, value_heads, allowed, score_scale
        )
        attended_low = attended.reshape(-1, inner).astype(low)
        if layer == 0:
            attended_low = after(attended_low, up_turned)
        middle = current + sum_to_slots(matmul(attended_low, out_w[layer]))
        unit_mid, inverse_mid = unit_rows(middle)
        ffn_low = (unit_mid * all_gains[layer, 2]).astype(low)
        ffn_low = from_slots(ffn_low) if layer else from_sequences(ffn_low)
        hidden_pre = matmul(ffn_low, up_w[layer])
        active_low = gelu_exact(hidden_pre).astype(low)
        if layer:
            current = middle + sum_to_slots(matmul(active_low, down_w[layer]))
        else:
            current = middle + sum_to_sequence(active_low, down_w[layer], matmul)
        saved.append(
            (
                unit_in,
                inverse_in,
                latent_low,
                query_heads,
                key_heads,
                value_heads,
                log_total,
                attended_low,
                unit_mid,
                inverse_mid,
                ffn_low,
                hidden_pre,
                active_low,
            )
        )

    def scatter(blocks):
        return lax.psum_scatter(blocks, dp, scatter_dimension=0, tiled=True)

    gain_rows = [None] * LAYERS
    media_scaled = None
    pieces = [None] * LAYERS
    for layer in (1, 0):
        (
            unit_in,
            inverse_in,
            latent_low,
            query_heads,
            key_heads,
            value_heads,
            log_total,
            attended_low,
            unit_mid,
            inverse_mid,
            ffn_low,
            hidden_pre,
            active_low,
        ) = saved[layer]
        grad_active = matmul_nt(grad_low, down_w[layer])
        grad_hidden = jax.vjp(gelu_exact, hidden_pre)[1](grad_active)[0].astype(low)
        down_grad = matmul_tn(active_low, grad_low)
        up_grad = matmul_tn(ffn_low, grad_hidden)
        if layer:
            ffn_piece = scatter(
                jnp.concatenate([up_grad.astype(low), down_grad.astype(low)], axis=1)
            )
            ffn_grad = sum_to_slots(matmul_nt(grad_hidden, up_w[layer]))
        else:
            ffn_grad = sum_to_sequence(grad_hidden, up_w[layer], matmul_nt)
            blocks = down_grad.reshape(2, 2, half_hidden, feature_width)
            own, ahead = pick(blocks[0, 0], blocks[0, 1])
            side, across = pick(blocks[1, 0], blocks[1, 1])
            down_half = sum_by_distance(own, side, ahead, across).astype(low)
            width = up_grad.shape[1] // 2
            blocks = up_grad.reshape(dp_count, 2, half_depth, 2 * width)
            blocks = [blocks[:, i].reshape(-1, 2 * width) for i in range(2)]
            own, ahead = pick(blocks[0][:, :width], blocks[1][:, :width])
            side, across = pick(blocks[0][:, width:], blocks[1][:, width:])
            up_half = sum_by_distance(own, side, ahead, across).astype(low)
            up_half = lax.all_to_all(up_half, dp, split_axis=0, concat_axis=1, tiled=True)
        gain_ffn_grad = jnp.sum(ffn_grad * unit_mid, axis=0)
        grad_middle = grad_rows + norm_back(
            unit_mid, inverse_mid, ffn_grad * all_gains[layer, 2]
        )
        middle_low = grad_middle.astype(low)
        if layer == 0:
            middle_low = after(middle_low, ffn_piece)
        middle_low = from_slots(middle_low)
        grad_heads = split_heads(matmul_nt(middle_low, out_w[layer]).astype(low))
        out_grad = matmul_tn(attended_low, middle_low)
        grad_query, grad_key, grad_value = attend_backward(
            query_heads, key_heads, value_heads, allowed, score_scale, log_total, grad_heads
        )
        grad_query = grad_query.reshape(-1, inner).astype(low)
        grad_key = grad_key.reshape(-1, inner).astype(low)
        grad_value = grad_value.reshape(-1, inner).astype(low)
        latent_part = (
            matmul_nt(grad_query, query_w[layer])
            + matmul_nt(grad_key[seq_rows:], key_w[layer])
            + matmul_nt(grad_value[seq_rows:], value_w[layer])
        )
        latent_grad_rows = sum_to_slots(latent_part)
        gain_latent_grad = jnp.sum(latent_grad_rows * unit_in, axis=0)
        grad_rows = grad_middle + norm_back(
            unit_in, inverse_in, latent_grad_rows * all_gains[layer, 1]
        )
        both_low = jnp.concatenate([media_low[layer], latent_low], axis=0)
        query_grad = matmul_tn(latent_low, grad_query)
        key_grad = matmul_tn(both_low, grad_key)
        value_grad = matmul_tn(both_low, grad_value)
        qkv_grad = jnp.concatenate(
            [query_grad.astype(low), key_grad.astype(low), value_grad.astype(low)], axis=1
        )
        pieces[layer] = scatter(
            jnp.concatenate([qkv_grad, fold_grad(out_grad.astype(low))], axis=1)
        )
        if layer > 0:
            grad_low = from_sequences(grad_rows.astype(low))
        media_part = matmul_nt(grad_key[:seq_rows], key_w[layer]) + matmul_nt(
            grad_value[:seq_rows], value_w[layer]
        )
        gain_media_grad = jnp.sum(media_part * media_unit, axis=0)
        scaled = media_part * all_gains[layer, 0]
        media_scaled = scaled if media_scaled is None else media_scaled + scaled
        gain_rows[layer] = jnp.stack([gain_media_grad, gain_latent_grad, gain_ffn_grad])
    latents_out = to_columns(current)
    latent_grad = to_columns(grad_rows)
    media_rows = seq_rows // section_count
    media_sum = sum_over_sections(media_scaled)
    own_unit = lax.dynamic_slice_in_dim(media_unit, section * media_rows, media_rows, 0)
    own_inverse = lax.dynamic_slice_in_dim(media_inverse, section * media_rows, media_rows, 0)
    media_grad = gather_sections(norm_back(own_unit, own_inverse, media_sum).astype(low)).astype(
        full
    )
    gain_parts = jnp.stack(gain_rows).reshape(LAYERS, 3, section_count, -1)
    gain_parts = jnp.sum(
        lax.all_to_all(gain_parts, "section", split_axis=2, concat_axis=2), axis=2
    )
    gain_parts = gain_parts.reshape(LAYERS, 3, dp_count, -1)
    gain_grad = jnp.sum(lax.all_to_all(gain_parts, dp, split_axis=2, concat_axis=2), axis=2)

    qkv_parts = [piece[:, : 3 * inner] for piece in pieces]
    own, other = pick(qkv_parts[0], qkv_parts[1])
    lower, upper = pick(own, swapped(other, 2))
    qkv_grads = [
        jnp.concatenate(
            [lower[:, i * inner : (i + 1) * inner], upper[:, i * inner : (i + 1) * inner]], axis=1
        ).astype(full)
        for i in range(3)
    ]
    out_grad = join_rows(*[unfold_piece(piece[:, 3 * inner :]) for piece in pieces])
    back = to_second(ffn_piece)
    up_second_grad = interleave(back[:, :hidden_width], ffn_piece[:, :hidden_width], half_hidden)
    down_second_grad = jnp.concatenate([back[:, hidden_width:], ffn_piece[:, hidden_width:]], axis=0)
    up_first_grad = jnp.concatenate([up_half, to_first(up_half)], axis=0)
    down_first_grad = jnp.concatenate([down_half, to_first(down_half)], axis=0)
    up_grad = jnp.where(on_first, up_first_grad, up_second_grad).astype(full)
    down_grad = jnp.where(on_first, down_first_grad, down_second_grad).astype(full)
    return (
        latents_out,
        latent_grad,
        media_grad,
        gain_grad,
        qkv_grads[0][None],
        qkv_grads[1][None],
        qkv_grads[2][None],
        out_grad[None],
        up_grad[None],
        down_grad[None],
    )


def solution(mesh):
    section_count, dp_count = mesh.devices.shape
    fine = Mesh(
        mesh.devices.reshape(section_count, dp_count // 2, 2), ("section", "pair", "core")
    )
    dp = ("pair", "core")
    placed = (
        P(dp, None),
        P(dp, None),
        P(dp, None),
        P(dp, None),
        P(None, None, ("section",) + dp),
        P("section", dp, None),
        P("section", dp, None),
        P("section", dp, None),
        P("section", dp, None),
        P("section", dp, None),
        P("section", dp, None),
        P(dp, None),
    )
    return jax.shard_map(
        per_device,
        mesh=fine,
        in_specs=placed,
        out_specs=(
            P(dp, "section"),
            P(dp, "section"),
            P(dp, None),
            P(None, None, ("section",) + dp),
            P("section", dp, None),
            P("section", dp, None),
            P("section", dp, None),
            P("section", dp, None),
            P("section", dp, None),
            P("section", dp, None),
        ),
        check_vma=False,
    )
```

```python
import math

import jax
import jax.numpy as jnp
from jax import lax
from jax.sharding import Mesh, PartitionSpec as P

HEAD_DIM = 96
LATENTS = 64
LAYERS = 2

epsilon = 1e-05
low = jnp.bfloat16
full = jnp.float32


def unit_rows(values):
    centered = values - jnp.mean(values, axis=-1, keepdims=True)
    variance = jnp.mean(centered * centered, axis=-1, keepdims=True)
    inverse = lax.rsqrt(variance + epsilon)
    return centered * inverse, inverse


def norm_back(unit, inverse, scaled):
    first = jnp.mean(scaled, axis=-1, keepdims=True)
    second = jnp.mean(scaled * unit, axis=-1, keepdims=True)
    return (scaled - first - unit * second) * inverse


def gelu_exact(values):
    return jax.nn.gelu(values, approximate=False)


def matmul(left, right):
    return jnp.dot(left, right, preferred_element_type=full)


def matmul_nt(left, right):
    return lax.dot_general(left, right, (((1,), (1,)), ((), ())), preferred_element_type=full)


def matmul_tn(left, right):
    return lax.dot_general(left, right, (((0,), (0,)), ((), ())), preferred_element_type=full)


def attend_forward(query_heads, key_heads, value_heads, allowed, score_scale):
    scores = jnp.einsum("qhd,khd->hqk", query_heads, key_heads, preferred_element_type=full)
    scores = jnp.where(allowed, scores * score_scale, -1e30)
    row_max = jnp.max(scores, axis=-1, keepdims=True)
    exponent = jnp.exp(scores - row_max)
    row_total = jnp.sum(exponent, axis=-1, keepdims=True)
    weights_low = (exponent / row_total).astype(low)
    attended = jnp.einsum("hqk,khd->qhd", weights_low, value_heads, preferred_element_type=full)
    return attended, row_max + jnp.log(row_total)


def attend_backward(
    query_heads, key_heads, value_heads, allowed, score_scale, log_total, grad_heads
):
    scores = jnp.einsum("qhd,khd->hqk", query_heads, key_heads, preferred_element_type=full)
    scores = jnp.where(allowed, scores * score_scale, -1e30)
    weights_full = jnp.exp(scores - log_total)
    weights_low = weights_full.astype(low)
    grad_value = jnp.einsum("hqk,qhd->khd", weights_low, grad_heads, preferred_element_type=full)
    grad_weights = jnp.einsum(
        "qhd,khd->hqk", grad_heads, value_heads, preferred_element_type=full
    )
    row_inner = jnp.sum(weights_full * grad_weights, axis=-1, keepdims=True)
    grad_scores = (weights_full * (grad_weights - row_inner)).astype(low)
    grad_query = (
        jnp.einsum("hqk,khd->qhd", grad_scores, key_heads, preferred_element_type=full)
        * score_scale
    )
    grad_key = (
        jnp.einsum("hqk,qhd->khd", grad_scores, query_heads, preferred_element_type=full)
        * score_scale
    )
    return grad_query, grad_key, grad_value


def per_device(
    latents,
    media,
    segment_ids,
    slot_map,
    gains,
    w_query,
    w_key,
    w_value,
    w_out,
    w_up,
    w_down,
    cotangent,
):
    dp = ("pair", "core")
    everywhere = ("section",) + dp
    section = lax.axis_index("section")
    section_count = lax.axis_size("section")
    dp_index = lax.axis_index(dp)
    dp_count = lax.axis_size("pair") * lax.axis_size("core")
    on_first = section // 2 == 0
    stride = dp_count // 2
    row_first = dp_index // stride == 0
    seq_rows = segment_ids.shape[1]
    slot_count = slot_map.shape[1]
    feature_width = latents.shape[1]
    latent_rows = latents.shape[0]
    slot_rows = latent_rows // section_count
    inner = w_query.shape[2] // 2
    heads = inner // HEAD_DIM
    score_scale = 1.0 / math.sqrt(HEAD_DIM)

    def pick(first, second):
        return jnp.where(on_first, first, second), jnp.where(on_first, second, first)

    def swapped(value, mask):
        pairs = [(source, source ^ mask) for source in range(section_count)]
        return lax.ppermute(value, "section", pairs)

    def other_core(value):
        return lax.ppermute(value, "core", [(0, 1), (1, 0)])

    def to_second(value):
        return lax.ppermute(value, "section", [(0, 2), (1, 3)])

    def to_first(value):
        return lax.ppermute(value, "section", [(2, 0), (3, 1)])

    def after(value, earlier):
        return lax.optimization_barrier((value, earlier))[0]

    def turn_pairs(flip, back):
        pairs = []
        for source in range(section_count):
            for index in range(dp_count):
                layer, half = divmod(source, 2)
                bit, lowest = divmod(index, stride)
                moved = (layer ^ flip) * stride + lowest
                target = (bit * 2 + half) * dp_count + moved
                pair = (source * dp_count + index, target)
                pairs.append(pair[::-1] if back else pair)
        return pairs

    def exchange_rows(weight):
        half = weight.shape[0] // 2
        near, far = pick(weight[:half], weight[half:])
        first = lax.ppermute(near, everywhere, turn_pairs(0, False))
        second = lax.ppermute(far, everywhere, turn_pairs(1, False))
        return (
            jnp.where(row_first, first, second),
            jnp.where(row_first, second, first),
        )

    def join_rows(first, second):
        near = jnp.where(row_first, first, second)
        far = jnp.where(row_first, second, first)
        near = lax.ppermute(near, everywhere, turn_pairs(0, True))
        far = lax.ppermute(far, everywhere, turn_pairs(1, True))
        return jnp.concatenate(pick(near, far), axis=0).astype(full)

    def fold(piece):
        blocks = [piece[:, i * inner : (i + 1) * inner] for i in range(feature_width // inner)]
        return jnp.concatenate(blocks, axis=0)

    def unfold(stacked):
        count = feature_width // inner
        blocks = stacked.reshape(2, stride, count, -1, inner).transpose(1, 0, 3, 2, 4)
        return blocks.reshape(-1, feature_width)

    def by_device(grad):
        blocks = grad.reshape(stride, 2, -1, feature_width).transpose(1, 0, 2, 3)
        return blocks.reshape(-1, feature_width)

    def sum_to_slots(partial):
        blocks = partial.astype(low).reshape(section_count, -1, feature_width)
        arrived = lax.all_to_all(blocks, "section", split_axis=0, concat_axis=0)
        return jnp.sum(arrived.astype(full), axis=0)

    def from_slots(rows):
        return lax.all_gather(rows, "section", axis=0, tiled=True)

    def to_columns(rows):
        moved = lax.all_to_all(
            rows.astype(low), "section", split_axis=1, concat_axis=0, tiled=True
        )
        return moved.astype(full)

    def from_sequences(rows):
        near = lax.all_gather(rows, "pair", axis=0, tiled=True)
        return jnp.concatenate([near, other_core(near)], axis=0)

    def sum_to_sequence(left, right, product):
        half = left.shape[0] // 2
        far = product(left[half:], right).astype(low)
        near = product(left[:half], right) + other_core(far).astype(full)
        blocks = near.astype(low).reshape(-1, slot_rows, feature_width)
        arrived = lax.all_to_all(blocks, "pair", split_axis=0, concat_axis=0)
        return jnp.sum(arrived.astype(full), axis=0)

    def by_distance(rows):
        half = rows.shape[0] // 2
        side = swapped(rows, 1)
        ahead = swapped(rows, 2)
        upper = swapped(side[:half], 2)
        lower = swapped(ahead[half:], 1)
        return rows, side, ahead, jnp.concatenate([upper, lower], axis=0)

    def sum_by_distance(own, side, ahead, across):
        half = own.shape[0] // 2
        across = across.astype(low)
        upper = swapped(across[:half], 2).astype(full)
        lower = swapped(across[half:], 1).astype(full)
        side = jnp.concatenate([side[:half] + upper, side[half:]], axis=0).astype(low)
        ahead = jnp.concatenate([ahead[:half], ahead[half:] + lower], axis=0).astype(low)
        return own + swapped(side, 1).astype(full) + swapped(ahead, 2).astype(full)

    def share_first(lower, upper):
        return jnp.where(on_first, lower, to_second(upper))

    def sum_over_sections(partial):
        blocks = partial.reshape(section_count, -1, feature_width)
        return sum_by_distance(
            *[
                lax.dynamic_index_in_dim(blocks, section ^ mask, 0, keepdims=False)
                for mask in range(4)
            ]
        )

    def gather_sections(rows):
        by_mask = by_distance(rows)
        ordered = []
        for target in range(section_count):
            chosen = by_mask[0]
            for mask in range(1, section_count):
                chosen = jnp.where(section ^ mask == target, by_mask[mask], chosen)
            ordered.append(chosen)
        return jnp.concatenate(ordered, axis=0)

    def column_parts(weight, block):
        rows, width = weight.shape
        split = weight.reshape(rows, width // (2 * block), 2, block)
        return split[:, :, 0].reshape(rows, -1), split[:, :, 1].reshape(rows, -1)

    def interleave(even, odd, block):
        rows, width = even.shape
        parts = [part.reshape(rows, width // block, 1, block) for part in (even, odd)]
        return jnp.concatenate(parts, axis=2).reshape(rows, 2 * width)

    halves = [pick(weight[0, :, :inner], weight[0, :, inner:]) for weight in (w_query, w_key, w_value)]
    own_heads = jnp.concatenate([half[0] for half in halves], axis=1)
    other_heads = swapped(jnp.concatenate([half[1] for half in halves], axis=1), 2)
    qkv_pieces = pick(own_heads, other_heads)
    near_gains = lax.all_gather(after(gains, other_heads), dp, axis=2, tiled=True)
    all_gains = lax.all_gather(near_gains, "section", axis=2, tiled=True)
    out_pieces = exchange_rows(after(w_out[0], other_heads))

    def gather(piece):
        return lax.all_gather(piece, dp, axis=0, tiled=True)

    stacked = [
        gather(jnp.concatenate([qkv_pieces[layer], fold(out_pieces[layer])], axis=1))
        for layer in range(LAYERS)
    ]
    qkv_w = [weight[:, : 3 * inner] for weight in stacked]
    out_w = [unfold(weight[:, 3 * inner :]) for weight in stacked]

    half_hidden = w_down.shape[1] // 2
    half_depth = w_up.shape[1] // 2
    up_turned = lax.all_to_all(
        share_first(*after((w_up[0, :half_depth], w_up[0, half_depth:]), other_heads)),
        dp,
        split_axis=1,
        concat_axis=0,
        tiled=True,
    )
    down_shared = by_distance(
        share_first(*after((w_down[0, :half_hidden], w_down[0, half_hidden:]), other_heads))
    )
    up_shared = by_distance(up_turned)

    def in_depth(near, far):
        parts = [part.reshape(dp_count, 1, half_depth, -1) for part in pick(near, far)]
        return jnp.concatenate(parts, axis=1).reshape(feature_width, -1)

    down_first = jnp.concatenate(
        pick(down_shared[0], down_shared[2]) + pick(down_shared[1], down_shared[3]), axis=0
    )
    up_first = jnp.concatenate(
        [in_depth(up_shared[0], up_shared[2]), in_depth(up_shared[1], up_shared[3])], axis=1
    )

    up_even, up_odd = column_parts(w_up[0], half_hidden)
    up_piece, down_piece = after((up_even, w_down[0, :half_hidden]), other_heads)
    down_second = gather(
        jnp.where(on_first, to_first(down_piece), w_down[0, half_hidden:])
    )
    up_second = gather(jnp.where(on_first, to_first(up_piece), up_odd))
    up_w = (up_first, up_second)
    down_w = (down_first, down_second)
    query_w = [weight[:, :inner] for weight in qkv_w]
    key_w = [weight[:, inner : 2 * inner] for weight in qkv_w]
    value_w = [weight[:, 2 * inner :] for weight in qkv_w]

    image_hot = segment_ids[:, :, None] == jnp.arange(slot_count, dtype=jnp.int32)[None, None, :]
    media_slot = jnp.sum(jnp.where(image_hot, slot_map[:, None, :], 0), axis=2) - (
        segment_ids < 0
    ).astype(jnp.int32)
    media_unit, media_inverse = unit_rows(media.astype(full))
    latent_slot = jnp.arange(latent_rows, dtype=jnp.int32) // LATENTS
    key_slot = jnp.concatenate([media_slot[0], latent_slot])
    allowed = latent_slot[None, :, None] == key_slot[None, None, :]

    def split_heads(rows):
        return rows.reshape(rows.shape[0], heads, HEAD_DIM)

    media_low = []
    media_key = []
    media_value = []
    for layer in range(LAYERS):
        media_low.append((media_unit * all_gains[layer, 0]).astype(low))
        media_key.append(matmul(media_low[layer], key_w[layer]).astype(low))
        media_value.append(matmul(media_low[layer], value_w[layer]).astype(low))

    saved = []
    current = lax.dynamic_slice_in_dim(latents, section * slot_rows, slot_rows, 0).astype(full)
    grad_rows = lax.dynamic_slice_in_dim(cotangent, section * slot_rows, slot_rows, 0).astype(full)
    grad_low = cotangent
    for layer in range(LAYERS):
        unit_in, inverse_in = unit_rows(current)
        if layer == 0:
            whole_unit = unit_rows(latents.astype(full))[0]
            latent_low = (whole_unit * all_gains[layer, 1]).astype(low)
        else:
            latent_low = from_slots((unit_in * all_gains[layer, 1]).astype(low))
        projected = matmul(latent_low, qkv_w[layer]).astype(low)
        query_low = projected[:, :inner]
        key_heads = split_heads(
            jnp.concatenate([media_key[layer], projected[:, inner : 2 * inner]], axis=0)
        )
        value_heads = split_heads(
            jnp.concatenate([media_value[layer], projected[:, 2 * inner :]], axis=0)
        )
        query_heads = split_heads(query_low)
        attended, log_total = attend_forward(
            query_heads, key_heads, value_heads, allowed, score_scale
        )
        attended_low = attended.reshape(-1, inner).astype(low)
        middle = current + sum_to_slots(matmul(attended_low, out_w[layer]))
        unit_mid, inverse_mid = unit_rows(middle)
        ffn_low = (unit_mid * all_gains[layer, 2]).astype(low)
        ffn_low = from_slots(ffn_low) if layer else from_sequences(ffn_low)
        hidden_pre = matmul(ffn_low, up_w[layer])
        active_low = gelu_exact(hidden_pre).astype(low)
        if layer:
            current = middle + sum_to_slots(matmul(active_low, down_w[layer]))
        else:
            current = middle + sum_to_sequence(active_low, down_w[layer], matmul)
        saved.append(
            (
                unit_in,
                inverse_in,
                latent_low,
                query_heads,
                key_heads,
                value_heads,
                log_total,
                attended_low,
                unit_mid,
                inverse_mid,
                ffn_low,
                hidden_pre,
                active_low,
            )
        )

    def scatter(blocks):
        return lax.psum_scatter(blocks, dp, scatter_dimension=0, tiled=True)

    gain_rows = [None] * LAYERS
    media_scaled = None
    pieces = [None] * LAYERS
    for layer in (1, 0):
        (
            unit_in,
            inverse_in,
            latent_low,
            query_heads,
            key_heads,
            value_heads,
            log_total,
            attended_low,
            unit_mid,
            inverse_mid,
            ffn_low,
            hidden_pre,
            active_low,
        ) = saved[layer]
        grad_active = matmul_nt(grad_low, down_w[layer])
        grad_hidden = jax.vjp(gelu_exact, hidden_pre)[1](grad_active)[0].astype(low)
        down_grad = matmul_tn(active_low, grad_low)
        if layer:
            down_grad = down_grad.astype(low)
            grad_hidden = after(grad_hidden, down_grad)
        up_grad = matmul_tn(ffn_low, grad_hidden)
        if layer:
            ffn_pieces = (scatter(down_grad), scatter(up_grad.astype(low)))
            ffn_grad = sum_to_slots(matmul_nt(grad_hidden, up_w[layer]))
        else:
            ffn_grad = sum_to_sequence(grad_hidden, up_w[layer], matmul_nt)
            blocks = down_grad.reshape(2, 2, half_hidden, feature_width)
            own, ahead = pick(blocks[0, 0], blocks[0, 1])
            side, across = pick(blocks[1, 0], blocks[1, 1])
            down_half = sum_by_distance(own, side, ahead, across).astype(low)
            width = up_grad.shape[1] // 2
            blocks = up_grad.reshape(dp_count, 2, half_depth, 2 * width)
            blocks = [blocks[:, i].reshape(-1, 2 * width) for i in range(2)]
            own, ahead = pick(blocks[0][:, :width], blocks[1][:, :width])
            side, across = pick(blocks[0][:, width:], blocks[1][:, width:])
            up_half = sum_by_distance(own, side, ahead, across).astype(low)
            up_half = lax.all_to_all(up_half, dp, split_axis=0, concat_axis=1, tiled=True)
        gain_ffn_grad = jnp.sum(ffn_grad * unit_mid, axis=0)
        grad_middle = grad_rows + norm_back(
            unit_mid, inverse_mid, ffn_grad * all_gains[layer, 2]
        )
        middle_low = from_slots(grad_middle.astype(low))
        grad_heads = split_heads(matmul_nt(middle_low, out_w[layer]).astype(low))
        out_piece = scatter(by_device(matmul_tn(attended_low, middle_low)).astype(low))
        grad_query, grad_key, grad_value = attend_backward(
            query_heads, key_heads, value_heads, allowed, score_scale, log_total, grad_heads
        )
        grad_query = grad_query.reshape(-1, inner).astype(low)
        grad_key = grad_key.reshape(-1, inner).astype(low)
        grad_value = grad_value.reshape(-1, inner).astype(low)
        latent_part = (
            matmul_nt(grad_query, query_w[layer])
            + matmul_nt(grad_key[seq_rows:], key_w[layer])
            + matmul_nt(grad_value[seq_rows:], value_w[layer])
        )
        latent_grad_rows = sum_to_slots(latent_part)
        gain_latent_grad = jnp.sum(latent_grad_rows * unit_in, axis=0)
        grad_rows = grad_middle + norm_back(
            unit_in, inverse_in, latent_grad_rows * all_gains[layer, 1]
        )
        both_low = jnp.concatenate([media_low[layer], latent_low], axis=0)
        all_grads = jnp.concatenate(
            [jnp.pad(grad_query, ((seq_rows, 0), (0, 0))), grad_key, grad_value], axis=1
        )
        qkv_grad = matmul_tn(both_low, all_grads).astype(low)
        pieces[layer] = (scatter(qkv_grad), out_piece)
        if layer > 0:
            grad_low = from_sequences(grad_rows.astype(low))
            grad_low = after(grad_low, ffn_pieces)
        media_part = matmul_nt(grad_key[:seq_rows], key_w[layer]) + matmul_nt(
            grad_value[:seq_rows], value_w[layer]
        )
        gain_media_grad = jnp.sum(media_part * media_unit, axis=0)
        scaled = media_part * all_gains[layer, 0]
        media_scaled = scaled if media_scaled is None else media_scaled + scaled
        gain_rows[layer] = jnp.stack([gain_media_grad, gain_latent_grad, gain_ffn_grad])
    latents_out = to_columns(current)
    latent_grad = to_columns(after(grad_rows, pieces[1]))
    media_rows = seq_rows // section_count
    media_sum = sum_over_sections(media_scaled)
    own_unit = lax.dynamic_slice_in_dim(media_unit, section * media_rows, media_rows, 0)
    own_inverse = lax.dynamic_slice_in_dim(media_inverse, section * media_rows, media_rows, 0)
    media_grad = gather_sections(norm_back(own_unit, own_inverse, media_sum).astype(low)).astype(
        full
    )
    gain_parts = jnp.stack(gain_rows).reshape(LAYERS, 3, section_count, -1)
    gain_parts = jnp.sum(
        lax.all_to_all(gain_parts, "section", split_axis=2, concat_axis=2), axis=2
    )
    gain_parts = gain_parts.reshape(LAYERS, 3, dp_count, -1)
    gain_grad = jnp.sum(lax.all_to_all(gain_parts, dp, split_axis=2, concat_axis=2), axis=2)

    qkv_parts = [piece[0] for piece in pieces]
    own, other = pick(qkv_parts[0], qkv_parts[1])
    lower, upper = pick(own, swapped(other, 2))
    qkv_grads = [
        jnp.concatenate(
            [lower[:, i * inner : (i + 1) * inner], upper[:, i * inner : (i + 1) * inner]], axis=1
        ).astype(full)
        for i in range(3)
    ]
    out_grad = join_rows(*[piece[1] for piece in pieces])
    down_piece, up_piece = ffn_pieces
    up_second_grad = interleave(to_second(up_piece), up_piece, half_hidden)
    down_second_grad = jnp.concatenate([to_second(down_piece), down_piece], axis=0)
    up_first_grad = jnp.concatenate([up_half, to_first(up_half)], axis=0)
    down_first_grad = jnp.concatenate([down_half, to_first(down_half)], axis=0)
    up_grad = jnp.where(on_first, up_first_grad, up_second_grad).astype(full)
    down_grad = jnp.where(on_first, down_first_grad, down_second_grad).astype(full)
    return (
        latents_out,
        latent_grad,
        media_grad,
        gain_grad,
        qkv_grads[0][None],
        qkv_grads[1][None],
        qkv_grads[2][None],
        out_grad[None],
        up_grad[None],
        down_grad[None],
    )


def solution(mesh):
    section_count, dp_count = mesh.devices.shape
    fine = Mesh(
        mesh.devices.reshape(section_count, dp_count // 2, 2), ("section", "pair", "core")
    )
    dp = ("pair", "core")
    placed = (
        P(dp, None),
        P(dp, None),
        P(dp, None),
        P(dp, None),
        P(None, None, ("section",) + dp),
        P("section", dp, None),
        P("section", dp, None),
        P("section", dp, None),
        P("section", dp, None),
        P("section", dp, None),
        P("section", dp, None),
        P(dp, None),
    )
    return jax.shard_map(
        per_device,
        mesh=fine,
        in_specs=placed,
        out_specs=(
            P(dp, "section"),
            P(dp, "section"),
            P(dp, None),
            P(None, None, ("section",) + dp),
            P("section", dp, None),
            P("section", dp, None),
            P("section", dp, None),
            P("section", dp, None),
            P("section", dp, None),
            P("section", dp, None),
        ),
        check_vma=False,
    )
```

```python
import math

import jax
import jax.numpy as jnp
from jax import lax
from jax.sharding import Mesh, PartitionSpec as P

HEAD_DIM = 96
LATENTS = 64
LAYERS = 2

epsilon = 1e-05
low = jnp.bfloat16
full = jnp.float32


def unit_rows(values):
    centered = values - jnp.mean(values, axis=-1, keepdims=True)
    variance = jnp.mean(centered * centered, axis=-1, keepdims=True)
    inverse = lax.rsqrt(variance + epsilon)
    return centered * inverse, inverse


def norm_back(unit, inverse, scaled):
    first = jnp.mean(scaled, axis=-1, keepdims=True)
    second = jnp.mean(scaled * unit, axis=-1, keepdims=True)
    return (scaled - first - unit * second) * inverse


def gelu_exact(values):
    return jax.nn.gelu(values, approximate=False)


def matmul(left, right):
    return jnp.dot(left, right, preferred_element_type=full)


def matmul_nt(left, right):
    return lax.dot_general(left, right, (((1,), (1,)), ((), ())), preferred_element_type=full)


def matmul_tn(left, right):
    return lax.dot_general(left, right, (((0,), (0,)), ((), ())), preferred_element_type=full)


def attend_forward(query_heads, key_heads, value_heads, allowed, score_scale):
    scores = jnp.einsum("qhd,khd->hqk", query_heads, key_heads, preferred_element_type=full)
    scores = jnp.where(allowed, scores * score_scale, -1e30)
    row_max = jnp.max(scores, axis=-1, keepdims=True)
    exponent = jnp.exp(scores - row_max)
    row_total = jnp.sum(exponent, axis=-1, keepdims=True)
    weights_low = (exponent / row_total).astype(low)
    attended = jnp.einsum("hqk,khd->qhd", weights_low, value_heads, preferred_element_type=full)
    return attended, row_max + jnp.log(row_total)


def attend_backward(
    query_heads, key_heads, value_heads, allowed, score_scale, log_total, grad_heads
):
    scores = jnp.einsum("qhd,khd->hqk", query_heads, key_heads, preferred_element_type=full)
    scores = jnp.where(allowed, scores * score_scale, -1e30)
    weights_full = jnp.exp(scores - log_total)
    weights_low = weights_full.astype(low)
    grad_value = jnp.einsum("hqk,qhd->khd", weights_low, grad_heads, preferred_element_type=full)
    grad_weights = jnp.einsum(
        "qhd,khd->hqk", grad_heads, value_heads, preferred_element_type=full
    )
    row_inner = jnp.sum(weights_full * grad_weights, axis=-1, keepdims=True)
    grad_scores = (weights_full * (grad_weights - row_inner)).astype(low)
    grad_query = (
        jnp.einsum("hqk,khd->qhd", grad_scores, key_heads, preferred_element_type=full)
        * score_scale
    )
    grad_key = (
        jnp.einsum("hqk,qhd->khd", grad_scores, query_heads, preferred_element_type=full)
        * score_scale
    )
    return grad_query, grad_key, grad_value


def per_device(
    latents,
    media,
    segment_ids,
    slot_map,
    gains,
    w_query,
    w_key,
    w_value,
    w_out,
    w_up,
    w_down,
    cotangent,
):
    dp = ("pair", "core")
    everywhere = ("section",) + dp
    section = lax.axis_index("section")
    section_count = lax.axis_size("section")
    dp_index = lax.axis_index(dp)
    dp_count = lax.axis_size("pair") * lax.axis_size("core")
    on_first = section // 2 == 0
    stride = dp_count // 2
    row_first = dp_index // stride == 0
    seq_rows = segment_ids.shape[1]
    slot_count = slot_map.shape[1]
    feature_width = latents.shape[1]
    latent_rows = latents.shape[0]
    slot_rows = latent_rows // section_count
    inner = w_query.shape[2] // 2
    heads = inner // HEAD_DIM
    score_scale = 1.0 / math.sqrt(HEAD_DIM)

    def pick(first, second):
        return jnp.where(on_first, first, second), jnp.where(on_first, second, first)

    def swapped(value, mask):
        pairs = [(source, source ^ mask) for source in range(section_count)]
        return lax.ppermute(value, "section", pairs)

    def other_core(value):
        return lax.ppermute(value, "core", [(0, 1), (1, 0)])

    def to_second(value):
        return lax.ppermute(value, "section", [(0, 2), (1, 3)])

    def to_first(value):
        return lax.ppermute(value, "section", [(2, 0), (3, 1)])

    def after(value, earlier):
        return lax.optimization_barrier((value, earlier))[0]

    def turn_pairs(flip, back):
        pairs = []
        for source in range(section_count):
            for index in range(dp_count):
                layer, half = divmod(source, 2)
                bit, lowest = divmod(index, stride)
                moved = (layer ^ flip) * stride + lowest
                target = (bit * 2 + half) * dp_count + moved
                pair = (source * dp_count + index, target)
                pairs.append(pair[::-1] if back else pair)
        return pairs

    def exchange_rows(weight):
        half = weight.shape[0] // 2
        near, far = pick(weight[:half], weight[half:])
        first = lax.ppermute(near, everywhere, turn_pairs(0, False))
        second = lax.ppermute(far, everywhere, turn_pairs(1, False))
        return (
            jnp.where(row_first, first, second),
            jnp.where(row_first, second, first),
        )

    def join_rows(first, second):
        near = jnp.where(row_first, first, second)
        far = jnp.where(row_first, second, first)
        near = lax.ppermute(near, everywhere, turn_pairs(0, True))
        far = lax.ppermute(far, everywhere, turn_pairs(1, True))
        return jnp.concatenate(pick(near, far), axis=0).astype(full)

    def fold(piece):
        blocks = [piece[:, i * inner : (i + 1) * inner] for i in range(feature_width // inner)]
        return jnp.concatenate(blocks, axis=0)

    def unfold(stacked):
        count = feature_width // inner
        blocks = stacked.reshape(2, stride, count, -1, inner).transpose(1, 0, 3, 2, 4)
        return blocks.reshape(-1, feature_width)

    def by_device(grad):
        blocks = grad.reshape(stride, 2, -1, feature_width).transpose(1, 0, 2, 3)
        return blocks.reshape(-1, feature_width)

    def sum_to_slots(partial):
        blocks = partial.astype(low).reshape(section_count, -1, feature_width)
        arrived = lax.all_to_all(blocks, "section", split_axis=0, concat_axis=0)
        return jnp.sum(arrived.astype(full), axis=0)

    def from_slots(rows):
        return lax.all_gather(rows, "section", axis=0, tiled=True)

    def to_columns(rows):
        moved = lax.all_to_all(
            rows.astype(low), "section", split_axis=1, concat_axis=0, tiled=True
        )
        return moved.astype(full)

    def from_sequences(rows):
        near = lax.all_gather(rows, "pair", axis=0, tiled=True)
        return jnp.concatenate([near, other_core(near)], axis=0)

    def sum_to_sequence(left, right, product):
        half = left.shape[0] // 2
        far = product(left[half:], right).astype(low)
        near = product(left[:half], right) + other_core(far).astype(full)
        blocks = near.astype(low).reshape(-1, slot_rows, feature_width)
        arrived = lax.all_to_all(blocks, "pair", split_axis=0, concat_axis=0)
        return jnp.sum(arrived.astype(full), axis=0)

    def by_distance(rows):
        half = rows.shape[0] // 2
        side = swapped(rows, 1)
        ahead = swapped(rows, 2)
        upper = swapped(side[:half], 2)
        lower = swapped(ahead[half:], 1)
        return rows, side, ahead, jnp.concatenate([upper, lower], axis=0)

    def sum_by_distance(own, side, ahead, across, gate=None):
        half = own.shape[0] // 2
        across = across.astype(low)
        upper = swapped(across[:half], 2).astype(full)
        lower = swapped(across[half:], 1).astype(full)
        if gate is not None:
            upper, lower = after((upper, lower), gate)
        side = jnp.concatenate([side[:half] + upper, side[half:]], axis=0).astype(low)
        ahead = jnp.concatenate([ahead[:half], ahead[half:] + lower], axis=0).astype(low)
        return own + swapped(side, 1).astype(full) + swapped(ahead, 2).astype(full)

    def share_first(lower, upper):
        return jnp.where(on_first, lower, to_second(upper))

    def sum_over_sections(partial):
        blocks = partial.reshape(section_count, -1, feature_width)
        return sum_by_distance(
            *[
                lax.dynamic_index_in_dim(blocks, section ^ mask, 0, keepdims=False)
                for mask in range(4)
            ]
        )

    def gather_sections(rows):
        by_mask = by_distance(rows)
        ordered = []
        for target in range(section_count):
            chosen = by_mask[0]
            for mask in range(1, section_count):
                chosen = jnp.where(section ^ mask == target, by_mask[mask], chosen)
            ordered.append(chosen)
        return jnp.concatenate(ordered, axis=0)

    def column_parts(weight, block):
        rows, width = weight.shape
        split = weight.reshape(rows, width // (2 * block), 2, block)
        return split[:, :, 0].reshape(rows, -1), split[:, :, 1].reshape(rows, -1)

    def interleave(even, odd, block):
        rows, width = even.shape
        parts = [part.reshape(rows, width // block, 1, block) for part in (even, odd)]
        return jnp.concatenate(parts, axis=2).reshape(rows, 2 * width)

    halves = [pick(weight[0, :, :inner], weight[0, :, inner:]) for weight in (w_query, w_key, w_value)]
    own_heads = jnp.concatenate([half[0] for half in halves], axis=1)
    other_heads = swapped(jnp.concatenate([half[1] for half in halves], axis=1), 2)
    qkv_pieces = pick(own_heads, other_heads)
    all_gains = after(gains, other_heads)
    for axis in ("core", "pair", "section"):
        all_gains = lax.all_gather(all_gains, axis, axis=2, tiled=True)
    out_pieces = exchange_rows(after(w_out[0], other_heads))

    def gather(piece):
        return lax.all_gather(piece, dp, axis=0, tiled=True)

    stacked = [
        gather(jnp.concatenate([qkv_pieces[layer], fold(out_pieces[layer])], axis=1))
        for layer in range(LAYERS)
    ]
    qkv_w = [weight[:, : 3 * inner] for weight in stacked]
    out_w = [unfold(weight[:, 3 * inner :]) for weight in stacked]

    half_hidden = w_down.shape[1] // 2
    half_depth = w_up.shape[1] // 2
    up_turned = lax.all_to_all(
        share_first(*after((w_up[0, :half_depth], w_up[0, half_depth:]), all_gains)),
        dp,
        split_axis=1,
        concat_axis=0,
        tiled=True,
    )
    down_shared = by_distance(
        share_first(*after((w_down[0, :half_hidden], w_down[0, half_hidden:]), all_gains))
    )
    up_shared = by_distance(up_turned)

    def in_depth(near, far):
        parts = [part.reshape(dp_count, 1, half_depth, -1) for part in pick(near, far)]
        return jnp.concatenate(parts, axis=1).reshape(feature_width, -1)

    down_first = jnp.concatenate(
        pick(down_shared[0], down_shared[2]) + pick(down_shared[1], down_shared[3]), axis=0
    )
    up_first = jnp.concatenate(
        [in_depth(up_shared[0], up_shared[2]), in_depth(up_shared[1], up_shared[3])], axis=1
    )

    up_even, up_odd = column_parts(w_up[0], half_hidden)
    up_piece, down_piece = after((up_even, w_down[0, :half_hidden]), all_gains)
    down_second = gather(
        jnp.where(on_first, to_first(down_piece), w_down[0, half_hidden:])
    )
    up_second = gather(jnp.where(on_first, to_first(up_piece), up_odd))
    up_w = (up_first, up_second)
    down_w = (down_first, down_second)
    query_w = [weight[:, :inner] for weight in qkv_w]
    key_w = [weight[:, inner : 2 * inner] for weight in qkv_w]
    value_w = [weight[:, 2 * inner :] for weight in qkv_w]

    image_hot = segment_ids[:, :, None] == jnp.arange(slot_count, dtype=jnp.int32)[None, None, :]
    media_slot = jnp.sum(jnp.where(image_hot, slot_map[:, None, :], 0), axis=2) - (
        segment_ids < 0
    ).astype(jnp.int32)
    media_unit, media_inverse = unit_rows(media.astype(full))
    latent_slot = jnp.arange(latent_rows, dtype=jnp.int32) // LATENTS
    key_slot = jnp.concatenate([media_slot[0], latent_slot])
    allowed = latent_slot[None, :, None] == key_slot[None, None, :]

    def split_heads(rows):
        return rows.reshape(rows.shape[0], heads, HEAD_DIM)

    media_low = []
    media_key = []
    media_value = []
    for layer in range(LAYERS):
        media_low.append((media_unit * all_gains[layer, 0]).astype(low))
        media_key.append(matmul(media_low[layer], key_w[layer]).astype(low))
        media_value.append(matmul(media_low[layer], value_w[layer]).astype(low))

    saved = []
    current = lax.dynamic_slice_in_dim(latents, section * slot_rows, slot_rows, 0).astype(full)
    grad_rows = lax.dynamic_slice_in_dim(cotangent, section * slot_rows, slot_rows, 0).astype(full)
    grad_low = cotangent
    for layer in range(LAYERS):
        unit_in, inverse_in = unit_rows(current)
        if layer == 0:
            whole_unit = unit_rows(latents.astype(full))[0]
            latent_low = (whole_unit * all_gains[layer, 1]).astype(low)
        else:
            latent_low = from_slots((unit_in * all_gains[layer, 1]).astype(low))
        projected = matmul(latent_low, qkv_w[layer]).astype(low)
        query_low = projected[:, :inner]
        key_heads = split_heads(
            jnp.concatenate([media_key[layer], projected[:, inner : 2 * inner]], axis=0)
        )
        value_heads = split_heads(
            jnp.concatenate([media_value[layer], projected[:, 2 * inner :]], axis=0)
        )
        query_heads = split_heads(query_low)
        attended, log_total = attend_forward(
            query_heads, key_heads, value_heads, allowed, score_scale
        )
        attended_low = attended.reshape(-1, inner).astype(low)
        middle = current + sum_to_slots(matmul(attended_low, out_w[layer]))
        unit_mid, inverse_mid = unit_rows(middle)
        ffn_low = (unit_mid * all_gains[layer, 2]).astype(low)
        ffn_low = from_slots(ffn_low) if layer else from_sequences(ffn_low)
        hidden_pre = matmul(ffn_low, up_w[layer])
        active_low = gelu_exact(hidden_pre).astype(low)
        if layer == 0:
            current = middle + sum_to_sequence(active_low, down_w[layer], matmul)
        saved.append(
            (
                unit_in,
                inverse_in,
                latent_low,
                query_heads,
                key_heads,
                value_heads,
                log_total,
                attended_low,
                unit_mid,
                inverse_mid,
                ffn_low,
                hidden_pre,
                active_low,
            )
        )

    def scatter(blocks):
        return lax.psum_scatter(blocks, dp, scatter_dimension=0, tiled=True)

    gain_rows = [None] * LAYERS
    media_scaled = None
    pieces = [None] * LAYERS
    for layer in (1, 0):
        (
            unit_in,
            inverse_in,
            latent_low,
            query_heads,
            key_heads,
            value_heads,
            log_total,
            attended_low,
            unit_mid,
            inverse_mid,
            ffn_low,
            hidden_pre,
            active_low,
        ) = saved[layer]
        grad_active = matmul_nt(grad_low, down_w[layer])
        grad_hidden = jax.vjp(gelu_exact, hidden_pre)[1](grad_active)[0].astype(low)
        down_grad = matmul_tn(active_low, grad_low)
        if layer:
            down_grad = down_grad.astype(low)
            grad_hidden = after(grad_hidden, down_grad)
        up_grad = matmul_tn(ffn_low, grad_hidden)
        if layer:
            ffn_pieces = (scatter(down_grad), scatter(up_grad.astype(low)))
            ffn_grad = sum_to_slots(matmul_nt(grad_hidden, up_w[layer]))
        else:
            ffn_grad = sum_to_sequence(grad_hidden, up_w[layer], matmul_nt)
            blocks = down_grad.reshape(2, 2, half_hidden, feature_width)
            own, ahead = pick(blocks[0, 0], blocks[0, 1])
            side, across = pick(blocks[1, 0], blocks[1, 1])
            down_blocks = (own, side, ahead, across)
            width = up_grad.shape[1] // 2
            blocks = up_grad.reshape(dp_count, 2, half_depth, 2 * width)
            blocks = [blocks[:, i].reshape(-1, 2 * width) for i in range(2)]
            own, ahead = pick(blocks[0][:, :width], blocks[1][:, :width])
            side, across = pick(blocks[0][:, width:], blocks[1][:, width:])
            up_blocks = (own, side, ahead, across)
        gain_ffn_grad = jnp.sum(ffn_grad * unit_mid, axis=0)
        grad_middle = grad_rows + norm_back(
            unit_mid, inverse_mid, ffn_grad * all_gains[layer, 2]
        )
        middle_low = from_slots(grad_middle.astype(low))
        if layer == 0:
            up_half = sum_by_distance(*up_blocks, middle_low).astype(low)
            up_half = lax.all_to_all(up_half, dp, split_axis=0, concat_axis=1, tiled=True)
            down_half = sum_by_distance(*down_blocks, middle_low).astype(low)
        grad_heads = split_heads(matmul_nt(middle_low, out_w[layer]).astype(low))
        out_piece = scatter(by_device(matmul_tn(attended_low, middle_low)).astype(low))
        grad_query, grad_key, grad_value = attend_backward(
            query_heads, key_heads, value_heads, allowed, score_scale, log_total, grad_heads
        )
        grad_query = grad_query.reshape(-1, inner).astype(low)
        grad_key = grad_key.reshape(-1, inner).astype(low)
        grad_value = grad_value.reshape(-1, inner).astype(low)
        latent_part = (
            matmul_nt(grad_query, query_w[layer])
            + matmul_nt(grad_key[seq_rows:], key_w[layer])
            + matmul_nt(grad_value[seq_rows:], value_w[layer])
        )
        latent_grad_rows = sum_to_slots(latent_part)
        gain_latent_grad = jnp.sum(latent_grad_rows * unit_in, axis=0)
        grad_rows = grad_middle + norm_back(
            unit_in, inverse_in, latent_grad_rows * all_gains[layer, 1]
        )
        both_low = jnp.concatenate([media_low[layer], latent_low], axis=0)
        all_grads = jnp.concatenate(
            [jnp.pad(grad_query, ((seq_rows, 0), (0, 0))), grad_key, grad_value], axis=1
        )
        qkv_grad = matmul_tn(both_low, all_grads).astype(low)
        pieces[layer] = (scatter(qkv_grad), out_piece)
        if layer > 0:
            grad_low = from_sequences(grad_rows.astype(low))
            grad_low = after(grad_low, ffn_pieces)
        media_part = matmul_nt(grad_key[:seq_rows], key_w[layer]) + matmul_nt(
            grad_value[:seq_rows], value_w[layer]
        )
        gain_media_grad = jnp.sum(media_part * media_unit, axis=0)
        scaled = media_part * all_gains[layer, 0]
        media_scaled = scaled if media_scaled is None else media_scaled + scaled
        gain_rows[layer] = jnp.stack([gain_media_grad, gain_latent_grad, gain_ffn_grad])
    current = middle + sum_to_slots(matmul(after(saved[1][12], latent_part), down_w[1]))
    latents_out = to_columns(current)
    latent_grad = to_columns(after(grad_rows, pieces[1]))
    media_rows = seq_rows // section_count
    media_sum = sum_over_sections(media_scaled)
    own_unit = lax.dynamic_slice_in_dim(media_unit, section * media_rows, media_rows, 0)
    own_inverse = lax.dynamic_slice_in_dim(media_inverse, section * media_rows, media_rows, 0)
    media_grad = gather_sections(norm_back(own_unit, own_inverse, media_sum).astype(low)).astype(
        full
    )
    gain_parts = jnp.stack(gain_rows).reshape(LAYERS, 3, section_count, -1)
    gain_parts = jnp.sum(
        lax.all_to_all(gain_parts, "section", split_axis=2, concat_axis=2), axis=2
    )
    gain_parts = gain_parts.reshape(LAYERS, 3, dp_count, -1)
    gain_grad = jnp.sum(lax.all_to_all(gain_parts, dp, split_axis=2, concat_axis=2), axis=2)

    qkv_parts = [piece[0] for piece in pieces]
    own, other = pick(qkv_parts[0], qkv_parts[1])
    lower, upper = pick(own, swapped(other, 2))
    qkv_grads = [
        jnp.concatenate(
            [lower[:, i * inner : (i + 1) * inner], upper[:, i * inner : (i + 1) * inner]], axis=1
        ).astype(full)
        for i in range(3)
    ]
    out_grad = join_rows(*[piece[1] for piece in pieces])
    down_piece, up_piece = ffn_pieces
    up_second_grad = interleave(to_second(up_piece), up_piece, half_hidden)
    down_second_grad = jnp.concatenate([to_second(down_piece), down_piece], axis=0)
    up_first_grad = jnp.concatenate([up_half, to_first(up_half)], axis=0)
    down_first_grad = jnp.concatenate([down_half, to_first(down_half)], axis=0)
    up_grad = jnp.where(on_first, up_first_grad, up_second_grad).astype(full)
    down_grad = jnp.where(on_first, down_first_grad, down_second_grad).astype(full)
    return (
        latents_out,
        latent_grad,
        media_grad,
        gain_grad,
        qkv_grads[0][None],
        qkv_grads[1][None],
        qkv_grads[2][None],
        out_grad[None],
        up_grad[None],
        down_grad[None],
    )


def solution(mesh):
    section_count, dp_count = mesh.devices.shape
    fine = Mesh(
        mesh.devices.reshape(section_count, dp_count // 2, 2), ("section", "pair", "core")
    )
    dp = ("pair", "core")
    placed = (
        P(dp, None),
        P(dp, None),
        P(dp, None),
        P(dp, None),
        P(None, None, ("section",) + dp),
        P("section", dp, None),
        P("section", dp, None),
        P("section", dp, None),
        P("section", dp, None),
        P("section", dp, None),
        P("section", dp, None),
        P(dp, None),
    )
    return jax.shard_map(
        per_device,
        mesh=fine,
        in_specs=placed,
        out_specs=(
            P(dp, "section"),
            P(dp, "section"),
            P(dp, None),
            P(None, None, ("section",) + dp),
            P("section", dp, None),
            P("section", dp, None),
            P("section", dp, None),
            P("section", dp, None),
            P("section", dp, None),
            P("section", dp, None),
        ),
        check_vma=False,
    )
```

```python
import math

import jax
import jax.numpy as jnp
from jax import lax
from jax.sharding import Mesh, PartitionSpec as P

HEAD_DIM = 96
LATENTS = 64
LAYERS = 2

epsilon = 1e-05
low = jnp.bfloat16
full = jnp.float32


def unit_rows(values):
    centered = values - jnp.mean(values, axis=-1, keepdims=True)
    variance = jnp.mean(centered * centered, axis=-1, keepdims=True)
    inverse = lax.rsqrt(variance + epsilon)
    return centered * inverse, inverse


def norm_back(unit, inverse, scaled):
    first = jnp.mean(scaled, axis=-1, keepdims=True)
    second = jnp.mean(scaled * unit, axis=-1, keepdims=True)
    return (scaled - first - unit * second) * inverse


def gelu_exact(values):
    return jax.nn.gelu(values, approximate=False)


def matmul(left, right):
    return jnp.dot(left, right, preferred_element_type=full)


def matmul_nt(left, right):
    return lax.dot_general(left, right, (((1,), (1,)), ((), ())), preferred_element_type=full)


def matmul_tn(left, right):
    return lax.dot_general(left, right, (((0,), (0,)), ((), ())), preferred_element_type=full)


def attend_forward(query_heads, key_heads, value_heads, allowed, score_scale):
    scores = jnp.einsum("qhd,khd->hqk", query_heads, key_heads, preferred_element_type=full)
    scores = jnp.where(allowed, scores * score_scale, -1e30)
    row_max = jnp.max(scores, axis=-1, keepdims=True)
    exponent = jnp.exp(scores - row_max)
    row_total = jnp.sum(exponent, axis=-1, keepdims=True)
    weights_low = (exponent / row_total).astype(low)
    attended = jnp.einsum("hqk,khd->qhd", weights_low, value_heads, preferred_element_type=full)
    return attended, row_max + jnp.log(row_total)


def attend_backward(
    query_heads, key_heads, value_heads, allowed, score_scale, log_total, grad_heads
):
    scores = jnp.einsum("qhd,khd->hqk", query_heads, key_heads, preferred_element_type=full)
    scores = jnp.where(allowed, scores * score_scale, -1e30)
    weights_full = jnp.exp(scores - log_total)
    weights_low = weights_full.astype(low)
    grad_value = jnp.einsum("hqk,qhd->khd", weights_low, grad_heads, preferred_element_type=full)
    grad_weights = jnp.einsum(
        "qhd,khd->hqk", grad_heads, value_heads, preferred_element_type=full
    )
    row_inner = jnp.sum(weights_full * grad_weights, axis=-1, keepdims=True)
    grad_scores = (weights_full * (grad_weights - row_inner)).astype(low)
    grad_query = (
        jnp.einsum("hqk,khd->qhd", grad_scores, key_heads, preferred_element_type=full)
        * score_scale
    )
    grad_key = (
        jnp.einsum("hqk,qhd->khd", grad_scores, query_heads, preferred_element_type=full)
        * score_scale
    )
    return grad_query, grad_key, grad_value


def per_device(
    latents,
    media,
    segment_ids,
    slot_map,
    gains,
    w_query,
    w_key,
    w_value,
    w_out,
    w_up,
    w_down,
    cotangent,
):
    dp = ("pair", "core")
    everywhere = ("section",) + dp
    section = lax.axis_index("section")
    section_count = lax.axis_size("section")
    dp_index = lax.axis_index(dp)
    dp_count = lax.axis_size("pair") * lax.axis_size("core")
    on_first = section // 2 == 0
    stride = dp_count // 2
    row_first = dp_index // stride == 0
    seq_rows = segment_ids.shape[1]
    slot_count = slot_map.shape[1]
    feature_width = latents.shape[1]
    latent_rows = latents.shape[0]
    slot_rows = latent_rows // section_count
    inner = w_query.shape[2] // 2
    heads = inner // HEAD_DIM
    score_scale = 1.0 / math.sqrt(HEAD_DIM)

    def pick(first, second):
        return jnp.where(on_first, first, second), jnp.where(on_first, second, first)

    def swapped(value, mask):
        pairs = [(source, source ^ mask) for source in range(section_count)]
        return lax.ppermute(value, "section", pairs)

    def other_core(value):
        return lax.ppermute(value, "core", [(0, 1), (1, 0)])

    def to_second(value):
        return lax.ppermute(value, "section", [(0, 2), (1, 3)])

    def to_first(value):
        return lax.ppermute(value, "section", [(2, 0), (3, 1)])

    def after(value, earlier):
        return lax.optimization_barrier((value, earlier))[0]

    def turn_pairs(flip, back):
        pairs = []
        for source in range(section_count):
            for index in range(dp_count):
                layer, half = divmod(source, 2)
                bit, lowest = divmod(index, stride)
                moved = (layer ^ flip) * stride + lowest
                target = (bit * 2 + half) * dp_count + moved
                pair = (source * dp_count + index, target)
                pairs.append(pair[::-1] if back else pair)
        return pairs

    def exchange_rows(weight):
        half = weight.shape[0] // 2
        near, far = pick(weight[:half], weight[half:])
        first = lax.ppermute(near, everywhere, turn_pairs(0, False))
        second = lax.ppermute(far, everywhere, turn_pairs(1, False))
        return (
            jnp.where(row_first, first, second),
            jnp.where(row_first, second, first),
        )

    def join_rows(first, second):
        near = jnp.where(row_first, first, second)
        far = jnp.where(row_first, second, first)
        near = lax.ppermute(near, everywhere, turn_pairs(0, True))
        far = lax.ppermute(far, everywhere, turn_pairs(1, True))
        return jnp.concatenate(pick(near, far), axis=0).astype(full)

    def fold(piece):
        blocks = [piece[:, i * inner : (i + 1) * inner] for i in range(feature_width // inner)]
        return jnp.concatenate(blocks, axis=0)

    def unfold(stacked):
        count = feature_width // inner
        blocks = stacked.reshape(2, stride, count, -1, inner).transpose(1, 0, 3, 2, 4)
        return blocks.reshape(-1, feature_width)

    def by_device(grad):
        blocks = grad.reshape(stride, 2, -1, feature_width).transpose(1, 0, 2, 3)
        return blocks.reshape(-1, feature_width)

    def sum_to_slots(partial):
        blocks = partial.astype(low).reshape(section_count, -1, feature_width)
        arrived = lax.all_to_all(blocks, "section", split_axis=0, concat_axis=0)
        return jnp.sum(arrived.astype(full), axis=0)

    def from_slots(rows):
        return lax.all_gather(rows, "section", axis=0, tiled=True)

    def to_columns(rows):
        moved = lax.all_to_all(
            rows.astype(low), "section", split_axis=1, concat_axis=0, tiled=True
        )
        return moved.astype(full)

    def from_sequences(rows):
        near = lax.all_gather(rows, "pair", axis=0, tiled=True)
        return jnp.concatenate([near, other_core(near)], axis=0)

    def sum_to_sequence(left, right, product):
        half = left.shape[0] // 2
        far = product(left[half:], right).astype(low)
        near = product(left[:half], right) + other_core(far).astype(full)
        blocks = near.astype(low).reshape(-1, slot_rows, feature_width)
        arrived = lax.all_to_all(blocks, "pair", split_axis=0, concat_axis=0)
        return jnp.sum(arrived.astype(full), axis=0)

    def by_distance(rows):
        half = rows.shape[0] // 2
        side = swapped(rows, 1)
        ahead = swapped(rows, 2)
        upper = swapped(side[:half], 2)
        lower = swapped(ahead[half:], 1)
        return rows, side, ahead, jnp.concatenate([upper, lower], axis=0)

    def sum_by_distance(own, side, ahead, across, gate=None):
        half = own.shape[0] // 2
        across = across.astype(low)
        upper = swapped(across[:half], 2).astype(full)
        lower = swapped(across[half:], 1).astype(full)
        if gate is not None:
            upper, lower = after((upper, lower), gate)
        side = jnp.concatenate([side[:half] + upper, side[half:]], axis=0).astype(low)
        ahead = jnp.concatenate([ahead[:half], ahead[half:] + lower], axis=0).astype(low)
        return own + swapped(side, 1).astype(full) + swapped(ahead, 2).astype(full)

    def share_first(lower, upper):
        return jnp.where(on_first, lower, to_second(upper))

    def sum_over_sections(partial):
        blocks = partial.reshape(section_count, -1, feature_width)
        return sum_by_distance(
            *[
                lax.dynamic_index_in_dim(blocks, section ^ mask, 0, keepdims=False)
                for mask in range(4)
            ]
        )

    def gather_sections(rows):
        by_mask = by_distance(rows)
        ordered = []
        for target in range(section_count):
            chosen = by_mask[0]
            for mask in range(1, section_count):
                chosen = jnp.where(section ^ mask == target, by_mask[mask], chosen)
            ordered.append(chosen)
        return jnp.concatenate(ordered, axis=0)

    def column_parts(weight, block):
        rows, width = weight.shape
        split = weight.reshape(rows, width // (2 * block), 2, block)
        return split[:, :, 0].reshape(rows, -1), split[:, :, 1].reshape(rows, -1)

    def interleave(even, odd, block):
        rows, width = even.shape
        parts = [part.reshape(rows, width // block, 1, block) for part in (even, odd)]
        return jnp.concatenate(parts, axis=2).reshape(rows, 2 * width)

    halves = [pick(weight[0, :, :inner], weight[0, :, inner:]) for weight in (w_query, w_key, w_value)]
    own_heads = jnp.concatenate([half[0] for half in halves], axis=1)
    other_heads = swapped(jnp.concatenate([half[1] for half in halves], axis=1), 2)
    qkv_pieces = pick(own_heads, other_heads)
    half_hidden = w_down.shape[1] // 2
    half_depth = w_up.shape[1] // 2
    up_share = share_first(w_up[0, :half_depth], w_up[0, half_depth:])
    all_gains = after(gains, (other_heads, up_share))
    for axis in ("core", "pair", "section"):
        all_gains = lax.all_gather(all_gains, axis, axis=2, tiled=True)
    out_pieces = exchange_rows(after(w_out[0], other_heads))

    def gather(piece):
        return lax.all_gather(piece, dp, axis=0, tiled=True)

    stacked = [
        gather(jnp.concatenate([qkv_pieces[layer], fold(out_pieces[layer])], axis=1))
        for layer in range(LAYERS)
    ]
    qkv_w = [weight[:, : 3 * inner] for weight in stacked]
    out_w = [unfold(weight[:, 3 * inner :]) for weight in stacked]

    up_turned = lax.all_to_all(up_share, dp, split_axis=1, concat_axis=0, tiled=True)
    down_shared = by_distance(
        share_first(*after((w_down[0, :half_hidden], w_down[0, half_hidden:]), all_gains))
    )
    up_shared = by_distance(up_turned)

    def in_depth(near, far):
        parts = [part.reshape(dp_count, 1, half_depth, -1) for part in pick(near, far)]
        return jnp.concatenate(parts, axis=1).reshape(feature_width, -1)

    down_first = jnp.concatenate(
        pick(down_shared[0], down_shared[2]) + pick(down_shared[1], down_shared[3]), axis=0
    )
    up_first = jnp.concatenate(
        [in_depth(up_shared[0], up_shared[2]), in_depth(up_shared[1], up_shared[3])], axis=1
    )

    up_even, up_odd = column_parts(w_up[0], half_hidden)
    up_piece, down_piece = after((up_even, w_down[0, :half_hidden]), all_gains)
    down_second = gather(
        jnp.where(on_first, to_first(down_piece), w_down[0, half_hidden:])
    )
    up_second = gather(jnp.where(on_first, to_first(up_piece), up_odd))
    up_w = (up_first, up_second)
    down_w = (down_first, down_second)
    query_w = [weight[:, :inner] for weight in qkv_w]
    key_w = [weight[:, inner : 2 * inner] for weight in qkv_w]
    value_w = [weight[:, 2 * inner :] for weight in qkv_w]

    image_hot = segment_ids[:, :, None] == jnp.arange(slot_count, dtype=jnp.int32)[None, None, :]
    media_slot = jnp.sum(jnp.where(image_hot, slot_map[:, None, :], 0), axis=2) - (
        segment_ids < 0
    ).astype(jnp.int32)
    media_unit, media_inverse = unit_rows(media.astype(full))
    latent_slot = jnp.arange(latent_rows, dtype=jnp.int32) // LATENTS
    key_slot = jnp.concatenate([media_slot[0], latent_slot])
    allowed = latent_slot[None, :, None] == key_slot[None, None, :]

    def split_heads(rows):
        return rows.reshape(rows.shape[0], heads, HEAD_DIM)

    media_low = []
    media_key = []
    media_value = []
    for layer in range(LAYERS):
        media_low.append((media_unit * all_gains[layer, 0]).astype(low))
        media_key.append(matmul(media_low[layer], key_w[layer]).astype(low))
        media_value.append(matmul(media_low[layer], value_w[layer]).astype(low))

    saved = []
    current = lax.dynamic_slice_in_dim(latents, section * slot_rows, slot_rows, 0).astype(full)
    grad_rows = lax.dynamic_slice_in_dim(cotangent, section * slot_rows, slot_rows, 0).astype(full)
    grad_low = cotangent
    for layer in range(LAYERS):
        unit_in, inverse_in = unit_rows(current)
        if layer == 0:
            whole_unit = unit_rows(latents.astype(full))[0]
            latent_low = (whole_unit * all_gains[layer, 1]).astype(low)
        else:
            latent_low = from_slots((unit_in * all_gains[layer, 1]).astype(low))
        projected = matmul(latent_low, qkv_w[layer]).astype(low)
        query_low = projected[:, :inner]
        key_heads = split_heads(
            jnp.concatenate([media_key[layer], projected[:, inner : 2 * inner]], axis=0)
        )
        value_heads = split_heads(
            jnp.concatenate([media_value[layer], projected[:, 2 * inner :]], axis=0)
        )
        query_heads = split_heads(query_low)
        attended, log_total = attend_forward(
            query_heads, key_heads, value_heads, allowed, score_scale
        )
        attended_low = attended.reshape(-1, inner).astype(low)
        middle = current + sum_to_slots(matmul(attended_low, out_w[layer]))
        unit_mid, inverse_mid = unit_rows(middle)
        ffn_low = (unit_mid * all_gains[layer, 2]).astype(low)
        ffn_low = from_slots(ffn_low) if layer else from_sequences(ffn_low)
        hidden_pre = matmul(ffn_low, up_w[layer])
        active_low = gelu_exact(hidden_pre).astype(low)
        if layer == 0:
            current = middle + sum_to_sequence(active_low, down_w[layer], matmul)
        saved.append(
            (
                unit_in,
                inverse_in,
                latent_low,
                query_heads,
                key_heads,
                value_heads,
                log_total,
                attended_low,
                unit_mid,
                inverse_mid,
                ffn_low,
                hidden_pre,
                active_low,
            )
        )

    def scatter(blocks):
        return lax.psum_scatter(blocks, dp, scatter_dimension=0, tiled=True)

    gain_rows = [None] * LAYERS
    media_scaled = None
    pieces = [None] * LAYERS
    for layer in (1, 0):
        (
            unit_in,
            inverse_in,
            latent_low,
            query_heads,
            key_heads,
            value_heads,
            log_total,
            attended_low,
            unit_mid,
            inverse_mid,
            ffn_low,
            hidden_pre,
            active_low,
        ) = saved[layer]
        grad_active = matmul_nt(grad_low, down_w[layer])
        grad_hidden = jax.vjp(gelu_exact, hidden_pre)[1](grad_active)[0].astype(low)
        down_grad = matmul_tn(active_low, grad_low)
        if layer:
            down_grad = down_grad.astype(low)
            grad_hidden = after(grad_hidden, down_grad)
        up_grad = matmul_tn(ffn_low, grad_hidden)
        if layer:
            ffn_pieces = (scatter(down_grad), scatter(up_grad.astype(low)))
            ffn_grad = sum_to_slots(matmul_nt(grad_hidden, up_w[layer]))
        else:
            ffn_grad = sum_to_sequence(grad_hidden, up_w[layer], matmul_nt)
            blocks = down_grad.reshape(2, 2, half_hidden, feature_width)
            own, ahead = pick(blocks[0, 0], blocks[0, 1])
            side, across = pick(blocks[1, 0], blocks[1, 1])
            down_blocks = (own, side, ahead, across)
            width = up_grad.shape[1] // 2
            blocks = up_grad.reshape(dp_count, 2, half_depth, 2 * width)
            blocks = [blocks[:, i].reshape(-1, 2 * width) for i in range(2)]
            own, ahead = pick(blocks[0][:, :width], blocks[1][:, :width])
            side, across = pick(blocks[0][:, width:], blocks[1][:, width:])
            up_blocks = (own, side, ahead, across)
        gain_ffn_grad = jnp.sum(ffn_grad * unit_mid, axis=0)
        grad_middle = grad_rows + norm_back(
            unit_mid, inverse_mid, ffn_grad * all_gains[layer, 2]
        )
        middle_low = from_slots(grad_middle.astype(low))
        if layer == 0:
            up_half = sum_by_distance(*up_blocks, middle_low).astype(low)
            down_half = sum_by_distance(*down_blocks, middle_low).astype(low)
        grad_heads = split_heads(matmul_nt(middle_low, out_w[layer]).astype(low))
        out_piece = scatter(by_device(matmul_tn(attended_low, middle_low)).astype(low))
        grad_query, grad_key, grad_value = attend_backward(
            query_heads, key_heads, value_heads, allowed, score_scale, log_total, grad_heads
        )
        grad_query = grad_query.reshape(-1, inner).astype(low)
        grad_key = grad_key.reshape(-1, inner).astype(low)
        grad_value = grad_value.reshape(-1, inner).astype(low)
        latent_part = (
            matmul_nt(grad_query, query_w[layer])
            + matmul_nt(grad_key[seq_rows:], key_w[layer])
            + matmul_nt(grad_value[seq_rows:], value_w[layer])
        )
        if layer == 0:
            latent_part = after(latent_part, up_half)
        latent_grad_rows = sum_to_slots(latent_part)
        gain_latent_grad = jnp.sum(latent_grad_rows * unit_in, axis=0)
        grad_rows = grad_middle + norm_back(
            unit_in, inverse_in, latent_grad_rows * all_gains[layer, 1]
        )
        both_low = jnp.concatenate([media_low[layer], latent_low], axis=0)
        all_grads = jnp.concatenate(
            [jnp.pad(grad_query, ((seq_rows, 0), (0, 0))), grad_key, grad_value], axis=1
        )
        qkv_grad = matmul_tn(both_low, all_grads).astype(low)
        if layer == 0:
            up_half, qkv_grad = lax.optimization_barrier((up_half, qkv_grad))
            up_half = lax.all_to_all(up_half, dp, split_axis=0, concat_axis=1, tiled=True)
        pieces[layer] = (scatter(qkv_grad), out_piece)
        if layer > 0:
            grad_low = from_sequences(grad_rows.astype(low))
            grad_low = after(grad_low, ffn_pieces)
        media_part = matmul_nt(grad_key[:seq_rows], key_w[layer]) + matmul_nt(
            grad_value[:seq_rows], value_w[layer]
        )
        gain_media_grad = jnp.sum(media_part * media_unit, axis=0)
        scaled = media_part * all_gains[layer, 0]
        media_scaled = scaled if media_scaled is None else media_scaled + scaled
        gain_rows[layer] = jnp.stack([gain_media_grad, gain_latent_grad, gain_ffn_grad])
    last = matmul(after(saved[1][12], latent_part), down_w[1])
    start = section * slot_rows
    rows = lax.dynamic_slice_in_dim(last, start, slot_rows, 0) + middle
    last = lax.dynamic_update_slice_in_dim(last, rows, start, 0).astype(low)
    last = last.reshape(latent_rows, section_count, -1)
    last = lax.all_to_all(last, "section", split_axis=1, concat_axis=0)
    latents_out = jnp.sum(last.astype(full), axis=0)
    latent_grad = to_columns(after(grad_rows, (pieces[1], up_half)))
    media_rows = seq_rows // section_count
    media_sum = sum_over_sections(media_scaled)
    own_unit = lax.dynamic_slice_in_dim(media_unit, section * media_rows, media_rows, 0)
    own_inverse = lax.dynamic_slice_in_dim(media_inverse, section * media_rows, media_rows, 0)
    media_grad = gather_sections(norm_back(own_unit, own_inverse, media_sum).astype(low)).astype(
        full
    )
    gain_parts = jnp.stack(gain_rows).reshape(LAYERS, 3, section_count, -1)
    gain_parts = jnp.sum(
        lax.all_to_all(gain_parts, "section", split_axis=2, concat_axis=2), axis=2
    )
    gain_parts = gain_parts.reshape(LAYERS, 3, dp_count, -1)
    gain_grad = jnp.sum(lax.all_to_all(gain_parts, dp, split_axis=2, concat_axis=2), axis=2)

    qkv_parts = [piece[0] for piece in pieces]
    own, other = pick(qkv_parts[0], qkv_parts[1])
    lower, upper = pick(own, swapped(other, 2))
    qkv_grads = [
        jnp.concatenate(
            [lower[:, i * inner : (i + 1) * inner], upper[:, i * inner : (i + 1) * inner]], axis=1
        ).astype(full)
        for i in range(3)
    ]
    out_grad = join_rows(*[piece[1] for piece in pieces])
    down_piece, up_piece = ffn_pieces
    up_second_grad = interleave(to_second(up_piece), up_piece, half_hidden)
    down_second_grad = jnp.concatenate([to_second(down_piece), down_piece], axis=0)
    up_first_grad = jnp.concatenate([up_half, to_first(up_half)], axis=0)
    down_first_grad = jnp.concatenate([down_half, to_first(down_half)], axis=0)
    up_grad = jnp.where(on_first, up_first_grad, up_second_grad).astype(full)
    down_grad = jnp.where(on_first, down_first_grad, down_second_grad).astype(full)
    return (
        latents_out,
        latent_grad,
        media_grad,
        gain_grad,
        qkv_grads[0][None],
        qkv_grads[1][None],
        qkv_grads[2][None],
        out_grad[None],
        up_grad[None],
        down_grad[None],
    )


def solution(mesh):
    section_count, dp_count = mesh.devices.shape
    fine = Mesh(
        mesh.devices.reshape(section_count, dp_count // 2, 2), ("section", "pair", "core")
    )
    dp = ("pair", "core")
    placed = (
        P(dp, None),
        P(dp, None),
        P(dp, None),
        P(dp, None),
        P(None, None, ("section",) + dp),
        P("section", dp, None),
        P("section", dp, None),
        P("section", dp, None),
        P("section", dp, None),
        P("section", dp, None),
        P("section", dp, None),
        P(dp, None),
    )
    return jax.shard_map(
        per_device,
        mesh=fine,
        in_specs=placed,
        out_specs=(
            P(dp, "section"),
            P(dp, "section"),
            P(dp, None),
            P(None, None, ("section",) + dp),
            P("section", dp, None),
            P("section", dp, None),
            P("section", dp, None),
            P("section", dp, None),
            P("section", dp, None),
            P("section", dp, None),
        ),
        check_vma=False,
    )
```

```python
import math

import jax
import jax.numpy as jnp
from jax import lax
from jax.sharding import Mesh, PartitionSpec as P

HEAD_DIM = 96
LATENTS = 64
LAYERS = 2

epsilon = 1e-05
low = jnp.bfloat16
full = jnp.float32


def unit_rows(values):
    centered = values - jnp.mean(values, axis=-1, keepdims=True)
    variance = jnp.mean(centered * centered, axis=-1, keepdims=True)
    inverse = lax.rsqrt(variance + epsilon)
    return centered * inverse, inverse


def norm_back(unit, inverse, scaled):
    first = jnp.mean(scaled, axis=-1, keepdims=True)
    second = jnp.mean(scaled * unit, axis=-1, keepdims=True)
    return (scaled - first - unit * second) * inverse


def gelu_exact(values):
    return jax.nn.gelu(values, approximate=False)


def matmul(left, right):
    return jnp.dot(left, right, preferred_element_type=full)


def matmul_nt(left, right):
    return lax.dot_general(left, right, (((1,), (1,)), ((), ())), preferred_element_type=full)


def matmul_tn(left, right):
    return lax.dot_general(left, right, (((0,), (0,)), ((), ())), preferred_element_type=full)


def attend_forward(query_heads, key_heads, value_heads, allowed, score_scale):
    scores = jnp.einsum("qhd,khd->hqk", query_heads, key_heads, preferred_element_type=full)
    scores = jnp.where(allowed, scores * score_scale, -1e30)
    row_max = jnp.max(scores, axis=-1, keepdims=True)
    exponent = jnp.exp(scores - row_max)
    row_total = jnp.sum(exponent, axis=-1, keepdims=True)
    weights_low = (exponent / row_total).astype(low)
    attended = jnp.einsum("hqk,khd->qhd", weights_low, value_heads, preferred_element_type=full)
    return attended, row_max + jnp.log(row_total)


def attend_backward(
    query_heads, key_heads, value_heads, allowed, score_scale, log_total, grad_heads
):
    scores = jnp.einsum("qhd,khd->hqk", query_heads, key_heads, preferred_element_type=full)
    scores = jnp.where(allowed, scores * score_scale, -1e30)
    weights_full = jnp.exp(scores - log_total)
    weights_low = weights_full.astype(low)
    grad_value = jnp.einsum("hqk,qhd->khd", weights_low, grad_heads, preferred_element_type=full)
    grad_weights = jnp.einsum(
        "qhd,khd->hqk", grad_heads, value_heads, preferred_element_type=full
    )
    row_inner = jnp.sum(weights_full * grad_weights, axis=-1, keepdims=True)
    grad_scores = (weights_full * (grad_weights - row_inner)).astype(low)
    grad_query = (
        jnp.einsum("hqk,khd->qhd", grad_scores, key_heads, preferred_element_type=full)
        * score_scale
    )
    grad_key = (
        jnp.einsum("hqk,qhd->khd", grad_scores, query_heads, preferred_element_type=full)
        * score_scale
    )
    return grad_query, grad_key, grad_value


def per_device(
    latents,
    media,
    segment_ids,
    slot_map,
    gains,
    w_query,
    w_key,
    w_value,
    w_out,
    w_up,
    w_down,
    cotangent,
):
    dp = ("pair", "core")
    everywhere = ("section",) + dp
    section = lax.axis_index("section")
    section_count = lax.axis_size("section")
    dp_index = lax.axis_index(dp)
    dp_count = lax.axis_size("pair") * lax.axis_size("core")
    on_first = section // 2 == 0
    stride = dp_count // 2
    row_first = dp_index // stride == 0
    seq_rows = segment_ids.shape[1]
    slot_count = slot_map.shape[1]
    feature_width = latents.shape[1]
    latent_rows = latents.shape[0]
    slot_rows = latent_rows // section_count
    inner = w_query.shape[2] // 2
    heads = inner // HEAD_DIM
    score_scale = 1.0 / math.sqrt(HEAD_DIM)

    def pick(first, second):
        return jnp.where(on_first, first, second), jnp.where(on_first, second, first)

    def swapped(value, mask):
        pairs = [(source, source ^ mask) for source in range(section_count)]
        return lax.ppermute(value, "section", pairs)

    def other_core(value):
        return lax.ppermute(value, "core", [(0, 1), (1, 0)])

    def to_second(value):
        return lax.ppermute(value, "section", [(0, 2), (1, 3)])

    def to_first(value):
        return lax.ppermute(value, "section", [(2, 0), (3, 1)])

    def after(value, earlier):
        return lax.optimization_barrier((value, earlier))[0]

    def turn_pairs(flip, back):
        pairs = []
        for source in range(section_count):
            for index in range(dp_count):
                layer, half = divmod(source, 2)
                bit, lowest = divmod(index, stride)
                moved = (layer ^ flip) * stride + lowest
                target = (bit * 2 + half) * dp_count + moved
                pair = (source * dp_count + index, target)
                pairs.append(pair[::-1] if back else pair)
        return pairs

    def exchange_rows(weight):
        half = weight.shape[0] // 2
        near, far = pick(weight[:half], weight[half:])
        first = lax.ppermute(near, everywhere, turn_pairs(0, False))
        second = lax.ppermute(far, everywhere, turn_pairs(1, False))
        return (
            jnp.where(row_first, first, second),
            jnp.where(row_first, second, first),
        )

    def join_rows(first, second):
        near = jnp.where(row_first, first, second)
        far = jnp.where(row_first, second, first)
        near = lax.ppermute(near, everywhere, turn_pairs(0, True))
        far = lax.ppermute(far, everywhere, turn_pairs(1, True))
        return jnp.concatenate(pick(near, far), axis=0).astype(full)

    def fold(piece):
        blocks = [piece[:, i * inner : (i + 1) * inner] for i in range(feature_width // inner)]
        return jnp.concatenate(blocks, axis=0)

    def unfold(stacked):
        count = feature_width // inner
        blocks = stacked.reshape(2, stride, count, -1, inner).transpose(1, 0, 3, 2, 4)
        return blocks.reshape(-1, feature_width)

    def by_device(grad):
        blocks = grad.reshape(stride, 2, -1, feature_width).transpose(1, 0, 2, 3)
        return blocks.reshape(-1, feature_width)

    def sum_to_slots(partial):
        blocks = partial.astype(low).reshape(section_count, -1, feature_width)
        arrived = lax.all_to_all(blocks, "section", split_axis=0, concat_axis=0)
        return jnp.sum(arrived.astype(full), axis=0)

    def from_slots(rows):
        return lax.all_gather(rows, "section", axis=0, tiled=True)

    def to_columns(rows):
        moved = lax.all_to_all(
            rows.astype(low), "section", split_axis=1, concat_axis=0, tiled=True
        )
        return moved.astype(full)

    def from_sequences(rows):
        near = lax.all_gather(rows, "pair", axis=0, tiled=True)
        return jnp.concatenate([near, other_core(near)], axis=0)

    def sum_to_sequence(left, right, product):
        half = left.shape[0] // 2
        far = product(left[half:], right).astype(low)
        near = product(left[:half], right) + other_core(far).astype(full)
        blocks = near.astype(low).reshape(-1, slot_rows, feature_width)
        arrived = lax.all_to_all(blocks, "pair", split_axis=0, concat_axis=0)
        return jnp.sum(arrived.astype(full), axis=0)

    def by_distance(rows):
        half = rows.shape[0] // 2
        side = swapped(rows, 1)
        ahead = swapped(rows, 2)
        upper = swapped(side[:half], 2)
        lower = swapped(ahead[half:], 1)
        return rows, side, ahead, jnp.concatenate([upper, lower], axis=0)

    def sum_by_distance(own, side, ahead, across, gate=None):
        half = own.shape[0] // 2
        across = across.astype(low)
        upper = swapped(across[:half], 2).astype(full)
        lower = swapped(across[half:], 1).astype(full)
        if gate is not None:
            upper, lower = after((upper, lower), gate)
        side = jnp.concatenate([side[:half] + upper, side[half:]], axis=0).astype(low)
        ahead = jnp.concatenate([ahead[:half], ahead[half:] + lower], axis=0).astype(low)
        return own + swapped(side, 1).astype(full) + swapped(ahead, 2).astype(full)

    def share_first(lower, upper):
        return jnp.where(on_first, lower, to_second(upper))

    def sum_over_sections(partial):
        blocks = partial.reshape(section_count, -1, feature_width)
        return sum_by_distance(
            *[
                lax.dynamic_index_in_dim(blocks, section ^ mask, 0, keepdims=False)
                for mask in range(4)
            ]
        )

    def gather_sections(rows):
        by_mask = by_distance(rows)
        ordered = []
        for target in range(section_count):
            chosen = by_mask[0]
            for mask in range(1, section_count):
                chosen = jnp.where(section ^ mask == target, by_mask[mask], chosen)
            ordered.append(chosen)
        return jnp.concatenate(ordered, axis=0)

    def column_parts(weight, block):
        rows, width = weight.shape
        split = weight.reshape(rows, width // (2 * block), 2, block)
        return split[:, :, 0].reshape(rows, -1), split[:, :, 1].reshape(rows, -1)

    def interleave(even, odd, block):
        rows, width = even.shape
        parts = [part.reshape(rows, width // block, 1, block) for part in (even, odd)]
        return jnp.concatenate(parts, axis=2).reshape(rows, 2 * width)

    halves = [pick(weight[0, :, :inner], weight[0, :, inner:]) for weight in (w_query, w_key, w_value)]
    own_heads = jnp.concatenate([half[0] for half in halves], axis=1)
    other_heads = swapped(jnp.concatenate([half[1] for half in halves], axis=1), 2)
    qkv_pieces = pick(own_heads, other_heads)
    half_hidden = w_down.shape[1] // 2
    half_depth = w_up.shape[1] // 2
    up_share = share_first(w_up[0, :half_depth], w_up[0, half_depth:])
    all_gains = after(gains, (other_heads, up_share))
    for axis in ("core", "pair", "section"):
        all_gains = lax.all_gather(all_gains, axis, axis=2, tiled=True)
    out_pieces = exchange_rows(after(w_out[0], other_heads))

    def gather(piece):
        return lax.all_gather(piece, dp, axis=0, tiled=True)

    stacked = [
        gather(jnp.concatenate([qkv_pieces[layer], fold(out_pieces[layer])], axis=1))
        for layer in range(LAYERS)
    ]
    qkv_w = [weight[:, : 3 * inner] for weight in stacked]
    out_w = [unfold(weight[:, 3 * inner :]) for weight in stacked]

    up_turned = lax.all_to_all(up_share, dp, split_axis=1, concat_axis=0, tiled=True)
    down_share = share_first(
        *after((w_down[0, :half_hidden], w_down[0, half_hidden:]), other_heads)
    )

    def in_depth(near, far):
        parts = [part.reshape(dp_count, 1, half_depth, -1) for part in pick(near, far)]
        return jnp.concatenate(parts, axis=1).reshape(feature_width, -1)

    def first_ffn(gate):
        down, up = after((down_share, up_turned), gate)
        down, up = by_distance(down), by_distance(up)
        return (
            jnp.concatenate([in_depth(up[0], up[2]), in_depth(up[1], up[3])], axis=1),
            jnp.concatenate(pick(down[0], down[2]) + pick(down[1], down[3]), axis=0),
        )

    up_even, up_odd = column_parts(w_up[0], half_hidden)
    up_piece, down_piece = after((up_even, w_down[0, :half_hidden]), all_gains)
    down_second = gather(
        jnp.where(on_first, to_first(down_piece), w_down[0, half_hidden:])
    )
    up_second = gather(jnp.where(on_first, to_first(up_piece), up_odd))
    up_w = [None, up_second]
    down_w = [None, down_second]
    query_w = [weight[:, :inner] for weight in qkv_w]
    key_w = [weight[:, inner : 2 * inner] for weight in qkv_w]
    value_w = [weight[:, 2 * inner :] for weight in qkv_w]

    image_hot = segment_ids[:, :, None] == jnp.arange(slot_count, dtype=jnp.int32)[None, None, :]
    media_slot = jnp.sum(jnp.where(image_hot, slot_map[:, None, :], 0), axis=2) - (
        segment_ids < 0
    ).astype(jnp.int32)
    media_unit, media_inverse = unit_rows(media.astype(full))
    latent_slot = jnp.arange(latent_rows, dtype=jnp.int32) // LATENTS
    key_slot = jnp.concatenate([media_slot[0], latent_slot])
    allowed = latent_slot[None, :, None] == key_slot[None, None, :]

    def split_heads(rows):
        return rows.reshape(rows.shape[0], heads, HEAD_DIM)

    media_low = []
    media_key = []
    media_value = []
    for layer in range(LAYERS):
        media_low.append((media_unit * all_gains[layer, 0]).astype(low))
        media_key.append(matmul(media_low[layer], key_w[layer]).astype(low))
        media_value.append(matmul(media_low[layer], value_w[layer]).astype(low))

    saved = []
    current = lax.dynamic_slice_in_dim(latents, section * slot_rows, slot_rows, 0).astype(full)
    grad_rows = lax.dynamic_slice_in_dim(cotangent, section * slot_rows, slot_rows, 0).astype(full)
    grad_low = cotangent
    for layer in range(LAYERS):
        unit_in, inverse_in = unit_rows(current)
        if layer == 0:
            whole_unit = unit_rows(latents.astype(full))[0]
            latent_low = (whole_unit * all_gains[layer, 1]).astype(low)
        else:
            latent_low = from_slots((unit_in * all_gains[layer, 1]).astype(low))
        projected = matmul(latent_low, qkv_w[layer]).astype(low)
        if layer == 0:
            up_w[0], down_w[0] = first_ffn(projected)
        query_low = projected[:, :inner]
        key_heads = split_heads(
            jnp.concatenate([media_key[layer], projected[:, inner : 2 * inner]], axis=0)
        )
        value_heads = split_heads(
            jnp.concatenate([media_value[layer], projected[:, 2 * inner :]], axis=0)
        )
        query_heads = split_heads(query_low)
        attended, log_total = attend_forward(
            query_heads, key_heads, value_heads, allowed, score_scale
        )
        attended_low = attended.reshape(-1, inner).astype(low)
        middle = current + sum_to_slots(matmul(attended_low, out_w[layer]))
        unit_mid, inverse_mid = unit_rows(middle)
        ffn_low = (unit_mid * all_gains[layer, 2]).astype(low)
        ffn_low = from_slots(ffn_low) if layer else from_sequences(ffn_low)
        hidden_pre = matmul(ffn_low, up_w[layer])
        active_low = gelu_exact(hidden_pre).astype(low)
        if layer == 0:
            current = middle + sum_to_sequence(active_low, down_w[layer], matmul)
        saved.append(
            (
                unit_in,
                inverse_in,
                latent_low,
                query_heads,
                key_heads,
                value_heads,
                log_total,
                attended_low,
                unit_mid,
                inverse_mid,
                ffn_low,
                hidden_pre,
                active_low,
            )
        )

    def scatter(blocks):
        return lax.psum_scatter(blocks, dp, scatter_dimension=0, tiled=True)

    gain_rows = [None] * LAYERS
    media_scaled = None
    pieces = [None] * LAYERS
    for layer in (1, 0):
        (
            unit_in,
            inverse_in,
            latent_low,
            query_heads,
            key_heads,
            value_heads,
            log_total,
            attended_low,
            unit_mid,
            inverse_mid,
            ffn_low,
            hidden_pre,
            active_low,
        ) = saved[layer]
        grad_active = matmul_nt(grad_low, down_w[layer])
        grad_hidden = jax.vjp(gelu_exact, hidden_pre)[1](grad_active)[0].astype(low)
        down_grad = matmul_tn(active_low, grad_low)
        if layer:
            down_grad = down_grad.astype(low)
            grad_hidden = after(grad_hidden, down_grad)
        up_grad = matmul_tn(ffn_low, grad_hidden)
        if layer:
            ffn_pieces = (scatter(down_grad), scatter(up_grad.astype(low)))
            ffn_grad = sum_to_slots(matmul_nt(grad_hidden, up_w[layer]))
        else:
            ffn_grad = sum_to_sequence(grad_hidden, up_w[layer], matmul_nt)
            blocks = down_grad.reshape(2, 2, half_hidden, feature_width)
            own, ahead = pick(blocks[0, 0], blocks[0, 1])
            side, across = pick(blocks[1, 0], blocks[1, 1])
            down_blocks = (own, side, ahead, across)
            width = up_grad.shape[1] // 2
            blocks = up_grad.reshape(dp_count, 2, half_depth, 2 * width)
            blocks = [blocks[:, i].reshape(-1, 2 * width) for i in range(2)]
            own, ahead = pick(blocks[0][:, :width], blocks[1][:, :width])
            side, across = pick(blocks[0][:, width:], blocks[1][:, width:])
            up_blocks = (own, side, ahead, across)
        gain_ffn_grad = jnp.sum(ffn_grad * unit_mid, axis=0)
        grad_middle = grad_rows + norm_back(
            unit_mid, inverse_mid, ffn_grad * all_gains[layer, 2]
        )
        middle_low = from_slots(grad_middle.astype(low))
        if layer == 0:
            up_half = sum_by_distance(*up_blocks, middle_low).astype(low)
            down_half = sum_by_distance(*down_blocks, middle_low).astype(low)
        grad_heads = split_heads(matmul_nt(middle_low, out_w[layer]).astype(low))
        out_grad = by_device(matmul_tn(attended_low, middle_low)).astype(low)
        out_piece = scatter(out_grad)
        grad_heads = after(grad_heads, out_grad)
        grad_query, grad_key, grad_value = attend_backward(
            query_heads, key_heads, value_heads, allowed, score_scale, log_total, grad_heads
        )
        grad_query = grad_query.reshape(-1, inner).astype(low)
        grad_key = grad_key.reshape(-1, inner).astype(low)
        grad_value = grad_value.reshape(-1, inner).astype(low)
        latent_part = (
            matmul_nt(grad_query, query_w[layer])
            + matmul_nt(grad_key[seq_rows:], key_w[layer])
            + matmul_nt(grad_value[seq_rows:], value_w[layer])
        )
        latent_grad_rows = sum_to_slots(latent_part)
        gain_latent_grad = jnp.sum(latent_grad_rows * unit_in, axis=0)
        grad_rows = grad_middle + norm_back(
            unit_in, inverse_in, latent_grad_rows * all_gains[layer, 1]
        )
        both_low = jnp.concatenate([media_low[layer], latent_low], axis=0)
        all_grads = jnp.concatenate(
            [jnp.pad(grad_query, ((seq_rows, 0), (0, 0))), grad_key, grad_value], axis=1
        )
        qkv_grad = matmul_tn(both_low, all_grads).astype(low)
        if layer == 0:
            up_half, qkv_grad = lax.optimization_barrier((up_half, qkv_grad))
            up_half = lax.all_to_all(up_half, dp, split_axis=0, concat_axis=1, tiled=True)
        pieces[layer] = (scatter(qkv_grad), out_piece)
        if layer > 0:
            grad_low = from_sequences(grad_rows.astype(low))
            last = matmul(after(active_low, latent_part), down_w[layer])
            start = section * slot_rows
            rows = lax.dynamic_slice_in_dim(last, start, slot_rows, 0) + middle
            last = lax.dynamic_update_slice_in_dim(last, rows, start, 0).astype(low)
            last = last.reshape(latent_rows, section_count, -1)
            last = lax.all_to_all(last, "section", split_axis=1, concat_axis=0)
            latents_out = jnp.sum(last.astype(full), axis=0)
            grad_low = after(grad_low, latents_out)
            grad_low = after(grad_low, ffn_pieces)
        media_part = matmul_nt(grad_key[:seq_rows], key_w[layer]) + matmul_nt(
            grad_value[:seq_rows], value_w[layer]
        )
        gain_media_grad = jnp.sum(media_part * media_unit, axis=0)
        scaled = media_part * all_gains[layer, 0]
        media_scaled = scaled if media_scaled is None else media_scaled + scaled
        gain_rows[layer] = jnp.stack([gain_media_grad, gain_latent_grad, gain_ffn_grad])
    latent_grad = to_columns(after(grad_rows, (pieces[1], up_half)))
    media_rows = seq_rows // section_count
    media_sum = sum_over_sections(media_scaled)
    own_unit = lax.dynamic_slice_in_dim(media_unit, section * media_rows, media_rows, 0)
    own_inverse = lax.dynamic_slice_in_dim(media_inverse, section * media_rows, media_rows, 0)
    media_grad = gather_sections(norm_back(own_unit, own_inverse, media_sum).astype(low)).astype(
        full
    )
    gain_parts = jnp.stack(gain_rows).reshape(LAYERS, 3, section_count, -1)
    gain_parts = jnp.sum(
        lax.all_to_all(gain_parts, "section", split_axis=2, concat_axis=2), axis=2
    )
    gain_parts = gain_parts.reshape(LAYERS, 3, dp_count, -1)
    gain_grad = jnp.sum(lax.all_to_all(gain_parts, dp, split_axis=2, concat_axis=2), axis=2)

    qkv_parts = [piece[0] for piece in pieces]
    own, other = pick(qkv_parts[0], qkv_parts[1])
    lower, upper = pick(own, swapped(other, 2))
    qkv_grads = [
        jnp.concatenate(
            [lower[:, i * inner : (i + 1) * inner], upper[:, i * inner : (i + 1) * inner]], axis=1
        ).astype(full)
        for i in range(3)
    ]
    out_grad = join_rows(*[piece[1] for piece in pieces])
    down_piece, up_piece = ffn_pieces
    up_second_grad = interleave(to_second(up_piece), up_piece, half_hidden)
    down_second_grad = jnp.concatenate([to_second(down_piece), down_piece], axis=0)
    up_first_grad = jnp.concatenate([up_half, to_first(up_half)], axis=0)
    down_first_grad = jnp.concatenate([down_half, to_first(down_half)], axis=0)
    up_grad = jnp.where(on_first, up_first_grad, up_second_grad).astype(full)
    down_grad = jnp.where(on_first, down_first_grad, down_second_grad).astype(full)
    return (
        latents_out,
        latent_grad,
        media_grad,
        gain_grad,
        qkv_grads[0][None],
        qkv_grads[1][None],
        qkv_grads[2][None],
        out_grad[None],
        up_grad[None],
        down_grad[None],
    )


def solution(mesh):
    section_count, dp_count = mesh.devices.shape
    fine = Mesh(
        mesh.devices.reshape(section_count, dp_count // 2, 2), ("section", "pair", "core")
    )
    dp = ("pair", "core")
    placed = (
        P(dp, None),
        P(dp, None),
        P(dp, None),
        P(dp, None),
        P(None, None, ("section",) + dp),
        P("section", dp, None),
        P("section", dp, None),
        P("section", dp, None),
        P("section", dp, None),
        P("section", dp, None),
        P("section", dp, None),
        P(dp, None),
    )
    return jax.shard_map(
        per_device,
        mesh=fine,
        in_specs=placed,
        out_specs=(
            P(dp, "section"),
            P(dp, "section"),
            P(dp, None),
            P(None, None, ("section",) + dp),
            P("section", dp, None),
            P("section", dp, None),
            P("section", dp, None),
            P("section", dp, None),
            P("section", dp, None),
            P("section", dp, None),
        ),
        check_vma=False,
    )
```

```python
import math

import jax
import jax.numpy as jnp
from jax import lax
from jax.sharding import Mesh, PartitionSpec as P

HEAD_DIM = 96
LATENTS = 64
LAYERS = 2

epsilon = 1e-05
low = jnp.bfloat16
full = jnp.float32


def unit_rows(values):
    centered = values - jnp.mean(values, axis=-1, keepdims=True)
    variance = jnp.mean(centered * centered, axis=-1, keepdims=True)
    inverse = lax.rsqrt(variance + epsilon)
    return centered * inverse, inverse


def norm_back(unit, inverse, scaled):
    first = jnp.mean(scaled, axis=-1, keepdims=True)
    second = jnp.mean(scaled * unit, axis=-1, keepdims=True)
    return (scaled - first - unit * second) * inverse


def gelu_exact(values):
    return jax.nn.gelu(values, approximate=False)


def matmul(left, right):
    return jnp.dot(left, right, preferred_element_type=full)


def matmul_nt(left, right):
    return lax.dot_general(left, right, (((1,), (1,)), ((), ())), preferred_element_type=full)


def matmul_tn(left, right):
    return lax.dot_general(left, right, (((0,), (0,)), ((), ())), preferred_element_type=full)


def attend_forward(query_heads, key_heads, value_heads, allowed, score_scale):
    scores = jnp.einsum("qhd,khd->hqk", query_heads, key_heads, preferred_element_type=full)
    scores = jnp.where(allowed, scores * score_scale, -1e30)
    row_max = jnp.max(scores, axis=-1, keepdims=True)
    exponent = jnp.exp(scores - row_max)
    row_total = jnp.sum(exponent, axis=-1, keepdims=True)
    weights_low = (exponent / row_total).astype(low)
    attended = jnp.einsum("hqk,khd->qhd", weights_low, value_heads, preferred_element_type=full)
    return attended, row_max + jnp.log(row_total)


def attend_backward(
    query_heads, key_heads, value_heads, allowed, score_scale, log_total, grad_heads
):
    scores = jnp.einsum("qhd,khd->hqk", query_heads, key_heads, preferred_element_type=full)
    scores = jnp.where(allowed, scores * score_scale, -1e30)
    weights_full = jnp.exp(scores - log_total)
    weights_low = weights_full.astype(low)
    grad_value = jnp.einsum("hqk,qhd->khd", weights_low, grad_heads, preferred_element_type=full)
    grad_weights = jnp.einsum(
        "qhd,khd->hqk", grad_heads, value_heads, preferred_element_type=full
    )
    row_inner = jnp.sum(weights_full * grad_weights, axis=-1, keepdims=True)
    grad_scores = (weights_full * (grad_weights - row_inner)).astype(low)
    grad_query = (
        jnp.einsum("hqk,khd->qhd", grad_scores, key_heads, preferred_element_type=full)
        * score_scale
    )
    grad_key = (
        jnp.einsum("hqk,qhd->khd", grad_scores, query_heads, preferred_element_type=full)
        * score_scale
    )
    return grad_query, grad_key, grad_value


def per_device(
    latents,
    media,
    segment_ids,
    slot_map,
    gains,
    w_query,
    w_key,
    w_value,
    w_out,
    w_up,
    w_down,
    cotangent,
):
    dp = ("pair", "core")
    everywhere = ("section",) + dp
    section = lax.axis_index("section")
    section_count = lax.axis_size("section")
    dp_index = lax.axis_index(dp)
    dp_count = lax.axis_size("pair") * lax.axis_size("core")
    on_first = section // 2 == 0
    stride = dp_count // 2
    row_first = dp_index // stride == 0
    seq_rows = segment_ids.shape[1]
    slot_count = slot_map.shape[1]
    feature_width = latents.shape[1]
    latent_rows = latents.shape[0]
    slot_rows = latent_rows // section_count
    inner = w_query.shape[2] // 2
    heads = inner // HEAD_DIM
    score_scale = 1.0 / math.sqrt(HEAD_DIM)

    def pick(first, second):
        return jnp.where(on_first, first, second), jnp.where(on_first, second, first)

    def swapped(value, mask):
        pairs = [(source, source ^ mask) for source in range(section_count)]
        return lax.ppermute(value, "section", pairs)

    def other_core(value):
        return lax.ppermute(value, "core", [(0, 1), (1, 0)])

    def to_second(value):
        return lax.ppermute(value, "section", [(0, 2), (1, 3)])

    def to_first(value):
        return lax.ppermute(value, "section", [(2, 0), (3, 1)])

    def after(value, earlier):
        return lax.optimization_barrier((value, earlier))[0]

    def turn_pairs(flip, back):
        pairs = []
        for source in range(section_count):
            for index in range(dp_count):
                layer, half = divmod(source, 2)
                bit, lowest = divmod(index, stride)
                moved = (layer ^ flip) * stride + lowest
                target = (bit * 2 + half) * dp_count + moved
                pair = (source * dp_count + index, target)
                pairs.append(pair[::-1] if back else pair)
        return pairs

    def exchange_rows(weight):
        half = weight.shape[0] // 2
        near, far = pick(weight[:half], weight[half:])
        first = lax.ppermute(near, everywhere, turn_pairs(0, False))
        second = lax.ppermute(far, everywhere, turn_pairs(1, False))
        return (
            jnp.where(row_first, first, second),
            jnp.where(row_first, second, first),
        )

    def join_rows(first, second):
        near = jnp.where(row_first, first, second)
        far = jnp.where(row_first, second, first)
        near = lax.ppermute(near, everywhere, turn_pairs(0, True))
        far = lax.ppermute(far, everywhere, turn_pairs(1, True))
        return jnp.concatenate(pick(near, far), axis=0).astype(full)

    def fold(piece):
        blocks = [piece[:, i * inner : (i + 1) * inner] for i in range(feature_width // inner)]
        return jnp.concatenate(blocks, axis=0)

    def unfold(stacked):
        count = feature_width // inner
        blocks = stacked.reshape(2, stride, count, -1, inner).transpose(1, 0, 3, 2, 4)
        return blocks.reshape(-1, feature_width)

    def by_device(grad):
        blocks = grad.reshape(stride, 2, -1, feature_width).transpose(1, 0, 2, 3)
        return blocks.reshape(-1, feature_width)

    def sum_to_slots(partial):
        blocks = partial.astype(low).reshape(section_count, -1, feature_width)
        arrived = lax.all_to_all(blocks, "section", split_axis=0, concat_axis=0)
        return jnp.sum(arrived.astype(full), axis=0)

    def from_slots(rows):
        return lax.all_gather(rows, "section", axis=0, tiled=True)

    def to_columns(rows):
        moved = lax.all_to_all(
            rows.astype(low), "section", split_axis=1, concat_axis=0, tiled=True
        )
        return moved.astype(full)

    def from_sequences(rows):
        near = lax.all_gather(rows, "pair", axis=0, tiled=True)
        return jnp.concatenate([near, other_core(near)], axis=0)

    def sum_to_sequence(left, right, product):
        half = left.shape[0] // 2
        far = product(left[half:], right).astype(low)
        near = product(left[:half], right) + other_core(far).astype(full)
        blocks = near.astype(low).reshape(-1, slot_rows, feature_width)
        arrived = lax.all_to_all(blocks, "pair", split_axis=0, concat_axis=0)
        return jnp.sum(arrived.astype(full), axis=0)

    def by_distance(rows):
        half = rows.shape[0] // 2
        side = swapped(rows, 1)
        ahead = swapped(rows, 2)
        upper = swapped(side[:half], 2)
        lower = swapped(ahead[half:], 1)
        return rows, side, ahead, jnp.concatenate([upper, lower], axis=0)

    def sum_by_distance(own, side, ahead, across, gate=None):
        half = own.shape[0] // 2
        across = across.astype(low)
        upper = swapped(across[:half], 2)
        lower = swapped(across[half:], 1)
        if gate is not None:
            upper, lower = after((upper, lower), gate)
        side = jnp.concatenate([side[:half] + upper.astype(full), side[half:]], axis=0)
        ahead = jnp.concatenate([ahead[:half], ahead[half:] + lower.astype(full)], axis=0)
        side, ahead = side.astype(low), ahead.astype(low)
        return own + swapped(side, 1).astype(full) + swapped(ahead, 2).astype(full)

    def share_first(lower, upper):
        return jnp.where(on_first, lower, to_second(upper))

    def sum_over_sections(partial):
        blocks = partial.reshape(section_count, -1, feature_width)
        return sum_by_distance(
            *[
                lax.dynamic_index_in_dim(blocks, section ^ mask, 0, keepdims=False)
                for mask in range(4)
            ]
        )

    def gather_sections(rows):
        by_mask = by_distance(rows)
        ordered = []
        for target in range(section_count):
            chosen = by_mask[0]
            for mask in range(1, section_count):
                chosen = jnp.where(section ^ mask == target, by_mask[mask], chosen)
            ordered.append(chosen)
        return jnp.concatenate(ordered, axis=0)

    def column_parts(weight, block):
        rows, width = weight.shape
        split = weight.reshape(rows, width // (2 * block), 2, block)
        return split[:, :, 0].reshape(rows, -1), split[:, :, 1].reshape(rows, -1)

    def interleave(even, odd, block):
        rows, width = even.shape
        parts = [part.reshape(rows, width // block, 1, block) for part in (even, odd)]
        return jnp.concatenate(parts, axis=2).reshape(rows, 2 * width)

    halves = [pick(weight[0, :, :inner], weight[0, :, inner:]) for weight in (w_query, w_key, w_value)]
    own_heads = jnp.concatenate([half[0] for half in halves], axis=1)
    other_heads = swapped(jnp.concatenate([half[1] for half in halves], axis=1), 2)
    qkv_pieces = pick(own_heads, other_heads)
    half_hidden = w_down.shape[1] // 2
    half_depth = w_up.shape[1] // 2
    up_share = share_first(w_up[0, :half_depth], w_up[0, half_depth:])
    all_gains = after(gains, (other_heads, up_share))
    for axis in ("core", "pair", "section"):
        all_gains = lax.all_gather(all_gains, axis, axis=2, tiled=True)
    out_pieces = exchange_rows(after(w_out[0], other_heads))

    def gather(piece):
        return lax.all_gather(piece, dp, axis=0, tiled=True)

    stacked = [
        gather(jnp.concatenate([qkv_pieces[layer], fold(out_pieces[layer])], axis=1))
        for layer in range(LAYERS)
    ]
    qkv_w = [weight[:, : 3 * inner] for weight in stacked]
    out_w = [unfold(weight[:, 3 * inner :]) for weight in stacked]

    up_turned = lax.all_to_all(up_share, dp, split_axis=1, concat_axis=0, tiled=True)
    down_share = share_first(
        *after((w_down[0, :half_hidden], w_down[0, half_hidden:]), other_heads)
    )

    def by_depth(rows):
        return rows.reshape(-1, dp_count, 2, half_depth).swapaxes(1, 2).reshape(rows.shape)

    def in_depth(rows):
        return rows.reshape(-1, 2, dp_count, half_depth).swapaxes(1, 2).reshape(rows.shape)

    def first_ffn(gate):
        down, up = after((down_share, up_turned), gate)
        down, up = by_distance(down), by_distance(up)
        return (
            jnp.concatenate(
                [
                    jnp.concatenate(pick(up[0], up[2]), axis=0),
                    jnp.concatenate(pick(up[1], up[3]), axis=0),
                ],
                axis=1,
            ),
            jnp.concatenate(pick(down[0], down[2]) + pick(down[1], down[3]), axis=0),
        )

    up_late, down_late = after((w_up[0], w_down[0]), all_gains)
    down_second = gather(
        jnp.where(on_first, to_first(down_late[:half_hidden]), down_late[half_hidden:])
    )
    up_even, up_odd = column_parts(up_late, half_hidden)
    up_second = gather(jnp.where(on_first, to_first(up_even), up_odd))
    up_w = [None, up_second]
    down_w = [None, down_second]
    query_w = [weight[:, :inner] for weight in qkv_w]
    key_w = [weight[:, inner : 2 * inner] for weight in qkv_w]
    value_w = [weight[:, 2 * inner :] for weight in qkv_w]

    image_hot = segment_ids[:, :, None] == jnp.arange(slot_count, dtype=jnp.int32)[None, None, :]
    media_slot = jnp.sum(jnp.where(image_hot, slot_map[:, None, :], 0), axis=2) - (
        segment_ids < 0
    ).astype(jnp.int32)
    media_unit, media_inverse = unit_rows(media.astype(full))
    latent_slot = jnp.arange(latent_rows, dtype=jnp.int32) // LATENTS
    key_slot = jnp.concatenate([media_slot[0], latent_slot])
    allowed = latent_slot[None, :, None] == key_slot[None, None, :]

    def split_heads(rows):
        return rows.reshape(rows.shape[0], heads, HEAD_DIM)

    media_low = []
    media_key = []
    media_value = []
    for layer in range(LAYERS):
        media_low.append((media_unit * all_gains[layer, 0]).astype(low))
        media_key.append(matmul(media_low[layer], key_w[layer]).astype(low))
        media_value.append(matmul(media_low[layer], value_w[layer]).astype(low))

    saved = []
    current = lax.dynamic_slice_in_dim(latents, section * slot_rows, slot_rows, 0).astype(full)
    grad_rows = lax.dynamic_slice_in_dim(cotangent, section * slot_rows, slot_rows, 0).astype(full)
    grad_low = cotangent
    for layer in range(LAYERS):
        unit_in, inverse_in = unit_rows(current)
        if layer == 0:
            whole_unit = unit_rows(latents.astype(full))[0]
            latent_low = (whole_unit * all_gains[layer, 1]).astype(low)
        else:
            latent_low = from_slots((unit_in * all_gains[layer, 1]).astype(low))
        projected = matmul(latent_low, qkv_w[layer]).astype(low)
        if layer == 0:
            up_w[0], down_w[0] = first_ffn(projected)
        query_low = projected[:, :inner]
        key_heads = split_heads(
            jnp.concatenate([media_key[layer], projected[:, inner : 2 * inner]], axis=0)
        )
        value_heads = split_heads(
            jnp.concatenate([media_value[layer], projected[:, 2 * inner :]], axis=0)
        )
        query_heads = split_heads(query_low)
        attended, log_total = attend_forward(
            query_heads, key_heads, value_heads, allowed, score_scale
        )
        attended_low = attended.reshape(-1, inner).astype(low)
        middle = current + sum_to_slots(matmul(attended_low, out_w[layer]))
        unit_mid, inverse_mid = unit_rows(middle)
        ffn_low = (unit_mid * all_gains[layer, 2]).astype(low)
        ffn_low = from_slots(ffn_low) if layer else from_sequences(by_depth(ffn_low))
        hidden_pre = matmul(ffn_low, up_w[layer])
        active_low = gelu_exact(hidden_pre).astype(low)
        if layer == 0:
            current = middle + sum_to_sequence(active_low, down_w[layer], matmul)
        saved.append(
            (
                unit_in,
                inverse_in,
                latent_low,
                query_heads,
                key_heads,
                value_heads,
                log_total,
                attended_low,
                unit_mid,
                inverse_mid,
                ffn_low,
                hidden_pre,
                active_low,
            )
        )

    def scatter(blocks):
        return lax.psum_scatter(blocks, dp, scatter_dimension=0, tiled=True)

    gain_rows = [None] * LAYERS
    media_parts = []
    media_gains = []

    def add_media(layer, grad_key, grad_value, gate):
        grad_key, grad_value = after((grad_key[:seq_rows], grad_value[:seq_rows]), gate)
        part = matmul_nt(grad_key, key_w[layer]) + matmul_nt(grad_value, value_w[layer])
        media_gains.append(jnp.sum(part * media_unit, axis=0))
        media_parts.append(part * all_gains[layer, 0])

    pieces = [None] * LAYERS
    for layer in (1, 0):
        (
            unit_in,
            inverse_in,
            latent_low,
            query_heads,
            key_heads,
            value_heads,
            log_total,
            attended_low,
            unit_mid,
            inverse_mid,
            ffn_low,
            hidden_pre,
            active_low,
        ) = saved[layer]
        grad_active = matmul_nt(grad_low, down_w[layer])
        grad_hidden = jax.vjp(gelu_exact, hidden_pre)[1](grad_active)[0].astype(low)
        if layer == 0:
            add_media(1, *media_grads, grad_hidden)
        down_grad = matmul_tn(active_low, grad_low)
        if layer:
            down_grad = down_grad.astype(low)
            grad_hidden = after(grad_hidden, down_grad)
        up_grad = matmul_tn(ffn_low, grad_hidden)
        if layer:
            ffn_pieces = (scatter(down_grad), scatter(up_grad.astype(low)))
            ffn_grad = sum_to_slots(matmul_nt(grad_hidden, up_w[layer]))
        else:
            ffn_grad = in_depth(sum_to_sequence(grad_hidden, up_w[layer], matmul_nt))
            blocks = down_grad.reshape(2, 2, half_hidden, feature_width)
            own, ahead = pick(blocks[0, 0], blocks[0, 1])
            side, across = pick(blocks[1, 0], blocks[1, 1])
            down_blocks = (own, side, ahead, across)
            width = up_grad.shape[1] // 2
            blocks = up_grad.reshape(2, -1, 2 * width)
            own, ahead = pick(blocks[0][:, :width], blocks[1][:, :width])
            side, across = pick(blocks[0][:, width:], blocks[1][:, width:])
            up_blocks = (own, side, ahead, across)
        gain_ffn_grad = jnp.sum(ffn_grad * unit_mid, axis=0)
        grad_middle = grad_rows + norm_back(
            unit_mid, inverse_mid, ffn_grad * all_gains[layer, 2]
        )
        middle_low = from_slots(grad_middle.astype(low))
        if layer == 0:
            up_half = sum_by_distance(*up_blocks, middle_low).astype(low)
            down_half = sum_by_distance(*down_blocks, middle_low).astype(low)
        grad_heads = split_heads(matmul_nt(middle_low, out_w[layer]).astype(low))
        out_grad = by_device(matmul_tn(attended_low, middle_low)).astype(low)
        out_piece = scatter(out_grad)
        grad_heads = after(grad_heads, out_grad)
        grad_query, grad_key, grad_value = attend_backward(
            query_heads, key_heads, value_heads, allowed, score_scale, log_total, grad_heads
        )
        grad_query = grad_query.reshape(-1, inner).astype(low)
        grad_key = grad_key.reshape(-1, inner).astype(low)
        grad_value = grad_value.reshape(-1, inner).astype(low)
        latent_part = (
            matmul_nt(grad_query, query_w[layer])
            + matmul_nt(grad_key[seq_rows:], key_w[layer])
            + matmul_nt(grad_value[seq_rows:], value_w[layer])
        )
        latent_grad_rows = sum_to_slots(latent_part)
        gain_latent_grad = jnp.sum(latent_grad_rows * unit_in, axis=0)
        grad_rows = grad_middle + norm_back(
            unit_in, inverse_in, latent_grad_rows * all_gains[layer, 1]
        )
        both_low = jnp.concatenate([media_low[layer], latent_low], axis=0)
        all_grads = jnp.concatenate(
            [jnp.pad(grad_query, ((seq_rows, 0), (0, 0))), grad_key, grad_value], axis=1
        )
        qkv_grad = matmul_tn(both_low, all_grads).astype(low)
        if layer == 0:
            up_half, qkv_grad = lax.optimization_barrier((up_half, qkv_grad))
            up_half = lax.all_to_all(up_half, dp, split_axis=0, concat_axis=1, tiled=True)
        pieces[layer] = (scatter(qkv_grad), out_piece)
        if layer > 0:
            grad_low = from_sequences(grad_rows.astype(low))
            late = after(active_low, latent_part)
            here = (latent_slot == section)[:, None]
            kept = jnp.where(here, jnp.tile(middle, (section_count, 1)), 0.0)
            width = feature_width // section_count
            last = []
            for i in range(section_count):
                cut = slice(i * width, (i + 1) * width)
                last.append((matmul(late, down_w[layer][:, cut]) + kept[:, cut]).astype(low))
            last = lax.all_to_all(jnp.stack(last), "section", split_axis=0, concat_axis=0)
            latents_out = jnp.sum(last.astype(full), axis=0)
            grad_low = after(grad_low, latents_out)
            grad_low = after(grad_low, ffn_pieces)
        if layer == 0:
            add_media(0, grad_key, grad_value, qkv_grad)
        else:
            media_grads = (grad_key, grad_value)
        gain_rows[layer] = (gain_latent_grad, gain_ffn_grad)
    latent_grad = to_columns(after(grad_rows, (pieces[1], up_half)))
    media_rows = seq_rows // section_count
    media_sum = sum_over_sections(media_parts[0] + media_parts[1])
    own_unit = lax.dynamic_slice_in_dim(media_unit, section * media_rows, media_rows, 0)
    own_inverse = lax.dynamic_slice_in_dim(media_inverse, section * media_rows, media_rows, 0)
    media_grad = gather_sections(norm_back(own_unit, own_inverse, media_sum).astype(low)).astype(
        full
    )
    gain_rows = [
        jnp.stack([media_gains[1 - layer], *gain_rows[layer]]) for layer in range(LAYERS)
    ]
    gain_parts = jnp.stack(gain_rows).reshape(LAYERS, 3, section_count, -1)
    gain_parts = jnp.sum(
        lax.all_to_all(gain_parts, "section", split_axis=2, concat_axis=2), axis=2
    )
    gain_parts = gain_parts.reshape(LAYERS, 3, dp_count, -1)
    gain_grad = jnp.sum(lax.all_to_all(gain_parts, dp, split_axis=2, concat_axis=2), axis=2)

    qkv_parts = [piece[0] for piece in pieces]
    own, other = pick(qkv_parts[0], qkv_parts[1])
    lower, upper = pick(own, swapped(other, 2))
    qkv_grads = [
        jnp.concatenate(
            [lower[:, i * inner : (i + 1) * inner], upper[:, i * inner : (i + 1) * inner]], axis=1
        ).astype(full)
        for i in range(3)
    ]
    out_grad = join_rows(*[piece[1] for piece in pieces])
    down_piece, up_piece = ffn_pieces
    up_second_grad = interleave(to_second(up_piece), up_piece, half_hidden)
    down_second_grad = jnp.concatenate([to_second(down_piece), down_piece], axis=0)
    up_first_grad = jnp.concatenate([up_half, to_first(up_half)], axis=0)
    down_first_grad = jnp.concatenate([down_half, to_first(down_half)], axis=0)
    up_grad = jnp.where(on_first, up_first_grad, up_second_grad).astype(full)
    down_grad = jnp.where(on_first, down_first_grad, down_second_grad).astype(full)
    return (
        latents_out,
        latent_grad,
        media_grad,
        gain_grad,
        qkv_grads[0][None],
        qkv_grads[1][None],
        qkv_grads[2][None],
        out_grad[None],
        up_grad[None],
        down_grad[None],
    )


def solution(mesh):
    section_count, dp_count = mesh.devices.shape
    fine = Mesh(
        mesh.devices.reshape(section_count, dp_count // 2, 2), ("section", "pair", "core")
    )
    dp = ("pair", "core")
    placed = (
        P(dp, None),
        P(dp, None),
        P(dp, None),
        P(dp, None),
        P(None, None, ("section",) + dp),
        P("section", dp, None),
        P("section", dp, None),
        P("section", dp, None),
        P("section", dp, None),
        P("section", dp, None),
        P("section", dp, None),
        P(dp, None),
    )
    return jax.shard_map(
        per_device,
        mesh=fine,
        in_specs=placed,
        out_specs=(
            P(dp, "section"),
            P(dp, "section"),
            P(dp, None),
            P(None, None, ("section",) + dp),
            P("section", dp, None),
            P("section", dp, None),
            P("section", dp, None),
            P("section", dp, None),
            P("section", dp, None),
            P("section", dp, None),
        ),
        check_vma=False,
    )
```

```python
import math

import jax
import jax.numpy as jnp
from jax import lax
from jax.sharding import Mesh, PartitionSpec as P

HEAD_DIM = 96
LATENTS = 64
LAYERS = 2

epsilon = 1e-05
low = jnp.bfloat16
full = jnp.float32


def unit_rows(values):
    centered = values - jnp.mean(values, axis=-1, keepdims=True)
    variance = jnp.mean(centered * centered, axis=-1, keepdims=True)
    inverse = lax.rsqrt(variance + epsilon)
    return centered * inverse, inverse


def norm_back(unit, inverse, scaled):
    first = jnp.mean(scaled, axis=-1, keepdims=True)
    second = jnp.mean(scaled * unit, axis=-1, keepdims=True)
    return (scaled - first - unit * second) * inverse


def gelu_exact(values):
    return 0.5 * values * (1.0 + lax.erf(values * math.sqrt(0.5)))


def gelu_slope(values):
    normal = 0.5 * (1.0 + lax.erf(values * math.sqrt(0.5)))
    return normal + values * jnp.exp(-0.5 * values * values) * (1.0 / math.sqrt(2.0 * math.pi))


def matmul(left, right):
    return jnp.dot(left, right, preferred_element_type=full)


def matmul_nt(left, right):
    return lax.dot_general(left, right, (((1,), (1,)), ((), ())), preferred_element_type=full)


def matmul_tn(left, right):
    return lax.dot_general(left, right, (((0,), (0,)), ((), ())), preferred_element_type=full)


def attend_forward(query_heads, key_heads, value_heads, allowed, score_scale):
    scores = jnp.einsum("qhd,khd->hqk", query_heads, key_heads, preferred_element_type=full)
    scores = jnp.where(allowed, scores * score_scale, -1e30)
    row_max = jnp.max(scores, axis=-1, keepdims=True)
    exponent = jnp.exp(scores - row_max)
    row_total = jnp.sum(exponent, axis=-1, keepdims=True)
    weights_low = (exponent / row_total).astype(low)
    attended = jnp.einsum("hqk,khd->qhd", weights_low, value_heads, preferred_element_type=full)
    return attended, row_max + jnp.log(row_total)


def attend_backward(
    query_heads, key_heads, value_heads, allowed, score_scale, log_total, grad_heads
):
    scores = jnp.einsum("qhd,khd->hqk", query_heads, key_heads, preferred_element_type=full)
    scores = jnp.where(allowed, scores * score_scale, -1e30)
    weights_full = jnp.exp(scores - log_total)
    weights_low = weights_full.astype(low)
    grad_value = jnp.einsum("hqk,qhd->khd", weights_low, grad_heads, preferred_element_type=full)
    grad_weights = jnp.einsum(
        "qhd,khd->hqk", grad_heads, value_heads, preferred_element_type=full
    )
    row_inner = jnp.sum(weights_full * grad_weights, axis=-1, keepdims=True)
    grad_scores = (weights_full * (grad_weights - row_inner)).astype(low)
    grad_query = (
        jnp.einsum("hqk,khd->qhd", grad_scores, key_heads, preferred_element_type=full)
        * score_scale
    )
    grad_key = (
        jnp.einsum("hqk,qhd->khd", grad_scores, query_heads, preferred_element_type=full)
        * score_scale
    )
    return grad_query, grad_key, grad_value


def per_device(
    latents,
    media,
    segment_ids,
    slot_map,
    gains,
    w_query,
    w_key,
    w_value,
    w_out,
    w_up,
    w_down,
    cotangent,
):
    dp = ("pair", "core")
    everywhere = ("section",) + dp
    section = lax.axis_index("section")
    section_count = lax.axis_size("section")
    dp_index = lax.axis_index(dp)
    dp_count = lax.axis_size("pair") * lax.axis_size("core")
    on_first = section // 2 == 0
    stride = dp_count // 2
    row_first = dp_index // stride == 0
    seq_rows = segment_ids.shape[1]
    slot_count = slot_map.shape[1]
    feature_width = latents.shape[1]
    latent_rows = latents.shape[0]
    slot_rows = latent_rows // section_count
    inner = w_query.shape[2] // 2
    heads = inner // HEAD_DIM
    score_scale = 1.0 / math.sqrt(HEAD_DIM)

    def pick(first, second):
        return jnp.where(on_first, first, second), jnp.where(on_first, second, first)

    def swapped(value, mask):
        pairs = [(source, source ^ mask) for source in range(section_count)]
        return lax.ppermute(value, "section", pairs)

    def other_core(value):
        return lax.ppermute(value, "core", [(0, 1), (1, 0)])

    def to_second(value):
        return lax.ppermute(value, "section", [(0, 2), (1, 3)])

    def to_first(value):
        return lax.ppermute(value, "section", [(2, 0), (3, 1)])

    def after(value, earlier):
        return lax.optimization_barrier((value, earlier))[0]

    def turn_pairs(flip, back):
        pairs = []
        for source in range(section_count):
            for index in range(dp_count):
                layer, half = divmod(source, 2)
                bit, lowest = divmod(index, stride)
                moved = (layer ^ flip) * stride + lowest
                target = (bit * 2 + half) * dp_count + moved
                pair = (source * dp_count + index, target)
                pairs.append(pair[::-1] if back else pair)
        return pairs

    def exchange_rows(weight):
        half = weight.shape[0] // 2
        near, far = pick(weight[:half], weight[half:])
        first = lax.ppermute(near, everywhere, turn_pairs(0, False))
        second = lax.ppermute(far, everywhere, turn_pairs(1, False))
        return (
            jnp.where(row_first, first, second),
            jnp.where(row_first, second, first),
        )

    def join_rows(first, second):
        near = jnp.where(row_first, first, second)
        far = jnp.where(row_first, second, first)
        near = lax.ppermute(near, everywhere, turn_pairs(0, True))
        far = lax.ppermute(far, everywhere, turn_pairs(1, True))
        return jnp.concatenate(pick(near, far), axis=0).astype(full)

    def fold(piece):
        blocks = [piece[:, i * inner : (i + 1) * inner] for i in range(feature_width // inner)]
        return jnp.concatenate(blocks, axis=0)

    def unfold(stacked):
        count = feature_width // inner
        blocks = stacked.reshape(2, stride, count, -1, inner).transpose(1, 0, 3, 2, 4)
        return blocks.reshape(-1, feature_width)

    def by_device(grad):
        blocks = grad.reshape(stride, 2, -1, feature_width).transpose(1, 0, 2, 3)
        return blocks.reshape(-1, feature_width)

    def sum_to_slots(partial):
        blocks = partial.astype(low).reshape(section_count, -1, feature_width)
        arrived = lax.all_to_all(blocks, "section", split_axis=0, concat_axis=0)
        return jnp.sum(arrived.astype(full), axis=0)

    def from_slots(rows):
        return lax.all_gather(rows, "section", axis=0, tiled=True)

    def to_columns(rows):
        moved = lax.all_to_all(
            rows.astype(low), "section", split_axis=1, concat_axis=0, tiled=True
        )
        return moved.astype(full)

    def from_sequences(rows):
        near = lax.all_gather(rows, "pair", axis=0, tiled=True)
        return jnp.concatenate([near, other_core(near)], axis=0)

    def sum_to_sequence(left, right, product):
        half = left.shape[0] // 2
        far = product(left[half:], right).astype(low)
        near = product(left[:half], right) + other_core(far).astype(full)
        blocks = near.astype(low).reshape(-1, slot_rows, feature_width)
        arrived = lax.all_to_all(blocks, "pair", split_axis=0, concat_axis=0)
        return jnp.sum(arrived.astype(full), axis=0)

    def by_distance(rows, gate=None):
        half = rows.shape[0] // 2
        side = swapped(rows, 1)
        ahead = swapped(rows, 2)
        if gate is not None:
            side, ahead = after((side, ahead), gate)
        upper = swapped(side[:half], 2)
        lower = swapped(ahead[half:], 1)
        return rows, side, ahead, jnp.concatenate([upper, lower], axis=0)

    def sum_by_distance(own, side, ahead, across, gate=None):
        half = own.shape[0] // 2
        across = across.astype(low)
        upper = swapped(across[:half], 2)
        lower = swapped(across[half:], 1)
        if gate is not None:
            upper, lower = after((upper, lower), gate)
        side = jnp.concatenate([side[:half] + upper.astype(full), side[half:]], axis=0)
        ahead = jnp.concatenate([ahead[:half], ahead[half:] + lower.astype(full)], axis=0)
        side, ahead = side.astype(low), ahead.astype(low)
        return own + swapped(side, 1).astype(full) + swapped(ahead, 2).astype(full)

    def share_first(lower, upper):
        return jnp.where(on_first, lower, to_second(upper))

    def sum_over_sections(partial):
        blocks = partial.reshape(section_count, -1, feature_width)
        return sum_by_distance(
            *[
                lax.dynamic_index_in_dim(blocks, section ^ mask, 0, keepdims=False)
                for mask in range(4)
            ]
        )

    def gather_sections(rows, gate):
        by_mask = by_distance(rows, gate)
        ordered = []
        for target in range(section_count):
            chosen = by_mask[0]
            for mask in range(1, section_count):
                chosen = jnp.where(section ^ mask == target, by_mask[mask], chosen)
            ordered.append(chosen)
        return jnp.concatenate(ordered, axis=0)

    def column_parts(weight, block):
        rows, width = weight.shape
        split = weight.reshape(rows, width // (2 * block), 2, block)
        return split[:, :, 0].reshape(rows, -1), split[:, :, 1].reshape(rows, -1)

    def interleave(even, odd, block):
        rows, width = even.shape
        parts = [part.reshape(rows, width // block, 1, block) for part in (even, odd)]
        return jnp.concatenate(parts, axis=2).reshape(rows, 2 * width)

    halves = [pick(weight[0, :, :inner], weight[0, :, inner:]) for weight in (w_query, w_key, w_value)]
    own_heads = jnp.concatenate([half[0] for half in halves], axis=1)
    other_heads = swapped(jnp.concatenate([half[1] for half in halves], axis=1), 2)
    qkv_pieces = pick(own_heads, other_heads)
    half_hidden = w_down.shape[1] // 2
    half_depth = w_up.shape[1] // 2
    up_share = share_first(w_up[0, :half_depth], w_up[0, half_depth:])
    all_gains = after(gains, (other_heads, up_share))
    for axis in ("core", "pair", "section"):
        all_gains = lax.all_gather(all_gains, axis, axis=2, tiled=True)
    out_pieces = exchange_rows(after(w_out[0], other_heads))

    def gather(piece):
        return lax.all_gather(piece, dp, axis=0, tiled=True)

    stacked = [
        gather(jnp.concatenate([qkv_pieces[layer], fold(out_pieces[layer])], axis=1))
        for layer in range(LAYERS)
    ]
    qkv_w = [weight[:, : 3 * inner] for weight in stacked]
    out_w = [unfold(weight[:, 3 * inner :]) for weight in stacked]

    up_turned = lax.all_to_all(up_share, dp, split_axis=1, concat_axis=0, tiled=True)
    down_share = share_first(
        *after((w_down[0, :half_hidden], w_down[0, half_hidden:]), other_heads)
    )

    def by_depth(rows):
        return rows.reshape(-1, dp_count, 2, half_depth).swapaxes(1, 2).reshape(rows.shape)

    def in_depth(rows):
        return rows.reshape(-1, 2, dp_count, half_depth).swapaxes(1, 2).reshape(rows.shape)

    def first_ffn(gate):
        down, up = after((down_share, up_turned), gate)
        down, up = by_distance(down), by_distance(up)
        return (
            jnp.concatenate(
                [
                    jnp.concatenate(pick(up[0], up[2]), axis=0),
                    jnp.concatenate(pick(up[1], up[3]), axis=0),
                ],
                axis=1,
            ),
            jnp.concatenate(pick(down[0], down[2]) + pick(down[1], down[3]), axis=0),
        )

    down_late = after(w_down[0], all_gains)
    down_second = gather(
        jnp.where(on_first, to_first(down_late[:half_hidden]), down_late[half_hidden:])
    )

    def second_ffn(gate):
        up_even, up_odd = column_parts(after(w_up[0], gate), half_hidden)
        return gather(jnp.where(on_first, to_first(up_even), up_odd)), down_second

    up_w = [None, None]
    down_w = [None, None]
    query_w = [weight[:, :inner] for weight in qkv_w]
    key_w = [weight[:, inner : 2 * inner] for weight in qkv_w]
    value_w = [weight[:, 2 * inner :] for weight in qkv_w]

    image_hot = segment_ids[:, :, None] == jnp.arange(slot_count, dtype=jnp.int32)[None, None, :]
    media_slot = jnp.sum(jnp.where(image_hot, slot_map[:, None, :], 0), axis=2) - (
        segment_ids < 0
    ).astype(jnp.int32)
    media_unit, media_inverse = unit_rows(media.astype(full))
    latent_slot = jnp.arange(latent_rows, dtype=jnp.int32) // LATENTS
    key_slot = jnp.concatenate([media_slot[0], latent_slot])
    allowed = latent_slot[None, :, None] == key_slot[None, None, :]

    def split_heads(rows):
        return rows.reshape(rows.shape[0], heads, HEAD_DIM)

    media_low = []
    media_key = []
    media_value = []
    for layer in range(LAYERS):
        media_low.append((media_unit * all_gains[layer, 0]).astype(low))
        media_key.append(matmul(media_low[layer], key_w[layer]).astype(low))
        media_value.append(matmul(media_low[layer], value_w[layer]).astype(low))

    saved = []
    current = lax.dynamic_slice_in_dim(latents, section * slot_rows, slot_rows, 0).astype(full)
    grad_rows = lax.dynamic_slice_in_dim(cotangent, section * slot_rows, slot_rows, 0).astype(full)
    grad_low = cotangent
    for layer in range(LAYERS):
        unit_in, inverse_in = unit_rows(current)
        if layer == 0:
            whole_unit = unit_rows(latents.astype(full))[0]
            latent_low = (whole_unit * all_gains[layer, 1]).astype(low)
        else:
            latent_low = from_slots((unit_in * all_gains[layer, 1]).astype(low))
        projected = matmul(latent_low, qkv_w[layer]).astype(low)
        if layer == 0:
            up_w[0], down_w[0] = lax.optimization_barrier(first_ffn(projected))
            up_w[1], down_w[1] = second_ffn(projected)
        query_low = projected[:, :inner]
        key_heads = split_heads(
            jnp.concatenate([media_key[layer], projected[:, inner : 2 * inner]], axis=0)
        )
        value_heads = split_heads(
            jnp.concatenate([media_value[layer], projected[:, 2 * inner :]], axis=0)
        )
        query_heads = split_heads(query_low)
        attended, log_total = attend_forward(
            query_heads, key_heads, value_heads, allowed, score_scale
        )
        attended_low = attended.reshape(-1, inner).astype(low)
        middle = current + sum_to_slots(matmul(attended_low, out_w[layer]))
        unit_mid, inverse_mid = unit_rows(middle)
        ffn_low = (unit_mid * all_gains[layer, 2]).astype(low)
        ffn_low = from_slots(ffn_low) if layer else from_sequences(by_depth(ffn_low))
        hidden_pre = matmul(ffn_low, up_w[layer])
        active_low = gelu_exact(hidden_pre).astype(low)
        if layer == 0:
            current = middle + sum_to_sequence(active_low, down_w[layer], matmul)
        saved.append(
            (
                unit_in,
                inverse_in,
                latent_low,
                query_heads,
                key_heads,
                value_heads,
                log_total,
                attended_low,
                unit_mid,
                inverse_mid,
                ffn_low,
                hidden_pre,
                active_low,
            )
        )

    def scatter(blocks):
        return lax.psum_scatter(blocks, dp, scatter_dimension=0, tiled=True)

    gain_rows = [None] * LAYERS
    media_parts = []
    media_gains = []

    def add_media(layer, grad_key, grad_value, gate):
        grad_key, grad_value = after((grad_key[:seq_rows], grad_value[:seq_rows]), gate)
        part = matmul_nt(grad_key, key_w[layer]) + matmul_nt(grad_value, value_w[layer])
        media_gains.append(jnp.sum(part * media_unit, axis=0))
        media_parts.append((part * all_gains[layer, 0]).astype(low if layer else full))

    pieces = [None] * LAYERS
    for layer in (1, 0):
        (
            unit_in,
            inverse_in,
            latent_low,
            query_heads,
            key_heads,
            value_heads,
            log_total,
            attended_low,
            unit_mid,
            inverse_mid,
            ffn_low,
            hidden_pre,
            active_low,
        ) = saved[layer]
        grad_active = matmul_nt(grad_low, down_w[layer])
        grad_hidden = (grad_active * gelu_slope(hidden_pre)).astype(low)
        if layer == 0:
            add_media(1, *media_grads, grad_hidden)
        down_grad = matmul_tn(active_low, grad_low)
        if layer:
            down_grad = down_grad.astype(low)
            grad_hidden = after(grad_hidden, down_grad)
        up_grad = matmul_tn(ffn_low, grad_hidden)
        if layer:
            ffn_pieces = (scatter(down_grad), scatter(up_grad.astype(low)))
            ffn_grad = sum_to_slots(matmul_nt(grad_hidden, up_w[layer]))
        else:
            ffn_grad = in_depth(sum_to_sequence(grad_hidden, up_w[layer], matmul_nt))
            blocks = down_grad.reshape(2, 2, half_hidden, feature_width)
            own, ahead = pick(blocks[0, 0], blocks[0, 1])
            side, across = pick(blocks[1, 0], blocks[1, 1])
            down_blocks = (own, side, ahead, across)
            width = up_grad.shape[1] // 2
            blocks = up_grad.reshape(2, -1, 2 * width)
            own, ahead = pick(blocks[0][:, :width], blocks[1][:, :width])
            side, across = pick(blocks[0][:, width:], blocks[1][:, width:])
            up_blocks = (own, side, ahead, across)
        gain_ffn_grad = jnp.sum(ffn_grad * unit_mid, axis=0)
        grad_middle = grad_rows + norm_back(
            unit_mid, inverse_mid, ffn_grad * all_gains[layer, 2]
        )
        middle_low = from_slots(grad_middle.astype(low))
        if layer == 0:
            up_half = sum_by_distance(*up_blocks, middle_low).astype(low)
            down_half = sum_by_distance(*down_blocks, middle_low).astype(low)
        grad_heads = split_heads(matmul_nt(middle_low, out_w[layer]).astype(low))
        out_grad = by_device(matmul_tn(attended_low, middle_low)).astype(low)
        out_piece = scatter(out_grad)
        grad_heads = after(grad_heads, out_grad)
        grad_query, grad_key, grad_value = attend_backward(
            query_heads, key_heads, value_heads, allowed, score_scale, log_total, grad_heads
        )
        grad_query = grad_query.reshape(-1, inner).astype(low)
        grad_key = grad_key.reshape(-1, inner).astype(low)
        grad_value = grad_value.reshape(-1, inner).astype(low)
        latent_part = (
            matmul_nt(grad_query, query_w[layer])
            + matmul_nt(grad_key[seq_rows:], key_w[layer])
            + matmul_nt(grad_value[seq_rows:], value_w[layer])
        )
        latent_grad_rows = sum_to_slots(latent_part)
        gain_latent_grad = jnp.sum(latent_grad_rows * unit_in, axis=0)
        grad_rows = grad_middle + norm_back(
            unit_in, inverse_in, latent_grad_rows * all_gains[layer, 1]
        )
        both_low = jnp.concatenate([media_low[layer], latent_low], axis=0)
        all_grads = jnp.concatenate(
            [jnp.pad(grad_query, ((seq_rows, 0), (0, 0))), grad_key, grad_value], axis=1
        )
        qkv_grad = matmul_tn(both_low, all_grads).astype(low)
        pieces[layer] = (scatter(qkv_grad), out_piece)
        if layer > 0:
            grad_low = from_sequences(grad_rows.astype(low))
            late = after(active_low, latent_part)
            here = (latent_slot == section)[:, None]
            kept = jnp.where(here, jnp.tile(middle, (section_count, 1)), 0.0)
            width = feature_width // section_count
            last = []
            for i in range(section_count):
                cut = slice(i * width, (i + 1) * width)
                last.append((matmul(late, down_w[layer][:, cut]) + kept[:, cut]).astype(low))
            last = lax.all_to_all(jnp.stack(last), "section", split_axis=0, concat_axis=0)
            latents_out = jnp.sum(last.astype(full), axis=0)
            grad_low = after(grad_low, latents_out)
            grad_low = after(grad_low, ffn_pieces)
        if layer == 0:
            add_media(0, grad_key, grad_value, qkv_grad)
        else:
            media_grads = (grad_key, grad_value)
        gain_rows[layer] = (gain_latent_grad, gain_ffn_grad)
    media_rows = seq_rows // section_count
    media_total = media_parts[0].astype(full) + media_parts[1]
    up_half = lax.all_to_all(
        after(up_half, media_total), dp, split_axis=0, concat_axis=1, tiled=True
    )
    media_sum = sum_over_sections(media_total)
    own_unit = lax.dynamic_slice_in_dim(media_unit, section * media_rows, media_rows, 0)
    own_inverse = lax.dynamic_slice_in_dim(media_inverse, section * media_rows, media_rows, 0)
    media_grad = norm_back(own_unit, own_inverse, media_sum).astype(low)

    qkv_parts = [piece[0] for piece in pieces]
    own, other = pick(qkv_parts[0], qkv_parts[1])
    lower, upper = pick(own, swapped(other, 2))
    out_grad = join_rows(*[piece[1] for piece in pieces])
    media_grad = gather_sections(after(media_grad, out_grad), lower).astype(full)
    qkv_grads = [
        jnp.concatenate(
            [lower[:, i * inner : (i + 1) * inner], upper[:, i * inner : (i + 1) * inner]], axis=1
        ).astype(full)
        for i in range(3)
    ]
    latent_grad = to_columns(after(grad_rows, media_sum))
    gain_rows = [
        jnp.stack([media_gains[1 - layer], *gain_rows[layer]]) for layer in range(LAYERS)
    ]
    gain_parts = after(jnp.stack(gain_rows), media_sum).reshape(LAYERS, 3, section_count, -1)
    gain_parts = jnp.sum(
        lax.all_to_all(gain_parts, "section", split_axis=2, concat_axis=2), axis=2
    )
    gain_parts = gain_parts.reshape(LAYERS, 3, dp_count, -1)
    gain_grad = jnp.sum(lax.all_to_all(gain_parts, dp, split_axis=2, concat_axis=2), axis=2)

    down_piece, up_piece = ffn_pieces
    up_second_grad = interleave(to_second(up_piece), up_piece, half_hidden)
    down_second_grad = jnp.concatenate([to_second(down_piece), down_piece], axis=0)
    up_first_grad = jnp.concatenate([up_half, to_first(up_half)], axis=0)
    down_first_grad = jnp.concatenate([down_half, to_first(down_half)], axis=0)
    up_grad = jnp.where(on_first, up_first_grad, up_second_grad).astype(full)
    down_grad = jnp.where(on_first, down_first_grad, down_second_grad).astype(full)
    return (
        latents_out,
        latent_grad,
        media_grad,
        gain_grad,
        qkv_grads[0][None],
        qkv_grads[1][None],
        qkv_grads[2][None],
        out_grad[None],
        up_grad[None],
        down_grad[None],
    )


def solution(mesh):
    section_count, dp_count = mesh.devices.shape
    fine = Mesh(
        mesh.devices.reshape(section_count, dp_count // 2, 2), ("section", "pair", "core")
    )
    dp = ("pair", "core")
    placed = (
        P(dp, None),
        P(dp, None),
        P(dp, None),
        P(dp, None),
        P(None, None, ("section",) + dp),
        P("section", dp, None),
        P("section", dp, None),
        P("section", dp, None),
        P("section", dp, None),
        P("section", dp, None),
        P("section", dp, None),
        P(dp, None),
    )
    return jax.shard_map(
        per_device,
        mesh=fine,
        in_specs=placed,
        out_specs=(
            P(dp, "section"),
            P(dp, "section"),
            P(dp, None),
            P(None, None, ("section",) + dp),
            P("section", dp, None),
            P("section", dp, None),
            P("section", dp, None),
            P("section", dp, None),
            P("section", dp, None),
            P("section", dp, None),
        ),
        check_vma=False,
    )
```

```python
import math

import jax
import jax.numpy as jnp
from jax import lax
from jax.sharding import Mesh, PartitionSpec as P

HEAD_DIM = 96
LATENTS = 64
LAYERS = 2

epsilon = 1e-05
low = jnp.bfloat16
full = jnp.float32


def unit_rows(values):
    centered = values - jnp.mean(values, axis=-1, keepdims=True)
    variance = jnp.mean(centered * centered, axis=-1, keepdims=True)
    inverse = lax.rsqrt(variance + epsilon)
    return centered * inverse, inverse


def norm_back(unit, inverse, scaled):
    first = jnp.mean(scaled, axis=-1, keepdims=True)
    second = jnp.mean(scaled * unit, axis=-1, keepdims=True)
    return (scaled - first - unit * second) * inverse


def gelu_exact(values):
    return 0.5 * values * (1.0 + lax.erf(values * math.sqrt(0.5)))


def gelu_slope(values):
    normal = 0.5 * (1.0 + lax.erf(values * math.sqrt(0.5)))
    return normal + values * jnp.exp(-0.5 * values * values) * (1.0 / math.sqrt(2.0 * math.pi))


def matmul(left, right):
    return jnp.dot(left, right, preferred_element_type=full)


def matmul_nt(left, right):
    return lax.dot_general(left, right, (((1,), (1,)), ((), ())), preferred_element_type=full)


def matmul_tn(left, right):
    return lax.dot_general(left, right, (((0,), (0,)), ((), ())), preferred_element_type=full)


def attend_forward(query_heads, key_heads, value_heads, allowed, score_scale):
    scores = jnp.einsum("qhd,khd->hqk", query_heads, key_heads, preferred_element_type=full)
    scores = jnp.where(allowed, scores * score_scale, -1e30)
    row_max = jnp.max(scores, axis=-1, keepdims=True)
    exponent = jnp.exp(scores - row_max)
    row_total = jnp.sum(exponent, axis=-1, keepdims=True)
    weights_low = (exponent / row_total).astype(low)
    attended = jnp.einsum("hqk,khd->qhd", weights_low, value_heads, preferred_element_type=full)
    return attended, row_max + jnp.log(row_total)


def attend_backward(
    query_heads, key_heads, value_heads, allowed, score_scale, log_total, grad_heads
):
    scores = jnp.einsum("qhd,khd->hqk", query_heads, key_heads, preferred_element_type=full)
    scores = jnp.where(allowed, scores * score_scale, -1e30)
    weights_full = jnp.exp(scores - log_total)
    weights_low = weights_full.astype(low)
    grad_value = jnp.einsum("hqk,qhd->khd", weights_low, grad_heads, preferred_element_type=full)
    grad_weights = jnp.einsum(
        "qhd,khd->hqk", grad_heads, value_heads, preferred_element_type=full
    )
    row_inner = jnp.sum(weights_full * grad_weights, axis=-1, keepdims=True)
    grad_scores = (weights_full * (grad_weights - row_inner)).astype(low)
    grad_query = (
        jnp.einsum("hqk,khd->qhd", grad_scores, key_heads, preferred_element_type=full)
        * score_scale
    )
    grad_key = (
        jnp.einsum("hqk,qhd->khd", grad_scores, query_heads, preferred_element_type=full)
        * score_scale
    )
    return grad_query, grad_key, grad_value


def per_device(
    latents,
    media,
    segment_ids,
    slot_map,
    gains,
    w_query,
    w_key,
    w_value,
    w_out,
    w_up,
    w_down,
    cotangent,
):
    dp = ("pair", "core")
    everywhere = ("section",) + dp
    section = lax.axis_index("section")
    section_count = lax.axis_size("section")
    dp_index = lax.axis_index(dp)
    dp_count = lax.axis_size("pair") * lax.axis_size("core")
    on_first = section // 2 == 0
    stride = dp_count // 2
    row_first = dp_index // stride == 0
    seq_rows = segment_ids.shape[1]
    slot_count = slot_map.shape[1]
    feature_width = latents.shape[1]
    latent_rows = latents.shape[0]
    slot_rows = latent_rows // section_count
    inner = w_query.shape[2] // 2
    heads = inner // HEAD_DIM
    score_scale = 1.0 / math.sqrt(HEAD_DIM)

    def pick(first, second):
        return jnp.where(on_first, first, second), jnp.where(on_first, second, first)

    def swapped(value, mask):
        pairs = [(source, source ^ mask) for source in range(section_count)]
        return lax.ppermute(value, "section", pairs)

    def other_core(value):
        return lax.ppermute(value, "core", [(0, 1), (1, 0)])

    def to_second(value):
        return lax.ppermute(value, "section", [(0, 2), (1, 3)])

    def to_first(value):
        return lax.ppermute(value, "section", [(2, 0), (3, 1)])

    def after(value, earlier):
        return lax.optimization_barrier((value, earlier))[0]

    def turn_pairs(flip, back):
        pairs = []
        for source in range(section_count):
            for index in range(dp_count):
                layer, half = divmod(source, 2)
                bit, lowest = divmod(index, stride)
                moved = (layer ^ flip) * stride + lowest
                target = (bit * 2 + half) * dp_count + moved
                pair = (source * dp_count + index, target)
                pairs.append(pair[::-1] if back else pair)
        return pairs

    def exchange_rows(weight):
        half = weight.shape[0] // 2
        near, far = pick(weight[:half], weight[half:])
        first = lax.ppermute(near, everywhere, turn_pairs(0, False))
        second = lax.ppermute(far, everywhere, turn_pairs(1, False))
        return (
            jnp.where(row_first, first, second),
            jnp.where(row_first, second, first),
        )

    def join_rows(first, second):
        near = jnp.where(row_first, first, second)
        far = jnp.where(row_first, second, first)
        near = lax.ppermute(near, everywhere, turn_pairs(0, True))
        far = lax.ppermute(far, everywhere, turn_pairs(1, True))
        return jnp.concatenate(pick(near, far), axis=0).astype(full)

    def fold(piece):
        blocks = [piece[:, i * inner : (i + 1) * inner] for i in range(feature_width // inner)]
        return jnp.concatenate(blocks, axis=0)

    def unfold(stacked):
        count = feature_width // inner
        blocks = stacked.reshape(2, stride, count, -1, inner).transpose(1, 0, 3, 2, 4)
        return blocks.reshape(-1, feature_width)

    def by_device(grad):
        blocks = grad.reshape(stride, 2, -1, feature_width).transpose(1, 0, 2, 3)
        return blocks.reshape(-1, feature_width)

    def sum_to_slots(partial):
        blocks = partial.astype(low).reshape(section_count, -1, feature_width)
        arrived = lax.all_to_all(blocks, "section", split_axis=0, concat_axis=0)
        return jnp.sum(arrived.astype(full), axis=0)

    def from_slots(rows):
        return lax.all_gather(rows, "section", axis=0, tiled=True)

    def to_columns(rows):
        moved = lax.all_to_all(
            rows.astype(low), "section", split_axis=1, concat_axis=0, tiled=True
        )
        return moved.astype(full)

    def from_sequences(rows):
        near = lax.all_gather(rows, "pair", axis=0, tiled=True)
        return jnp.concatenate([near, other_core(near)], axis=0)

    def sum_to_sequence(left, right, product):
        half = left.shape[0] // 2
        far = product(left[half:], right).astype(low)
        near = product(left[:half], right) + other_core(far).astype(full)
        blocks = near.astype(low).reshape(-1, slot_rows, feature_width)
        arrived = lax.all_to_all(blocks, "pair", split_axis=0, concat_axis=0)
        return jnp.sum(arrived.astype(full), axis=0)

    def by_distance(rows):
        half = rows.shape[0] // 2
        side = swapped(rows, 1)
        ahead = swapped(rows, 2)
        upper = swapped(side[:half], 2)
        lower = swapped(ahead[half:], 1)
        return rows, side, ahead, jnp.concatenate([upper, lower], axis=0)

    def sum_by_distance(own, side, ahead, across, gate=None):
        half = own.shape[0] // 2
        across = across.astype(low)
        upper = swapped(across[:half], 2)
        lower = swapped(across[half:], 1)
        if gate is not None:
            upper, lower = after((upper, lower), gate)
        side = jnp.concatenate([side[:half] + upper.astype(full), side[half:]], axis=0)
        ahead = jnp.concatenate([ahead[:half], ahead[half:] + lower.astype(full)], axis=0)
        side, ahead = side.astype(low), ahead.astype(low)
        return own + swapped(side, 1).astype(full) + swapped(ahead, 2).astype(full)

    def share_first(lower, upper):
        return jnp.where(on_first, lower, to_second(upper))

    def sum_over_sections(partial):
        blocks = partial.reshape(section_count, -1, feature_width)
        return sum_by_distance(
            *[
                lax.dynamic_index_in_dim(blocks, section ^ mask, 0, keepdims=False)
                for mask in range(4)
            ]
        )

    def gather_sections(rows):
        by_mask = by_distance(rows)
        ordered = []
        for target in range(section_count):
            chosen = by_mask[0]
            for mask in range(1, section_count):
                chosen = jnp.where(section ^ mask == target, by_mask[mask], chosen)
            ordered.append(chosen)
        return jnp.concatenate(ordered, axis=0)

    def column_parts(weight, block):
        rows, width = weight.shape
        split = weight.reshape(rows, width // (2 * block), 2, block)
        return split[:, :, 0].reshape(rows, -1), split[:, :, 1].reshape(rows, -1)

    def interleave(even, odd, block):
        rows, width = even.shape
        parts = [part.reshape(rows, width // block, 1, block) for part in (even, odd)]
        return jnp.concatenate(parts, axis=2).reshape(rows, 2 * width)

    halves = [pick(weight[0, :, :inner], weight[0, :, inner:]) for weight in (w_query, w_key, w_value)]
    own_heads = jnp.concatenate([half[0] for half in halves], axis=1)
    other_heads = swapped(jnp.concatenate([half[1] for half in halves], axis=1), 2)
    qkv_pieces = pick(own_heads, other_heads)
    half_hidden = w_down.shape[1] // 2
    all_gains = after(gains, other_heads)
    for axis in ("core", "pair", "section"):
        all_gains = lax.all_gather(all_gains, axis, axis=2, tiled=True)
    out_pieces = exchange_rows(after(w_out[0], other_heads))

    def gather(piece):
        return lax.all_gather(piece, dp, axis=0, tiled=True)

    stacked = [
        gather(jnp.concatenate([qkv_pieces[layer], fold(out_pieces[layer])], axis=1))
        for layer in range(LAYERS)
    ]
    qkv_w = [weight[:, : 3 * inner] for weight in stacked]
    out_w = [unfold(weight[:, 3 * inner :]) for weight in stacked]

    def share_first(shard):
        return jnp.where(on_first, shard, to_second(shard))

    up_turned = lax.all_to_all(w_up[0], dp, split_axis=1, concat_axis=0, tiled=True)
    up_own = share_first(up_turned)
    down_own = share_first(after(w_down[0], other_heads))
    down_other = swapped(after(down_own, all_gains), 1)

    def first_ffn(gate):
        up_other = swapped(after(up_own, gate), 1)
        return lax.optimization_barrier(
            (
                jnp.concatenate([up_own, up_other], axis=1),
                jnp.concatenate([down_own, down_other], axis=0),
            )
        )

    down_late = after(w_down[0], all_gains)
    down_second = gather(
        jnp.where(on_first, to_first(down_late[:half_hidden]), down_late[half_hidden:])
    )

    def second_ffn(gate):
        up_even, up_odd = column_parts(after(w_up[0], gate), half_hidden)
        return gather(jnp.where(on_first, to_first(up_even), up_odd)), down_second

    up_w = [None, None]
    down_w = [None, None]
    query_w = [weight[:, :inner] for weight in qkv_w]
    key_w = [weight[:, inner : 2 * inner] for weight in qkv_w]
    value_w = [weight[:, 2 * inner :] for weight in qkv_w]

    image_hot = segment_ids[:, :, None] == jnp.arange(slot_count, dtype=jnp.int32)[None, None, :]
    media_slot = jnp.sum(jnp.where(image_hot, slot_map[:, None, :], 0), axis=2) - (
        segment_ids < 0
    ).astype(jnp.int32)
    media_unit, media_inverse = unit_rows(media.astype(full))
    latent_slot = jnp.arange(latent_rows, dtype=jnp.int32) // LATENTS
    key_slot = jnp.concatenate([media_slot[0], latent_slot])
    allowed = latent_slot[None, :, None] == key_slot[None, None, :]

    def split_heads(rows):
        return rows.reshape(rows.shape[0], heads, HEAD_DIM)

    media_low = []
    media_key = []
    media_value = []
    for layer in range(LAYERS):
        media_low.append((media_unit * all_gains[layer, 0]).astype(low))
        media_key.append(matmul(media_low[layer], key_w[layer]).astype(low))
        media_value.append(matmul(media_low[layer], value_w[layer]).astype(low))

    saved = []
    current = lax.dynamic_slice_in_dim(latents, section * slot_rows, slot_rows, 0).astype(full)
    grad_rows = lax.dynamic_slice_in_dim(cotangent, section * slot_rows, slot_rows, 0).astype(full)
    grad_low = cotangent
    for layer in range(LAYERS):
        unit_in, inverse_in = unit_rows(current)
        if layer == 0:
            whole_unit = unit_rows(latents.astype(full))[0]
            latent_low = (whole_unit * all_gains[layer, 1]).astype(low)
        else:
            latent_low = from_slots((unit_in * all_gains[layer, 1]).astype(low))
        projected = matmul(latent_low, qkv_w[layer]).astype(low)
        if layer == 0:
            up_w[0], down_w[0] = first_ffn(projected)
            up_w[1], down_w[1] = second_ffn(projected)
        query_low = projected[:, :inner]
        key_heads = split_heads(
            jnp.concatenate([media_key[layer], projected[:, inner : 2 * inner]], axis=0)
        )
        value_heads = split_heads(
            jnp.concatenate([media_value[layer], projected[:, 2 * inner :]], axis=0)
        )
        query_heads = split_heads(query_low)
        attended, log_total = attend_forward(
            query_heads, key_heads, value_heads, allowed, score_scale
        )
        attended_low = attended.reshape(-1, inner).astype(low)
        middle = current + sum_to_slots(matmul(attended_low, out_w[layer]))
        unit_mid, inverse_mid = unit_rows(middle)
        ffn_low = (unit_mid * all_gains[layer, 2]).astype(low)
        ffn_low = from_slots(ffn_low) if layer else from_sequences(ffn_low)
        hidden_pre = matmul(ffn_low, up_w[layer])
        active_low = gelu_exact(hidden_pre).astype(low)
        if layer == 0:
            current = middle + sum_to_sequence(active_low, down_w[layer], matmul)
        saved.append(
            (
                unit_in,
                inverse_in,
                latent_low,
                query_heads,
                key_heads,
                value_heads,
                log_total,
                attended_low,
                unit_mid,
                inverse_mid,
                ffn_low,
                hidden_pre,
                active_low,
            )
        )

    def scatter(blocks):
        return lax.psum_scatter(blocks, dp, scatter_dimension=0, tiled=True)

    gain_rows = [None] * LAYERS
    media_parts = []
    media_gains = []

    def add_media(layer, grad_key, grad_value, gate):
        grad_key, grad_value = after((grad_key[:seq_rows], grad_value[:seq_rows]), gate)
        part = matmul_nt(grad_key, key_w[layer]) + matmul_nt(grad_value, value_w[layer])
        media_gains.append(jnp.sum(part * media_unit, axis=0))
        media_parts.append((part * all_gains[layer, 0]).astype(low if layer else full))

    pieces = [None] * LAYERS
    for layer in (1, 0):
        (
            unit_in,
            inverse_in,
            latent_low,
            query_heads,
            key_heads,
            value_heads,
            log_total,
            attended_low,
            unit_mid,
            inverse_mid,
            ffn_low,
            hidden_pre,
            active_low,
        ) = saved[layer]
        grad_active = matmul_nt(grad_low, down_w[layer])
        grad_hidden = (grad_active * gelu_slope(hidden_pre)).astype(low)
        if layer == 0:
            add_media(1, *media_grads, grad_hidden)
        down_grad = matmul_tn(active_low, grad_low)
        if layer:
            down_grad = down_grad.astype(low)
            grad_hidden = after(grad_hidden, down_grad)
        up_grad = matmul_tn(ffn_low, grad_hidden)
        if layer:
            ffn_pieces = (scatter(down_grad), scatter(up_grad.astype(low)))
            ffn_grad = sum_to_slots(matmul_nt(grad_hidden, up_w[layer]))
        else:
            ffn_grad = sum_to_sequence(grad_hidden, up_w[layer], matmul_nt)
            down_far = down_grad[down_grad.shape[0] // 2 :].astype(low)
            up_far = up_grad[:, up_grad.shape[1] // 2 :].astype(low)
            ffn_grad = after(ffn_grad, (down_far, up_far, media_parts))
            down_far, up_far = swapped(down_far, 1), swapped(up_far, 1)
        gain_ffn_grad = jnp.sum(ffn_grad * unit_mid, axis=0)
        grad_middle = grad_rows + norm_back(
            unit_mid, inverse_mid, ffn_grad * all_gains[layer, 2]
        )
        middle_low = from_slots(grad_middle.astype(low))
        if layer == 0:
            down_far, up_far = after((down_far, up_far), middle_low)
            down_half = down_grad[: down_far.shape[0]] + down_far.astype(full)
            up_half = up_grad[:, : up_far.shape[1]] + up_far.astype(full)
            down_half = down_half + to_first(down_half.astype(low)).astype(full)
            up_half = (up_half + to_first(up_half.astype(low)).astype(full)).astype(low)
        grad_heads = split_heads(matmul_nt(middle_low, out_w[layer]).astype(low))
        out_grad = by_device(matmul_tn(attended_low, middle_low)).astype(low)
        out_piece = scatter(out_grad)
        grad_heads = after(grad_heads, out_grad)
        grad_query, grad_key, grad_value = attend_backward(
            query_heads, key_heads, value_heads, allowed, score_scale, log_total, grad_heads
        )
        grad_query = grad_query.reshape(-1, inner).astype(low)
        grad_key = grad_key.reshape(-1, inner).astype(low)
        grad_value = grad_value.reshape(-1, inner).astype(low)
        both_low = jnp.concatenate([media_low[layer], latent_low], axis=0)
        all_grads = jnp.concatenate(
            [jnp.pad(grad_query, ((seq_rows, 0), (0, 0))), grad_key, grad_value], axis=1
        )
        qkv_grad = matmul_tn(both_low, all_grads).astype(low)
        latent_part = (
            matmul_nt(grad_query, query_w[layer])
            + matmul_nt(grad_key[seq_rows:], key_w[layer])
            + matmul_nt(grad_value[seq_rows:], value_w[layer])
        )
        latent_grad_rows = sum_to_slots(latent_part)
        if layer:
            latent_grad_rows = after(latent_grad_rows, qkv_grad)
        gain_latent_grad = jnp.sum(latent_grad_rows * unit_in, axis=0)
        grad_rows = grad_middle + norm_back(
            unit_in, inverse_in, latent_grad_rows * all_gains[layer, 1]
        )
        if layer == 0:
            up_half, qkv_grad = lax.optimization_barrier((up_half, qkv_grad))
            up_half = lax.all_to_all(up_half, dp, split_axis=0, concat_axis=1, tiled=True)
        pieces[layer] = (scatter(qkv_grad), out_piece)
        if layer > 0:
            grad_low = from_sequences(grad_rows.astype(low))
            late = after(active_low, latent_part)
            here = (latent_slot == section)[:, None]
            kept = jnp.where(here, jnp.tile(middle, (section_count, 1)), 0.0)
            width = feature_width // section_count
            last = []
            for i in range(section_count):
                cut = slice(i * width, (i + 1) * width)
                last.append((matmul(late, down_w[layer][:, cut]) + kept[:, cut]).astype(low))
            last = lax.all_to_all(jnp.stack(last), "section", split_axis=0, concat_axis=0)
            latents_out = jnp.sum(last.astype(full), axis=0)
            grad_low = after(grad_low, latents_out)
            grad_low = after(grad_low, ffn_pieces)
        if layer == 0:
            add_media(0, grad_key, grad_value, qkv_grad)
        else:
            media_grads = (grad_key, grad_value)
        gain_rows[layer] = (gain_latent_grad, gain_ffn_grad)
    latent_grad = to_columns(after(grad_rows, (pieces[1], up_half)))
    media_rows = seq_rows // section_count
    media_sum = sum_over_sections(media_parts[0].astype(full) + media_parts[1])
    own_unit = lax.dynamic_slice_in_dim(media_unit, section * media_rows, media_rows, 0)
    own_inverse = lax.dynamic_slice_in_dim(media_inverse, section * media_rows, media_rows, 0)
    media_grad = gather_sections(norm_back(own_unit, own_inverse, media_sum).astype(low)).astype(
        full
    )
    gain_rows = [
        jnp.stack([media_gains[1 - layer], *gain_rows[layer]]) for layer in range(LAYERS)
    ]
    gain_parts = jnp.stack(gain_rows).reshape(LAYERS, 3, section_count, -1)
    gain_parts = jnp.sum(
        lax.all_to_all(gain_parts, "section", split_axis=2, concat_axis=2), axis=2
    )
    gain_parts = gain_parts.reshape(LAYERS, 3, dp_count, -1)
    gain_grad = jnp.sum(lax.all_to_all(gain_parts, dp, split_axis=2, concat_axis=2), axis=2)

    qkv_parts = [piece[0] for piece in pieces]
    own, other = pick(qkv_parts[0], qkv_parts[1])
    lower, upper = pick(own, swapped(other, 2))
    qkv_grads = [
        jnp.concatenate(
            [lower[:, i * inner : (i + 1) * inner], upper[:, i * inner : (i + 1) * inner]], axis=1
        ).astype(full)
        for i in range(3)
    ]
    out_grad = join_rows(*[piece[1] for piece in pieces])
    down_piece, up_piece = ffn_pieces
    up_second_grad = interleave(to_second(up_piece), up_piece, half_hidden)
    down_second_grad = jnp.concatenate([to_second(down_piece), down_piece], axis=0)
    up_grad = jnp.where(on_first, up_half, up_second_grad).astype(full)
    down_grad = jnp.where(on_first, down_half, down_second_grad.astype(full))
    return (
        latents_out,
        latent_grad,
        media_grad,
        gain_grad,
        qkv_grads[0][None],
        qkv_grads[1][None],
        qkv_grads[2][None],
        out_grad[None],
        up_grad[None],
        down_grad[None],
    )


def solution(mesh):
    section_count, dp_count = mesh.devices.shape
    fine = Mesh(
        mesh.devices.reshape(section_count, dp_count // 2, 2), ("section", "pair", "core")
    )
    dp = ("pair", "core")
    placed = (
        P(dp, None),
        P(dp, None),
        P(dp, None),
        P(dp, None),
        P(None, None, ("section",) + dp),
        P("section", dp, None),
        P("section", dp, None),
        P("section", dp, None),
        P("section", dp, None),
        P("section", dp, None),
        P("section", dp, None),
        P(dp, None),
    )
    return jax.shard_map(
        per_device,
        mesh=fine,
        in_specs=placed,
        out_specs=(
            P(dp, "section"),
            P(dp, "section"),
            P(dp, None),
            P(None, None, ("section",) + dp),
            P("section", dp, None),
            P("section", dp, None),
            P("section", dp, None),
            P("section", dp, None),
            P("section", dp, None),
            P("section", dp, None),
        ),
        check_vma=False,
    )
```

```python
import math

import jax
import jax.numpy as jnp
from jax import lax
from jax.sharding import Mesh, PartitionSpec as P

HEAD_DIM = 96
LATENTS = 64
LAYERS = 2

epsilon = 1e-05
low = jnp.bfloat16
full = jnp.float32


def unit_rows(values):
    centered = values - jnp.mean(values, axis=-1, keepdims=True)
    variance = jnp.mean(centered * centered, axis=-1, keepdims=True)
    inverse = lax.rsqrt(variance + epsilon)
    return centered * inverse, inverse


def norm_back(unit, inverse, scaled):
    first = jnp.mean(scaled, axis=-1, keepdims=True)
    second = jnp.mean(scaled * unit, axis=-1, keepdims=True)
    return (scaled - first - unit * second) * inverse


def gelu_exact(values):
    return 0.5 * values * (1.0 + lax.erf(values * math.sqrt(0.5)))


def gelu_slope(values):
    normal = 0.5 * (1.0 + lax.erf(values * math.sqrt(0.5)))
    return normal + values * jnp.exp(-0.5 * values * values) * (1.0 / math.sqrt(2.0 * math.pi))


def matmul(left, right):
    return jnp.dot(left, right, preferred_element_type=full)


def matmul_nt(left, right):
    return lax.dot_general(left, right, (((1,), (1,)), ((), ())), preferred_element_type=full)


def matmul_tn(left, right):
    return lax.dot_general(left, right, (((0,), (0,)), ((), ())), preferred_element_type=full)


def attend_forward(query_heads, key_heads, value_heads, allowed, score_scale):
    scores = jnp.einsum("qhd,khd->hqk", query_heads, key_heads, preferred_element_type=full)
    scores = jnp.where(allowed, scores * score_scale, -1e30)
    row_max = jnp.max(scores, axis=-1, keepdims=True)
    exponent = jnp.exp(scores - row_max)
    row_total = jnp.sum(exponent, axis=-1, keepdims=True)
    weights_low = (exponent / row_total).astype(low)
    attended = jnp.einsum("hqk,khd->qhd", weights_low, value_heads, preferred_element_type=full)
    return attended, row_max + jnp.log(row_total)


def attend_backward(
    query_heads, key_heads, value_heads, allowed, score_scale, log_total, grad_heads
):
    scores = jnp.einsum("qhd,khd->hqk", query_heads, key_heads, preferred_element_type=full)
    scores = jnp.where(allowed, scores * score_scale, -1e30)
    weights_full = jnp.exp(scores - log_total)
    weights_low = weights_full.astype(low)
    grad_value = jnp.einsum("hqk,qhd->khd", weights_low, grad_heads, preferred_element_type=full)
    grad_weights = jnp.einsum(
        "qhd,khd->hqk", grad_heads, value_heads, preferred_element_type=full
    )
    row_inner = jnp.sum(weights_full * grad_weights, axis=-1, keepdims=True)
    grad_scores = (weights_full * (grad_weights - row_inner)).astype(low)
    grad_query = (
        jnp.einsum("hqk,khd->qhd", grad_scores, key_heads, preferred_element_type=full)
        * score_scale
    )
    grad_key = (
        jnp.einsum("hqk,qhd->khd", grad_scores, query_heads, preferred_element_type=full)
        * score_scale
    )
    return grad_query, grad_key, grad_value


def per_device(
    latents,
    media,
    segment_ids,
    slot_map,
    gains,
    w_query,
    w_key,
    w_value,
    w_out,
    w_up,
    w_down,
    cotangent,
):
    dp = ("pair", "core")
    everywhere = ("section",) + dp
    section = lax.axis_index("section")
    section_count = lax.axis_size("section")
    dp_index = lax.axis_index(dp)
    dp_count = lax.axis_size("pair") * lax.axis_size("core")
    on_first = section // 2 == 0
    stride = dp_count // 2
    row_first = dp_index // stride == 0
    seq_rows = segment_ids.shape[1]
    slot_count = slot_map.shape[1]
    feature_width = latents.shape[1]
    latent_rows = latents.shape[0]
    slot_rows = latent_rows // section_count
    inner = w_query.shape[2] // 2
    heads = inner // HEAD_DIM
    score_scale = 1.0 / math.sqrt(HEAD_DIM)

    def pick(first, second):
        return jnp.where(on_first, first, second), jnp.where(on_first, second, first)

    def swapped(value, mask):
        pairs = [(source, source ^ mask) for source in range(section_count)]
        return lax.ppermute(value, "section", pairs)

    def other_core(value):
        return lax.ppermute(value, "core", [(0, 1), (1, 0)])

    def to_second(value):
        return lax.ppermute(value, "section", [(0, 2), (1, 3)])

    def to_first(value):
        return lax.ppermute(value, "section", [(2, 0), (3, 1)])

    def after(value, earlier):
        return lax.optimization_barrier((value, earlier))[0]

    def turn_pairs(flip, back):
        pairs = []
        for source in range(section_count):
            for index in range(dp_count):
                layer, half = divmod(source, 2)
                bit, lowest = divmod(index, stride)
                moved = (layer ^ flip) * stride + lowest
                target = (bit * 2 + half) * dp_count + moved
                pair = (source * dp_count + index, target)
                pairs.append(pair[::-1] if back else pair)
        return pairs

    def exchange_rows(weight):
        half = weight.shape[0] // 2
        near, far = pick(weight[:half], weight[half:])
        first = lax.ppermute(near, everywhere, turn_pairs(0, False))
        second = lax.ppermute(far, everywhere, turn_pairs(1, False))
        return (
            jnp.where(row_first, first, second),
            jnp.where(row_first, second, first),
        )

    def join_rows(first, second):
        near = jnp.where(row_first, first, second)
        far = jnp.where(row_first, second, first)
        near = lax.ppermute(near, everywhere, turn_pairs(0, True))
        far = lax.ppermute(far, everywhere, turn_pairs(1, True))
        return jnp.concatenate(pick(near, far), axis=0).astype(full)

    def fold(piece):
        blocks = [piece[:, i * inner : (i + 1) * inner] for i in range(feature_width // inner)]
        return jnp.concatenate(blocks, axis=0)

    def unfold(stacked):
        count = feature_width // inner
        blocks = stacked.reshape(2, stride, count, -1, inner).transpose(1, 0, 3, 2, 4)
        return blocks.reshape(-1, feature_width)

    def by_device(grad):
        blocks = grad.reshape(stride, 2, -1, feature_width).transpose(1, 0, 2, 3)
        return blocks.reshape(-1, feature_width)

    def sum_to_slots(partial):
        blocks = partial.astype(low).reshape(section_count, -1, feature_width)
        arrived = lax.all_to_all(blocks, "section", split_axis=0, concat_axis=0)
        return jnp.sum(arrived.astype(full), axis=0)

    def from_slots(rows):
        return lax.all_gather(rows, "section", axis=0, tiled=True)

    def to_columns(rows):
        moved = lax.all_to_all(
            rows.astype(low), "section", split_axis=1, concat_axis=0, tiled=True
        )
        return moved.astype(full)

    def from_sequences(rows):
        near = lax.all_gather(rows, "pair", axis=0, tiled=True)
        return jnp.concatenate([near, other_core(near)], axis=0)

    def sum_to_sequence(left, right, product):
        half = left.shape[0] // 2
        far = product(left[half:], right).astype(low)
        near = product(left[:half], right) + other_core(far).astype(full)
        blocks = near.astype(low).reshape(-1, slot_rows, feature_width)
        arrived = lax.all_to_all(blocks, "pair", split_axis=0, concat_axis=0)
        return jnp.sum(arrived.astype(full), axis=0)

    def by_distance(rows):
        half = rows.shape[0] // 2
        side = swapped(rows, 1)
        ahead = swapped(rows, 2)
        upper = swapped(side[:half], 2)
        lower = swapped(ahead[half:], 1)
        return rows, side, ahead, jnp.concatenate([upper, lower], axis=0)

    def sum_by_distance(own, side, ahead, across, gate=None):
        half = own.shape[0] // 2
        across = across.astype(low)
        upper = swapped(across[:half], 2)
        lower = swapped(across[half:], 1)
        if gate is not None:
            upper, lower = after((upper, lower), gate)
        side = jnp.concatenate([side[:half] + upper.astype(full), side[half:]], axis=0)
        ahead = jnp.concatenate([ahead[:half], ahead[half:] + lower.astype(full)], axis=0)
        side, ahead = side.astype(low), ahead.astype(low)
        return own + swapped(side, 1).astype(full) + swapped(ahead, 2).astype(full)

    def share_first(lower, upper):
        return jnp.where(on_first, lower, to_second(upper))

    def sum_over_sections(partial):
        blocks = partial.reshape(section_count, -1, feature_width)
        return sum_by_distance(
            *[
                lax.dynamic_index_in_dim(blocks, section ^ mask, 0, keepdims=False)
                for mask in range(4)
            ]
        )

    def gather_sections(rows):
        by_mask = by_distance(rows)
        ordered = []
        for target in range(section_count):
            chosen = by_mask[0]
            for mask in range(1, section_count):
                chosen = jnp.where(section ^ mask == target, by_mask[mask], chosen)
            ordered.append(chosen)
        return jnp.concatenate(ordered, axis=0)

    def column_parts(weight, block):
        rows, width = weight.shape
        split = weight.reshape(rows, width // (2 * block), 2, block)
        return split[:, :, 0].reshape(rows, -1), split[:, :, 1].reshape(rows, -1)

    def interleave(even, odd, block):
        rows, width = even.shape
        parts = [part.reshape(rows, width // block, 1, block) for part in (even, odd)]
        return jnp.concatenate(parts, axis=2).reshape(rows, 2 * width)

    halves = [pick(weight[0, :, :inner], weight[0, :, inner:]) for weight in (w_query, w_key, w_value)]
    own_heads = jnp.concatenate([half[0] for half in halves], axis=1)
    other_heads = swapped(jnp.concatenate([half[1] for half in halves], axis=1), 2)
    qkv_pieces = pick(own_heads, other_heads)
    half_hidden = w_down.shape[1] // 2
    half_depth = w_up.shape[1] // 2
    up_share = share_first(w_up[0, :half_depth], w_up[0, half_depth:])
    all_gains = after(gains, (other_heads, up_share))
    for axis in ("core", "pair", "section"):
        all_gains = lax.all_gather(all_gains, axis, axis=2, tiled=True)
    out_pieces = exchange_rows(after(w_out[0], other_heads))

    def gather(piece):
        return lax.all_gather(piece, dp, axis=0, tiled=True)

    stacked = [
        gather(jnp.concatenate([qkv_pieces[layer], fold(out_pieces[layer])], axis=1))
        for layer in range(LAYERS)
    ]
    qkv_w = [weight[:, : 3 * inner] for weight in stacked]
    out_w = [unfold(weight[:, 3 * inner :]) for weight in stacked]

    up_turned = lax.all_to_all(up_share, dp, split_axis=1, concat_axis=0, tiled=True)
    down_share = share_first(
        *after((w_down[0, :half_hidden], w_down[0, half_hidden:]), other_heads)
    )

    def by_depth(rows):
        return rows.reshape(-1, dp_count, 2, half_depth).swapaxes(1, 2).reshape(rows.shape)

    def in_depth(rows):
        return rows.reshape(-1, 2, dp_count, half_depth).swapaxes(1, 2).reshape(rows.shape)

    def first_ffn(gate):
        down, up = after((down_share, up_turned), gate)
        down, up = by_distance(down), by_distance(up)
        return (
            jnp.concatenate(
                [
                    jnp.concatenate(pick(up[0], up[2]), axis=0),
                    jnp.concatenate(pick(up[1], up[3]), axis=0),
                ],
                axis=1,
            ),
            jnp.concatenate(pick(down[0], down[2]) + pick(down[1], down[3]), axis=0),
        )

    down_late = after(w_down[0], all_gains)
    down_second = gather(
        jnp.where(on_first, to_first(down_late[:half_hidden]), down_late[half_hidden:])
    )

    def second_ffn(gate):
        up_even, up_odd = column_parts(after(w_up[0], gate), half_hidden)
        return gather(jnp.where(on_first, to_first(up_even), up_odd)), down_second

    up_w = [None, None]
    down_w = [None, None]
    query_w = [weight[:, :inner] for weight in qkv_w]
    key_w = [weight[:, inner : 2 * inner] for weight in qkv_w]
    value_w = [weight[:, 2 * inner :] for weight in qkv_w]

    image_hot = segment_ids[:, :, None] == jnp.arange(slot_count, dtype=jnp.int32)[None, None, :]
    media_slot = jnp.sum(jnp.where(image_hot, slot_map[:, None, :], 0), axis=2) - (
        segment_ids < 0
    ).astype(jnp.int32)
    media_unit, media_inverse = unit_rows(media.astype(full))
    latent_slot = jnp.arange(latent_rows, dtype=jnp.int32) // LATENTS
    key_slot = jnp.concatenate([media_slot[0], latent_slot])
    allowed = latent_slot[None, :, None] == key_slot[None, None, :]

    def split_heads(rows):
        return rows.reshape(rows.shape[0], heads, HEAD_DIM)

    media_low = []
    media_key = []
    media_value = []
    for layer in range(LAYERS):
        media_low.append((media_unit * all_gains[layer, 0]).astype(low))
        media_key.append(matmul(media_low[layer], key_w[layer]).astype(low))
        media_value.append(matmul(media_low[layer], value_w[layer]).astype(low))

    saved = []
    current = lax.dynamic_slice_in_dim(latents, section * slot_rows, slot_rows, 0).astype(full)
    grad_rows = lax.dynamic_slice_in_dim(cotangent, section * slot_rows, slot_rows, 0).astype(full)
    grad_low = cotangent
    for layer in range(LAYERS):
        unit_in, inverse_in = unit_rows(current)
        if layer == 0:
            whole_unit = unit_rows(latents.astype(full))[0]
            latent_low = (whole_unit * all_gains[layer, 1]).astype(low)
        else:
            latent_low = from_slots((unit_in * all_gains[layer, 1]).astype(low))
        projected = matmul(latent_low, qkv_w[layer]).astype(low)
        if layer == 0:
            up_w[0], down_w[0] = lax.optimization_barrier(first_ffn(projected))
            up_w[1], down_w[1] = second_ffn(media_value[0])
        query_low = projected[:, :inner]
        key_heads = split_heads(
            jnp.concatenate([media_key[layer], projected[:, inner : 2 * inner]], axis=0)
        )
        value_heads = split_heads(
            jnp.concatenate([media_value[layer], projected[:, 2 * inner :]], axis=0)
        )
        query_heads = split_heads(query_low)
        attended, log_total = attend_forward(
            query_heads, key_heads, value_heads, allowed, score_scale
        )
        attended_low = attended.reshape(-1, inner).astype(low)
        middle = current + sum_to_slots(matmul(attended_low, out_w[layer]))
        unit_mid, inverse_mid = unit_rows(middle)
        ffn_low = (unit_mid * all_gains[layer, 2]).astype(low)
        ffn_low = from_slots(ffn_low) if layer else from_sequences(by_depth(ffn_low))
        hidden_pre = matmul(ffn_low, up_w[layer])
        active_low = gelu_exact(hidden_pre).astype(low)
        if layer == 0:
            current = middle + sum_to_sequence(active_low, down_w[layer], matmul)
        saved.append(
            (
                unit_in,
                inverse_in,
                latent_low,
                query_heads,
                key_heads,
                value_heads,
                log_total,
                attended_low,
                unit_mid,
                inverse_mid,
                ffn_low,
                hidden_pre,
                active_low,
            )
        )

    def scatter(blocks):
        return lax.psum_scatter(blocks, dp, scatter_dimension=0, tiled=True)

    gain_rows = [None] * LAYERS
    media_parts = []
    media_gains = []

    def add_media(layer, grad_key, grad_value, gate):
        grad_key, grad_value = after((grad_key[:seq_rows], grad_value[:seq_rows]), gate)
        part = matmul_nt(grad_key, key_w[layer]) + matmul_nt(grad_value, value_w[layer])
        media_gains.append(jnp.sum(part * media_unit, axis=0))
        media_parts.append((part * all_gains[layer, 0]).astype(low if layer else full))

    pieces = [None] * LAYERS
    for layer in (1, 0):
        (
            unit_in,
            inverse_in,
            latent_low,
            query_heads,
            key_heads,
            value_heads,
            log_total,
            attended_low,
            unit_mid,
            inverse_mid,
            ffn_low,
            hidden_pre,
            active_low,
        ) = saved[layer]
        grad_active = matmul_nt(grad_low, down_w[layer])
        grad_hidden = (grad_active * gelu_slope(hidden_pre)).astype(low)
        if layer == 0:
            add_media(1, *media_grads, grad_hidden)
        down_grad = matmul_tn(active_low, grad_low)
        if layer:
            down_grad = down_grad.astype(low)
            grad_hidden = after(grad_hidden, down_grad)
        up_grad = matmul_tn(ffn_low, grad_hidden)
        if layer:
            ffn_pieces = (scatter(down_grad), scatter(up_grad.astype(low)))
            ffn_grad = sum_to_slots(matmul_nt(grad_hidden, up_w[layer]))
        else:
            ffn_grad = in_depth(sum_to_sequence(grad_hidden, up_w[layer], matmul_nt))
            blocks = down_grad.reshape(2, 2, half_hidden, feature_width)
            own, ahead = pick(blocks[0, 0], blocks[0, 1])
            side, across = pick(blocks[1, 0], blocks[1, 1])
            down_blocks = (own, side, ahead, across)
            width = up_grad.shape[1] // 2
            blocks = up_grad.reshape(2, -1, 2 * width)
            own, ahead = pick(blocks[0][:, :width], blocks[1][:, :width])
            side, across = pick(blocks[0][:, width:], blocks[1][:, width:])
            up_blocks = (own, side, ahead, across)
        gain_ffn_grad = jnp.sum(ffn_grad * unit_mid, axis=0)
        grad_middle = grad_rows + norm_back(
            unit_mid, inverse_mid, ffn_grad * all_gains[layer, 2]
        )
        middle_low = from_slots(grad_middle.astype(low))
        if layer == 0:
            up_half = sum_by_distance(*up_blocks, middle_low).astype(low)
            down_half = sum_by_distance(*down_blocks, middle_low).astype(low)
        grad_heads = split_heads(matmul_nt(middle_low, out_w[layer]).astype(low))
        out_grad = by_device(matmul_tn(attended_low, middle_low)).astype(low)
        out_piece = scatter(out_grad)
        grad_heads = after(grad_heads, out_grad)
        grad_query, grad_key, grad_value = attend_backward(
            query_heads, key_heads, value_heads, allowed, score_scale, log_total, grad_heads
        )
        grad_query = grad_query.reshape(-1, inner).astype(low)
        grad_key = grad_key.reshape(-1, inner).astype(low)
        grad_value = grad_value.reshape(-1, inner).astype(low)
        latent_part = (
            matmul_nt(grad_query, query_w[layer])
            + matmul_nt(grad_key[seq_rows:], key_w[layer])
            + matmul_nt(grad_value[seq_rows:], value_w[layer])
        )
        latent_grad_rows = sum_to_slots(latent_part)
        gain_latent_grad = jnp.sum(latent_grad_rows * unit_in, axis=0)
        grad_rows = grad_middle + norm_back(
            unit_in, inverse_in, latent_grad_rows * all_gains[layer, 1]
        )
        both_low = jnp.concatenate([media_low[layer], latent_low], axis=0)
        all_grads = jnp.concatenate(
            [jnp.pad(grad_query, ((seq_rows, 0), (0, 0))), grad_key, grad_value], axis=1
        )
        qkv_grad = matmul_tn(both_low, all_grads).astype(low)
        if layer == 0:
            up_half, qkv_grad = lax.optimization_barrier((up_half, qkv_grad))
            up_half = lax.all_to_all(up_half, dp, split_axis=0, concat_axis=1, tiled=True)
        pieces[layer] = (scatter(qkv_grad), out_piece)
        if layer > 0:
            grad_low = from_sequences(grad_rows.astype(low))
            late = after(active_low, latent_part)
            here = (latent_slot == section)[:, None]
            kept = jnp.where(here, jnp.tile(middle, (section_count, 1)), 0.0)
            last = lax.optimization_barrier((matmul(late, down_w[layer]) + kept).astype(low))
            last = last.reshape(latent_rows, section_count, -1).swapaxes(0, 1)
            last = lax.all_to_all(last, "section", split_axis=0, concat_axis=0)
            latents_out = jnp.sum(last.astype(full), axis=0)
            grad_low = after(grad_low, latents_out)
            grad_low = after(grad_low, ffn_pieces)
        if layer == 0:
            add_media(0, grad_key, grad_value, qkv_grad)
        else:
            media_grads = (grad_key, grad_value)
        gain_rows[layer] = (gain_latent_grad, gain_ffn_grad)
    latent_grad = to_columns(after(grad_rows, (pieces[1], up_half)))
    media_rows = seq_rows // section_count
    media_sum = sum_over_sections(media_parts[0].astype(full) + media_parts[1])
    own_unit = lax.dynamic_slice_in_dim(media_unit, section * media_rows, media_rows, 0)
    own_inverse = lax.dynamic_slice_in_dim(media_inverse, section * media_rows, media_rows, 0)
    media_grad = gather_sections(norm_back(own_unit, own_inverse, media_sum).astype(low)).astype(
        full
    )
    gain_rows = [
        jnp.stack([media_gains[1 - layer], *gain_rows[layer]]) for layer in range(LAYERS)
    ]
    gain_parts = jnp.stack(gain_rows).reshape(LAYERS, 3, section_count, -1)
    gain_parts = jnp.sum(
        lax.all_to_all(gain_parts, "section", split_axis=2, concat_axis=2), axis=2
    )
    gain_parts = gain_parts.reshape(LAYERS, 3, dp_count, -1)
    gain_grad = jnp.sum(lax.all_to_all(gain_parts, dp, split_axis=2, concat_axis=2), axis=2)

    qkv_parts = [piece[0] for piece in pieces]
    own, other = pick(qkv_parts[0], qkv_parts[1])
    lower, upper = pick(own, swapped(other, 2))
    qkv_grads = [
        jnp.concatenate(
            [lower[:, i * inner : (i + 1) * inner], upper[:, i * inner : (i + 1) * inner]], axis=1
        ).astype(full)
        for i in range(3)
    ]
    out_grad = join_rows(*[piece[1] for piece in pieces])
    down_piece, up_piece = ffn_pieces
    up_second_grad = interleave(to_second(up_piece), up_piece, half_hidden)
    down_second_grad = jnp.concatenate([to_second(down_piece), down_piece], axis=0)
    up_first_grad = jnp.concatenate([up_half, to_first(up_half)], axis=0)
    down_first_grad = jnp.concatenate([down_half, to_first(down_half)], axis=0)
    up_grad = jnp.where(on_first, up_first_grad, up_second_grad).astype(full)
    down_grad = jnp.where(on_first, down_first_grad, down_second_grad).astype(full)
    return (
        latents_out,
        latent_grad,
        media_grad,
        gain_grad,
        qkv_grads[0][None],
        qkv_grads[1][None],
        qkv_grads[2][None],
        out_grad[None],
        up_grad[None],
        down_grad[None],
    )


def solution(mesh):
    section_count, dp_count = mesh.devices.shape
    fine = Mesh(
        mesh.devices.reshape(section_count, dp_count // 2, 2), ("section", "pair", "core")
    )
    dp = ("pair", "core")
    placed = (
        P(dp, None),
        P(dp, None),
        P(dp, None),
        P(dp, None),
        P(None, None, ("section",) + dp),
        P("section", dp, None),
        P("section", dp, None),
        P("section", dp, None),
        P("section", dp, None),
        P("section", dp, None),
        P("section", dp, None),
        P(dp, None),
    )
    return jax.shard_map(
        per_device,
        mesh=fine,
        in_specs=placed,
        out_specs=(
            P(dp, "section"),
            P(dp, "section"),
            P(dp, None),
            P(None, None, ("section",) + dp),
            P("section", dp, None),
            P("section", dp, None),
            P("section", dp, None),
            P("section", dp, None),
            P("section", dp, None),
            P("section", dp, None),
        ),
        check_vma=False,
    )
```

```python
import math

import jax
import jax.numpy as jnp
from jax import lax
from jax.sharding import Mesh, PartitionSpec as P

HEAD_DIM = 96
LATENTS = 64
LAYERS = 2

epsilon = 1e-05
low = jnp.bfloat16
full = jnp.float32


def unit_rows(values):
    centered = values - jnp.mean(values, axis=-1, keepdims=True)
    variance = jnp.mean(centered * centered, axis=-1, keepdims=True)
    inverse = lax.rsqrt(variance + epsilon)
    return centered * inverse, inverse


def norm_back(unit, inverse, scaled):
    first = jnp.mean(scaled, axis=-1, keepdims=True)
    second = jnp.mean(scaled * unit, axis=-1, keepdims=True)
    return (scaled - first - unit * second) * inverse


def gelu_exact(values):
    return 0.5 * values * (1.0 + lax.erf(values * math.sqrt(0.5)))


def gelu_slope(values):
    normal = 0.5 * (1.0 + lax.erf(values * math.sqrt(0.5)))
    return normal + values * jnp.exp(-0.5 * values * values) * (1.0 / math.sqrt(2.0 * math.pi))


def matmul(left, right):
    return jnp.dot(left, right, preferred_element_type=full)


def matmul_nt(left, right):
    return lax.dot_general(left, right, (((1,), (1,)), ((), ())), preferred_element_type=full)


def matmul_tn(left, right):
    return lax.dot_general(left, right, (((0,), (0,)), ((), ())), preferred_element_type=full)


def attend_forward(query_heads, key_heads, value_heads, allowed, score_scale):
    scores = jnp.einsum("qhd,khd->hqk", query_heads, key_heads, preferred_element_type=full)
    scores = jnp.where(allowed, scores * score_scale, -1e30)
    row_max = jnp.max(scores, axis=-1, keepdims=True)
    exponent = jnp.exp(scores - row_max)
    row_total = jnp.sum(exponent, axis=-1, keepdims=True)
    weights_low = (exponent / row_total).astype(low)
    attended = jnp.einsum("hqk,khd->qhd", weights_low, value_heads, preferred_element_type=full)
    return attended, row_max + jnp.log(row_total)


def attend_backward(
    query_heads, key_heads, value_heads, allowed, score_scale, log_total, grad_heads
):
    scores = jnp.einsum("qhd,khd->hqk", query_heads, key_heads, preferred_element_type=full)
    scores = jnp.where(allowed, scores * score_scale, -1e30)
    weights_full = jnp.exp(scores - log_total)
    weights_low = weights_full.astype(low)
    grad_value = jnp.einsum("hqk,qhd->khd", weights_low, grad_heads, preferred_element_type=full)
    grad_weights = jnp.einsum(
        "qhd,khd->hqk", grad_heads, value_heads, preferred_element_type=full
    )
    row_inner = jnp.sum(weights_full * grad_weights, axis=-1, keepdims=True)
    grad_scores = (weights_full * (grad_weights - row_inner)).astype(low)
    grad_query = (
        jnp.einsum("hqk,khd->qhd", grad_scores, key_heads, preferred_element_type=full)
        * score_scale
    )
    grad_key = (
        jnp.einsum("hqk,qhd->khd", grad_scores, query_heads, preferred_element_type=full)
        * score_scale
    )
    return grad_query, grad_key, grad_value


def per_device(
    latents,
    media,
    segment_ids,
    slot_map,
    gains,
    w_query,
    w_key,
    w_value,
    w_out,
    w_up,
    w_down,
    cotangent,
):
    dp = ("pair", "core")
    everywhere = ("section",) + dp
    section = lax.axis_index("section")
    section_count = lax.axis_size("section")
    dp_index = lax.axis_index(dp)
    dp_count = lax.axis_size("pair") * lax.axis_size("core")
    on_first = section // 2 == 0
    stride = dp_count // 2
    seq_rows = segment_ids.shape[1]
    slot_count = slot_map.shape[1]
    feature_width = latents.shape[1]
    latent_rows = latents.shape[0]
    slot_rows = latent_rows // section_count
    inner = w_query.shape[2] // 2
    heads = inner // HEAD_DIM
    score_scale = 1.0 / math.sqrt(HEAD_DIM)

    def pick(first, second):
        return jnp.where(on_first, first, second), jnp.where(on_first, second, first)

    def swapped(value, mask):
        pairs = [(source, source ^ mask) for source in range(section_count)]
        return lax.ppermute(value, "section", pairs)

    def other_core(value):
        return lax.ppermute(value, "core", [(0, 1), (1, 0)])

    def to_second(value):
        return lax.ppermute(value, "section", [(0, 2), (1, 3)])

    def to_first(value):
        return lax.ppermute(value, "section", [(2, 0), (3, 1)])

    def after(value, earlier):
        return lax.optimization_barrier((value, earlier))[0]

    def turn_pairs(span, flip, back):
        pairs = []
        for source in range(section_count):
            for index in range(dp_count):
                layer, half = divmod(source, 2)
                high, bit, lowest = index // (2 * span), index // span % 2, index % span
                moved = (2 * high + (layer ^ flip)) * span + lowest
                target = (bit * 2 + half) * dp_count + moved
                pair = (source * dp_count + index, target)
                pairs.append(pair[::-1] if back else pair)
        return pairs

    def first_bit(span):
        return dp_index // span % 2 == 0

    def exchange_rows(weight, span):
        half = weight.shape[0] // 2
        near, far = pick(weight[:half], weight[half:])
        first = lax.ppermute(near, everywhere, turn_pairs(span, 0, False))
        second = lax.ppermute(far, everywhere, turn_pairs(span, 1, False))
        chosen = first_bit(span)
        return jnp.where(chosen, first, second), jnp.where(chosen, second, first)

    def join_rows(first, second, span):
        chosen = first_bit(span)
        near = jnp.where(chosen, first, second)
        far = jnp.where(chosen, second, first)
        near = lax.ppermute(near, everywhere, turn_pairs(span, 0, True))
        far = lax.ppermute(far, everywhere, turn_pairs(span, 1, True))
        return jnp.concatenate(pick(near, far), axis=0).astype(full)

    def exchange_second(weight, span):
        half = weight.shape[0] // 2
        parts = []
        for bit in range(2):
            pairs = [
                pair
                for flip in range(2)
                for pair in turn_pairs(span, flip, False)
                if pair[0] >= 2 * dp_count and pair[1] // span % 2 == bit
            ]
            parts.append(lax.ppermute(weight[bit * half : (bit + 1) * half], everywhere, pairs))
        return jnp.where(first_bit(span), parts[0], parts[1])

    def join_second(piece, span):
        parts = []
        for bit in range(2):
            pairs = [
                pair[::-1]
                for flip in range(2)
                for pair in turn_pairs(span, flip, False)
                if pair[0] >= 2 * dp_count and pair[1] // span % 2 == bit
            ]
            parts.append(lax.ppermute(piece, everywhere, pairs))
        return jnp.concatenate(parts, axis=0)

    def in_rows(gathered, span):
        if span > 1:
            width = gathered.shape[1]
            gathered = gathered.reshape(-1, 2, span, gathered.shape[0] // dp_count, width)
            gathered = gathered.swapaxes(1, 2).reshape(-1, width)
        return gathered

    def in_shards(grad, span):
        if span > 1:
            width = grad.shape[1]
            grad = grad.reshape(-1, span, 2, grad.shape[0] // dp_count, width)
            grad = grad.swapaxes(1, 2).reshape(-1, width)
        return grad

    def fold(piece):
        blocks = [piece[:, i * inner : (i + 1) * inner] for i in range(feature_width // inner)]
        return jnp.concatenate(blocks, axis=0)

    def unfold(stacked):
        count = feature_width // inner
        blocks = stacked.reshape(2, stride, count, -1, inner).transpose(1, 0, 3, 2, 4)
        return blocks.reshape(-1, feature_width)

    def by_device(grad):
        blocks = grad.reshape(stride, 2, -1, feature_width).transpose(1, 0, 2, 3)
        return blocks.reshape(-1, feature_width)

    def sum_to_slots(partial):
        blocks = partial.astype(low).reshape(section_count, -1, feature_width)
        arrived = lax.all_to_all(blocks, "section", split_axis=0, concat_axis=0)
        return jnp.sum(arrived.astype(full), axis=0)

    def from_slots(rows):
        return lax.all_gather(rows, "section", axis=0, tiled=True)

    def to_columns(rows):
        moved = lax.all_to_all(
            rows.astype(low), "section", split_axis=1, concat_axis=0, tiled=True
        )
        return moved.astype(full)

    def from_sequences(rows):
        near = lax.all_gather(rows, "pair", axis=0, tiled=True)
        return jnp.concatenate([near, other_core(near)], axis=0)

    def sum_to_sequence(left, right, product):
        half = left.shape[0] // 2
        far = product(left[half:], right).astype(low)
        near = product(left[:half], right) + other_core(far).astype(full)
        blocks = near.astype(low).reshape(-1, slot_rows, feature_width)
        arrived = lax.all_to_all(blocks, "pair", split_axis=0, concat_axis=0)
        return jnp.sum(arrived.astype(full), axis=0)

    def by_distance(rows):
        half = rows.shape[0] // 2
        side = swapped(rows, 1)
        ahead = swapped(rows, 2)
        upper = swapped(side[:half], 2)
        lower = swapped(ahead[half:], 1)
        return rows, side, ahead, jnp.concatenate([upper, lower], axis=0)

    def sum_by_distance(own, side, ahead, across, gate=None):
        half = own.shape[0] // 2
        across = across.astype(low)
        upper = swapped(across[:half], 2)
        lower = swapped(across[half:], 1)
        if gate is not None:
            upper, lower = after((upper, lower), gate)
        side = jnp.concatenate([side[:half] + upper.astype(full), side[half:]], axis=0)
        ahead = jnp.concatenate([ahead[:half], ahead[half:] + lower.astype(full)], axis=0)
        side, ahead = side.astype(low), ahead.astype(low)
        return own + swapped(side, 1).astype(full) + swapped(ahead, 2).astype(full)

    def share_first(lower, upper):
        return jnp.where(on_first, lower, to_second(upper))

    def sum_over_sections(partial):
        blocks = partial.reshape(section_count, -1, feature_width)
        return sum_by_distance(
            *[
                lax.dynamic_index_in_dim(blocks, section ^ mask, 0, keepdims=False)
                for mask in range(4)
            ]
        )

    def gather_sections(rows):
        by_mask = by_distance(rows)
        ordered = []
        for target in range(section_count):
            chosen = by_mask[0]
            for mask in range(1, section_count):
                chosen = jnp.where(section ^ mask == target, by_mask[mask], chosen)
            ordered.append(chosen)
        return jnp.concatenate(ordered, axis=0)

    def column_parts(weight, block):
        rows, width = weight.shape
        split = weight.reshape(rows, width // (2 * block), 2, block)
        return split[:, :, 0].reshape(rows, -1), split[:, :, 1].reshape(rows, -1)

    def interleave(even, odd, block):
        rows, width = even.shape
        parts = [part.reshape(rows, width // block, 1, block) for part in (even, odd)]
        return jnp.concatenate(parts, axis=2).reshape(rows, 2 * width)

    halves = [pick(weight[0, :, :inner], weight[0, :, inner:]) for weight in (w_query, w_key, w_value)]
    own_heads = jnp.concatenate([half[0] for half in halves], axis=1)
    other_heads = swapped(jnp.concatenate([half[1] for half in halves], axis=1), 2)
    qkv_pieces = pick(own_heads, other_heads)
    half_hidden = w_down.shape[1] // 2
    half_depth = w_up.shape[1] // 2
    up_share = share_first(w_up[0, :half_depth], w_up[0, half_depth:])
    all_gains = after(gains, (other_heads, up_share))
    for axis in ("core", "pair", "section"):
        all_gains = lax.all_gather(all_gains, axis, axis=2, tiled=True)
    out_pieces = exchange_rows(after(w_out[0], other_heads), stride)

    def gather(piece):
        return lax.all_gather(piece, dp, axis=0, tiled=True)

    stacked = [
        gather(jnp.concatenate([qkv_pieces[layer], fold(out_pieces[layer])], axis=1))
        for layer in range(LAYERS)
    ]
    qkv_w = [weight[:, : 3 * inner] for weight in stacked]
    out_w = [unfold(weight[:, 3 * inner :]) for weight in stacked]

    up_turned = lax.all_to_all(up_share, dp, split_axis=1, concat_axis=0, tiled=True)
    down_share = share_first(
        *after((w_down[0, :half_hidden], w_down[0, half_hidden:]), other_heads)
    )

    def by_depth(rows):
        return rows.reshape(-1, dp_count, 2, half_depth).swapaxes(1, 2).reshape(rows.shape)

    def in_depth(rows):
        return rows.reshape(-1, 2, dp_count, half_depth).swapaxes(1, 2).reshape(rows.shape)

    def first_ffn(gate):
        down, up = after((down_share, up_turned), gate)
        down, up = by_distance(down), by_distance(up)
        return (
            jnp.concatenate(
                [
                    jnp.concatenate(pick(up[0], up[2]), axis=0),
                    jnp.concatenate(pick(up[1], up[3]), axis=0),
                ],
                axis=1,
            ),
            jnp.concatenate(pick(down[0], down[2]) + pick(down[1], down[3]), axis=0),
        )

    span = max(1, dp_count // 8)
    hidden_block = w_up.shape[2] // 8
    down_piece = exchange_second(after(w_down[0], all_gains), span)

    def second_ffn(gate):
        up_even, up_odd = column_parts(after(w_up[0], gate), hidden_block)
        return gather(jnp.where(on_first, to_first(up_even), up_odd))

    up_w = [None, None]
    down_w = [None, None]
    query_w = [weight[:, :inner] for weight in qkv_w]
    key_w = [weight[:, inner : 2 * inner] for weight in qkv_w]
    value_w = [weight[:, 2 * inner :] for weight in qkv_w]

    image_hot = segment_ids[:, :, None] == jnp.arange(slot_count, dtype=jnp.int32)[None, None, :]
    media_slot = jnp.sum(jnp.where(image_hot, slot_map[:, None, :], 0), axis=2) - (
        segment_ids < 0
    ).astype(jnp.int32)
    media_unit, media_inverse = unit_rows(media.astype(full))
    latent_slot = jnp.arange(latent_rows, dtype=jnp.int32) // LATENTS
    key_slot = jnp.concatenate([media_slot[0], latent_slot])
    allowed = latent_slot[None, :, None] == key_slot[None, None, :]

    def split_heads(rows):
        return rows.reshape(rows.shape[0], heads, HEAD_DIM)

    media_low = []
    media_key = []
    media_value = []
    for layer in range(LAYERS):
        media_low.append((media_unit * all_gains[layer, 0]).astype(low))
        if layer == 0:
            media_low[0], down_piece = lax.optimization_barrier((media_low[0], down_piece))
        media_key.append(matmul(media_low[layer], key_w[layer]).astype(low))
        media_value.append(matmul(media_low[layer], value_w[layer]).astype(low))

    down_second = in_rows(gather(down_piece), span)
    saved = []
    current = lax.dynamic_slice_in_dim(latents, section * slot_rows, slot_rows, 0).astype(full)
    grad_rows = lax.dynamic_slice_in_dim(cotangent, section * slot_rows, slot_rows, 0).astype(full)
    grad_low = cotangent
    for layer in range(LAYERS):
        unit_in, inverse_in = unit_rows(current)
        if layer == 0:
            whole_unit = unit_rows(latents.astype(full))[0]
            latent_low = (whole_unit * all_gains[layer, 1]).astype(low)
        else:
            latent_low = from_slots((unit_in * all_gains[layer, 1]).astype(low))
        projected = matmul(latent_low, qkv_w[layer]).astype(low)
        if layer == 0:
            up_w[0], down_w[0] = lax.optimization_barrier(first_ffn(projected))
        query_low = projected[:, :inner]
        key_heads = split_heads(
            jnp.concatenate([media_key[layer], projected[:, inner : 2 * inner]], axis=0)
        )
        value_heads = split_heads(
            jnp.concatenate([media_value[layer], projected[:, 2 * inner :]], axis=0)
        )
        query_heads = split_heads(query_low)
        attended, log_total = attend_forward(
            query_heads, key_heads, value_heads, allowed, score_scale
        )
        attended_low = attended.reshape(-1, inner).astype(low)
        middle = current + sum_to_slots(matmul(attended_low, out_w[layer]))
        unit_mid, inverse_mid = unit_rows(middle)
        ffn_low = (unit_mid * all_gains[layer, 2]).astype(low)
        ffn_low = from_slots(ffn_low) if layer else from_sequences(by_depth(ffn_low))
        if layer == 0:
            up_w[1], down_w[1] = second_ffn(ffn_low), down_second
        hidden_pre = matmul(ffn_low, up_w[layer])
        active_low = gelu_exact(hidden_pre).astype(low)
        if layer == 0:
            current = middle + sum_to_sequence(active_low, down_w[layer], matmul)
        saved.append(
            (
                unit_in,
                inverse_in,
                latent_low,
                query_heads,
                key_heads,
                value_heads,
                log_total,
                attended_low,
                unit_mid,
                inverse_mid,
                ffn_low,
                hidden_pre,
                active_low,
            )
        )

    def scatter(blocks):
        return lax.psum_scatter(blocks, dp, scatter_dimension=0, tiled=True)

    gain_rows = [None] * LAYERS
    media_parts = []
    media_gains = []

    def add_media(layer, grad_key, grad_value, gate):
        grad_key, grad_value = after((grad_key[:seq_rows], grad_value[:seq_rows]), gate)
        part = matmul_nt(grad_key, key_w[layer]) + matmul_nt(grad_value, value_w[layer])
        media_gains.append(jnp.sum(part * media_unit, axis=0))
        media_parts.append((part * all_gains[layer, 0]).astype(low if layer else full))

    pieces = [None] * LAYERS
    for layer in (1, 0):
        (
            unit_in,
            inverse_in,
            latent_low,
            query_heads,
            key_heads,
            value_heads,
            log_total,
            attended_low,
            unit_mid,
            inverse_mid,
            ffn_low,
            hidden_pre,
            active_low,
        ) = saved[layer]
        grad_active = matmul_nt(grad_low, down_w[layer])
        grad_hidden = (grad_active * gelu_slope(hidden_pre)).astype(low)
        if layer == 0:
            add_media(1, *media_grads, grad_hidden)
        down_grad = matmul_tn(active_low, grad_low)
        if layer:
            down_grad = down_grad.astype(low)
            grad_hidden = after(grad_hidden, down_grad)
        up_grad = matmul_tn(ffn_low, grad_hidden)
        if layer:
            ffn_pieces = (scatter(in_shards(down_grad, span)), scatter(up_grad.astype(low)))
            ffn_grad = sum_to_slots(matmul_nt(grad_hidden, up_w[layer]))
        else:
            ffn_grad = in_depth(sum_to_sequence(grad_hidden, up_w[layer], matmul_nt))
            blocks = down_grad.reshape(2, 2, half_hidden, feature_width)
            own, ahead = pick(blocks[0, 0], blocks[0, 1])
            side, across = pick(blocks[1, 0], blocks[1, 1])
            down_blocks = (own, side, ahead, across)
            width = up_grad.shape[1] // 2
            blocks = up_grad.reshape(2, -1, 2 * width)
            own, ahead = pick(blocks[0][:, :width], blocks[1][:, :width])
            side, across = pick(blocks[0][:, width:], blocks[1][:, width:])
            up_blocks = (own, side, ahead, across)
        gain_ffn_grad = jnp.sum(ffn_grad * unit_mid, axis=0)
        grad_middle = grad_rows + norm_back(
            unit_mid, inverse_mid, ffn_grad * all_gains[layer, 2]
        )
        middle_low = from_slots(grad_middle.astype(low))
        if layer == 0:
            up_half = sum_by_distance(*up_blocks, middle_low).astype(low)
            down_half = sum_by_distance(*down_blocks, middle_low).astype(low)
        grad_heads = split_heads(matmul_nt(middle_low, out_w[layer]).astype(low))
        out_grad = by_device(matmul_tn(attended_low, middle_low)).astype(low)
        out_piece = scatter(out_grad)
        grad_heads = after(grad_heads, out_grad)
        grad_query, grad_key, grad_value = attend_backward(
            query_heads, key_heads, value_heads, allowed, score_scale, log_total, grad_heads
        )
        grad_query = grad_query.reshape(-1, inner).astype(low)
        grad_key = grad_key.reshape(-1, inner).astype(low)
        grad_value = grad_value.reshape(-1, inner).astype(low)
        latent_part = (
            matmul_nt(grad_query, query_w[layer])
            + matmul_nt(grad_key[seq_rows:], key_w[layer])
            + matmul_nt(grad_value[seq_rows:], value_w[layer])
        )
        latent_grad_rows = sum_to_slots(latent_part)
        gain_latent_grad = jnp.sum(latent_grad_rows * unit_in, axis=0)
        grad_rows = grad_middle + norm_back(
            unit_in, inverse_in, latent_grad_rows * all_gains[layer, 1]
        )
        both_low = jnp.concatenate([media_low[layer], latent_low], axis=0)
        all_grads = jnp.concatenate(
            [jnp.pad(grad_query, ((seq_rows, 0), (0, 0))), grad_key, grad_value], axis=1
        )
        qkv_grad = matmul_tn(both_low, all_grads).astype(low)
        if layer == 0:
            up_half, qkv_grad = lax.optimization_barrier((up_half, qkv_grad))
            up_half = lax.all_to_all(up_half, dp, split_axis=0, concat_axis=1, tiled=True)
        pieces[layer] = (scatter(qkv_grad), out_piece)
        if layer > 0:
            grad_low = from_sequences(grad_rows.astype(low))
            late = after(active_low, latent_part)
            here = (latent_slot == section)[:, None]
            kept = jnp.where(here, jnp.tile(middle, (section_count, 1)), 0.0)
            last = lax.optimization_barrier((matmul(late, down_w[layer]) + kept).astype(low))
            last = last.reshape(latent_rows, section_count, -1).swapaxes(0, 1)
            last = lax.all_to_all(last, "section", split_axis=0, concat_axis=0)
            latents_out = jnp.sum(last.astype(full), axis=0)
            grad_low = after(grad_low, latents_out)
            grad_low = after(grad_low, ffn_pieces)
        if layer == 0:
            add_media(0, grad_key, grad_value, qkv_grad)
        else:
            media_grads = (grad_key, grad_value)
        gain_rows[layer] = (gain_latent_grad, gain_ffn_grad)
    qkv_parts = [piece[0] for piece in pieces]
    own, other = pick(qkv_parts[0], qkv_parts[1])
    lower, upper = pick(own, swapped(other, 2))
    out_grad = join_rows(*[piece[1] for piece in pieces], stride)
    latent_grad = to_columns(after(grad_rows, (lower, up_half)))
    media_rows = seq_rows // section_count
    media_sum = sum_over_sections(media_parts[0].astype(full) + media_parts[1])
    own_unit = lax.dynamic_slice_in_dim(media_unit, section * media_rows, media_rows, 0)
    own_inverse = lax.dynamic_slice_in_dim(media_inverse, section * media_rows, media_rows, 0)
    media_grad = gather_sections(norm_back(own_unit, own_inverse, media_sum).astype(low)).astype(
        full
    )
    gain_rows = [
        jnp.stack([media_gains[1 - layer], *gain_rows[layer]]) for layer in range(LAYERS)
    ]
    gain_parts = jnp.stack(gain_rows).reshape(LAYERS, 3, section_count, -1)
    gain_parts = jnp.sum(
        lax.all_to_all(gain_parts, "section", split_axis=2, concat_axis=2), axis=2
    )
    gain_parts = after(gain_parts, out_grad).reshape(LAYERS, 3, dp_count, -1)
    gain_grad = jnp.sum(lax.all_to_all(gain_parts, dp, split_axis=2, concat_axis=2), axis=2)

    qkv_grads = [
        jnp.concatenate(
            [lower[:, i * inner : (i + 1) * inner], upper[:, i * inner : (i + 1) * inner]], axis=1
        ).astype(full)
        for i in range(3)
    ]
    down_piece, up_piece = ffn_pieces
    up_second_grad = interleave(to_second(up_piece), up_piece, hidden_block)
    down_second_grad = join_second(down_piece, span)
    up_first_grad = jnp.concatenate([up_half, to_first(up_half)], axis=0)
    down_first_grad = jnp.concatenate([down_half, to_first(down_half)], axis=0)
    up_grad = jnp.where(on_first, up_first_grad, up_second_grad).astype(full)
    down_grad = jnp.where(on_first, down_first_grad, down_second_grad).astype(full)
    return (
        latents_out,
        latent_grad,
        media_grad,
        gain_grad,
        qkv_grads[0][None],
        qkv_grads[1][None],
        qkv_grads[2][None],
        out_grad[None],
        up_grad[None],
        down_grad[None],
    )


def solution(mesh):
    section_count, dp_count = mesh.devices.shape
    fine = Mesh(
        mesh.devices.reshape(section_count, dp_count // 2, 2), ("section", "pair", "core")
    )
    dp = ("pair", "core")
    placed = (
        P(dp, None),
        P(dp, None),
        P(dp, None),
        P(dp, None),
        P(None, None, ("section",) + dp),
        P("section", dp, None),
        P("section", dp, None),
        P("section", dp, None),
        P("section", dp, None),
        P("section", dp, None),
        P("section", dp, None),
        P(dp, None),
    )
    return jax.shard_map(
        per_device,
        mesh=fine,
        in_specs=placed,
        out_specs=(
            P(dp, "section"),
            P(dp, "section"),
            P(dp, None),
            P(None, None, ("section",) + dp),
            P("section", dp, None),
            P("section", dp, None),
            P("section", dp, None),
            P("section", dp, None),
            P("section", dp, None),
            P("section", dp, None),
        ),
        check_vma=False,
    )
```

```python
import math

import jax
import jax.numpy as jnp
from jax import lax
from jax.sharding import Mesh, PartitionSpec as P

HEAD_DIM = 96
LATENTS = 64
LAYERS = 2

epsilon = 1e-05
low = jnp.bfloat16
full = jnp.float32


def unit_rows(values):
    centered = values - jnp.mean(values, axis=-1, keepdims=True)
    variance = jnp.mean(centered * centered, axis=-1, keepdims=True)
    inverse = lax.rsqrt(variance + epsilon)
    return centered * inverse, inverse


def norm_back(unit, inverse, scaled):
    first = jnp.mean(scaled, axis=-1, keepdims=True)
    second = jnp.mean(scaled * unit, axis=-1, keepdims=True)
    return (scaled - first - unit * second) * inverse


def gelu_exact(values):
    return 0.5 * values * (1.0 + lax.erf(values * math.sqrt(0.5)))


def gelu_slope(values):
    normal = 0.5 * (1.0 + lax.erf(values * math.sqrt(0.5)))
    return normal + values * jnp.exp(-0.5 * values * values) * (1.0 / math.sqrt(2.0 * math.pi))


def matmul(left, right):
    return jnp.dot(left, right, preferred_element_type=full)


def matmul_nt(left, right):
    return lax.dot_general(left, right, (((1,), (1,)), ((), ())), preferred_element_type=full)


def matmul_tn(left, right):
    return lax.dot_general(left, right, (((0,), (0,)), ((), ())), preferred_element_type=full)


def attend_forward(query_heads, key_heads, value_heads, allowed, score_scale):
    scores = jnp.einsum("qhd,khd->hqk", query_heads, key_heads, preferred_element_type=full)
    scores = jnp.where(allowed, scores * score_scale, -1e30)
    row_max = jnp.max(scores, axis=-1, keepdims=True)
    exponent = jnp.exp(scores - row_max)
    row_total = jnp.sum(exponent, axis=-1, keepdims=True)
    weights_low = (exponent / row_total).astype(low)
    attended = jnp.einsum("hqk,khd->qhd", weights_low, value_heads, preferred_element_type=full)
    return attended, row_max + jnp.log(row_total)


def attend_backward(
    query_heads, key_heads, value_heads, allowed, score_scale, log_total, grad_heads
):
    scores = jnp.einsum("qhd,khd->hqk", query_heads, key_heads, preferred_element_type=full)
    scores = jnp.where(allowed, scores * score_scale, -1e30)
    weights_full = jnp.exp(scores - log_total)
    weights_low = weights_full.astype(low)
    grad_value = jnp.einsum("hqk,qhd->khd", weights_low, grad_heads, preferred_element_type=full)
    grad_weights = jnp.einsum(
        "qhd,khd->hqk", grad_heads, value_heads, preferred_element_type=full
    )
    row_inner = jnp.sum(weights_full * grad_weights, axis=-1, keepdims=True)
    grad_scores = (weights_full * (grad_weights - row_inner)).astype(low)
    grad_query = (
        jnp.einsum("hqk,khd->qhd", grad_scores, key_heads, preferred_element_type=full)
        * score_scale
    )
    grad_key = (
        jnp.einsum("hqk,qhd->khd", grad_scores, query_heads, preferred_element_type=full)
        * score_scale
    )
    return grad_query, grad_key, grad_value


def per_device(
    latents,
    media,
    segment_ids,
    slot_map,
    gains,
    w_query,
    w_key,
    w_value,
    w_out,
    w_up,
    w_down,
    cotangent,
):
    dp = ("pair", "core")
    everywhere = ("section",) + dp
    section = lax.axis_index("section")
    section_count = lax.axis_size("section")
    dp_index = lax.axis_index(dp)
    dp_count = lax.axis_size("pair") * lax.axis_size("core")
    on_first = section // 2 == 0
    stride = dp_count // 2
    seq_rows = segment_ids.shape[1]
    slot_count = slot_map.shape[1]
    feature_width = latents.shape[1]
    latent_rows = latents.shape[0]
    slot_rows = latent_rows // section_count
    inner = w_query.shape[2] // 2
    heads = inner // HEAD_DIM
    score_scale = 1.0 / math.sqrt(HEAD_DIM)

    def pick(first, second):
        return jnp.where(on_first, first, second), jnp.where(on_first, second, first)

    def swapped(value, mask):
        pairs = [(source, source ^ mask) for source in range(section_count)]
        return lax.ppermute(value, "section", pairs)

    def other_core(value):
        return lax.ppermute(value, "core", [(0, 1), (1, 0)])

    def to_second(value):
        return lax.ppermute(value, "section", [(0, 2), (1, 3)])

    def to_first(value):
        return lax.ppermute(value, "section", [(2, 0), (3, 1)])

    def after(value, earlier):
        return lax.optimization_barrier((value, earlier))[0]

    def turn_pairs(span, flip, back):
        pairs = []
        for source in range(section_count):
            for index in range(dp_count):
                layer, half = divmod(source, 2)
                high, bit, lowest = index // (2 * span), index // span % 2, index % span
                moved = (2 * high + (layer ^ flip)) * span + lowest
                target = (bit * 2 + half) * dp_count + moved
                pair = (source * dp_count + index, target)
                pairs.append(pair[::-1] if back else pair)
        return pairs

    def first_bit(span):
        return dp_index // span % 2 == 0

    def exchange_rows(weight, span):
        half = weight.shape[0] // 2
        near, far = pick(weight[:half], weight[half:])
        first = lax.ppermute(near, everywhere, turn_pairs(span, 0, False))
        second = lax.ppermute(far, everywhere, turn_pairs(span, 1, False))
        chosen = first_bit(span)
        return jnp.where(chosen, first, second), jnp.where(chosen, second, first)

    def join_rows(first, second, span):
        chosen = first_bit(span)
        near = jnp.where(chosen, first, second)
        far = jnp.where(chosen, second, first)
        near = lax.ppermute(near, everywhere, turn_pairs(span, 0, True))
        far = lax.ppermute(far, everywhere, turn_pairs(span, 1, True))
        return jnp.concatenate(pick(near, far), axis=0).astype(full)

    def exchange_second(weight, span):
        half = weight.shape[0] // 2
        parts = []
        for bit in range(2):
            pairs = [
                pair
                for flip in range(2)
                for pair in turn_pairs(span, flip, False)
                if pair[0] >= 2 * dp_count and pair[1] // span % 2 == bit
            ]
            parts.append(lax.ppermute(weight[bit * half : (bit + 1) * half], everywhere, pairs))
        return jnp.where(first_bit(span), parts[0], parts[1])

    def join_second(piece, span):
        parts = []
        for bit in range(2):
            pairs = [
                pair[::-1]
                for flip in range(2)
                for pair in turn_pairs(span, flip, False)
                if pair[0] >= 2 * dp_count and pair[1] // span % 2 == bit
            ]
            parts.append(lax.ppermute(piece, everywhere, pairs))
        return jnp.concatenate(parts, axis=0)

    def in_rows(gathered, span):
        if span > 1:
            width = gathered.shape[1]
            gathered = gathered.reshape(-1, 2, span, gathered.shape[0] // dp_count, width)
            gathered = gathered.swapaxes(1, 2).reshape(-1, width)
        return gathered

    def in_shards(grad, span):
        if span > 1:
            width = grad.shape[1]
            grad = grad.reshape(-1, span, 2, grad.shape[0] // dp_count, width)
            grad = grad.swapaxes(1, 2).reshape(-1, width)
        return grad

    def fold(piece):
        blocks = [piece[:, i * inner : (i + 1) * inner] for i in range(feature_width // inner)]
        return jnp.concatenate(blocks, axis=0)

    def unfold(stacked):
        count = feature_width // inner
        blocks = stacked.reshape(2, stride, count, -1, inner).transpose(1, 0, 3, 2, 4)
        return blocks.reshape(-1, feature_width)

    def by_device(grad):
        blocks = grad.reshape(stride, 2, -1, feature_width).transpose(1, 0, 2, 3)
        return blocks.reshape(-1, feature_width)

    def sum_to_slots(partial):
        blocks = partial.astype(low).reshape(section_count, -1, feature_width)
        arrived = lax.all_to_all(blocks, "section", split_axis=0, concat_axis=0)
        return jnp.sum(arrived.astype(full), axis=0)

    def from_slots(rows):
        return lax.all_gather(rows, "section", axis=0, tiled=True)

    def to_columns(rows):
        moved = lax.all_to_all(
            rows.astype(low), "section", split_axis=1, concat_axis=0, tiled=True
        )
        return moved.astype(full)

    def from_sequences(rows):
        near = lax.all_gather(rows, "pair", axis=0, tiled=True)
        return jnp.concatenate([near, other_core(near)], axis=0)

    def sum_to_sequence(left, right, product):
        half = left.shape[0] // 2
        far = product(left[half:], right).astype(low)
        near = product(left[:half], right) + other_core(far).astype(full)
        blocks = near.astype(low).reshape(-1, slot_rows, feature_width)
        arrived = lax.all_to_all(blocks, "pair", split_axis=0, concat_axis=0)
        return jnp.sum(arrived.astype(full), axis=0)

    def by_distance(rows):
        half = rows.shape[0] // 2
        side = swapped(rows, 1)
        ahead = swapped(rows, 2)
        upper = swapped(side[:half], 2)
        lower = swapped(ahead[half:], 1)
        return rows, side, ahead, jnp.concatenate([upper, lower], axis=0)

    def sum_by_distance(own, side, ahead, across, gate=None):
        half = own.shape[0] // 2
        across = across.astype(low)
        upper = swapped(across[:half], 2)
        lower = swapped(across[half:], 1)
        if gate is not None:
            upper, lower = after((upper, lower), gate)
        side = jnp.concatenate([side[:half] + upper.astype(full), side[half:]], axis=0)
        ahead = jnp.concatenate([ahead[:half], ahead[half:] + lower.astype(full)], axis=0)
        side, ahead = side.astype(low), ahead.astype(low)
        return own + swapped(side, 1).astype(full) + swapped(ahead, 2).astype(full)

    def share_first(lower, upper):
        return jnp.where(on_first, lower, to_second(upper))

    def sum_over_sections(partial):
        blocks = partial.reshape(section_count, -1, feature_width)
        return sum_by_distance(
            *[
                lax.dynamic_index_in_dim(blocks, section ^ mask, 0, keepdims=False)
                for mask in range(4)
            ]
        )

    def gather_sections(rows):
        by_mask = by_distance(rows)
        ordered = []
        for target in range(section_count):
            chosen = by_mask[0]
            for mask in range(1, section_count):
                chosen = jnp.where(section ^ mask == target, by_mask[mask], chosen)
            ordered.append(chosen)
        return jnp.concatenate(ordered, axis=0)

    def column_parts(weight, block):
        rows, width = weight.shape
        split = weight.reshape(rows, width // (2 * block), 2, block)
        return split[:, :, 0].reshape(rows, -1), split[:, :, 1].reshape(rows, -1)

    def interleave(even, odd, block):
        rows, width = even.shape
        parts = [part.reshape(rows, width // block, 1, block) for part in (even, odd)]
        return jnp.concatenate(parts, axis=2).reshape(rows, 2 * width)

    halves = [pick(weight[0, :, :inner], weight[0, :, inner:]) for weight in (w_query, w_key, w_value)]
    own_heads = jnp.concatenate([half[0] for half in halves], axis=1)
    other_heads = swapped(jnp.concatenate([half[1] for half in halves], axis=1), 2)
    qkv_pieces = pick(own_heads, other_heads)
    half_hidden = w_down.shape[1] // 2
    half_depth = w_up.shape[1] // 2
    up_share = share_first(w_up[0, :half_depth], w_up[0, half_depth:])
    all_gains = after(gains, (other_heads, up_share))
    for axis in ("core", "pair", "section"):
        all_gains = lax.all_gather(all_gains, axis, axis=2, tiled=True)
    out_pieces = exchange_rows(after(w_out[0], other_heads), stride)

    def gather(piece):
        return lax.all_gather(piece, dp, axis=0, tiled=True)

    stacked = [
        gather(jnp.concatenate([qkv_pieces[layer], fold(out_pieces[layer])], axis=1))
        for layer in range(LAYERS)
    ]
    qkv_w = [weight[:, : 3 * inner] for weight in stacked]
    out_w = [unfold(weight[:, 3 * inner :]) for weight in stacked]

    up_turned = lax.all_to_all(up_share, dp, split_axis=1, concat_axis=0, tiled=True)
    down_share = share_first(
        *after((w_down[0, :half_hidden], w_down[0, half_hidden:]), other_heads)
    )

    def by_depth(rows):
        return rows.reshape(-1, dp_count, 2, half_depth).swapaxes(1, 2).reshape(rows.shape)

    def in_depth(rows):
        return rows.reshape(-1, 2, dp_count, half_depth).swapaxes(1, 2).reshape(rows.shape)

    def first_hops(gate):
        down, up = after((down_share, up_turned), gate)
        return [(rows, swapped(rows, 1), swapped(rows, 2)) for rows in (down, up)]

    def second_hops(hops):
        out = []
        for rows, side, ahead in hops:
            half = rows.shape[0] // 2
            upper, lower = swapped(side[:half], 2), swapped(ahead[half:], 1)
            across = jnp.concatenate([upper, lower], axis=0)
            near, far = pick(rows, ahead), pick(side, across)
            out.append([jnp.concatenate(pair, axis=0) for pair in (near, far)])
        down, up = out
        return lax.optimization_barrier(
            (jnp.concatenate(up, axis=1), jnp.concatenate(down, axis=0))
        )

    span = max(1, dp_count // 8)
    hidden_block = w_up.shape[2] // 8
    down_piece = exchange_second(after(w_down[0], all_gains), span)

    def second_ffn(gate):
        up_even, up_odd = column_parts(after(w_up[0], gate), hidden_block)
        return gather(jnp.where(on_first, to_first(up_even), up_odd))

    up_w = [None, None]
    down_w = [None, None]
    query_w = [weight[:, :inner] for weight in qkv_w]
    key_w = [weight[:, inner : 2 * inner] for weight in qkv_w]
    value_w = [weight[:, 2 * inner :] for weight in qkv_w]

    image_hot = segment_ids[:, :, None] == jnp.arange(slot_count, dtype=jnp.int32)[None, None, :]
    media_slot = jnp.sum(jnp.where(image_hot, slot_map[:, None, :], 0), axis=2) - (
        segment_ids < 0
    ).astype(jnp.int32)
    media_unit, media_inverse = unit_rows(media.astype(full))
    latent_slot = jnp.arange(latent_rows, dtype=jnp.int32) // LATENTS
    key_slot = jnp.concatenate([media_slot[0], latent_slot])
    allowed = latent_slot[None, :, None] == key_slot[None, None, :]

    def split_heads(rows):
        return rows.reshape(rows.shape[0], heads, HEAD_DIM)

    media_low = []
    media_key = []
    media_value = []
    for layer in range(LAYERS):
        media_low.append((media_unit * all_gains[layer, 0]).astype(low))
        if layer == 0:
            media_low[0], down_piece = lax.optimization_barrier((media_low[0], down_piece))
        media_key.append(matmul(media_low[layer], key_w[layer]).astype(low))
        media_value.append(matmul(media_low[layer], value_w[layer]).astype(low))

    down_second = in_rows(gather(down_piece), span)
    saved = []
    current = lax.dynamic_slice_in_dim(latents, section * slot_rows, slot_rows, 0).astype(full)
    grad_rows = lax.dynamic_slice_in_dim(cotangent, section * slot_rows, slot_rows, 0).astype(full)
    grad_low = cotangent
    for layer in range(LAYERS):
        unit_in, inverse_in = unit_rows(current)
        if layer == 0:
            whole_unit = unit_rows(latents.astype(full))[0]
            latent_low = (whole_unit * all_gains[layer, 1]).astype(low)
        else:
            latent_low = from_slots((unit_in * all_gains[layer, 1]).astype(low))
        projected = matmul(latent_low, qkv_w[layer]).astype(low)
        if layer == 0:
            media_key[0], up_turned = lax.optimization_barrier((media_key[0], up_turned))
            hops = first_hops(projected)
        query_low = projected[:, :inner]
        key_heads = split_heads(
            jnp.concatenate([media_key[layer], projected[:, inner : 2 * inner]], axis=0)
        )
        value_heads = split_heads(
            jnp.concatenate([media_value[layer], projected[:, 2 * inner :]], axis=0)
        )
        query_heads = split_heads(query_low)
        attended, log_total = attend_forward(
            query_heads, key_heads, value_heads, allowed, score_scale
        )
        attended_low = attended.reshape(-1, inner).astype(low)
        middle = current + sum_to_slots(matmul(attended_low, out_w[layer]))
        unit_mid, inverse_mid = unit_rows(middle)
        ffn_low = (unit_mid * all_gains[layer, 2]).astype(low)
        if layer:
            ffn_low = from_slots(ffn_low)
        else:
            ffn_low, hops = lax.optimization_barrier((by_depth(ffn_low), hops))
            up_w[0], down_w[0] = second_hops(hops)
            ffn_low = from_sequences(ffn_low)
        if layer == 0:
            up_w[1], down_w[1] = second_ffn(ffn_low), down_second
        hidden_pre = matmul(ffn_low, up_w[layer])
        active_low = gelu_exact(hidden_pre).astype(low)
        if layer == 0:
            current = middle + sum_to_sequence(active_low, down_w[layer], matmul)
        saved.append(
            (
                unit_in,
                inverse_in,
                latent_low,
                query_heads,
                key_heads,
                value_heads,
                log_total,
                attended_low,
                unit_mid,
                inverse_mid,
                ffn_low,
                hidden_pre,
                active_low,
            )
        )

    def scatter(blocks):
        return lax.psum_scatter(blocks, dp, scatter_dimension=0, tiled=True)

    gain_rows = [None] * LAYERS
    media_parts = []
    media_gains = []

    def add_media(layer, grad_key, grad_value, gate):
        grad_key, grad_value = after((grad_key[:seq_rows], grad_value[:seq_rows]), gate)
        part = matmul_nt(grad_key, key_w[layer]) + matmul_nt(grad_value, value_w[layer])
        media_gains.append(jnp.sum(part * media_unit, axis=0))
        media_parts.append((part * all_gains[layer, 0]).astype(low if layer else full))

    pieces = [None] * LAYERS
    for layer in (1, 0):
        (
            unit_in,
            inverse_in,
            latent_low,
            query_heads,
            key_heads,
            value_heads,
            log_total,
            attended_low,
            unit_mid,
            inverse_mid,
            ffn_low,
            hidden_pre,
            active_low,
        ) = saved[layer]
        grad_active = matmul_nt(grad_low, down_w[layer])
        grad_hidden = (grad_active * gelu_slope(hidden_pre)).astype(low)
        if layer == 0:
            add_media(1, *media_grads, grad_hidden)
        down_grad = matmul_tn(active_low, grad_low)
        if layer:
            down_grad = down_grad.astype(low)
            grad_hidden = after(grad_hidden, down_grad)
        up_grad = matmul_tn(ffn_low, grad_hidden)
        if layer:
            ffn_pieces = (scatter(in_shards(down_grad, span)), scatter(up_grad.astype(low)))
            ffn_grad = sum_to_slots(matmul_nt(grad_hidden, up_w[layer]))
        else:
            ffn_grad = in_depth(sum_to_sequence(grad_hidden, up_w[layer], matmul_nt))
            blocks = down_grad.reshape(2, 2, half_hidden, feature_width)
            own, ahead = pick(blocks[0, 0], blocks[0, 1])
            side, across = pick(blocks[1, 0], blocks[1, 1])
            down_blocks = (own, side, ahead, across)
            width = up_grad.shape[1] // 2
            blocks = up_grad.reshape(2, -1, 2 * width)
            own, ahead = pick(blocks[0][:, :width], blocks[1][:, :width])
            side, across = pick(blocks[0][:, width:], blocks[1][:, width:])
            up_blocks = (own, side, ahead, across)
        gain_ffn_grad = jnp.sum(ffn_grad * unit_mid, axis=0)
        grad_middle = grad_rows + norm_back(
            unit_mid, inverse_mid, ffn_grad * all_gains[layer, 2]
        )
        middle_low = grad_middle.astype(low)
        if layer == 0:
            middle_low = after(middle_low, (up_grad, down_grad, media_parts[0], latents_out))
        middle_low = from_slots(middle_low)
        if layer == 0:
            up_half = sum_by_distance(*up_blocks, middle_low).astype(low)
            down_half = sum_by_distance(*down_blocks, middle_low).astype(low)
        grad_heads = split_heads(matmul_nt(middle_low, out_w[layer]).astype(low))
        out_grad = by_device(matmul_tn(attended_low, middle_low)).astype(low)
        out_piece = scatter(out_grad)
        grad_heads = after(grad_heads, out_grad)
        grad_query, grad_key, grad_value = attend_backward(
            query_heads, key_heads, value_heads, allowed, score_scale, log_total, grad_heads
        )
        grad_query = grad_query.reshape(-1, inner).astype(low)
        grad_key = grad_key.reshape(-1, inner).astype(low)
        grad_value = grad_value.reshape(-1, inner).astype(low)
        both_low = jnp.concatenate([media_low[layer], latent_low], axis=0)
        all_grads = jnp.concatenate(
            [jnp.pad(grad_query, ((seq_rows, 0), (0, 0))), grad_key, grad_value], axis=1
        )
        qkv_grad = matmul_tn(both_low, all_grads).astype(low)
        latent_part = (
            matmul_nt(grad_query, query_w[layer])
            + matmul_nt(grad_key[seq_rows:], key_w[layer])
            + matmul_nt(grad_value[seq_rows:], value_w[layer])
        )
        latent_grad_rows = sum_to_slots(latent_part)
        if layer:
            latent_grad_rows = after(latent_grad_rows, qkv_grad)
        gain_latent_grad = jnp.sum(latent_grad_rows * unit_in, axis=0)
        grad_rows = grad_middle + norm_back(
            unit_in, inverse_in, latent_grad_rows * all_gains[layer, 1]
        )
        if layer == 0:
            up_half, qkv_grad = lax.optimization_barrier((up_half, qkv_grad))
            up_half = lax.all_to_all(up_half, dp, split_axis=0, concat_axis=1, tiled=True)
        pieces[layer] = (scatter(qkv_grad), out_piece)
        if layer > 0:
            grad_low = from_sequences(grad_rows.astype(low))
            late = after(active_low, latent_part)
            here = (latent_slot == section)[:, None]
            kept = jnp.where(here, jnp.tile(middle, (section_count, 1)), 0.0)
            last = lax.optimization_barrier((matmul(late, down_w[layer]) + kept).astype(low))
            last = last.reshape(latent_rows, section_count, -1).swapaxes(0, 1)
            last = lax.all_to_all(last, "section", split_axis=0, concat_axis=0)
            latents_out = jnp.sum(last.astype(full), axis=0)
            grad_low = after(grad_low, ffn_pieces)
        if layer == 0:
            add_media(0, grad_key, grad_value, qkv_grad)
        else:
            media_grads = (grad_key, grad_value)
        gain_rows[layer] = (gain_latent_grad, gain_ffn_grad)
    qkv_parts = [piece[0] for piece in pieces]
    own, other = pick(qkv_parts[0], qkv_parts[1])
    lower, upper = pick(own, swapped(other, 2))
    out_grad = join_rows(*[piece[1] for piece in pieces], stride)
    latent_grad = to_columns(after(grad_rows, (pieces[1], up_half)))
    media_rows = seq_rows // section_count
    media_sum = sum_over_sections(media_parts[0].astype(full) + media_parts[1])
    own_unit = lax.dynamic_slice_in_dim(media_unit, section * media_rows, media_rows, 0)
    own_inverse = lax.dynamic_slice_in_dim(media_inverse, section * media_rows, media_rows, 0)
    media_grad = gather_sections(norm_back(own_unit, own_inverse, media_sum).astype(low)).astype(
        full
    )
    gain_rows = [
        jnp.stack([media_gains[1 - layer], *gain_rows[layer]]) for layer in range(LAYERS)
    ]
    gain_parts = jnp.stack(gain_rows).reshape(LAYERS, 3, section_count, -1)
    gain_parts = jnp.sum(
        lax.all_to_all(gain_parts, "section", split_axis=2, concat_axis=2), axis=2
    )
    gain_parts = gain_parts.reshape(LAYERS, 3, dp_count, -1)
    gain_grad = jnp.sum(lax.all_to_all(gain_parts, dp, split_axis=2, concat_axis=2), axis=2)

    qkv_grads = [
        jnp.concatenate(
            [lower[:, i * inner : (i + 1) * inner], upper[:, i * inner : (i + 1) * inner]], axis=1
        ).astype(full)
        for i in range(3)
    ]
    down_piece, up_piece = ffn_pieces
    up_second_grad = interleave(to_second(up_piece), up_piece, hidden_block)
    down_second_grad = join_second(down_piece, span)
    up_first_grad = jnp.concatenate([up_half, to_first(up_half)], axis=0)
    down_first_grad = jnp.concatenate([down_half, to_first(down_half)], axis=0)
    up_grad = jnp.where(on_first, up_first_grad, up_second_grad).astype(full)
    down_grad = jnp.where(on_first, down_first_grad, down_second_grad).astype(full)
    return (
        latents_out,
        latent_grad,
        media_grad,
        gain_grad,
        qkv_grads[0][None],
        qkv_grads[1][None],
        qkv_grads[2][None],
        out_grad[None],
        up_grad[None],
        down_grad[None],
    )


def solution(mesh):
    section_count, dp_count = mesh.devices.shape
    fine = Mesh(
        mesh.devices.reshape(section_count, dp_count // 2, 2), ("section", "pair", "core")
    )
    dp = ("pair", "core")
    placed = (
        P(dp, None),
        P(dp, None),
        P(dp, None),
        P(dp, None),
        P(None, None, ("section",) + dp),
        P("section", dp, None),
        P("section", dp, None),
        P("section", dp, None),
        P("section", dp, None),
        P("section", dp, None),
        P("section", dp, None),
        P(dp, None),
    )
    return jax.shard_map(
        per_device,
        mesh=fine,
        in_specs=placed,
        out_specs=(
            P(dp, "section"),
            P(dp, "section"),
            P(dp, None),
            P(None, None, ("section",) + dp),
            P("section", dp, None),
            P("section", dp, None),
            P("section", dp, None),
            P("section", dp, None),
            P("section", dp, None),
            P("section", dp, None),
        ),
        check_vma=False,
    )
```

```python
import math

import jax
import jax.numpy as jnp
from jax import lax
from jax.sharding import Mesh, PartitionSpec as P

HEAD_DIM = 96
LATENTS = 64
LAYERS = 2

epsilon = 1e-05
low = jnp.bfloat16
full = jnp.float32


def unit_rows(values):
    centered = values - jnp.mean(values, axis=-1, keepdims=True)
    variance = jnp.mean(centered * centered, axis=-1, keepdims=True)
    inverse = lax.rsqrt(variance + epsilon)
    return centered * inverse, inverse


def norm_back(unit, inverse, scaled):
    first = jnp.mean(scaled, axis=-1, keepdims=True)
    second = jnp.mean(scaled * unit, axis=-1, keepdims=True)
    return (scaled - first - unit * second) * inverse


def gelu_exact(values):
    return 0.5 * values * (1.0 + lax.erf(values * math.sqrt(0.5)))


def gelu_slope(values):
    normal = 0.5 * (1.0 + lax.erf(values * math.sqrt(0.5)))
    return normal + values * jnp.exp(-0.5 * values * values) * (1.0 / math.sqrt(2.0 * math.pi))


def matmul(left, right):
    return jnp.dot(left, right, preferred_element_type=full)


def matmul_nt(left, right):
    return lax.dot_general(left, right, (((1,), (1,)), ((), ())), preferred_element_type=full)


def matmul_tn(left, right):
    return lax.dot_general(left, right, (((0,), (0,)), ((), ())), preferred_element_type=full)


def attend_forward(query_heads, key_heads, value_heads, allowed, score_scale):
    scores = jnp.einsum("qhd,khd->hqk", query_heads, key_heads, preferred_element_type=full)
    scores = jnp.where(allowed, scores * score_scale, -1e30)
    row_max = jnp.max(scores, axis=-1, keepdims=True)
    exponent = jnp.exp(scores - row_max)
    row_total = jnp.sum(exponent, axis=-1, keepdims=True)
    weights_low = (exponent / row_total).astype(low)
    attended = jnp.einsum("hqk,khd->qhd", weights_low, value_heads, preferred_element_type=full)
    return attended, row_max + jnp.log(row_total)


def attend_backward(
    query_heads, key_heads, value_heads, allowed, score_scale, log_total, grad_heads
):
    scores = jnp.einsum("qhd,khd->hqk", query_heads, key_heads, preferred_element_type=full)
    scores = jnp.where(allowed, scores * score_scale, -1e30)
    weights_full = jnp.exp(scores - log_total)
    weights_low = weights_full.astype(low)
    grad_value = jnp.einsum("hqk,qhd->khd", weights_low, grad_heads, preferred_element_type=full)
    grad_weights = jnp.einsum(
        "qhd,khd->hqk", grad_heads, value_heads, preferred_element_type=full
    )
    row_inner = jnp.sum(weights_full * grad_weights, axis=-1, keepdims=True)
    grad_scores = (weights_full * (grad_weights - row_inner)).astype(low)
    grad_query = (
        jnp.einsum("hqk,khd->qhd", grad_scores, key_heads, preferred_element_type=full)
        * score_scale
    )
    grad_key = (
        jnp.einsum("hqk,qhd->khd", grad_scores, query_heads, preferred_element_type=full)
        * score_scale
    )
    return grad_query, grad_key, grad_value


def per_device(
    latents,
    media,
    segment_ids,
    slot_map,
    gains,
    w_query,
    w_key,
    w_value,
    w_out,
    w_up,
    w_down,
    cotangent,
):
    dp = ("pair", "core")
    everywhere = ("section",) + dp
    section = lax.axis_index("section")
    section_count = lax.axis_size("section")
    dp_index = lax.axis_index(dp)
    dp_count = lax.axis_size("pair") * lax.axis_size("core")
    on_first = section // 2 == 0
    stride = dp_count // 2
    seq_rows = segment_ids.shape[1]
    slot_count = slot_map.shape[1]
    feature_width = latents.shape[1]
    latent_rows = latents.shape[0]
    slot_rows = latent_rows // section_count
    inner = w_query.shape[2] // 2
    heads = inner // HEAD_DIM
    score_scale = 1.0 / math.sqrt(HEAD_DIM)

    def pick(first, second):
        return jnp.where(on_first, first, second), jnp.where(on_first, second, first)

    def swapped(value, mask):
        pairs = [(source, source ^ mask) for source in range(section_count)]
        return lax.ppermute(value, "section", pairs)

    def other_core(value):
        return lax.ppermute(value, "core", [(0, 1), (1, 0)])

    def to_second(value):
        return lax.ppermute(value, "section", [(0, 2), (1, 3)])

    def to_first(value):
        return lax.ppermute(value, "section", [(2, 0), (3, 1)])

    def after(value, earlier):
        return lax.optimization_barrier((value, earlier))[0]

    def turn_pairs(span, flip, back):
        pairs = []
        for source in range(section_count):
            for index in range(dp_count):
                layer, half = divmod(source, 2)
                high, bit, lowest = index // (2 * span), index // span % 2, index % span
                moved = (2 * high + (layer ^ flip)) * span + lowest
                target = (bit * 2 + half) * dp_count + moved
                pair = (source * dp_count + index, target)
                pairs.append(pair[::-1] if back else pair)
        return pairs

    def first_bit(span):
        return dp_index // span % 2 == 0

    def exchange_rows(weight, span):
        half = weight.shape[0] // 2
        near, far = pick(weight[:half], weight[half:])
        first = lax.ppermute(near, everywhere, turn_pairs(span, 0, False))
        second = lax.ppermute(far, everywhere, turn_pairs(span, 1, False))
        chosen = first_bit(span)
        return jnp.where(chosen, first, second), jnp.where(chosen, second, first)

    def join_rows(first, second, span):
        chosen = first_bit(span)
        near = jnp.where(chosen, first, second)
        far = jnp.where(chosen, second, first)
        near = lax.ppermute(near, everywhere, turn_pairs(span, 0, True))
        far = lax.ppermute(far, everywhere, turn_pairs(span, 1, True))
        return jnp.concatenate(pick(near, far), axis=0).astype(full)

    def exchange_second(weight, span):
        half = weight.shape[0] // 2
        parts = []
        for bit in range(2):
            pairs = [
                pair
                for flip in range(2)
                for pair in turn_pairs(span, flip, False)
                if pair[0] >= 2 * dp_count and pair[1] // span % 2 == bit
            ]
            parts.append(lax.ppermute(weight[bit * half : (bit + 1) * half], everywhere, pairs))
        return jnp.where(first_bit(span), parts[0], parts[1])

    def join_second(piece, span):
        parts = []
        for bit in range(2):
            pairs = [
                pair[::-1]
                for flip in range(2)
                for pair in turn_pairs(span, flip, False)
                if pair[0] >= 2 * dp_count and pair[1] // span % 2 == bit
            ]
            parts.append(lax.ppermute(piece, everywhere, pairs))
        return jnp.concatenate(parts, axis=0)

    def in_rows(gathered, span):
        if span > 1:
            width = gathered.shape[1]
            gathered = gathered.reshape(-1, 2, span, gathered.shape[0] // dp_count, width)
            gathered = gathered.swapaxes(1, 2).reshape(-1, width)
        return gathered

    def in_shards(grad, span):
        if span > 1:
            width = grad.shape[1]
            grad = grad.reshape(-1, span, 2, grad.shape[0] // dp_count, width)
            grad = grad.swapaxes(1, 2).reshape(-1, width)
        return grad

    def fold(piece):
        blocks = [piece[:, i * inner : (i + 1) * inner] for i in range(feature_width // inner)]
        return jnp.concatenate(blocks, axis=0)

    def unfold(stacked):
        count = feature_width // inner
        blocks = stacked.reshape(2, stride, count, -1, inner).transpose(1, 0, 3, 2, 4)
        return blocks.reshape(-1, feature_width)

    def by_device(grad):
        blocks = grad.reshape(stride, 2, -1, feature_width).transpose(1, 0, 2, 3)
        return blocks.reshape(-1, feature_width)

    def sum_to_slots(partial):
        blocks = partial.astype(low).reshape(section_count, -1, feature_width)
        arrived = lax.all_to_all(blocks, "section", split_axis=0, concat_axis=0)
        return jnp.sum(arrived.astype(full), axis=0)

    def from_slots(rows):
        return lax.all_gather(rows, "section", axis=0, tiled=True)

    def to_columns(rows):
        moved = lax.all_to_all(
            rows.astype(low), "section", split_axis=1, concat_axis=0, tiled=True
        )
        return moved.astype(full)

    def from_sequences(rows):
        near = lax.all_gather(rows, "pair", axis=0, tiled=True)
        return jnp.concatenate([near, other_core(near)], axis=0)

    def sum_to_sequence(left, right, product):
        half = left.shape[0] // 2
        far = product(left[half:], right).astype(low)
        near = product(left[:half], right) + other_core(far).astype(full)
        blocks = near.astype(low).reshape(-1, slot_rows, feature_width)
        arrived = lax.all_to_all(blocks, "pair", split_axis=0, concat_axis=0)
        return jnp.sum(arrived.astype(full), axis=0)

    def by_distance(rows):
        half = rows.shape[0] // 2
        side = swapped(rows, 1)
        ahead = swapped(rows, 2)
        upper = swapped(side[:half], 2)
        lower = swapped(ahead[half:], 1)
        return rows, side, ahead, jnp.concatenate([upper, lower], axis=0)

    def sum_by_distance(own, side, ahead, across, gate=None):
        half = own.shape[0] // 2
        across = across.astype(low)
        upper = swapped(across[:half], 2)
        lower = swapped(across[half:], 1)
        if gate is not None:
            upper, lower = after((upper, lower), gate)
        side = jnp.concatenate([side[:half] + upper.astype(full), side[half:]], axis=0)
        ahead = jnp.concatenate([ahead[:half], ahead[half:] + lower.astype(full)], axis=0)
        side, ahead = side.astype(low), ahead.astype(low)
        return own + swapped(side, 1).astype(full) + swapped(ahead, 2).astype(full)

    def share_first(lower, upper):
        return jnp.where(on_first, lower, to_second(upper))

    def sum_over_sections(partial):
        blocks = partial.reshape(section_count, -1, feature_width)
        return sum_by_distance(
            *[
                lax.dynamic_index_in_dim(blocks, section ^ mask, 0, keepdims=False)
                for mask in range(4)
            ]
        )

    def gather_sections(rows):
        by_mask = by_distance(rows)
        ordered = []
        for target in range(section_count):
            chosen = by_mask[0]
            for mask in range(1, section_count):
                chosen = jnp.where(section ^ mask == target, by_mask[mask], chosen)
            ordered.append(chosen)
        return jnp.concatenate(ordered, axis=0)

    def column_parts(weight, block):
        rows, width = weight.shape
        split = weight.reshape(rows, width // (2 * block), 2, block)
        return split[:, :, 0].reshape(rows, -1), split[:, :, 1].reshape(rows, -1)

    def interleave(even, odd, block):
        rows, width = even.shape
        parts = [part.reshape(rows, width // block, 1, block) for part in (even, odd)]
        return jnp.concatenate(parts, axis=2).reshape(rows, 2 * width)

    halves = [pick(weight[0, :, :inner], weight[0, :, inner:]) for weight in (w_query, w_key, w_value)]
    own_heads = jnp.concatenate([half[0] for half in halves], axis=1)
    other_heads = swapped(jnp.concatenate([half[1] for half in halves], axis=1), 2)
    qkv_pieces = pick(own_heads, other_heads)
    half_hidden = w_down.shape[1] // 2
    half_depth = w_up.shape[1] // 2
    up_share = share_first(w_up[0, :half_depth], w_up[0, half_depth:])
    all_gains = after(gains, (other_heads, up_share))
    for axis in ("core", "pair", "section"):
        all_gains = lax.all_gather(all_gains, axis, axis=2, tiled=True)
    out_pieces = exchange_rows(after(w_out[0], other_heads), stride)

    def gather(piece):
        return lax.all_gather(piece, dp, axis=0, tiled=True)

    stacked = [
        gather(jnp.concatenate([qkv_pieces[layer], fold(out_pieces[layer])], axis=1))
        for layer in range(LAYERS)
    ]
    qkv_w = [weight[:, : 3 * inner] for weight in stacked]
    out_w = [unfold(weight[:, 3 * inner :]) for weight in stacked]

    up_turned = lax.all_to_all(up_share, dp, split_axis=1, concat_axis=0, tiled=True)
    down_share = share_first(
        *after((w_down[0, :half_hidden], w_down[0, half_hidden:]), other_heads)
    )

    def by_depth(rows):
        return rows.reshape(-1, dp_count, 2, half_depth).swapaxes(1, 2).reshape(rows.shape)

    def in_depth(rows):
        return rows.reshape(-1, 2, dp_count, half_depth).swapaxes(1, 2).reshape(rows.shape)

    def first_ffn(gate):
        down, up = after((down_share, up_turned), gate)
        down, up = by_distance(down), by_distance(up)
        return (
            jnp.concatenate(
                [
                    jnp.concatenate(pick(up[0], up[2]), axis=0),
                    jnp.concatenate(pick(up[1], up[3]), axis=0),
                ],
                axis=1,
            ),
            jnp.concatenate(pick(down[0], down[2]) + pick(down[1], down[3]), axis=0),
        )

    span = max(1, dp_count // 8)
    hidden_block = w_up.shape[2] // 8
    down_piece = exchange_second(after(w_down[0], all_gains), span)

    def second_ffn(gate):
        up_even, up_odd = column_parts(after(w_up[0], gate), hidden_block)
        return gather(jnp.where(on_first, to_first(up_even), up_odd))

    up_w = [None, None]
    down_w = [None, None]
    query_w = [weight[:, :inner] for weight in qkv_w]
    key_w = [weight[:, inner : 2 * inner] for weight in qkv_w]
    value_w = [weight[:, 2 * inner :] for weight in qkv_w]

    image_hot = segment_ids[:, :, None] == jnp.arange(slot_count, dtype=jnp.int32)[None, None, :]
    media_slot = jnp.sum(jnp.where(image_hot, slot_map[:, None, :], 0), axis=2) - (
        segment_ids < 0
    ).astype(jnp.int32)
    media_unit, media_inverse = unit_rows(media.astype(full))
    latent_slot = jnp.arange(latent_rows, dtype=jnp.int32) // LATENTS
    key_slot = jnp.concatenate([media_slot[0], latent_slot])
    allowed = latent_slot[None, :, None] == key_slot[None, None, :]

    def split_heads(rows):
        return rows.reshape(rows.shape[0], heads, HEAD_DIM)

    media_low = []
    media_key = []
    media_value = []
    for layer in range(LAYERS):
        media_low.append((media_unit * all_gains[layer, 0]).astype(low))
        media_key.append(matmul(media_low[layer], key_w[layer]).astype(low))
        media_value.append(matmul(media_low[layer], value_w[layer]).astype(low))

    down_second = in_rows(gather(down_piece), span)
    saved = []
    current = lax.dynamic_slice_in_dim(latents, section * slot_rows, slot_rows, 0).astype(full)
    grad_rows = lax.dynamic_slice_in_dim(cotangent, section * slot_rows, slot_rows, 0).astype(full)
    grad_low = cotangent
    for layer in range(LAYERS):
        unit_in, inverse_in = unit_rows(current)
        if layer == 0:
            whole_unit = unit_rows(latents.astype(full))[0]
            latent_low = (whole_unit * all_gains[layer, 1]).astype(low)
        else:
            latent_low = from_slots((unit_in * all_gains[layer, 1]).astype(low))
        projected = matmul(latent_low, qkv_w[layer]).astype(low)
        if layer == 0:
            up_w[0], down_w[0] = lax.optimization_barrier(first_ffn(projected))
            up_w[1], down_w[1] = second_ffn(projected), down_second
        query_low = projected[:, :inner]
        key_heads = split_heads(
            jnp.concatenate([media_key[layer], projected[:, inner : 2 * inner]], axis=0)
        )
        value_heads = split_heads(
            jnp.concatenate([media_value[layer], projected[:, 2 * inner :]], axis=0)
        )
        query_heads = split_heads(query_low)
        attended, log_total = attend_forward(
            query_heads, key_heads, value_heads, allowed, score_scale
        )
        attended_low = attended.reshape(-1, inner).astype(low)
        middle = current + sum_to_slots(matmul(attended_low, out_w[layer]))
        unit_mid, inverse_mid = unit_rows(middle)
        ffn_low = (unit_mid * all_gains[layer, 2]).astype(low)
        ffn_low = from_slots(ffn_low) if layer else from_sequences(by_depth(ffn_low))
        hidden_pre = matmul(ffn_low, up_w[layer])
        active_low = gelu_exact(hidden_pre).astype(low)
        if layer == 0:
            current = middle + sum_to_sequence(active_low, down_w[layer], matmul)
        saved.append(
            (
                unit_in,
                inverse_in,
                latent_low,
                query_heads,
                key_heads,
                value_heads,
                log_total,
                attended_low,
                unit_mid,
                inverse_mid,
                ffn_low,
                hidden_pre,
                active_low,
            )
        )

    def scatter(blocks):
        return lax.psum_scatter(blocks, dp, scatter_dimension=0, tiled=True)

    gain_rows = [None] * LAYERS
    media_parts = []
    media_gains = []

    def add_media(layer, grad_key, grad_value, gate):
        grad_key, grad_value = after((grad_key[:seq_rows], grad_value[:seq_rows]), gate)
        part = matmul_nt(grad_key, key_w[layer]) + matmul_nt(grad_value, value_w[layer])
        media_gains.append(jnp.sum(part * media_unit, axis=0))
        media_parts.append((part * all_gains[layer, 0]).astype(low if layer else full))

    pieces = [None] * LAYERS
    for layer in (1, 0):
        (
            unit_in,
            inverse_in,
            latent_low,
            query_heads,
            key_heads,
            value_heads,
            log_total,
            attended_low,
            unit_mid,
            inverse_mid,
            ffn_low,
            hidden_pre,
            active_low,
        ) = saved[layer]
        grad_active = matmul_nt(grad_low, down_w[layer])
        grad_hidden = (grad_active * gelu_slope(hidden_pre)).astype(low)
        if layer == 0:
            add_media(1, *media_grads, grad_hidden)
        down_grad = matmul_tn(active_low, grad_low)
        if layer:
            down_grad = down_grad.astype(low)
            grad_hidden = after(grad_hidden, down_grad)
        up_grad = matmul_tn(ffn_low, grad_hidden)
        if layer:
            ffn_pieces = (scatter(in_shards(down_grad, span)), scatter(up_grad.astype(low)))
            ffn_grad = sum_to_slots(matmul_nt(grad_hidden, up_w[layer]))
        else:
            ffn_grad = in_depth(sum_to_sequence(grad_hidden, up_w[layer], matmul_nt))
            blocks = down_grad.reshape(2, 2, half_hidden, feature_width)
            own, ahead = pick(blocks[0, 0], blocks[0, 1])
            side, across = pick(blocks[1, 0], blocks[1, 1])
            down_blocks = (own, side, ahead, across)
            width = up_grad.shape[1] // 2
            blocks = up_grad.reshape(2, -1, 2 * width)
            own, ahead = pick(blocks[0][:, :width], blocks[1][:, :width])
            side, across = pick(blocks[0][:, width:], blocks[1][:, width:])
            up_blocks = (own, side, ahead, across)
        gain_ffn_grad = jnp.sum(ffn_grad * unit_mid, axis=0)
        grad_middle = grad_rows + norm_back(
            unit_mid, inverse_mid, ffn_grad * all_gains[layer, 2]
        )
        middle_low = from_slots(grad_middle.astype(low))
        if layer == 0:
            up_half = sum_by_distance(*up_blocks, middle_low).astype(low)
            down_half = sum_by_distance(*down_blocks, middle_low).astype(low)
        grad_heads = split_heads(matmul_nt(middle_low, out_w[layer]).astype(low))
        out_grad = by_device(matmul_tn(attended_low, middle_low)).astype(low)
        out_piece = scatter(out_grad)
        grad_heads = after(grad_heads, out_grad)
        grad_query, grad_key, grad_value = attend_backward(
            query_heads, key_heads, value_heads, allowed, score_scale, log_total, grad_heads
        )
        grad_query = grad_query.reshape(-1, inner).astype(low)
        grad_key = grad_key.reshape(-1, inner).astype(low)
        grad_value = grad_value.reshape(-1, inner).astype(low)
        both_low = jnp.concatenate([media_low[layer], latent_low], axis=0)
        all_grads = jnp.concatenate(
            [jnp.pad(grad_query, ((seq_rows, 0), (0, 0))), grad_key, grad_value], axis=1
        )
        qkv_grad = matmul_tn(both_low, all_grads).astype(low)
        latent_part = (
            matmul_nt(grad_query, query_w[layer])
            + matmul_nt(grad_key[seq_rows:], key_w[layer])
            + matmul_nt(grad_value[seq_rows:], value_w[layer])
        )
        latent_grad_rows = sum_to_slots(latent_part)
        if layer:
            latent_grad_rows = after(latent_grad_rows, qkv_grad)
        gain_latent_grad = jnp.sum(latent_grad_rows * unit_in, axis=0)
        grad_rows = grad_middle + norm_back(
            unit_in, inverse_in, latent_grad_rows * all_gains[layer, 1]
        )
        if layer == 0:
            up_half, qkv_grad = lax.optimization_barrier((up_half, qkv_grad))
            up_half = lax.all_to_all(up_half, dp, split_axis=0, concat_axis=1, tiled=True)
        pieces[layer] = (scatter(qkv_grad), out_piece)
        if layer > 0:
            grad_low = from_sequences(grad_rows.astype(low))
            late = after(active_low, latent_part)
            here = (latent_slot == section)[:, None]
            kept = jnp.where(here, jnp.tile(middle, (section_count, 1)), 0.0)
            last = lax.optimization_barrier((matmul(late, down_w[layer]) + kept).astype(low))
            last = last.reshape(latent_rows, section_count, -1).swapaxes(0, 1)
            last = lax.all_to_all(last, "section", split_axis=0, concat_axis=0)
            latents_out = jnp.sum(last.astype(full), axis=0)
            grad_low = after(grad_low, latents_out)
            grad_low = after(grad_low, ffn_pieces)
        if layer == 0:
            add_media(0, grad_key, grad_value, qkv_grad)
        else:
            media_grads = (grad_key, grad_value)
        gain_rows[layer] = (gain_latent_grad, gain_ffn_grad)
    out_grad = join_rows(*[piece[1] for piece in pieces], stride)
    latent_grad = to_columns(after(grad_rows, (pieces[1], up_half)))
    media_rows = seq_rows // section_count
    media_sum = sum_over_sections(media_parts[0].astype(full) + media_parts[1])
    own_unit = lax.dynamic_slice_in_dim(media_unit, section * media_rows, media_rows, 0)
    own_inverse = lax.dynamic_slice_in_dim(media_inverse, section * media_rows, media_rows, 0)
    media_grad = gather_sections(norm_back(own_unit, own_inverse, media_sum).astype(low)).astype(
        full
    )
    gain_rows = [
        jnp.stack([media_gains[1 - layer], *gain_rows[layer]]) for layer in range(LAYERS)
    ]
    gain_parts = jnp.stack(gain_rows).reshape(LAYERS, 3, section_count, -1)
    gain_parts = jnp.sum(
        lax.all_to_all(gain_parts, "section", split_axis=2, concat_axis=2), axis=2
    )
    gain_parts = gain_parts.reshape(LAYERS, 3, dp_count, -1)
    gain_grad = jnp.sum(lax.all_to_all(gain_parts, dp, split_axis=2, concat_axis=2), axis=2)

    qkv_parts = [piece[0] for piece in pieces]
    own, other = pick(qkv_parts[0], qkv_parts[1])
    lower, upper = pick(own, swapped(other, 2))
    qkv_grads = [
        jnp.concatenate(
            [lower[:, i * inner : (i + 1) * inner], upper[:, i * inner : (i + 1) * inner]], axis=1
        ).astype(full)
        for i in range(3)
    ]
    down_piece, up_piece = ffn_pieces
    up_second_grad = interleave(to_second(up_piece), up_piece, hidden_block)
    down_second_grad = join_second(down_piece, span)
    up_first_grad = jnp.concatenate([up_half, to_first(up_half)], axis=0)
    down_first_grad = jnp.concatenate([down_half, to_first(down_half)], axis=0)
    up_grad = jnp.where(on_first, up_first_grad, up_second_grad).astype(full)
    down_grad = jnp.where(on_first, down_first_grad, down_second_grad).astype(full)
    return (
        latents_out,
        latent_grad,
        media_grad,
        gain_grad,
        qkv_grads[0][None],
        qkv_grads[1][None],
        qkv_grads[2][None],
        out_grad[None],
        up_grad[None],
        down_grad[None],
    )


def solution(mesh):
    section_count, dp_count = mesh.devices.shape
    fine = Mesh(
        mesh.devices.reshape(section_count, dp_count // 2, 2), ("section", "pair", "core")
    )
    dp = ("pair", "core")
    placed = (
        P(dp, None),
        P(dp, None),
        P(dp, None),
        P(dp, None),
        P(None, None, ("section",) + dp),
        P("section", dp, None),
        P("section", dp, None),
        P("section", dp, None),
        P("section", dp, None),
        P("section", dp, None),
        P("section", dp, None),
        P(dp, None),
    )
    return jax.shard_map(
        per_device,
        mesh=fine,
        in_specs=placed,
        out_specs=(
            P(dp, "section"),
            P(dp, "section"),
            P(dp, None),
            P(None, None, ("section",) + dp),
            P("section", dp, None),
            P("section", dp, None),
            P("section", dp, None),
            P("section", dp, None),
            P("section", dp, None),
            P("section", dp, None),
        ),
        check_vma=False,
    )
```

```python
import math

import jax
import jax.numpy as jnp
from jax import lax
from jax.sharding import Mesh, PartitionSpec as P

HEAD_DIM = 96
LATENTS = 64
LAYERS = 2

epsilon = 1e-05
low = jnp.bfloat16
full = jnp.float32


def unit_rows(values):
    centered = values - jnp.mean(values, axis=-1, keepdims=True)
    variance = jnp.mean(centered * centered, axis=-1, keepdims=True)
    inverse = lax.rsqrt(variance + epsilon)
    return centered * inverse, inverse


def norm_back(unit, inverse, scaled):
    first = jnp.mean(scaled, axis=-1, keepdims=True)
    second = jnp.mean(scaled * unit, axis=-1, keepdims=True)
    return (scaled - first - unit * second) * inverse


def gelu_exact(values):
    return 0.5 * values * (1.0 + lax.erf(values * math.sqrt(0.5)))


def gelu_slope(values):
    normal = 0.5 * (1.0 + lax.erf(values * math.sqrt(0.5)))
    return normal + values * jnp.exp(-0.5 * values * values) * (1.0 / math.sqrt(2.0 * math.pi))


def matmul(left, right):
    return jnp.dot(left, right, preferred_element_type=full)


def matmul_nt(left, right):
    return lax.dot_general(left, right, (((1,), (1,)), ((), ())), preferred_element_type=full)


def matmul_tn(left, right):
    return lax.dot_general(left, right, (((0,), (0,)), ((), ())), preferred_element_type=full)


def attend_forward(query_heads, key_heads, value_heads, allowed, score_scale):
    scores = jnp.einsum("qhd,khd->hqk", query_heads, key_heads, preferred_element_type=full)
    scores = jnp.where(allowed, scores * score_scale, -1e30)
    row_max = jnp.max(scores, axis=-1, keepdims=True)
    exponent = jnp.exp(scores - row_max)
    row_total = jnp.sum(exponent, axis=-1, keepdims=True)
    weights_low = (exponent / row_total).astype(low)
    attended = jnp.einsum("hqk,khd->qhd", weights_low, value_heads, preferred_element_type=full)
    return attended, row_max + jnp.log(row_total)


def attend_backward(
    query_heads, key_heads, value_heads, allowed, score_scale, log_total, grad_heads
):
    scores = jnp.einsum("qhd,khd->hqk", query_heads, key_heads, preferred_element_type=full)
    scores = jnp.where(allowed, scores * score_scale, -1e30)
    weights_full = jnp.exp(scores - log_total)
    weights_low = weights_full.astype(low)
    grad_value = jnp.einsum("hqk,qhd->khd", weights_low, grad_heads, preferred_element_type=full)
    grad_weights = jnp.einsum(
        "qhd,khd->hqk", grad_heads, value_heads, preferred_element_type=full
    )
    row_inner = jnp.sum(weights_full * grad_weights, axis=-1, keepdims=True)
    grad_scores = (weights_full * (grad_weights - row_inner)).astype(low)
    grad_query = (
        jnp.einsum("hqk,khd->qhd", grad_scores, key_heads, preferred_element_type=full)
        * score_scale
    )
    grad_key = (
        jnp.einsum("hqk,qhd->khd", grad_scores, query_heads, preferred_element_type=full)
        * score_scale
    )
    return grad_query, grad_key, grad_value


def per_device(
    latents,
    media,
    segment_ids,
    slot_map,
    gains,
    w_query,
    w_key,
    w_value,
    w_out,
    w_up,
    w_down,
    cotangent,
):
    dp = ("pair", "core")
    everywhere = ("section",) + dp
    section = lax.axis_index("section")
    section_count = lax.axis_size("section")
    dp_index = lax.axis_index(dp)
    dp_count = lax.axis_size("pair") * lax.axis_size("core")
    on_first = section // 2 == 0
    stride = dp_count // 2
    seq_rows = segment_ids.shape[1]
    slot_count = slot_map.shape[1]
    feature_width = latents.shape[1]
    latent_rows = latents.shape[0]
    slot_rows = latent_rows // section_count
    inner = w_query.shape[2] // 2
    heads = inner // HEAD_DIM
    score_scale = 1.0 / math.sqrt(HEAD_DIM)

    def pick(first, second):
        return jnp.where(on_first, first, second), jnp.where(on_first, second, first)

    def swapped(value, mask):
        pairs = [(source, source ^ mask) for source in range(section_count)]
        return lax.ppermute(value, "section", pairs)

    def other_core(value):
        return lax.ppermute(value, "core", [(0, 1), (1, 0)])

    def to_second(value):
        return lax.ppermute(value, "section", [(0, 2), (1, 3)])

    def to_first(value):
        return lax.ppermute(value, "section", [(2, 0), (3, 1)])

    def after(value, earlier):
        return lax.optimization_barrier((value, earlier))[0]

    def turn_pairs(span, flip, back):
        pairs = []
        for source in range(section_count):
            for index in range(dp_count):
                layer, half = divmod(source, 2)
                high, bit, lowest = index // (2 * span), index // span % 2, index % span
                moved = (2 * high + (layer ^ flip)) * span + lowest
                target = (bit * 2 + half) * dp_count + moved
                pair = (source * dp_count + index, target)
                pairs.append(pair[::-1] if back else pair)
        return pairs

    def first_bit(span):
        return dp_index // span % 2 == 0

    def exchange_rows(weight, span):
        half = weight.shape[0] // 2
        near, far = pick(weight[:half], weight[half:])
        first = lax.ppermute(near, everywhere, turn_pairs(span, 0, False))
        second = lax.ppermute(far, everywhere, turn_pairs(span, 1, False))
        chosen = first_bit(span)
        return jnp.where(chosen, first, second), jnp.where(chosen, second, first)

    def join_rows(first, second, span):
        chosen = first_bit(span)
        near = jnp.where(chosen, first, second)
        far = jnp.where(chosen, second, first)
        near = lax.ppermute(near, everywhere, turn_pairs(span, 0, True))
        far = lax.ppermute(far, everywhere, turn_pairs(span, 1, True))
        return jnp.concatenate(pick(near, far), axis=0).astype(full)

    def exchange_second(weight, span):
        half = weight.shape[0] // 2
        parts = []
        for bit in range(2):
            pairs = [
                pair
                for flip in range(2)
                for pair in turn_pairs(span, flip, False)
                if pair[0] >= 2 * dp_count and pair[1] // span % 2 == bit
            ]
            parts.append(lax.ppermute(weight[bit * half : (bit + 1) * half], everywhere, pairs))
        return jnp.where(first_bit(span), parts[0], parts[1])

    def join_second(piece, span):
        parts = []
        for bit in range(2):
            pairs = [
                pair[::-1]
                for flip in range(2)
                for pair in turn_pairs(span, flip, False)
                if pair[0] >= 2 * dp_count and pair[1] // span % 2 == bit
            ]
            parts.append(lax.ppermute(piece, everywhere, pairs))
        return jnp.concatenate(parts, axis=0)

    def in_rows(gathered, span):
        if span > 1:
            width = gathered.shape[1]
            gathered = gathered.reshape(-1, 2, span, gathered.shape[0] // dp_count, width)
            gathered = gathered.swapaxes(1, 2).reshape(-1, width)
        return gathered

    def in_shards(grad, span):
        if span > 1:
            width = grad.shape[1]
            grad = grad.reshape(-1, span, 2, grad.shape[0] // dp_count, width)
            grad = grad.swapaxes(1, 2).reshape(-1, width)
        return grad

    def fold(piece):
        blocks = [piece[:, i * inner : (i + 1) * inner] for i in range(feature_width // inner)]
        return jnp.concatenate(blocks, axis=0)

    def unfold(stacked):
        count = feature_width // inner
        blocks = stacked.reshape(2, stride, count, -1, inner).transpose(1, 0, 3, 2, 4)
        return blocks.reshape(-1, feature_width)

    def by_device(grad):
        blocks = grad.reshape(stride, 2, -1, feature_width).transpose(1, 0, 2, 3)
        return blocks.reshape(-1, feature_width)

    def sum_to_slots(partial):
        blocks = partial.astype(low).reshape(section_count, -1, feature_width)
        arrived = lax.all_to_all(blocks, "section", split_axis=0, concat_axis=0)
        return jnp.sum(arrived.astype(full), axis=0)

    def from_slots(rows):
        return lax.all_gather(rows, "section", axis=0, tiled=True)

    def to_columns(rows):
        moved = lax.all_to_all(
            rows.astype(low), "section", split_axis=1, concat_axis=0, tiled=True
        )
        return moved.astype(full)

    def from_sequences(rows):
        near = lax.all_gather(rows, "pair", axis=0, tiled=True)
        return jnp.concatenate([near, other_core(near)], axis=0)

    def sum_to_sequence(left, right, product):
        half = left.shape[0] // 2
        far = product(left[half:], right).astype(low)
        near = product(left[:half], right) + other_core(far).astype(full)
        blocks = near.astype(low).reshape(-1, slot_rows, feature_width)
        arrived = lax.all_to_all(blocks, "pair", split_axis=0, concat_axis=0)
        return jnp.sum(arrived.astype(full), axis=0)

    def by_distance(rows):
        half = rows.shape[0] // 2
        side = swapped(rows, 1)
        ahead = swapped(rows, 2)
        upper = swapped(side[:half], 2)
        lower = swapped(ahead[half:], 1)
        return rows, side, ahead, jnp.concatenate([upper, lower], axis=0)

    def sum_by_distance(own, side, ahead, across, gate=None):
        half = own.shape[0] // 2
        across = across.astype(low)
        upper = swapped(across[:half], 2)
        lower = swapped(across[half:], 1)
        if gate is not None:
            upper, lower = after((upper, lower), gate)
        side = jnp.concatenate([side[:half] + upper.astype(full), side[half:]], axis=0)
        ahead = jnp.concatenate([ahead[:half], ahead[half:] + lower.astype(full)], axis=0)
        side, ahead = side.astype(low), ahead.astype(low)
        return own + swapped(side, 1).astype(full) + swapped(ahead, 2).astype(full)

    def share_first(lower, upper):
        return jnp.where(on_first, lower, to_second(upper))

    def sum_over_sections(partial):
        blocks = partial.reshape(section_count, -1, feature_width)
        return sum_by_distance(
            *[
                lax.dynamic_index_in_dim(blocks, section ^ mask, 0, keepdims=False)
                for mask in range(4)
            ]
        )

    def gather_sections(rows):
        by_mask = by_distance(rows)
        ordered = []
        for target in range(section_count):
            chosen = by_mask[0]
            for mask in range(1, section_count):
                chosen = jnp.where(section ^ mask == target, by_mask[mask], chosen)
            ordered.append(chosen)
        return jnp.concatenate(ordered, axis=0)

    def column_parts(weight, block):
        rows, width = weight.shape
        split = weight.reshape(rows, width // (2 * block), 2, block)
        return split[:, :, 0].reshape(rows, -1), split[:, :, 1].reshape(rows, -1)

    def interleave(even, odd, block):
        rows, width = even.shape
        parts = [part.reshape(rows, width // block, 1, block) for part in (even, odd)]
        return jnp.concatenate(parts, axis=2).reshape(rows, 2 * width)

    halves = [pick(weight[0, :, :inner], weight[0, :, inner:]) for weight in (w_query, w_key, w_value)]
    own_heads = jnp.concatenate([half[0] for half in halves], axis=1)
    other_heads = swapped(jnp.concatenate([half[1] for half in halves], axis=1), 2)
    qkv_pieces = pick(own_heads, other_heads)
    half_hidden = w_down.shape[1] // 2
    half_depth = w_up.shape[1] // 2
    up_share = share_first(w_up[0, :half_depth], w_up[0, half_depth:])
    all_gains = after(gains, (other_heads, up_share))
    for axis in ("core", "pair", "section"):
        all_gains = lax.all_gather(all_gains, axis, axis=2, tiled=True)
    out_pieces = exchange_rows(after(w_out[0], other_heads), stride)

    def gather(piece):
        return lax.all_gather(piece, dp, axis=0, tiled=True)

    stacked = [
        gather(jnp.concatenate([qkv_pieces[layer], fold(out_pieces[layer])], axis=1))
        for layer in range(LAYERS)
    ]
    qkv_w = [weight[:, : 3 * inner] for weight in stacked]
    out_w = [unfold(weight[:, 3 * inner :]) for weight in stacked]

    up_turned = lax.all_to_all(up_share, dp, split_axis=1, concat_axis=0, tiled=True)
    down_share = share_first(
        *after((w_down[0, :half_hidden], w_down[0, half_hidden:]), other_heads)
    )

    def by_depth(rows):
        return rows.reshape(-1, dp_count, 2, half_depth).swapaxes(1, 2).reshape(rows.shape)

    def in_depth(rows):
        return rows.reshape(-1, 2, dp_count, half_depth).swapaxes(1, 2).reshape(rows.shape)

    def first_ffn(gate):
        down, up = after((down_share, up_turned), gate)
        down, up = by_distance(down), by_distance(up)
        return (
            jnp.concatenate(
                [
                    jnp.concatenate(pick(up[0], up[2]), axis=0),
                    jnp.concatenate(pick(up[1], up[3]), axis=0),
                ],
                axis=1,
            ),
            jnp.concatenate(pick(down[0], down[2]) + pick(down[1], down[3]), axis=0),
        )

    span = max(1, dp_count // 8)
    hidden_block = w_up.shape[2] // 8
    down_piece = exchange_second(after(w_down[0], all_gains), span)

    def second_ffn(gate):
        up_even, up_odd = column_parts(after(w_up[0], gate), hidden_block)
        return gather(jnp.where(on_first, to_first(up_even), up_odd))

    up_w = [None, None]
    down_w = [None, None]
    query_w = [weight[:, :inner] for weight in qkv_w]
    key_w = [weight[:, inner : 2 * inner] for weight in qkv_w]
    value_w = [weight[:, 2 * inner :] for weight in qkv_w]

    image_hot = segment_ids[:, :, None] == jnp.arange(slot_count, dtype=jnp.int32)[None, None, :]
    media_slot = jnp.sum(jnp.where(image_hot, slot_map[:, None, :], 0), axis=2) - (
        segment_ids < 0
    ).astype(jnp.int32)
    media_unit, media_inverse = unit_rows(media.astype(full))
    latent_slot = jnp.arange(latent_rows, dtype=jnp.int32) // LATENTS
    key_slot = jnp.concatenate([media_slot[0], latent_slot])
    allowed = latent_slot[None, :, None] == key_slot[None, None, :]

    def split_heads(rows):
        return rows.reshape(rows.shape[0], heads, HEAD_DIM)

    media_low = []
    media_key = []
    media_value = []
    for layer in range(LAYERS):
        media_low.append((media_unit * all_gains[layer, 0]).astype(low))
        media_key.append(matmul(media_low[layer], key_w[layer]).astype(low))
        media_value.append(matmul(media_low[layer], value_w[layer]).astype(low))

    down_second = in_rows(gather(down_piece), span)
    saved = []
    current = lax.dynamic_slice_in_dim(latents, section * slot_rows, slot_rows, 0).astype(full)
    grad_rows = lax.dynamic_slice_in_dim(cotangent, section * slot_rows, slot_rows, 0).astype(full)
    grad_low = cotangent
    for layer in range(LAYERS):
        unit_in, inverse_in = unit_rows(current)
        if layer == 0:
            whole_unit = unit_rows(latents.astype(full))[0]
            latent_low = (whole_unit * all_gains[layer, 1]).astype(low)
        else:
            latent_low = from_slots((unit_in * all_gains[layer, 1]).astype(low))
        projected = matmul(latent_low, qkv_w[layer]).astype(low)
        if layer == 0:
            up_w[0], down_w[0] = lax.optimization_barrier(first_ffn(projected))
            up_w[1], down_w[1] = second_ffn(projected), down_second
        query_low = projected[:, :inner]
        key_heads = split_heads(
            jnp.concatenate([media_key[layer], projected[:, inner : 2 * inner]], axis=0)
        )
        value_heads = split_heads(
            jnp.concatenate([media_value[layer], projected[:, 2 * inner :]], axis=0)
        )
        query_heads = split_heads(query_low)
        attended, log_total = attend_forward(
            query_heads, key_heads, value_heads, allowed, score_scale
        )
        attended_low = attended.reshape(-1, inner).astype(low)
        middle = current + sum_to_slots(matmul(attended_low, out_w[layer]))
        unit_mid, inverse_mid = unit_rows(middle)
        ffn_low = (unit_mid * all_gains[layer, 2]).astype(low)
        ffn_low = from_slots(ffn_low) if layer else from_sequences(by_depth(ffn_low))
        hidden_pre = matmul(ffn_low, up_w[layer])
        active_low = gelu_exact(hidden_pre).astype(low)
        if layer == 0:
            current = middle + sum_to_sequence(active_low, down_w[layer], matmul)
        saved.append(
            (
                unit_in,
                inverse_in,
                latent_low,
                query_heads,
                key_heads,
                value_heads,
                log_total,
                attended_low,
                unit_mid,
                inverse_mid,
                ffn_low,
                hidden_pre,
                active_low,
            )
        )

    def scatter(blocks):
        return lax.psum_scatter(blocks, dp, scatter_dimension=0, tiled=True)

    gain_rows = [None] * LAYERS
    media_parts = []
    media_gains = []

    def add_media(layer, grad_key, grad_value, gate):
        grad_key, grad_value = after((grad_key[:seq_rows], grad_value[:seq_rows]), gate)
        part = matmul_nt(grad_key, key_w[layer]) + matmul_nt(grad_value, value_w[layer])
        media_gains.append(jnp.sum(part * media_unit, axis=0))
        media_parts.append((part * all_gains[layer, 0]).astype(low if layer else full))

    pieces = [None] * LAYERS
    for layer in (1, 0):
        (
            unit_in,
            inverse_in,
            latent_low,
            query_heads,
            key_heads,
            value_heads,
            log_total,
            attended_low,
            unit_mid,
            inverse_mid,
            ffn_low,
            hidden_pre,
            active_low,
        ) = saved[layer]
        grad_active = matmul_nt(grad_low, down_w[layer])
        grad_hidden = (grad_active * gelu_slope(hidden_pre)).astype(low)
        if layer == 0:
            add_media(1, *media_grads, grad_hidden)
        down_grad = matmul_tn(active_low, grad_low)
        if layer:
            down_grad = down_grad.astype(low)
            grad_hidden = after(grad_hidden, down_grad)
        up_grad = matmul_tn(ffn_low, grad_hidden)
        if layer:
            ffn_pieces = (scatter(in_shards(down_grad, span)), scatter(up_grad.astype(low)))
            ffn_grad = sum_to_slots(matmul_nt(grad_hidden, up_w[layer]))
        else:
            ffn_grad = in_depth(sum_to_sequence(grad_hidden, up_w[layer], matmul_nt))
            blocks = down_grad.reshape(2, 2, half_hidden, feature_width)
            own, ahead = pick(blocks[0, 0], blocks[0, 1])
            side, across = pick(blocks[1, 0], blocks[1, 1])
            down_blocks = (own, side, ahead, across)
            width = up_grad.shape[1] // 2
            blocks = up_grad.reshape(2, -1, 2 * width)
            own, ahead = pick(blocks[0][:, :width], blocks[1][:, :width])
            side, across = pick(blocks[0][:, width:], blocks[1][:, width:])
            up_blocks = (own, side, ahead, across)
        gain_ffn_grad = jnp.sum(ffn_grad * unit_mid, axis=0)
        grad_middle = grad_rows + norm_back(
            unit_mid, inverse_mid, ffn_grad * all_gains[layer, 2]
        )
        middle_low = grad_middle.astype(low)
        if layer == 0:
            middle_low = after(middle_low, latents_out)
        middle_low = from_slots(middle_low)
        if layer == 0:
            up_half = sum_by_distance(*up_blocks, middle_low).astype(low)
            down_half = sum_by_distance(*down_blocks, middle_low).astype(low)
        grad_heads = split_heads(matmul_nt(middle_low, out_w[layer]).astype(low))
        out_grad = by_device(matmul_tn(attended_low, middle_low)).astype(low)
        out_piece = scatter(out_grad)
        grad_heads = after(grad_heads, out_grad)
        grad_query, grad_key, grad_value = attend_backward(
            query_heads, key_heads, value_heads, allowed, score_scale, log_total, grad_heads
        )
        grad_query = grad_query.reshape(-1, inner).astype(low)
        grad_key = grad_key.reshape(-1, inner).astype(low)
        grad_value = grad_value.reshape(-1, inner).astype(low)
        both_low = jnp.concatenate([media_low[layer], latent_low], axis=0)
        all_grads = jnp.concatenate(
            [jnp.pad(grad_query, ((seq_rows, 0), (0, 0))), grad_key, grad_value], axis=1
        )
        qkv_grad = matmul_tn(both_low, all_grads).astype(low)
        latent_part = (
            matmul_nt(grad_query, query_w[layer])
            + matmul_nt(grad_key[seq_rows:], key_w[layer])
            + matmul_nt(grad_value[seq_rows:], value_w[layer])
        )
        latent_grad_rows = sum_to_slots(latent_part)
        if layer:
            latent_grad_rows = after(latent_grad_rows, qkv_grad)
        gain_latent_grad = jnp.sum(latent_grad_rows * unit_in, axis=0)
        grad_rows = grad_middle + norm_back(
            unit_in, inverse_in, latent_grad_rows * all_gains[layer, 1]
        )
        if layer == 0:
            up_half, qkv_grad = lax.optimization_barrier((up_half, qkv_grad))
            up_half = lax.all_to_all(up_half, dp, split_axis=0, concat_axis=1, tiled=True)
        pieces[layer] = (scatter(qkv_grad), out_piece)
        if layer > 0:
            grad_low = from_sequences(grad_rows.astype(low))
            late = after(active_low, grad_low)
            here = (latent_slot == section)[:, None]
            kept = jnp.where(here, jnp.tile(middle, (section_count, 1)), 0.0)
            last = lax.optimization_barrier((matmul(late, down_w[layer]) + kept).astype(low))
            last = last.reshape(latent_rows, section_count, -1).swapaxes(0, 1)
            last = lax.all_to_all(last, "section", split_axis=0, concat_axis=0)
            latents_out = jnp.sum(last.astype(full), axis=0)
            grad_low = after(grad_low, ffn_pieces)
        if layer == 0:
            add_media(0, grad_key, grad_value, qkv_grad)
        else:
            media_grads = (grad_key, grad_value)
        gain_rows[layer] = (gain_latent_grad, gain_ffn_grad)
    out_grad = join_rows(*[piece[1] for piece in pieces], stride)
    latent_grad = to_columns(after(grad_rows, (pieces[1], up_half)))
    media_rows = seq_rows // section_count
    media_sum = sum_over_sections(media_parts[0].astype(full) + media_parts[1])
    own_unit = lax.dynamic_slice_in_dim(media_unit, section * media_rows, media_rows, 0)
    own_inverse = lax.dynamic_slice_in_dim(media_inverse, section * media_rows, media_rows, 0)
    media_grad = gather_sections(norm_back(own_unit, own_inverse, media_sum).astype(low)).astype(
        full
    )
    gain_rows = [
        jnp.stack([media_gains[1 - layer], *gain_rows[layer]]) for layer in range(LAYERS)
    ]
    gain_parts = jnp.stack(gain_rows).reshape(LAYERS, 3, section_count, -1)
    gain_parts = jnp.sum(
        lax.all_to_all(gain_parts, "section", split_axis=2, concat_axis=2), axis=2
    )
    gain_parts = gain_parts.reshape(LAYERS, 3, dp_count, -1)
    gain_grad = jnp.sum(lax.all_to_all(gain_parts, dp, split_axis=2, concat_axis=2), axis=2)

    qkv_parts = [piece[0] for piece in pieces]
    own, other = pick(qkv_parts[0], qkv_parts[1])
    lower, upper = pick(own, swapped(other, 2))
    qkv_grads = [
        jnp.concatenate(
            [lower[:, i * inner : (i + 1) * inner], upper[:, i * inner : (i + 1) * inner]], axis=1
        ).astype(full)
        for i in range(3)
    ]
    down_piece, up_piece = ffn_pieces
    up_second_grad = interleave(to_second(up_piece), up_piece, hidden_block)
    down_second_grad = join_second(down_piece, span)
    up_first_grad = jnp.concatenate([up_half, to_first(up_half)], axis=0)
    down_first_grad = jnp.concatenate([down_half, to_first(down_half)], axis=0)
    up_grad = jnp.where(on_first, up_first_grad, up_second_grad).astype(full)
    down_grad = jnp.where(on_first, down_first_grad, down_second_grad).astype(full)
    return (
        latents_out,
        latent_grad,
        media_grad,
        gain_grad,
        qkv_grads[0][None],
        qkv_grads[1][None],
        qkv_grads[2][None],
        out_grad[None],
        up_grad[None],
        down_grad[None],
    )


def solution(mesh):
    section_count, dp_count = mesh.devices.shape
    fine = Mesh(
        mesh.devices.reshape(section_count, dp_count // 2, 2), ("section", "pair", "core")
    )
    dp = ("pair", "core")
    placed = (
        P(dp, None),
        P(dp, None),
        P(dp, None),
        P(dp, None),
        P(None, None, ("section",) + dp),
        P("section", dp, None),
        P("section", dp, None),
        P("section", dp, None),
        P("section", dp, None),
        P("section", dp, None),
        P("section", dp, None),
        P(dp, None),
    )
    return jax.shard_map(
        per_device,
        mesh=fine,
        in_specs=placed,
        out_specs=(
            P(dp, "section"),
            P(dp, "section"),
            P(dp, None),
            P(None, None, ("section",) + dp),
            P("section", dp, None),
            P("section", dp, None),
            P("section", dp, None),
            P("section", dp, None),
            P("section", dp, None),
            P("section", dp, None),
        ),
        check_vma=False,
    )
```

```python
import math

import jax
import jax.numpy as jnp
from jax import lax
from jax.sharding import Mesh, PartitionSpec as P

HEAD_DIM = 96
LATENTS = 64
LAYERS = 2

epsilon = 1e-05
low = jnp.bfloat16
full = jnp.float32


def unit_rows(values):
    centered = values - jnp.mean(values, axis=-1, keepdims=True)
    variance = jnp.mean(centered * centered, axis=-1, keepdims=True)
    inverse = lax.rsqrt(variance + epsilon)
    return centered * inverse, inverse


def norm_back(unit, inverse, scaled):
    first = jnp.mean(scaled, axis=-1, keepdims=True)
    second = jnp.mean(scaled * unit, axis=-1, keepdims=True)
    return (scaled - first - unit * second) * inverse


def gelu_exact(values):
    return 0.5 * values * (1.0 + lax.erf(values * math.sqrt(0.5)))


def gelu_slope(values):
    normal = 0.5 * (1.0 + lax.erf(values * math.sqrt(0.5)))
    return normal + values * jnp.exp(-0.5 * values * values) * (1.0 / math.sqrt(2.0 * math.pi))


def matmul(left, right):
    return jnp.dot(left, right, preferred_element_type=full)


def matmul_nt(left, right):
    return lax.dot_general(left, right, (((1,), (1,)), ((), ())), preferred_element_type=full)


def matmul_tn(left, right):
    return lax.dot_general(left, right, (((0,), (0,)), ((), ())), preferred_element_type=full)


def attend_forward(query_heads, key_heads, value_heads, allowed, score_scale):
    scores = jnp.einsum("qhd,khd->hqk", query_heads, key_heads, preferred_element_type=full)
    scores = jnp.where(allowed, scores * score_scale, -1e30)
    row_max = jnp.max(scores, axis=-1, keepdims=True)
    exponent = jnp.exp(scores - row_max)
    row_total = jnp.sum(exponent, axis=-1, keepdims=True)
    weights_low = (exponent / row_total).astype(low)
    attended = jnp.einsum("hqk,khd->qhd", weights_low, value_heads, preferred_element_type=full)
    return attended, row_max + jnp.log(row_total)


def attend_backward(
    query_heads, key_heads, value_heads, allowed, score_scale, log_total, grad_heads
):
    scores = jnp.einsum("qhd,khd->hqk", query_heads, key_heads, preferred_element_type=full)
    scores = jnp.where(allowed, scores * score_scale, -1e30)
    weights_full = jnp.exp(scores - log_total)
    weights_low = weights_full.astype(low)
    grad_value = jnp.einsum("hqk,qhd->khd", weights_low, grad_heads, preferred_element_type=full)
    grad_weights = jnp.einsum(
        "qhd,khd->hqk", grad_heads, value_heads, preferred_element_type=full
    )
    row_inner = jnp.sum(weights_full * grad_weights, axis=-1, keepdims=True)
    grad_scores = (weights_full * (grad_weights - row_inner)).astype(low)
    grad_query = (
        jnp.einsum("hqk,khd->qhd", grad_scores, key_heads, preferred_element_type=full)
        * score_scale
    )
    grad_key = (
        jnp.einsum("hqk,qhd->khd", grad_scores, query_heads, preferred_element_type=full)
        * score_scale
    )
    return grad_query, grad_key, grad_value


def per_device(
    latents,
    media,
    segment_ids,
    slot_map,
    gains,
    w_query,
    w_key,
    w_value,
    w_out,
    w_up,
    w_down,
    cotangent,
):
    dp = ("pair", "core")
    everywhere = ("section",) + dp
    section = lax.axis_index("section")
    section_count = lax.axis_size("section")
    dp_index = lax.axis_index(dp)
    dp_count = lax.axis_size("pair") * lax.axis_size("core")
    on_first = section // 2 == 0
    stride = dp_count // 2
    seq_rows = segment_ids.shape[1]
    slot_count = slot_map.shape[1]
    feature_width = latents.shape[1]
    latent_rows = latents.shape[0]
    slot_rows = latent_rows // section_count
    inner = w_query.shape[2] // 2
    heads = inner // HEAD_DIM
    score_scale = 1.0 / math.sqrt(HEAD_DIM)

    def pick(first, second):
        return jnp.where(on_first, first, second), jnp.where(on_first, second, first)

    def swapped(value, mask):
        pairs = [(source, source ^ mask) for source in range(section_count)]
        return lax.ppermute(value, "section", pairs)

    def other_core(value):
        return lax.ppermute(value, "core", [(0, 1), (1, 0)])

    def to_second(value):
        return lax.ppermute(value, "section", [(0, 2), (1, 3)])

    def to_first(value):
        return lax.ppermute(value, "section", [(2, 0), (3, 1)])

    def after(value, earlier):
        return lax.optimization_barrier((value, earlier))[0]

    def turn_pairs(span, flip, back):
        pairs = []
        for source in range(section_count):
            for index in range(dp_count):
                layer, half = divmod(source, 2)
                high, bit, lowest = index // (2 * span), index // span % 2, index % span
                moved = (2 * high + (layer ^ flip)) * span + lowest
                target = (bit * 2 + half) * dp_count + moved
                pair = (source * dp_count + index, target)
                pairs.append(pair[::-1] if back else pair)
        return pairs

    def first_bit(span):
        return dp_index // span % 2 == 0

    def exchange_rows(weight, span):
        half = weight.shape[0] // 2
        near, far = pick(weight[:half], weight[half:])
        first = lax.ppermute(near, everywhere, turn_pairs(span, 0, False))
        second = lax.ppermute(far, everywhere, turn_pairs(span, 1, False))
        chosen = first_bit(span)
        return jnp.where(chosen, first, second), jnp.where(chosen, second, first)

    def join_rows(first, second, span):
        chosen = first_bit(span)
        near = jnp.where(chosen, first, second)
        far = jnp.where(chosen, second, first)
        near = lax.ppermute(near, everywhere, turn_pairs(span, 0, True))
        far = lax.ppermute(far, everywhere, turn_pairs(span, 1, True))
        return jnp.concatenate(pick(near, far), axis=0).astype(full)

    def exchange_second(weight, span):
        half = weight.shape[0] // 2
        parts = []
        for bit in range(2):
            pairs = [
                pair
                for flip in range(2)
                for pair in turn_pairs(span, flip, False)
                if pair[0] >= 2 * dp_count and pair[1] // span % 2 == bit
            ]
            parts.append(lax.ppermute(weight[bit * half : (bit + 1) * half], everywhere, pairs))
        return jnp.where(first_bit(span), parts[0], parts[1])

    def join_second(piece, span):
        parts = []
        for bit in range(2):
            pairs = [
                pair[::-1]
                for flip in range(2)
                for pair in turn_pairs(span, flip, False)
                if pair[0] >= 2 * dp_count and pair[1] // span % 2 == bit
            ]
            parts.append(lax.ppermute(piece, everywhere, pairs))
        return jnp.concatenate(parts, axis=0)

    def in_rows(gathered, span):
        if span > 1:
            width = gathered.shape[1]
            gathered = gathered.reshape(-1, 2, span, gathered.shape[0] // dp_count, width)
            gathered = gathered.swapaxes(1, 2).reshape(-1, width)
        return gathered

    def in_shards(grad, span):
        if span > 1:
            width = grad.shape[1]
            grad = grad.reshape(-1, span, 2, grad.shape[0] // dp_count, width)
            grad = grad.swapaxes(1, 2).reshape(-1, width)
        return grad

    def fold(piece):
        blocks = [piece[:, i * inner : (i + 1) * inner] for i in range(feature_width // inner)]
        return jnp.concatenate(blocks, axis=0)

    def unfold(stacked):
        count = feature_width // inner
        blocks = stacked.reshape(2, stride, count, -1, inner).transpose(1, 0, 3, 2, 4)
        return blocks.reshape(-1, feature_width)

    def by_device(grad):
        blocks = grad.reshape(stride, 2, -1, feature_width).transpose(1, 0, 2, 3)
        return blocks.reshape(-1, feature_width)

    def sum_to_slots(partial):
        blocks = partial.astype(low).reshape(section_count, -1, feature_width)
        arrived = lax.all_to_all(blocks, "section", split_axis=0, concat_axis=0)
        return jnp.sum(arrived.astype(full), axis=0)

    def from_slots(rows):
        return lax.all_gather(rows, "section", axis=0, tiled=True)

    def to_columns(rows):
        moved = lax.all_to_all(
            rows.astype(low), "section", split_axis=1, concat_axis=0, tiled=True
        )
        return moved.astype(full)

    def from_sequences(rows):
        near = lax.all_gather(rows, "pair", axis=0, tiled=True)
        return jnp.concatenate([near, other_core(near)], axis=0)

    def sum_to_sequence(left, right, product):
        half = left.shape[0] // 2
        far = product(left[half:], right).astype(low)
        near = product(left[:half], right) + other_core(far).astype(full)
        blocks = near.astype(low).reshape(-1, slot_rows, feature_width)
        arrived = lax.all_to_all(blocks, "pair", split_axis=0, concat_axis=0)
        return jnp.sum(arrived.astype(full), axis=0)

    def by_distance(rows):
        half = rows.shape[0] // 2
        side = swapped(rows, 1)
        ahead = swapped(rows, 2)
        upper = swapped(side[:half], 2)
        lower = swapped(ahead[half:], 1)
        return rows, side, ahead, jnp.concatenate([upper, lower], axis=0)

    def sum_by_distance(own, side, ahead, across, gate=None):
        half = own.shape[0] // 2
        across = across.astype(low)
        upper = swapped(across[:half], 2)
        lower = swapped(across[half:], 1)
        if gate is not None:
            upper, lower = after((upper, lower), gate)
        side = jnp.concatenate([side[:half] + upper.astype(full), side[half:]], axis=0)
        ahead = jnp.concatenate([ahead[:half], ahead[half:] + lower.astype(full)], axis=0)
        side, ahead = side.astype(low), ahead.astype(low)
        return own + swapped(side, 1).astype(full) + swapped(ahead, 2).astype(full)

    def share_first(lower, upper):
        return jnp.where(on_first, lower, to_second(upper))

    def sum_over_sections(partial):
        blocks = partial.reshape(section_count, -1, feature_width)
        return sum_by_distance(
            *[
                lax.dynamic_index_in_dim(blocks, section ^ mask, 0, keepdims=False)
                for mask in range(4)
            ]
        )

    def gather_sections(rows):
        by_mask = by_distance(rows)
        ordered = []
        for target in range(section_count):
            chosen = by_mask[0]
            for mask in range(1, section_count):
                chosen = jnp.where(section ^ mask == target, by_mask[mask], chosen)
            ordered.append(chosen)
        return jnp.concatenate(ordered, axis=0)

    def column_parts(weight, block):
        rows, width = weight.shape
        split = weight.reshape(rows, width // (2 * block), 2, block)
        return split[:, :, 0].reshape(rows, -1), split[:, :, 1].reshape(rows, -1)

    def interleave(even, odd, block):
        rows, width = even.shape
        parts = [part.reshape(rows, width // block, 1, block) for part in (even, odd)]
        return jnp.concatenate(parts, axis=2).reshape(rows, 2 * width)

    halves = [pick(weight[0, :, :inner], weight[0, :, inner:]) for weight in (w_query, w_key, w_value)]
    own_heads = jnp.concatenate([half[0] for half in halves], axis=1)
    other_heads = swapped(jnp.concatenate([half[1] for half in halves], axis=1), 2)
    qkv_pieces = pick(own_heads, other_heads)
    half_hidden = w_down.shape[1] // 2
    half_depth = w_up.shape[1] // 2
    up_share = share_first(w_up[0, :half_depth], w_up[0, half_depth:])
    all_gains = after(gains, (other_heads, up_share))
    for axis in ("core", "pair", "section"):
        all_gains = lax.all_gather(all_gains, axis, axis=2, tiled=True)
    out_pieces = exchange_rows(after(w_out[0], other_heads), stride)

    def gather(piece):
        return lax.all_gather(piece, dp, axis=0, tiled=True)

    stacked = [
        gather(jnp.concatenate([qkv_pieces[layer], fold(out_pieces[layer])], axis=1))
        for layer in range(LAYERS)
    ]
    qkv_w = [weight[:, : 3 * inner] for weight in stacked]
    out_w = [unfold(weight[:, 3 * inner :]) for weight in stacked]

    up_turned = lax.all_to_all(up_share, dp, split_axis=1, concat_axis=0, tiled=True)
    down_share = share_first(
        *after((w_down[0, :half_hidden], w_down[0, half_hidden:]), other_heads)
    )

    def by_depth(rows):
        return rows.reshape(-1, dp_count, 2, half_depth).swapaxes(1, 2).reshape(rows.shape)

    def in_depth(rows):
        return rows.reshape(-1, 2, dp_count, half_depth).swapaxes(1, 2).reshape(rows.shape)

    def first_ffn(gate):
        down, up = after((down_share, up_turned), gate)
        down, up = by_distance(down), by_distance(up)
        return (
            jnp.concatenate(
                [
                    jnp.concatenate(pick(up[0], up[2]), axis=0),
                    jnp.concatenate(pick(up[1], up[3]), axis=0),
                ],
                axis=1,
            ),
            jnp.concatenate(pick(down[0], down[2]) + pick(down[1], down[3]), axis=0),
        )

    span = max(1, dp_count // 8)
    hidden_block = w_up.shape[2] // 8
    down_piece = exchange_second(after(w_down[0], all_gains), span)

    def second_ffn(gate):
        up_even, up_odd = column_parts(after(w_up[0], gate), hidden_block)
        return gather(jnp.where(on_first, to_first(up_even), up_odd))

    up_w = [None, None]
    down_w = [None, None]
    query_w = [weight[:, :inner] for weight in qkv_w]
    key_w = [weight[:, inner : 2 * inner] for weight in qkv_w]
    value_w = [weight[:, 2 * inner :] for weight in qkv_w]

    image_hot = segment_ids[:, :, None] == jnp.arange(slot_count, dtype=jnp.int32)[None, None, :]
    media_slot = jnp.sum(jnp.where(image_hot, slot_map[:, None, :], 0), axis=2) - (
        segment_ids < 0
    ).astype(jnp.int32)
    media_unit, media_inverse = unit_rows(media.astype(full))
    latent_slot = jnp.arange(latent_rows, dtype=jnp.int32) // LATENTS
    key_slot = jnp.concatenate([media_slot[0], latent_slot])
    allowed = latent_slot[None, :, None] == key_slot[None, None, :]

    def split_heads(rows):
        return rows.reshape(rows.shape[0], heads, HEAD_DIM)

    media_low = []
    media_key = []
    media_value = []
    for layer in range(LAYERS):
        media_low.append((media_unit * all_gains[layer, 0]).astype(low))
        media_key.append(matmul(media_low[layer], key_w[layer]).astype(low))
        media_value.append(matmul(media_low[layer], value_w[layer]).astype(low))

    down_second = in_rows(gather(down_piece), span)
    saved = []
    current = lax.dynamic_slice_in_dim(latents, section * slot_rows, slot_rows, 0).astype(full)
    grad_rows = lax.dynamic_slice_in_dim(cotangent, section * slot_rows, slot_rows, 0).astype(full)
    grad_low = cotangent
    for layer in range(LAYERS):
        unit_in, inverse_in = unit_rows(current)
        if layer == 0:
            whole_unit = unit_rows(latents.astype(full))[0]
            latent_low = (whole_unit * all_gains[layer, 1]).astype(low)
        else:
            latent_low = from_slots((unit_in * all_gains[layer, 1]).astype(low))
        projected = matmul(latent_low, qkv_w[layer]).astype(low)
        if layer == 0:
            up_w[0], down_w[0] = lax.optimization_barrier(first_ffn(projected))
            up_w[1], down_w[1] = second_ffn(projected), down_second
        query_low = projected[:, :inner]
        key_heads = split_heads(
            jnp.concatenate([media_key[layer], projected[:, inner : 2 * inner]], axis=0)
        )
        value_heads = split_heads(
            jnp.concatenate([media_value[layer], projected[:, 2 * inner :]], axis=0)
        )
        query_heads = split_heads(query_low)
        attended, log_total = attend_forward(
            query_heads, key_heads, value_heads, allowed, score_scale
        )
        attended_low = attended.reshape(-1, inner).astype(low)
        middle = current + sum_to_slots(matmul(attended_low, out_w[layer]))
        unit_mid, inverse_mid = unit_rows(middle)
        ffn_low = (unit_mid * all_gains[layer, 2]).astype(low)
        ffn_low = from_slots(ffn_low) if layer else from_sequences(by_depth(ffn_low))
        hidden_pre = matmul(ffn_low, up_w[layer])
        active_low = gelu_exact(hidden_pre).astype(low)
        if layer == 0:
            current = middle + sum_to_sequence(active_low, down_w[layer], matmul)
        saved.append(
            (
                unit_in,
                inverse_in,
                latent_low,
                query_heads,
                key_heads,
                value_heads,
                log_total,
                attended_low,
                unit_mid,
                inverse_mid,
                ffn_low,
                hidden_pre,
                active_low,
            )
        )

    def scatter(blocks):
        return lax.psum_scatter(blocks, dp, scatter_dimension=0, tiled=True)

    gain_rows = [None] * LAYERS
    media_parts = []
    media_gains = []

    def add_media(layer, grad_key, grad_value, gate):
        grad_key, grad_value = after((grad_key[:seq_rows], grad_value[:seq_rows]), gate)
        part = matmul_nt(grad_key, key_w[layer]) + matmul_nt(grad_value, value_w[layer])
        media_gains.append(jnp.sum(part * media_unit, axis=0))
        media_parts.append((part * all_gains[layer, 0]).astype(low if layer else full))

    pieces = [None] * LAYERS
    for layer in (1, 0):
        (
            unit_in,
            inverse_in,
            latent_low,
            query_heads,
            key_heads,
            value_heads,
            log_total,
            attended_low,
            unit_mid,
            inverse_mid,
            ffn_low,
            hidden_pre,
            active_low,
        ) = saved[layer]
        grad_active = matmul_nt(grad_low, down_w[layer])
        grad_hidden = (grad_active * gelu_slope(hidden_pre)).astype(low)
        if layer == 0:
            add_media(1, *media_grads, grad_hidden)
        down_grad = matmul_tn(active_low, grad_low)
        if layer:
            down_grad = down_grad.astype(low)
            grad_hidden = after(grad_hidden, down_grad)
        up_grad = matmul_tn(ffn_low, grad_hidden)
        if layer:
            ffn_pieces = (scatter(in_shards(down_grad, span)), scatter(up_grad.astype(low)))
            ffn_grad = sum_to_slots(matmul_nt(grad_hidden, up_w[layer]))
        else:
            ffn_grad = in_depth(sum_to_sequence(grad_hidden, up_w[layer], matmul_nt))
            blocks = down_grad.reshape(2, 2, half_hidden, feature_width)
            own, ahead = pick(blocks[0, 0], blocks[0, 1])
            side, across = pick(blocks[1, 0], blocks[1, 1])
            down_blocks = (own, side, ahead, across)
            width = up_grad.shape[1] // 2
            blocks = up_grad.reshape(2, -1, 2 * width)
            own, ahead = pick(blocks[0][:, :width], blocks[1][:, :width])
            side, across = pick(blocks[0][:, width:], blocks[1][:, width:])
            up_blocks = (own, side, ahead, across)
        gain_ffn_grad = jnp.sum(ffn_grad * unit_mid, axis=0)
        grad_middle = grad_rows + norm_back(
            unit_mid, inverse_mid, ffn_grad * all_gains[layer, 2]
        )
        middle_low = from_slots(grad_middle.astype(low))
        if layer == 0:
            up_half = sum_by_distance(*up_blocks, middle_low).astype(low)
            down_half = sum_by_distance(*down_blocks, middle_low).astype(low)
        grad_heads = split_heads(matmul_nt(middle_low, out_w[layer]).astype(low))
        out_grad = by_device(matmul_tn(attended_low, middle_low)).astype(low)
        out_piece = scatter(out_grad)
        grad_heads = after(grad_heads, out_grad)
        grad_query, grad_key, grad_value = attend_backward(
            query_heads, key_heads, value_heads, allowed, score_scale, log_total, grad_heads
        )
        grad_query = grad_query.reshape(-1, inner).astype(low)
        grad_key = grad_key.reshape(-1, inner).astype(low)
        grad_value = grad_value.reshape(-1, inner).astype(low)
        both_low = jnp.concatenate([media_low[layer], latent_low], axis=0)
        all_grads = jnp.concatenate(
            [jnp.pad(grad_query, ((seq_rows, 0), (0, 0))), grad_key, grad_value], axis=1
        )
        qkv_grad = matmul_tn(both_low, all_grads).astype(low)
        latent_part = (
            matmul_nt(grad_query, query_w[layer])
            + matmul_nt(grad_key[seq_rows:], key_w[layer])
            + matmul_nt(grad_value[seq_rows:], value_w[layer])
        )
        latent_grad_rows = sum_to_slots(latent_part)
        if layer:
            latent_grad_rows = after(latent_grad_rows, qkv_grad)
        gain_latent_grad = jnp.sum(latent_grad_rows * unit_in, axis=0)
        grad_rows = grad_middle + norm_back(
            unit_in, inverse_in, latent_grad_rows * all_gains[layer, 1]
        )
        if layer == 0:
            up_half, qkv_grad = lax.optimization_barrier((up_half, qkv_grad))
            up_half = lax.all_to_all(up_half, dp, split_axis=0, concat_axis=1, tiled=True)
        pieces[layer] = (scatter(qkv_grad), out_piece)
        if layer > 0:
            grad_low = from_sequences(grad_rows.astype(low))
            late = after(active_low, latent_part)
            here = (latent_slot == section)[:, None]
            kept = jnp.where(here, jnp.tile(middle, (section_count, 1)), 0.0)
            last = lax.optimization_barrier((matmul(late, down_w[layer]) + kept).astype(low))
            last = last.reshape(latent_rows, section_count, -1).swapaxes(0, 1)
            last = lax.all_to_all(last, "section", split_axis=0, concat_axis=0)
            latents_out = jnp.sum(last.astype(full), axis=0)
            grad_low = after(grad_low, latents_out)
            grad_low = after(grad_low, ffn_pieces)
        if layer == 0:
            add_media(0, grad_key, grad_value, qkv_grad)
        else:
            media_grads = (grad_key, grad_value)
        gain_rows[layer] = (gain_latent_grad, gain_ffn_grad)
    out_grad = join_rows(*[piece[1] for piece in pieces], stride)
    latent_grad = to_columns(after(grad_rows, (pieces[1], up_half)))
    media_rows = seq_rows // section_count
    media_sum = sum_over_sections(media_parts[0].astype(full) + media_parts[1])
    own_unit = lax.dynamic_slice_in_dim(media_unit, section * media_rows, media_rows, 0)
    own_inverse = lax.dynamic_slice_in_dim(media_inverse, section * media_rows, media_rows, 0)
    media_grad = gather_sections(norm_back(own_unit, own_inverse, media_sum).astype(low)).astype(
        full
    )
    gain_rows = [
        jnp.stack([media_gains[1 - layer], *gain_rows[layer]]) for layer in range(LAYERS)
    ]
    gain_parts = after(jnp.stack(gain_rows), media_sum).reshape(LAYERS, 3, section_count, -1)
    gain_parts = jnp.sum(
        lax.all_to_all(gain_parts, "section", split_axis=2, concat_axis=2), axis=2
    )
    gain_parts = gain_parts.reshape(LAYERS, 3, dp_count, -1)
    gain_grad = jnp.sum(lax.all_to_all(gain_parts, dp, split_axis=2, concat_axis=2), axis=2)

    qkv_parts = [piece[0] for piece in pieces]
    own, other = pick(qkv_parts[0], qkv_parts[1])
    lower, upper = pick(own, swapped(other, 2))
    qkv_grads = [
        jnp.concatenate(
            [lower[:, i * inner : (i + 1) * inner], upper[:, i * inner : (i + 1) * inner]], axis=1
        ).astype(full)
        for i in range(3)
    ]
    down_piece, up_piece = ffn_pieces
    up_second_grad = interleave(to_second(up_piece), up_piece, hidden_block)
    down_second_grad = join_second(down_piece, span)
    up_first_grad = jnp.concatenate([up_half, to_first(up_half)], axis=0)
    down_first_grad = jnp.concatenate([down_half, to_first(down_half)], axis=0)
    up_grad = jnp.where(on_first, up_first_grad, up_second_grad).astype(full)
    down_grad = jnp.where(on_first, down_first_grad, down_second_grad).astype(full)
    return (
        latents_out,
        latent_grad,
        media_grad,
        gain_grad,
        qkv_grads[0][None],
        qkv_grads[1][None],
        qkv_grads[2][None],
        out_grad[None],
        up_grad[None],
        down_grad[None],
    )


def solution(mesh):
    section_count, dp_count = mesh.devices.shape
    fine = Mesh(
        mesh.devices.reshape(section_count, dp_count // 2, 2), ("section", "pair", "core")
    )
    dp = ("pair", "core")
    placed = (
        P(dp, None),
        P(dp, None),
        P(dp, None),
        P(dp, None),
        P(None, None, ("section",) + dp),
        P("section", dp, None),
        P("section", dp, None),
        P("section", dp, None),
        P("section", dp, None),
        P("section", dp, None),
        P("section", dp, None),
        P(dp, None),
    )
    return jax.shard_map(
        per_device,
        mesh=fine,
        in_specs=placed,
        out_specs=(
            P(dp, "section"),
            P(dp, "section"),
            P(dp, None),
            P(None, None, ("section",) + dp),
            P("section", dp, None),
            P("section", dp, None),
            P("section", dp, None),
            P("section", dp, None),
            P("section", dp, None),
            P("section", dp, None),
        ),
        check_vma=False,
    )
```

```python
import math

import jax
import jax.numpy as jnp
from jax import lax
from jax.sharding import Mesh, PartitionSpec as P

HEAD_DIM = 96
LATENTS = 64
LAYERS = 2

epsilon = 1e-05
low = jnp.bfloat16
full = jnp.float32


def unit_rows(values):
    centered = values - jnp.mean(values, axis=-1, keepdims=True)
    variance = jnp.mean(centered * centered, axis=-1, keepdims=True)
    inverse = lax.rsqrt(variance + epsilon)
    return centered * inverse, inverse


def norm_back(unit, inverse, scaled):
    first = jnp.mean(scaled, axis=-1, keepdims=True)
    second = jnp.mean(scaled * unit, axis=-1, keepdims=True)
    return (scaled - first - unit * second) * inverse


def gelu_exact(values):
    return 0.5 * values * (1.0 + lax.erf(values * math.sqrt(0.5)))


def gelu_slope(values):
    normal = 0.5 * (1.0 + lax.erf(values * math.sqrt(0.5)))
    return normal + values * jnp.exp(-0.5 * values * values) * (1.0 / math.sqrt(2.0 * math.pi))


def matmul(left, right):
    return jnp.dot(left, right, preferred_element_type=full)


def matmul_nt(left, right):
    return lax.dot_general(left, right, (((1,), (1,)), ((), ())), preferred_element_type=full)


def matmul_tn(left, right):
    return lax.dot_general(left, right, (((0,), (0,)), ((), ())), preferred_element_type=full)


def attend_forward(query_heads, key_heads, value_heads, allowed, score_scale):
    scores = jnp.einsum("qhd,khd->hqk", query_heads, key_heads, preferred_element_type=full)
    scores = jnp.where(allowed, scores * score_scale, -1e30)
    row_max = jnp.max(scores, axis=-1, keepdims=True)
    exponent = jnp.exp(scores - row_max)
    row_total = jnp.sum(exponent, axis=-1, keepdims=True)
    weights_low = (exponent / row_total).astype(low)
    attended = jnp.einsum("hqk,khd->qhd", weights_low, value_heads, preferred_element_type=full)
    return attended, row_max + jnp.log(row_total)


def attend_backward(
    query_heads, key_heads, value_heads, allowed, score_scale, log_total, grad_heads
):
    scores = jnp.einsum("qhd,khd->hqk", query_heads, key_heads, preferred_element_type=full)
    scores = jnp.where(allowed, scores * score_scale, -1e30)
    weights_full = jnp.exp(scores - log_total)
    weights_low = weights_full.astype(low)
    grad_value = jnp.einsum("hqk,qhd->khd", weights_low, grad_heads, preferred_element_type=full)
    grad_weights = jnp.einsum(
        "qhd,khd->hqk", grad_heads, value_heads, preferred_element_type=full
    )
    row_inner = jnp.sum(weights_full * grad_weights, axis=-1, keepdims=True)
    grad_scores = (weights_full * (grad_weights - row_inner)).astype(low)
    grad_query = (
        jnp.einsum("hqk,khd->qhd", grad_scores, key_heads, preferred_element_type=full)
        * score_scale
    )
    grad_key = (
        jnp.einsum("hqk,qhd->khd", grad_scores, query_heads, preferred_element_type=full)
        * score_scale
    )
    return grad_query, grad_key, grad_value


def per_device(
    latents,
    media,
    segment_ids,
    slot_map,
    gains,
    w_query,
    w_key,
    w_value,
    w_out,
    w_up,
    w_down,
    cotangent,
):
    dp = ("pair", "core")
    everywhere = ("section",) + dp
    section = lax.axis_index("section")
    section_count = lax.axis_size("section")
    dp_index = lax.axis_index(dp)
    dp_count = lax.axis_size("pair") * lax.axis_size("core")
    on_first = section // 2 == 0
    stride = dp_count // 2
    seq_rows = segment_ids.shape[1]
    slot_count = slot_map.shape[1]
    feature_width = latents.shape[1]
    latent_rows = latents.shape[0]
    slot_rows = latent_rows // section_count
    inner = w_query.shape[2] // 2
    heads = inner // HEAD_DIM
    score_scale = 1.0 / math.sqrt(HEAD_DIM)

    def pick(first, second):
        return jnp.where(on_first, first, second), jnp.where(on_first, second, first)

    def swapped(value, mask):
        pairs = [(source, source ^ mask) for source in range(section_count)]
        return lax.ppermute(value, "section", pairs)

    def other_core(value):
        return lax.ppermute(value, "core", [(0, 1), (1, 0)])

    def to_second(value):
        return lax.ppermute(value, "section", [(0, 2), (1, 3)])

    def to_first(value):
        return lax.ppermute(value, "section", [(2, 0), (3, 1)])

    def after(value, earlier):
        return lax.optimization_barrier((value, earlier))[0]

    def turn_pairs(span, flip, back):
        pairs = []
        for source in range(section_count):
            for index in range(dp_count):
                layer, half = divmod(source, 2)
                high, bit, lowest = index // (2 * span), index // span % 2, index % span
                moved = (2 * high + (layer ^ flip)) * span + lowest
                target = (bit * 2 + half) * dp_count + moved
                pair = (source * dp_count + index, target)
                pairs.append(pair[::-1] if back else pair)
        return pairs

    def first_bit(span):
        return dp_index // span % 2 == 0

    def exchange_rows(weight, span):
        half = weight.shape[0] // 2
        near, far = pick(weight[:half], weight[half:])
        first = lax.ppermute(near, everywhere, turn_pairs(span, 0, False))
        second = lax.ppermute(far, everywhere, turn_pairs(span, 1, False))
        chosen = first_bit(span)
        return jnp.where(chosen, first, second), jnp.where(chosen, second, first)

    def join_rows(first, second, span):
        chosen = first_bit(span)
        near = jnp.where(chosen, first, second)
        far = jnp.where(chosen, second, first)
        near = lax.ppermute(near, everywhere, turn_pairs(span, 0, True))
        far = lax.ppermute(far, everywhere, turn_pairs(span, 1, True))
        return jnp.concatenate(pick(near, far), axis=0).astype(full)

    def exchange_second(weight, span):
        half = weight.shape[0] // 2
        parts = []
        for bit in range(2):
            pairs = [
                pair
                for flip in range(2)
                for pair in turn_pairs(span, flip, False)
                if pair[0] >= 2 * dp_count and pair[1] // span % 2 == bit
            ]
            parts.append(lax.ppermute(weight[bit * half : (bit + 1) * half], everywhere, pairs))
        return jnp.where(first_bit(span), parts[0], parts[1])

    def join_second(piece, span):
        parts = []
        for bit in range(2):
            pairs = [
                pair[::-1]
                for flip in range(2)
                for pair in turn_pairs(span, flip, False)
                if pair[0] >= 2 * dp_count and pair[1] // span % 2 == bit
            ]
            parts.append(lax.ppermute(piece, everywhere, pairs))
        return jnp.concatenate(parts, axis=0)

    def in_rows(gathered, span):
        if span > 1:
            width = gathered.shape[1]
            gathered = gathered.reshape(-1, 2, span, gathered.shape[0] // dp_count, width)
            gathered = gathered.swapaxes(1, 2).reshape(-1, width)
        return gathered

    def in_shards(grad, span):
        if span > 1:
            width = grad.shape[1]
            grad = grad.reshape(-1, span, 2, grad.shape[0] // dp_count, width)
            grad = grad.swapaxes(1, 2).reshape(-1, width)
        return grad

    def fold(piece):
        blocks = [piece[:, i * inner : (i + 1) * inner] for i in range(feature_width // inner)]
        return jnp.concatenate(blocks, axis=0)

    def unfold(stacked):
        count = feature_width // inner
        blocks = stacked.reshape(2, stride, count, -1, inner).transpose(1, 0, 3, 2, 4)
        return blocks.reshape(-1, feature_width)

    def by_device(grad):
        blocks = grad.reshape(stride, 2, -1, feature_width).transpose(1, 0, 2, 3)
        return blocks.reshape(-1, feature_width)

    def sum_to_slots(partial):
        blocks = partial.astype(low).reshape(section_count, -1, feature_width)
        arrived = lax.all_to_all(blocks, "section", split_axis=0, concat_axis=0)
        return jnp.sum(arrived.astype(full), axis=0)

    def from_slots(rows):
        return lax.all_gather(rows, "section", axis=0, tiled=True)

    def to_columns(rows):
        moved = lax.all_to_all(
            rows.astype(low), "section", split_axis=1, concat_axis=0, tiled=True
        )
        return moved.astype(full)

    def from_sequences(rows):
        near = lax.all_gather(rows, "pair", axis=0, tiled=True)
        return jnp.concatenate([near, other_core(near)], axis=0)

    def sum_to_sequence(left, right, product):
        half = left.shape[0] // 2
        far = product(left[half:], right).astype(low)
        near = product(left[:half], right) + other_core(far).astype(full)
        blocks = near.astype(low).reshape(-1, slot_rows, feature_width)
        arrived = lax.all_to_all(blocks, "pair", split_axis=0, concat_axis=0)
        return jnp.sum(arrived.astype(full), axis=0)

    def by_distance(rows):
        half = rows.shape[0] // 2
        side = swapped(rows, 1)
        ahead = swapped(rows, 2)
        upper = swapped(side[:half], 2)
        lower = swapped(ahead[half:], 1)
        return rows, side, ahead, jnp.concatenate([upper, lower], axis=0)

    def sum_by_distance(own, side, ahead, across, gate=None):
        half = own.shape[0] // 2
        across = across.astype(low)
        upper = swapped(across[:half], 2)
        lower = swapped(across[half:], 1)
        if gate is not None:
            upper, lower = after((upper, lower), gate)
        side = jnp.concatenate([side[:half] + upper.astype(full), side[half:]], axis=0)
        ahead = jnp.concatenate([ahead[:half], ahead[half:] + lower.astype(full)], axis=0)
        side, ahead = side.astype(low), ahead.astype(low)
        return own + swapped(side, 1).astype(full) + swapped(ahead, 2).astype(full)

    def share_first(lower, upper):
        return jnp.where(on_first, lower, to_second(upper))

    def sum_over_sections(partial):
        blocks = partial.reshape(section_count, -1, feature_width)
        return sum_by_distance(
            *[
                lax.dynamic_index_in_dim(blocks, section ^ mask, 0, keepdims=False)
                for mask in range(4)
            ]
        )

    def gather_sections(rows):
        by_mask = by_distance(rows)
        ordered = []
        for target in range(section_count):
            chosen = by_mask[0]
            for mask in range(1, section_count):
                chosen = jnp.where(section ^ mask == target, by_mask[mask], chosen)
            ordered.append(chosen)
        return jnp.concatenate(ordered, axis=0), by_mask[1]

    def column_parts(weight, block):
        rows, width = weight.shape
        split = weight.reshape(rows, width // (2 * block), 2, block)
        return split[:, :, 0].reshape(rows, -1), split[:, :, 1].reshape(rows, -1)

    def interleave(even, odd, block):
        rows, width = even.shape
        parts = [part.reshape(rows, width // block, 1, block) for part in (even, odd)]
        return jnp.concatenate(parts, axis=2).reshape(rows, 2 * width)

    halves = [pick(weight[0, :, :inner], weight[0, :, inner:]) for weight in (w_query, w_key, w_value)]
    own_heads = jnp.concatenate([half[0] for half in halves], axis=1)
    other_heads = swapped(jnp.concatenate([half[1] for half in halves], axis=1), 2)
    qkv_pieces = pick(own_heads, other_heads)
    half_hidden = w_down.shape[1] // 2
    half_depth = w_up.shape[1] // 2
    up_share = share_first(w_up[0, :half_depth], w_up[0, half_depth:])
    all_gains = after(gains, (other_heads, up_share))
    for axis in ("core", "pair", "section"):
        all_gains = lax.all_gather(all_gains, axis, axis=2, tiled=True)
    out_pieces = exchange_rows(after(w_out[0], other_heads), stride)

    def gather(piece):
        return lax.all_gather(piece, dp, axis=0, tiled=True)

    stacked = [
        gather(jnp.concatenate([qkv_pieces[layer], fold(out_pieces[layer])], axis=1))
        for layer in range(LAYERS)
    ]
    qkv_w = [weight[:, : 3 * inner] for weight in stacked]
    out_w = [unfold(weight[:, 3 * inner :]) for weight in stacked]

    up_turned = lax.all_to_all(up_share, dp, split_axis=1, concat_axis=0, tiled=True)
    down_share = share_first(
        *after((w_down[0, :half_hidden], w_down[0, half_hidden:]), other_heads)
    )

    def by_depth(rows):
        return rows.reshape(-1, dp_count, 2, half_depth).swapaxes(1, 2).reshape(rows.shape)

    def in_depth(rows):
        return rows.reshape(-1, 2, dp_count, half_depth).swapaxes(1, 2).reshape(rows.shape)

    def first_ffn(gate):
        down, up = after((down_share, up_turned), gate)
        down, up = by_distance(down), by_distance(up)
        return (
            jnp.concatenate(
                [
                    jnp.concatenate(pick(up[0], up[2]), axis=0),
                    jnp.concatenate(pick(up[1], up[3]), axis=0),
                ],
                axis=1,
            ),
            jnp.concatenate(pick(down[0], down[2]) + pick(down[1], down[3]), axis=0),
        )

    span = max(1, dp_count // 8)
    hidden_block = w_up.shape[2] // 8
    down_piece = exchange_second(after(w_down[0], all_gains), span)

    def second_ffn(gate):
        up_even, up_odd = column_parts(after(w_up[0], gate), hidden_block)
        return gather(jnp.where(on_first, to_first(up_even), up_odd))

    up_w = [None, None]
    down_w = [None, None]
    query_w = [weight[:, :inner] for weight in qkv_w]
    key_w = [weight[:, inner : 2 * inner] for weight in qkv_w]
    value_w = [weight[:, 2 * inner :] for weight in qkv_w]

    image_hot = segment_ids[:, :, None] == jnp.arange(slot_count, dtype=jnp.int32)[None, None, :]
    media_slot = jnp.sum(jnp.where(image_hot, slot_map[:, None, :], 0), axis=2) - (
        segment_ids < 0
    ).astype(jnp.int32)
    media_unit, media_inverse = unit_rows(media.astype(full))
    latent_slot = jnp.arange(latent_rows, dtype=jnp.int32) // LATENTS
    key_slot = jnp.concatenate([media_slot[0], latent_slot])
    allowed = latent_slot[None, :, None] == key_slot[None, None, :]

    def split_heads(rows):
        return rows.reshape(rows.shape[0], heads, HEAD_DIM)

    media_low = []
    media_key = []
    media_value = []
    for layer in range(LAYERS):
        media_low.append((media_unit * all_gains[layer, 0]).astype(low))
        media_key.append(matmul(media_low[layer], key_w[layer]).astype(low))
        media_value.append(matmul(media_low[layer], value_w[layer]).astype(low))

    down_second = in_rows(gather(down_piece), span)
    saved = []
    current = lax.dynamic_slice_in_dim(latents, section * slot_rows, slot_rows, 0).astype(full)
    grad_rows = lax.dynamic_slice_in_dim(cotangent, section * slot_rows, slot_rows, 0).astype(full)
    grad_low = cotangent
    for layer in range(LAYERS):
        unit_in, inverse_in = unit_rows(current)
        if layer == 0:
            whole_unit = unit_rows(latents.astype(full))[0]
            latent_low = (whole_unit * all_gains[layer, 1]).astype(low)
        else:
            latent_low = from_slots((unit_in * all_gains[layer, 1]).astype(low))
        projected = matmul(latent_low, qkv_w[layer]).astype(low)
        if layer == 0:
            up_w[0], down_w[0] = lax.optimization_barrier(first_ffn(projected))
            up_w[1], down_w[1] = second_ffn(projected), down_second
        query_low = projected[:, :inner]
        key_heads = split_heads(
            jnp.concatenate([media_key[layer], projected[:, inner : 2 * inner]], axis=0)
        )
        value_heads = split_heads(
            jnp.concatenate([media_value[layer], projected[:, 2 * inner :]], axis=0)
        )
        query_heads = split_heads(query_low)
        attended, log_total = attend_forward(
            query_heads, key_heads, value_heads, allowed, score_scale
        )
        attended_low = attended.reshape(-1, inner).astype(low)
        middle = current + sum_to_slots(matmul(attended_low, out_w[layer]))
        unit_mid, inverse_mid = unit_rows(middle)
        ffn_low = (unit_mid * all_gains[layer, 2]).astype(low)
        ffn_low = from_slots(ffn_low) if layer else from_sequences(by_depth(ffn_low))
        hidden_pre = matmul(ffn_low, up_w[layer])
        active_low = gelu_exact(hidden_pre).astype(low)
        if layer == 0:
            current = middle + sum_to_sequence(active_low, down_w[layer], matmul)
        saved.append(
            (
                unit_in,
                inverse_in,
                latent_low,
                query_heads,
                key_heads,
                value_heads,
                log_total,
                attended_low,
                unit_mid,
                inverse_mid,
                ffn_low,
                hidden_pre,
                active_low,
            )
        )

    def scatter(blocks):
        return lax.psum_scatter(blocks, dp, scatter_dimension=0, tiled=True)

    gain_rows = [None] * LAYERS
    media_parts = []
    media_gains = []

    def add_media(layer, grad_key, grad_value, gate):
        grad_key, grad_value = after((grad_key[:seq_rows], grad_value[:seq_rows]), gate)
        part = matmul_nt(grad_key, key_w[layer]) + matmul_nt(grad_value, value_w[layer])
        media_gains.append(jnp.sum(part * media_unit, axis=0))
        media_parts.append((part * all_gains[layer, 0]).astype(low if layer else full))

    pieces = [None] * LAYERS
    for layer in (1, 0):
        (
            unit_in,
            inverse_in,
            latent_low,
            query_heads,
            key_heads,
            value_heads,
            log_total,
            attended_low,
            unit_mid,
            inverse_mid,
            ffn_low,
            hidden_pre,
            active_low,
        ) = saved[layer]
        grad_active = matmul_nt(grad_low, down_w[layer])
        grad_hidden = (grad_active * gelu_slope(hidden_pre)).astype(low)
        if layer == 0:
            add_media(1, *media_grads, grad_hidden)
        down_grad = matmul_tn(active_low, grad_low)
        if layer:
            down_grad = down_grad.astype(low)
            grad_hidden = after(grad_hidden, down_grad)
        up_grad = matmul_tn(ffn_low, grad_hidden)
        if layer:
            ffn_pieces = (scatter(in_shards(down_grad, span)), scatter(up_grad.astype(low)))
            ffn_grad = sum_to_slots(matmul_nt(grad_hidden, up_w[layer]))
        else:
            ffn_grad = in_depth(sum_to_sequence(grad_hidden, up_w[layer], matmul_nt))
            blocks = down_grad.reshape(2, 2, half_hidden, feature_width)
            own, ahead = pick(blocks[0, 0], blocks[0, 1])
            side, across = pick(blocks[1, 0], blocks[1, 1])
            down_blocks = (own, side, ahead, across)
            width = up_grad.shape[1] // 2
            blocks = up_grad.reshape(2, -1, 2 * width)
            own, ahead = pick(blocks[0][:, :width], blocks[1][:, :width])
            side, across = pick(blocks[0][:, width:], blocks[1][:, width:])
            up_blocks = (own, side, ahead, across)
        gain_ffn_grad = jnp.sum(ffn_grad * unit_mid, axis=0)
        grad_middle = grad_rows + norm_back(
            unit_mid, inverse_mid, ffn_grad * all_gains[layer, 2]
        )
        middle_low = from_slots(grad_middle.astype(low))
        if layer == 0:
            up_half = sum_by_distance(*up_blocks, middle_low).astype(low)
            down_half = sum_by_distance(*down_blocks, middle_low).astype(low)
        grad_heads = split_heads(matmul_nt(middle_low, out_w[layer]).astype(low))
        out_grad = by_device(matmul_tn(attended_low, middle_low)).astype(low)
        out_piece = scatter(out_grad)
        grad_heads = after(grad_heads, out_grad)
        grad_query, grad_key, grad_value = attend_backward(
            query_heads, key_heads, value_heads, allowed, score_scale, log_total, grad_heads
        )
        grad_query = grad_query.reshape(-1, inner).astype(low)
        grad_key = grad_key.reshape(-1, inner).astype(low)
        grad_value = grad_value.reshape(-1, inner).astype(low)
        both_low = jnp.concatenate([media_low[layer], latent_low], axis=0)
        all_grads = jnp.concatenate(
            [jnp.pad(grad_query, ((seq_rows, 0), (0, 0))), grad_key, grad_value], axis=1
        )
        qkv_grad = matmul_tn(both_low, all_grads).astype(low)
        latent_part = (
            matmul_nt(grad_query, query_w[layer])
            + matmul_nt(grad_key[seq_rows:], key_w[layer])
            + matmul_nt(grad_value[seq_rows:], value_w[layer])
        )
        latent_grad_rows = sum_to_slots(latent_part)
        if layer:
            latent_grad_rows = after(latent_grad_rows, qkv_grad)
        gain_latent_grad = jnp.sum(latent_grad_rows * unit_in, axis=0)
        grad_rows = grad_middle + norm_back(
            unit_in, inverse_in, latent_grad_rows * all_gains[layer, 1]
        )
        if layer == 0:
            up_half, qkv_grad = lax.optimization_barrier((up_half, qkv_grad))
            up_half = lax.all_to_all(up_half, dp, split_axis=0, concat_axis=1, tiled=True)
        pieces[layer] = (scatter(qkv_grad), out_piece)
        if layer > 0:
            grad_low = from_sequences(grad_rows.astype(low))
            late = after(active_low, latent_part)
            here = (latent_slot == section)[:, None]
            kept = jnp.where(here, jnp.tile(middle, (section_count, 1)), 0.0)
            last = lax.optimization_barrier((matmul(late, down_w[layer]) + kept).astype(low))
            last = last.reshape(latent_rows, section_count, -1).swapaxes(0, 1)
            last = lax.all_to_all(last, "section", split_axis=0, concat_axis=0)
            latents_out = jnp.sum(last.astype(full), axis=0)
            grad_low = after(grad_low, latents_out)
            grad_low = after(grad_low, ffn_pieces)
        if layer == 0:
            add_media(0, grad_key, grad_value, qkv_grad)
        else:
            media_grads = (grad_key, grad_value)
        gain_rows[layer] = (gain_latent_grad, gain_ffn_grad)
    out_grad = join_rows(*[piece[1] for piece in pieces], stride)
    media_rows = seq_rows // section_count
    media_sum = sum_over_sections(media_parts[0].astype(full) + media_parts[1])
    own_unit = lax.dynamic_slice_in_dim(media_unit, section * media_rows, media_rows, 0)
    own_inverse = lax.dynamic_slice_in_dim(media_inverse, section * media_rows, media_rows, 0)
    media_grad, media_hop = gather_sections(norm_back(own_unit, own_inverse, media_sum).astype(low))
    media_grad = media_grad.astype(full)
    latent_grad = to_columns(after(grad_rows, (pieces[1], up_half, media_hop)))
    gain_rows = [
        jnp.stack([media_gains[1 - layer], *gain_rows[layer]]) for layer in range(LAYERS)
    ]
    gain_parts = after(jnp.stack(gain_rows), media_hop).reshape(LAYERS, 3, section_count, -1)
    gain_parts = jnp.sum(
        lax.all_to_all(gain_parts, "section", split_axis=2, concat_axis=2), axis=2
    )
    gain_parts = gain_parts.reshape(LAYERS, 3, dp_count, -1)
    gain_grad = jnp.sum(lax.all_to_all(gain_parts, dp, split_axis=2, concat_axis=2), axis=2)

    qkv_parts = [piece[0] for piece in pieces]
    own, other = pick(qkv_parts[0], qkv_parts[1])
    lower, upper = pick(own, swapped(other, 2))
    qkv_grads = [
        jnp.concatenate(
            [lower[:, i * inner : (i + 1) * inner], upper[:, i * inner : (i + 1) * inner]], axis=1
        ).astype(full)
        for i in range(3)
    ]
    down_piece, up_piece = ffn_pieces
    up_second_grad = interleave(to_second(up_piece), up_piece, hidden_block)
    down_second_grad = join_second(down_piece, span)
    up_first_grad = jnp.concatenate([up_half, to_first(up_half)], axis=0)
    down_first_grad = jnp.concatenate([down_half, to_first(down_half)], axis=0)
    up_grad = jnp.where(on_first, up_first_grad, up_second_grad).astype(full)
    down_grad = jnp.where(on_first, down_first_grad, down_second_grad).astype(full)
    return (
        latents_out,
        latent_grad,
        media_grad,
        gain_grad,
        qkv_grads[0][None],
        qkv_grads[1][None],
        qkv_grads[2][None],
        out_grad[None],
        up_grad[None],
        down_grad[None],
    )


def solution(mesh):
    section_count, dp_count = mesh.devices.shape
    fine = Mesh(
        mesh.devices.reshape(section_count, dp_count // 2, 2), ("section", "pair", "core")
    )
    dp = ("pair", "core")
    placed = (
        P(dp, None),
        P(dp, None),
        P(dp, None),
        P(dp, None),
        P(None, None, ("section",) + dp),
        P("section", dp, None),
        P("section", dp, None),
        P("section", dp, None),
        P("section", dp, None),
        P("section", dp, None),
        P("section", dp, None),
        P(dp, None),
    )
    return jax.shard_map(
        per_device,
        mesh=fine,
        in_specs=placed,
        out_specs=(
            P(dp, "section"),
            P(dp, "section"),
            P(dp, None),
            P(None, None, ("section",) + dp),
            P("section", dp, None),
            P("section", dp, None),
            P("section", dp, None),
            P("section", dp, None),
            P("section", dp, None),
            P("section", dp, None),
        ),
        check_vma=False,
    )
```
